32 devices in a mesh: dp: 8 (over y, x, core), mp: 4 (over z).
Axes of the slice: x: 2, y: 2, z: 4, core: 2. Of those that a mesh axis runs over, the one named last changes fastest.
Arguments:
- tokens: bfloat16 [16384, 1280], P(('dp', 'mp')), may hold values from -6 to 6
- segments: int32 [8, 2048], P('dp'), may hold values from 0 to 15, never falling along the last dimension, each value on 1 to 1024 neighbouring positions
- w_query: bfloat16 [1280, 1280], P('dp', 'mp'), may hold values from -0.15625 to 0.15625
- w_key: bfloat16 [1280, 1280], P('dp', 'mp'), may hold values from -0.15625 to 0.15625
- w_value: bfloat16 [1280, 1280], P('dp', 'mp'), may hold values from -0.15625 to 0.15625
- w_output: bfloat16 [1280, 1280], P('mp', 'dp'), may hold values from -1.25 to 1.25
- w_up: bfloat16 [1280, 1280], P('dp', 'mp'), may hold values from -0.15625 to 0.15625
- b_up: float32 [1280], P('mp'), may hold values from -3 to 3
- w_down: bfloat16 [1280, 1280], P('mp', 'dp'), may hold values from -0.25 to 0.25
- b_down: float32 [1280], replicated, may hold values from -3 to 3
- gain_attn: float32 [1280], replicated, may hold values from 0.5 to 1.5
- gain_mlp: float32 [1280], replicated, may hold values from 0.5 to 1.5
- query_scale: float32 [80], replicated, may hold values from -0.5 to 1
- cotangent: bfloat16 [16384, 1280], P(('dp', 'mp')), may hold values from -6 to 6
Outputs:
- layer_out: bfloat16 [16384, 1280], P(('dp', 'mp'))
- tokens_grad: bfloat16 [16384, 1280], P(('dp', 'mp'))
- grad_w_query: float32 [1280, 1280], P('dp', 'mp')
- grad_w_key: float32 [1280, 1280], P('dp', 'mp')
- grad_w_value: float32 [1280, 1280], P('dp', 'mp')
- grad_w_output: float32 [1280, 1280], P('mp', 'dp')
- grad_w_up: float32 [1280, 1280], P('dp', 'mp')
- grad_b_up: float32 [1280], P('mp')
- grad_w_down: float32 [1280, 1280], P('mp', 'dp')
- grad_b_down: float32 [1280], replicated
- grad_gain_attn: float32 [1280], replicated
- grad_gain_mlp: float32 [1280], replicated
- grad_query_scale: float32 [80], replicated
The draws below stay inside these ranges and needn't reach their ends.
Inputs may be any that keep to these rules, and one draw needn't show every extreme that they name: `segments`: within a sequence segment numbers never fall; documents are 1 to 1024 tokens long.
All inputs are finite; a program needn't handle non-finite values.
Results may differ from the reference program's by a relative error of at most 0.014.
Values may be sent and summed in bfloat16 or wider, within the bound.
A program may use at most 192 MiB of HBM per device.

```python
import math
import jax
import jax.numpy as jnp
import numpy as np
from jax import lax

D = 1280
HEADS = 16
HD = 80
FF = 1280
TOK_DEV = 2048
DOCS = 16
SEQS = 8
TOKENS = 16384


def levels(key, shape, cuts, least, top_value):
    level = 1.0
    for axis_at, parts in cuts:
        steps = jax.random.uniform(jax.random.fold_in(jax.random.fold_in(key, 6), axis_at), (parts,), jnp.float32, least / len(cuts), top_value / len(cuts))
        level = level * jnp.repeat(jnp.exp(steps), shape[axis_at] // parts).reshape((-1,) + (1,) * (len(shape) - 1 - axis_at))
    return level


def split_up(count, total, most, lean):
    weights = [(1 << 20) // math.isqrt(grade ** lean) + 1 for grade in range(2, count + 1)]
    surplus, counts = total - most - (count - 1), [1] * (count - 1)
    while surplus > 0:
        free = [i for i in range(count - 1) if counts[i] < most]
        whole, budget = sum([weights[i] for i in free]), surplus
        for i in free:
            addition = min(most - counts[i], max(1, budget * weights[i] // whole), surplus)
            counts[i] = counts[i] + addition
            surplus = surplus - addition
    return np.array([most] + counts)


def uneven(rng, count, total, most, lean):
    if count == 2:
        one = jax.random.randint(rng, (), max(1, total - most), min(most, total - 1) + 1)
        return jnp.stack([one, total - one])
    lengths = jnp.asarray(split_up(count, total, most, lean), jnp.int32)
    couples = (count - 1) // 2
    source_of, taker = lengths[1:1 + 2 * couples:2], lengths[2:2 + 2 * couples:2]
    slack = jnp.minimum(source_of - 1, most - taker)
    shifted = jax.random.randint(jax.random.fold_in(rng, 1), (couples,), 0, 1 << 20) % (slack + 1)
    lengths = lengths.at[1:1 + 2 * couples:2].set(source_of - shifted).at[2:2 + 2 * couples:2].set(taker + shifted)
    return lengths[jax.random.permutation(jax.random.fold_in(rng, 2), count)]


def bell_draw(rng, shape, width, reach, pieces=(), kind=jnp.bfloat16):
    entries = jax.random.normal(rng, shape, jnp.float32) * width
    if len(pieces) > 0:
        entries = levels(rng, shape, pieces, -0.22, 0.18) * entries
    return jnp.clip(entries, min=-reach, max=reach).astype(kind)


def setup_inputs(seed: int = 0) -> dict:
    key_list = jax.random.split(jax.random.key(seed), 15)
    return {
        "tokens": bell_draw(key_list[0], (TOKENS, D), 1.0, 6.0, ((0, 32),)),
        "segments": jax.vmap(lambda own: jnp.searchsorted(jnp.cumsum(uneven(own, DOCS, TOK_DEV, TOK_DEV // 2, 2)), jnp.arange(TOK_DEV), side="right"))(jax.random.split(key_list[1], SEQS)).reshape((SEQS, TOK_DEV)).astype(jnp.int32),
        "w_query": bell_draw(key_list[2], (D, HEADS * HD), D ** -0.5, 0.15625, ((0, 8), (1, 4))),
        "w_key": bell_draw(key_list[3], (D, HEADS * HD), D ** -0.5, 0.15625, ((0, 8), (1, 4))),
        "w_value": bell_draw(key_list[4], (D, HEADS * HD), D ** -0.5, 0.15625, ((0, 8), (1, 4))),
        "w_output": bell_draw(key_list[5], (HEADS * HD, D), (max(HEADS * HD // 64, 1)) ** -0.5, 1.25, ((0, 4), (1, 8))),
        "w_up": bell_draw(key_list[6], (D, FF), D ** -0.5, 0.15625, ((0, 8), (1, 4))),
        "b_up": bell_draw(key_list[7], (FF,), 0.5, 3.0, ((0, 4),), jnp.float32),
        "w_down": bell_draw(key_list[8], (FF, D), (FF // 2) ** -0.5, 0.25, ((0, 4), (1, 8))),
        "b_down": bell_draw(key_list[9], (D,), 0.5, 3.0, (), jnp.float32),
        "gain_attn": jnp.clip(1.0 + 0.1 * jax.random.normal(key_list[10], (D,), jnp.float32), 0.5, 1.5),
        "gain_mlp": jnp.clip(1.0 + 0.1 * jax.random.normal(key_list[11], (D,), jnp.float32), 0.5, 1.5),
        "query_scale": jnp.clip(jax.random.uniform(key_list[12], (HD,), jnp.float32, -0.5, 1.0), -0.5, 1.0),
        "cotangent": bell_draw(key_list[13], (TOKENS, D), 1.0, 6.0, ((0, 32),)),
    }


@jax.custom_vjp
def low(v):
    return lax.optimization_barrier(v.astype(jnp.bfloat16)).astype(jnp.float32)

@jax.custom_vjp
def low_back(v):
    return v

def low_keep(v):
    return (low(v), None)

def low_pass(kept, grad):
    return (grad,)

def back_keep(v):
    return (v, None)

def back_low(kept, grad):
    return (low(grad),)
low.defvjp(low_keep, low_pass)
low_back.defvjp(back_keep, back_low)
EPSILON = 1e-06
LOG2E = 1.442695
HIGHEST = lax.Precision.HIGHEST

def attend(scaled, keys, values, seg):
    length = scaled.shape[0]
    rows = min(512, length)
    count = length // rows

    def one_block(index):
        start = (index * rows).astype(jnp.int32)
        query_block = lax.dynamic_slice_in_dim(scaled, start, rows, 0)
        scores = jnp.einsum('qhd,khd->hqk', query_block, keys, precision=HIGHEST)
        scores = low_back(scores)
        pos_query = start + jnp.arange(rows, dtype=jnp.int32)
        pos_key = jnp.arange(length, dtype=jnp.int32)
        seg_query = lax.dynamic_slice_in_dim(seg, start, rows, 0)
        allowed = (pos_query[:, None] >= pos_key[None, :]) & (seg_query[:, None] == seg[None, :])
        scores = jnp.where(allowed[None], scores, -1e+30)
        top = lax.optimization_barrier(jnp.max(scores, axis=-1, keepdims=True))
        expo = jnp.exp(scores - top)
        probs = low(expo / lax.optimization_barrier(jnp.sum(expo, axis=-1, keepdims=True)))
        return jnp.einsum('hqk,khd->qhd', probs, values, precision=HIGHEST)
    outs = lax.map(jax.checkpoint(one_block), jnp.arange(count, dtype=jnp.int32))
    return outs.reshape(length, -1)

def layer(inputs, w_query, w_key, w_value, w_output, w_up, b_up, w_down, b_down, gain_attn, gain_mlp, query_scale, seg):
    length = inputs.shape[0]
    inv_first = lax.rsqrt(lax.optimization_barrier(jnp.mean(inputs * inputs, axis=-1, keepdims=True)) + EPSILON)
    normed_first = low(inputs * inv_first * gain_attn)
    query_raw = low_back(jnp.dot(normed_first, w_query, precision=HIGHEST))
    factor = jnp.tile(jax.nn.softplus(query_scale) * (LOG2E / math.sqrt(HD)), HEADS)
    scaled = low(low_back(query_raw * factor))
    keys = low(low_back(jnp.dot(normed_first, w_key, precision=HIGHEST)))
    values = low(low_back(jnp.dot(normed_first, w_value, precision=HIGHEST)))
    shape3 = (length, HEADS, HD)
    mixed = attend(scaled.reshape(shape3), keys.reshape(shape3), values.reshape(shape3), seg)
    mixed = low(low_back(mixed))
    hidden = inputs + low_back(jnp.dot(mixed, w_output, precision=HIGHEST))
    inv_second = lax.rsqrt(lax.optimization_barrier(jnp.mean(hidden * hidden, axis=-1, keepdims=True)) + EPSILON)
    normed_second = low(hidden * inv_second * gain_mlp)
    preact = low_back(jnp.dot(normed_second, w_up, precision=HIGHEST) + b_up)
    active = low(jax.nn.silu(preact))
    return hidden + low_back(jnp.dot(active, w_down, precision=HIGHEST)) + b_down

def reference(tokens, segments, w_query, w_key, w_value, w_output, w_up, b_up, w_down, b_down, gain_attn, gain_mlp, query_scale, cotangent):
    params = (w_query.astype(jnp.float32), w_key.astype(jnp.float32), w_value.astype(jnp.float32), w_output.astype(jnp.float32), w_up.astype(jnp.float32), b_up.astype(jnp.float32), w_down.astype(jnp.float32), b_down.astype(jnp.float32), gain_attn.astype(jnp.float32), gain_mlp.astype(jnp.float32), query_scale.astype(jnp.float32))
    inputs = tokens.astype(jnp.float32).reshape(SEQS, TOK_DEV, D)
    upstream = cotangent.astype(jnp.float32).reshape(SEQS, TOK_DEV, D)

    def one_sequence(totals, item):
        seq_in, seg, seq_up = item

        def forward(seq_x, *weights):
            return layer(seq_x, *weights, seg)
        result, pull = jax.vjp(forward, seq_in, *params)
        grads = pull(seq_up)
        totals = tuple((total + grad for total, grad in zip(totals, grads[1:])))
        return (totals, (result.astype(jnp.bfloat16), grads[0].astype(jnp.bfloat16)))
    start_totals = tuple((jnp.zeros(p.shape, jnp.float32) for p in params))
    totals, (outputs, input_grads) = lax.scan(one_sequence, start_totals, (inputs, segments, upstream))
    return (outputs.reshape(TOKENS, D), input_grads.reshape(TOKENS, D), totals[0], totals[1], totals[2], totals[3], totals[4], totals[5], totals[6], totals[7], totals[8], totals[9], totals[10])
```

```python
import functools
import math

import jax
import jax.numpy as jnp
from jax import lax
from jax.experimental import pallas as pl
from jax.experimental.pallas import tpu as pltpu
from jax.sharding import PartitionSpec as P

HD = 80
LANES = 128
EPSILON = 1e-06
LOG2E = 1.442695
DOC_MAX = 1024
GROUP = 8
FAR = -1e30
F32 = jnp.float32
BF16 = jnp.bfloat16


def dot(a, b, ca, cb):
    return lax.dot_general(a, b, (((ca,), (cb,)), ((), ())), preferred_element_type=F32)


def row_inverse(values):
    return lax.rsqrt(jnp.mean(values * values, axis=1, keepdims=True) + EPSILON)


def split_heads(src, dst, rows):
    def step(index, carry):
        at = pl.ds(pl.multiple_of(index * rows, rows), rows)
        block = src[at, :]
        pad = jnp.zeros((rows, LANES - HD), block.dtype)
        for h in range(GROUP):
            dst[h, at, :] = jnp.concatenate([block[:, HD * h : HD * (h + 1)], pad], axis=1)
        return carry

    lax.fori_loop(0, src.shape[0] // rows, step, 0)


def join_heads(src, dst, rows):
    def step(index, carry):
        at = pl.ds(pl.multiple_of(index * rows, rows), rows)
        dst[at, :] = jnp.concatenate([src[h, at, :HD] for h in range(GROUP)], axis=1)
        return carry

    lax.fori_loop(0, dst.shape[0] // rows, step, 0)


def fill_bias(low_ref, seg_query, seg_key, bias, block, own):
    count = seg_query.shape[1] // block
    for qb in range(count):
        row = seg_query[:, qb * block : (qb + 1) * block]
        pos_query = own + qb * block + lax.broadcasted_iota(jnp.int32, (block, block), 1)
        sub = lax.broadcasted_iota(jnp.int32, (block, block), 0)

        def step(kb, carry):
            at = pl.ds(pl.multiple_of(kb * block, block), block)
            allowed = (seg_key[at, :] == row) & (sub + kb * block <= pos_query)
            bias[qb, at, :] = jnp.where(allowed, 0.0, FAR)
            return carry

        lax.fori_loop(low_ref[qb], own // block + qb + 1, step, 0)


def forward_kernel(
    block, own, low_ref, q_ref, k_ref, v_ref, seg_query, seg_key, o_ref, lse_ref,
    qh, kh, vt, oh, bias, scores,
):
    count = q_ref.shape[0] // block

    @pl.when(pl.program_id(0) == 0)
    def _():
        fill_bias(low_ref, seg_query, seg_key, bias, block, own)

    split_heads(q_ref, qh, block)
    split_heads(k_ref, kh, block)

    def turn(kb, carry):
        at = pl.ds(pl.multiple_of(kb * block, block), block)
        tile = v_ref[at, :]
        pad = jnp.zeros((block, LANES - HD), tile.dtype)
        for h in range(GROUP):
            one = jnp.concatenate([tile[:, HD * h : HD * (h + 1)], pad], axis=1)
            vt[h, kb] = one.T
        return carry

    lax.fori_loop(0, k_ref.shape[0] // block, turn, 0)
    for qb in range(count):
        low, high = low_ref[qb], own // block + qb + 1
        span = pl.ds(qb * block, block)

        def head(h, carry):
            query = qh[h, span, :]

            def first(kb, top):
                at = pl.ds(pl.multiple_of(kb * block, block), block)
                s = dot(kh[h, at, :], query, 1, 1) + bias[qb, at, :]
                scores[at, :] = s
                return jnp.maximum(top, jnp.max(s.reshape(block // 8, 8, block), axis=0))

            top = lax.fori_loop(low, high, first, jnp.full((8, block), FAR, F32))
            top = jnp.max(top, axis=0, keepdims=True)

            def second(kb, state):
                total, acc = state
                at = pl.ds(pl.multiple_of(kb * block, block), block)
                p = jnp.exp(scores[at, :] - top)
                total = total + jnp.sum(p.reshape(block // 8, 8, block), axis=0)
                acc = acc + dot(vt[h, kb], p.astype(BF16), 1, 0)
                return total, acc

            total, acc = lax.fori_loop(
                low, high, second, (jnp.zeros((8, block), F32), jnp.zeros((LANES, block), F32))
            )
            total = jnp.sum(total, axis=0, keepdims=True)
            oh[h, span, :] = (acc / total).T.astype(BF16)
            lse_ref[pl.ds(h, 1), span] = top + jnp.log(total)
            return carry

        lax.fori_loop(0, GROUP, head, 0)
    join_heads(oh, o_ref, block)


def backward_kernel(
    block, own, low_ref, q_ref, k_ref, v_ref, g_ref, lse_ref, delta_ref, seg_query, seg_key,
    dq_ref, dk_ref, dv_ref, qh, gh, kh, vh, kt, dqh, dkh, dvh, dk_acc, dv_acc, bias,
):
    count = q_ref.shape[0] // block
    blocks = k_ref.shape[0] // block

    @pl.when(pl.program_id(0) == 0)
    def _():
        fill_bias(low_ref, seg_query, seg_key, bias, block, own)

    split_heads(q_ref, qh, block)
    split_heads(g_ref, gh, block)
    split_heads(k_ref, kh, block)
    split_heads(v_ref, vh, block)

    def head(h, carry):
        def turn(kb, inner):
            at = pl.ds(pl.multiple_of(kb * block, block), block)
            kt[kb] = kh[h, at, :].T
            dk_acc[at, :] = jnp.zeros((block, LANES), F32)
            dv_acc[at, :] = jnp.zeros((block, LANES), F32)
            return inner

        lax.fori_loop(0, blocks, turn, 0)
        for qb in range(count):
            span = pl.ds(qb * block, block)
            query, grad = qh[h, span, :], gh[h, span, :]
            lse, delta = lse_ref[pl.ds(h, 1), span], delta_ref[pl.ds(h, 1), span]

            def step(kb, acc):
                at = pl.ds(pl.multiple_of(kb * block, block), block)
                s = dot(kh[h, at, :], query, 1, 1) + bias[qb, at, :]
                p = jnp.exp(s - lse)
                dp = dot(vh[h, at, :], grad, 1, 1)
                ds = (p * (dp - delta)).astype(BF16)
                dv_acc[at, :] += dot(p.astype(BF16), grad, 1, 0)
                dk_acc[at, :] += dot(ds, query, 1, 0)
                return acc + dot(kt[kb], ds, 1, 0)

            acc = lax.fori_loop(
                low_ref[qb], own // block + qb + 1, step, jnp.zeros((LANES, block), F32)
            )
            dqh[h, span, :] = acc.T.astype(BF16)

        def keep(kb, inner):
            at = pl.ds(pl.multiple_of(kb * block, block), block)
            dkh[h, at, :] = dk_acc[at, :].astype(BF16)
            dvh[h, at, :] = dv_acc[at, :].astype(BF16)
            return inner

        lax.fori_loop(0, blocks, keep, 0)
        return carry

    lax.fori_loop(0, GROUP, head, 0)
    join_heads(dqh, dq_ref, block)
    join_heads(dkh, dk_ref, block)
    join_heads(dvh, dv_ref, block)


def attention_specs(rows, width, features):
    cols = GROUP * HD
    by_group = lambda n: pl.BlockSpec((n, cols), lambda g, low: (0, g))
    stats = pl.BlockSpec((GROUP, rows), lambda g, low: (g, 0))
    seg_q = pl.BlockSpec((1, rows), lambda g, low: (0, 0))
    seg_k = pl.BlockSpec((width, 1), lambda g, low: (0, 0))
    return by_group, stats, seg_q, seg_k


def attend_forward(low, q, k, v, seg_query, seg_key, block):
    rows, features = q.shape
    width = k.shape[0]
    by_group, stats, seg_q, seg_k = attention_specs(rows, width, features)
    heads = features // HD
    return pl.pallas_call(
        functools.partial(forward_kernel, block, width - rows),
        grid_spec=pltpu.PrefetchScalarGridSpec(
            num_scalar_prefetch=1,
            grid=(heads // GROUP,),
            in_specs=[by_group(rows), by_group(width), by_group(width), seg_q, seg_k],
            out_specs=[by_group(rows), stats],
            scratch_shapes=[
                pltpu.VMEM((GROUP, rows, LANES), BF16),
                pltpu.VMEM((GROUP, width, LANES), BF16),
                pltpu.VMEM((GROUP, width // block, LANES, block), BF16),
                pltpu.VMEM((GROUP, rows, LANES), BF16),
                pltpu.VMEM((rows // block, width, block), F32),
                pltpu.VMEM((width, block), F32),
            ],
        ),
        out_shape=[
            jax.ShapeDtypeStruct((rows, features), BF16),
            jax.ShapeDtypeStruct((heads, rows), F32),
        ],
        compiler_params=pltpu.CompilerParams(vmem_limit_bytes=48 << 20),
        cost_estimate=pl.CostEstimate(
            flops=4 * rows * width * features, bytes_accessed=4 * (rows + width) * features,
            transcendentals=rows * width * heads,
        ),
        name="attend_forward",
    )(low, q, k, v, seg_query, seg_key)


def attend_backward(low, q, k, v, grad, lse, delta, seg_query, seg_key, block):
    rows, features = q.shape
    width = k.shape[0]
    by_group, stats, seg_q, seg_k = attention_specs(rows, width, features)
    heads = features // HD
    return pl.pallas_call(
        functools.partial(backward_kernel, block, width - rows),
        grid_spec=pltpu.PrefetchScalarGridSpec(
            num_scalar_prefetch=1,
            grid=(heads // GROUP,),
            in_specs=[
                by_group(rows), by_group(width), by_group(width), by_group(rows),
                stats, stats, seg_q, seg_k,
            ],
            out_specs=[by_group(rows), by_group(width), by_group(width)],
            scratch_shapes=[
                pltpu.VMEM((GROUP, rows, LANES), BF16),
                pltpu.VMEM((GROUP, rows, LANES), BF16),
                pltpu.VMEM((GROUP, width, LANES), BF16),
                pltpu.VMEM((GROUP, width, LANES), BF16),
                pltpu.VMEM((width // block, LANES, block), BF16),
                pltpu.VMEM((GROUP, rows, LANES), BF16),
                pltpu.VMEM((GROUP, width, LANES), BF16),
                pltpu.VMEM((GROUP, width, LANES), BF16),
                pltpu.VMEM((width, LANES), F32),
                pltpu.VMEM((width, LANES), F32),
                pltpu.VMEM((rows // block, width, block), F32),
            ],
        ),
        out_shape=[
            jax.ShapeDtypeStruct((rows, features), BF16),
            jax.ShapeDtypeStruct((width, features), BF16),
            jax.ShapeDtypeStruct((width, features), BF16),
        ],
        compiler_params=pltpu.CompilerParams(vmem_limit_bytes=56 << 20),
        cost_estimate=pl.CostEstimate(
            flops=10 * rows * width * features, bytes_accessed=6 * (rows + width) * features,
            transcendentals=rows * width * heads,
        ),
        name="attend_backward",
    )(low, q, k, v, grad, lse, delta, seg_query, seg_key)


def gather_weight(block, row_axis, col_axis):
    wide = lax.all_gather(block, "mp", axis=1 if col_axis == "mp" else 0, tiled=True)
    return lax.all_gather(wide, "dp", axis=1 if col_axis == "dp" else 0, tiled=True)


def scatter_grad(grad, row_axis, col_axis):
    low = grad.astype(BF16)
    mine = lax.psum_scatter(low, "dp", scatter_dimension=1 if col_axis == "dp" else 0, tiled=True)
    mine = lax.psum_scatter(mine, "mp", scatter_dimension=1 if col_axis == "mp" else 0, tiled=True)
    return mine.astype(F32)


def body(
    tokens, segments, w_query, w_key, w_value, w_output, w_up, b_up, w_down, b_down,
    gain_attn, gain_mlp, query_scale, cotangent,
):
    stages = lax.axis_size("mp")
    z = lax.axis_index("mp")
    seg = segments[0]
    rows, features = tokens.shape
    back = min(stages - 1, -(-(DOC_MAX - 1) // rows))
    own = back * rows
    block = min(256, rows)
    up = [(i, i + 1) for i in range(stages - 1)]
    down = [(i + 1, i) for i in range(stages - 1)]

    wq, wk, wv, wu = (
        gather_weight(w, "dp", "mp") for w in (w_query, w_key, w_value, w_up)
    )
    wo, wd = (gather_weight(w, "mp", "dp") for w in (w_output, w_down))
    b_full = lax.all_gather(b_up, "mp", axis=0, tiled=True)

    inputs = tokens.astype(F32)
    inv_first = row_inverse(inputs)
    normed = (inputs * inv_first * gain_attn).astype(BF16)
    window = [normed]
    for _ in range(back):
        window.append(lax.ppermute(window[-1], "mp", up))
    first = jnp.concatenate(window[::-1], axis=0)

    seg_wide = jnp.concatenate([jnp.full((own,), -1, jnp.int32), seg])
    seg_window = lax.dynamic_slice_in_dim(seg_wide, z * rows, own + rows, 0)
    seg_query = seg_window[own:]
    heads_of_block = seg_query[::block]
    low = jnp.sum(seg_window[None, :] < heads_of_block[:, None], axis=1, dtype=jnp.int32) // block
    seg_query, seg_key = seg_query[None, :], seg_window[:, None]

    heads = features // HD
    factor = jax.nn.softplus(query_scale) * (LOG2E / math.sqrt(HD))
    factor_cols = jnp.tile(factor, heads)
    query_raw = jnp.dot(normed, wq, preferred_element_type=F32)
    scaled = (query_raw * factor_cols).astype(BF16)
    keys = jnp.dot(first, wk, preferred_element_type=F32).astype(BF16)
    values = jnp.dot(first, wv, preferred_element_type=F32).astype(BF16)
    mixed, lse = attend_forward(low, scaled, keys, values, seg_query, seg_key, block)

    hidden = inputs + jnp.dot(mixed, wo, preferred_element_type=F32)
    inv_second = row_inverse(hidden)
    second = (hidden * inv_second * gain_mlp).astype(BF16)
    preact = jnp.dot(second, wu, preferred_element_type=F32) + b_full
    active = jax.nn.silu(preact).astype(BF16)
    layer_out = (hidden + jnp.dot(active, wd, preferred_element_type=F32) + b_down).astype(BF16)

    upstream = cotangent.astype(F32)
    sigma = jax.nn.sigmoid(preact)
    d_active = dot(cotangent, wd, 1, 1)
    d_preact = (d_active * sigma * (1.0 + preact * (1.0 - sigma))).astype(BF16)
    d_second = dot(d_preact, wu, 1, 1)
    weighted = d_second * gain_mlp
    dots = jnp.sum(weighted * hidden, axis=1, keepdims=True)
    cube = inv_second * inv_second * inv_second
    d_hidden = upstream + inv_second * weighted - hidden * cube / features * dots
    d_attn = d_hidden.astype(BF16)
    d_mixed = dot(d_attn, wo, 1, 1).astype(BF16)

    owner = (jnp.arange(features)[None, :] // HD == jnp.arange(heads)[:, None]).astype(F32)
    delta = lax.dot_general(
        owner, d_mixed.astype(F32) * mixed.astype(F32), (((1,), (1,)), ((), ())),
        precision=lax.Precision.HIGHEST, preferred_element_type=F32,
    )
    d_scaled, d_keys, d_values = attend_backward(
        low, scaled, keys, values, d_mixed, lse, delta, seg_query, seg_key, block
    )
    d_scaled_wide = d_scaled.astype(F32)
    d_query = (d_scaled_wide * factor_cols).astype(BF16)
    scale_part = jnp.sum(jnp.sum(d_scaled_wide * query_raw, axis=0).reshape(heads, HD), axis=0)

    part = None
    for c in range(back + 1):
        at = slice(c * rows, (c + 1) * rows)
        term = dot(d_keys[at], wk, 1, 1) + dot(d_values[at], wv, 1, 1)
        if c == back:
            term = term + dot(d_query, wq, 1, 1)
        if part is not None:
            term = term + part
        if c < back:
            part = lax.ppermute(term.astype(BF16), "mp", down).astype(F32)
    d_first = term

    weighted_first = d_first * gain_attn
    cube_first = inv_first * inv_first * inv_first
    first_dots = jnp.sum(weighted_first * inputs, axis=1, keepdims=True)
    tokens_grad = (
        d_hidden + inv_first * weighted_first - inputs * cube_first / features * first_dots
    ).astype(BF16)

    grad_gain_attn = jnp.sum(d_first * inputs * inv_first, axis=0)
    grad_gain_mlp = jnp.sum(d_second * hidden * inv_second, axis=0)
    grad_b_up = jnp.sum(d_preact.astype(F32), axis=0)
    sums = jnp.concatenate(
        [grad_gain_mlp, jnp.sum(upstream, axis=0), grad_b_up, grad_gain_attn, scale_part]
    )
    sums = lax.psum(sums, ("dp", "mp"))
    sum_gain_mlp, sum_b_down, sum_b_up, sum_gain_attn, scale_total = jnp.split(
        sums, [features, 2 * features, 3 * features, 4 * features]
    )
    mine = b_up.shape[0]
    sum_b_up = lax.dynamic_slice_in_dim(sum_b_up, z * mine, mine, 0)
    grad_query_scale = scale_total * (LOG2E / math.sqrt(HD)) * jax.nn.sigmoid(query_scale)

    grads = (
        scatter_grad(dot(normed, d_query, 0, 0), "dp", "mp"),
        scatter_grad(dot(first, d_keys, 0, 0), "dp", "mp"),
        scatter_grad(dot(first, d_values, 0, 0), "dp", "mp"),
        scatter_grad(dot(mixed, d_attn, 0, 0), "mp", "dp"),
        scatter_grad(dot(second, d_preact, 0, 0), "dp", "mp"),
        scatter_grad(dot(active, cotangent, 0, 0), "mp", "dp"),
    )
    return (
        layer_out, tokens_grad, grads[0], grads[1], grads[2], grads[3], grads[4], sum_b_up,
        grads[5], sum_b_down, sum_gain_attn, sum_gain_mlp, grad_query_scale,
    )


def solution(mesh):
    tokens, rows_dp, rows_mp = P(("dp", "mp"), None), P("dp", "mp"), P("mp", "dp")
    return jax.shard_map(
        body,
        mesh=mesh,
        in_specs=(
            tokens, P("dp", None), rows_dp, rows_dp, rows_dp, rows_mp, rows_dp, P("mp"), rows_mp,
            P(), P(), P(), P(), tokens,
        ),
        out_specs=(
            tokens, tokens, rows_dp, rows_dp, rows_dp, rows_mp, rows_dp, P("mp"), rows_mp,
            P(), P(), P(), P(),
        ),
        check_vma=False,
    )
```

```python
import functools
import math

import jax
import jax.numpy as jnp
from jax import lax
from jax.experimental import pallas as pl
from jax.experimental.pallas import tpu as pltpu
from jax.sharding import PartitionSpec as P

HD = 80
LANES = 128
EPSILON = 1e-06
LOG2E = 1.442695
DOC_MAX = 1024
FAR = -1e30
F32 = jnp.float32
BF16 = jnp.bfloat16


def dot(a, b, ca, cb):
    return lax.dot_general(a, b, (((ca,), (cb,)), ((), ())), preferred_element_type=F32)


def row_inverse(values):
    return lax.rsqrt(jnp.mean(values * values, axis=1, keepdims=True) + EPSILON)


def spans(rows, width, block):
    own = width - rows
    out=[]
    for qb in range(rows//block):
        hi = own + (qb+1)*block
        lo = max(0, (own + qb*block - (DOC_MAX-1))//block*block)
        out.append((lo,hi))
    return out

def head_lanes(h, features):
    first = h*HD
    off = jnp.minimum(lax.div(first, LANES)*LANES, features-2*LANES)
    off = pl.multiple_of(off, LANES)
    lane = lax.broadcasted_iota(jnp.int32,(1,2*LANES),1) + (off-first)
    return pl.ds(off, 2*LANES), (lane>=0)&(lane<HD)

def fill_bias(seg_query, seg_key, bias, block, own):
    rows = seg_query.shape[1]; width=seg_key.shape[0]
    for kb in range(width//block):
        for qb in range(rows//block):
            row = seg_query[:, qb*block:(qb+1)*block]
            col = seg_key[kb*block:(kb+1)*block,:]
            ahead = (lax.broadcasted_iota(jnp.int32,(block,block),0)+(kb*block)) <= (lax.broadcasted_iota(jnp.int32,(block,block),1)+(own+qb*block))
            bias[kb*block:(kb+1)*block, qb*block:(qb+1)*block] = jnp.where((col==row)&ahead, 0.0, FAR)

def transpose_out(src, dst):
    for i in range(src.shape[0]//LANES):
        at = slice(i*LANES,(i+1)*LANES)
        dst[:, at] = src[at,:].T.astype(dst.dtype)

def forward_kernel(block, q_ref, k_ref, vt_ref, seg_query, seg_key, o_ref, lse_ref, ot, bias, scores, tops):
    rows, features = q_ref.shape; width=k_ref.shape[0]; own=width-rows
    fill_bias(seg_query, seg_key, bias, block, own)
    sp = spans(rows,width,block)
    heads = features//HD
    tiles=[]
    for kb in range(width//block):
        qs=[i for i,(lo,hi) in enumerate(sp) if lo<=kb*block<hi]
        if qs: tiles.append((kb,qs))
    def score(h, slot):
        lanes, mine = head_lanes(h, features)
        query = jnp.where(mine, q_ref[:, lanes], jnp.zeros((), BF16))
        top=[jnp.full((8,block),FAR,F32) for _ in sp]
        for kb,qs in tiles:
            qa, qz = qs[0]*block, (qs[-1]+1)*block
            at = slice(kb*block,(kb+1)*block)
            s = dot(k_ref[at,lanes], query[qa:qz],1,1) + bias[at,qa:qz]
            scores[slot, at, qa:qz] = s
            for i in qs:
                top[i] = jnp.maximum(top[i], jnp.max(s[:, i*block-qa:(i+1)*block-qa].reshape(block//8,8,block),axis=0))
        for i in range(len(sp)):
            tops[slot, :, i*block:(i+1)*block] = jnp.max(top[i],axis=0,keepdims=True)
    def head(h, carry):
        slot = lax.rem(h,2)
        score(h, slot)
        feats = pl.ds(pl.multiple_of(h*HD,16), HD)
        top = tops[slot]
        acc=[jnp.zeros((HD,block),F32) for _ in sp]; total=[jnp.zeros((8,block),F32) for _ in sp]
        for kb,qs in tiles:
            qa, qz = qs[0]*block, (qs[-1]+1)*block
            at = slice(kb*block,(kb+1)*block)
            p = jnp.exp(scores[slot, at, qa:qz] - top[:,qa:qz])
            part = dot(vt_ref[feats,at], p.astype(BF16), 1, 0)
            for i in qs:
                cut = slice(i*block-qa,(i+1)*block-qa)
                total[i] = total[i] + jnp.sum(p[:,cut].reshape(block//8,8,block),axis=0)
                acc[i] = acc[i] + part[:,cut]
        for i in range(len(sp)):
            at = slice(i*block,(i+1)*block)
            one = jnp.sum(total[i],axis=0,keepdims=True)
            ot[feats, at] = acc[i] / one
            lse_ref[pl.ds(h,1), at] = top[:,at] + jnp.log(one)
        return carry
    lax.fori_loop(0, heads, head, 0)
    transpose_out(ot, o_ref)

def attend_forward(q,k,vt,seg_q,seg_k,block):
    rows,features=q.shape; width=k.shape[0]
    return pl.pallas_call(functools.partial(forward_kernel, block),
        out_shape=[jax.ShapeDtypeStruct((rows,features),BF16), jax.ShapeDtypeStruct((features//HD,rows),F32)],
        scratch_shapes=[pltpu.VMEM((features,rows),F32), pltpu.VMEM((width,rows),F32), pltpu.VMEM((2,width,rows),F32), pltpu.VMEM((2,1,rows),F32)],
        compiler_params=pltpu.CompilerParams(vmem_limit_bytes=56<<20), name="attend_forward")(q,k,vt,seg_q,seg_k)

def backward_kernel(block, q_ref,k_ref,kt_ref,v_ref,g_ref,lse_ref,delta_ref,seg_query,seg_key,dq_ref,dk_ref,dv_ref,dqt,bias):
    rows, features = q_ref.shape; width=k_ref.shape[0]; own=width-rows
    fill_bias(seg_query, seg_key, bias, block, own)
    dk_ref[...] = jnp.zeros_like(dk_ref); dv_ref[...] = jnp.zeros_like(dv_ref)
    sp = spans(rows,width,block)
    def head(h, carry):
        lanes, mine = head_lanes(h, features)
        feats = pl.ds(pl.multiple_of(h*HD,16), HD)
        zero = jnp.zeros((), BF16)
        query = jnp.where(mine, q_ref[:, lanes], zero)
        grad = jnp.where(mine, g_ref[:, lanes], zero)
        lse = lse_ref[pl.ds(h,1),:]; delta=delta_ref[pl.ds(h,1),:]
        acc = [jnp.zeros((HD,block),F32) for _ in sp]
        for kb in range(width//block):
            qs=[i for i,(lo,hi) in enumerate(sp) if lo<=kb*block<hi]
            if not qs: continue
            qa, qz = qs[0]*block, (qs[-1]+1)*block
            at = slice(kb*block,(kb+1)*block)
            s = dot(k_ref[at,lanes], query[qa:qz],1,1) + bias[at,qa:qz]
            p = jnp.exp(s - lse[:,qa:qz])
            dp = dot(v_ref[at,lanes], grad[qa:qz],1,1)
            ds = (p*(dp-delta[:,qa:qz])).astype(BF16)
            dv_ref[at,lanes] += dot(p.astype(BF16), grad[qa:qz],1,0).astype(BF16)
            dk_ref[at,lanes] += dot(ds, query[qa:qz],1,0).astype(BF16)
            part = dot(kt_ref[feats,at], ds, 1, 0)
            for i in qs:
                acc[i] = acc[i] + part[:, i*block-qa:(i+1)*block-qa]
        for i in range(len(sp)):
            dqt[feats, i*block:(i+1)*block] = acc[i]
        return carry
    lax.fori_loop(0, features//HD, head, 0)
    transpose_out(dqt, dq_ref)

def attend_backward(q,k,kt,v,g,lse,delta,seg_q,seg_k,block):
    rows,features=q.shape; width=k.shape[0]
    return pl.pallas_call(functools.partial(backward_kernel, block),
        out_shape=[jax.ShapeDtypeStruct((rows,features),BF16), jax.ShapeDtypeStruct((width,features),BF16), jax.ShapeDtypeStruct((width,features),BF16)],
        scratch_shapes=[pltpu.VMEM((features,rows),F32), pltpu.VMEM((width,rows),F32)],
        compiler_params=pltpu.CompilerParams(vmem_limit_bytes=60<<20), name="attend_backward")(q,k,kt,v,g,lse,delta,seg_q,seg_k)

def gather_weight(block, row_axis, col_axis):
    wide = lax.all_gather(block, "mp", axis=1 if col_axis == "mp" else 0, tiled=True)
    return lax.all_gather(wide, "dp", axis=1 if col_axis == "dp" else 0, tiled=True)


def scatter_grad(grad, row_axis, col_axis):
    low = grad.astype(BF16)
    mine = lax.psum_scatter(low, "dp", scatter_dimension=1 if col_axis == "dp" else 0, tiled=True)
    mine = lax.psum_scatter(mine, "mp", scatter_dimension=1 if col_axis == "mp" else 0, tiled=True)
    return mine.astype(F32)


def body(
    tokens, segments, w_query, w_key, w_value, w_output, w_up, b_up, w_down, b_down,
    gain_attn, gain_mlp, query_scale, cotangent,
):
    stages = lax.axis_size("mp")
    z = lax.axis_index("mp")
    seg = segments[0]
    rows, features = tokens.shape
    back = min(stages - 1, -(-(DOC_MAX - 1) // rows))
    own = back * rows
    block = min(256, rows)
    up = [(i, i + 1) for i in range(stages - 1)]
    down = [(i + 1, i) for i in range(stages - 1)]

    wq, wk, wv, wu = (
        gather_weight(w, "dp", "mp") for w in (w_query, w_key, w_value, w_up)
    )
    wo, wd = (gather_weight(w, "mp", "dp") for w in (w_output, w_down))
    b_full = lax.all_gather(b_up, "mp", axis=0, tiled=True)

    inputs = tokens.astype(F32)
    inv_first = row_inverse(inputs)
    normed = (inputs * inv_first * gain_attn).astype(BF16)
    window = [normed]
    for _ in range(back):
        window.append(lax.ppermute(window[-1], "mp", up))
    first = jnp.concatenate(window[::-1], axis=0)

    seg_wide = jnp.concatenate([jnp.full((own,), -1, jnp.int32), seg])
    seg_window = lax.dynamic_slice_in_dim(seg_wide, z * rows, own + rows, 0)
    seg_query = seg_window[own:]
    seg_query, seg_key = seg_query[None, :], seg_window[:, None]

    heads = features // HD
    factor = jax.nn.softplus(query_scale) * (LOG2E / math.sqrt(HD))
    factor_cols = jnp.tile(factor, heads)
    query_raw = jnp.dot(normed, wq, preferred_element_type=F32)
    scaled = (query_raw * factor_cols).astype(BF16)
    keys = jnp.dot(first, wk, preferred_element_type=F32).astype(BF16)
    values = jnp.dot(first, wv, preferred_element_type=F32).astype(BF16)
    mixed, lse = attend_forward(scaled, keys, values.T, seg_query, seg_key, block)

    hidden = inputs + jnp.dot(mixed, wo, preferred_element_type=F32)
    inv_second = row_inverse(hidden)
    second = (hidden * inv_second * gain_mlp).astype(BF16)
    preact = jnp.dot(second, wu, preferred_element_type=F32) + b_full
    active = jax.nn.silu(preact).astype(BF16)
    layer_out = (hidden + jnp.dot(active, wd, preferred_element_type=F32) + b_down).astype(BF16)

    upstream = cotangent.astype(F32)
    sigma = jax.nn.sigmoid(preact)
    d_active = dot(cotangent, wd, 1, 1)
    d_preact = (d_active * sigma * (1.0 + preact * (1.0 - sigma))).astype(BF16)
    d_second = dot(d_preact, wu, 1, 1)
    weighted = d_second * gain_mlp
    dots = jnp.sum(weighted * hidden, axis=1, keepdims=True)
    cube = inv_second * inv_second * inv_second
    d_hidden = upstream + inv_second * weighted - hidden * cube / features * dots
    d_attn = d_hidden.astype(BF16)
    d_mixed = dot(d_attn, wo, 1, 1).astype(BF16)

    owner = (jnp.arange(features)[None, :] // HD == jnp.arange(heads)[:, None]).astype(F32)
    delta = lax.dot_general(
        owner, d_mixed.astype(F32) * mixed.astype(F32), (((1,), (1,)), ((), ())),
        precision=lax.Precision.HIGHEST, preferred_element_type=F32,
    )
    d_scaled, d_keys, d_values = attend_backward(
        scaled, keys, keys.T, values, d_mixed, lse, delta, seg_query, seg_key, block
    )
    d_scaled_wide = d_scaled.astype(F32)
    d_query = (d_scaled_wide * factor_cols).astype(BF16)
    scale_part = jnp.sum(jnp.sum(d_scaled_wide * query_raw, axis=0).reshape(heads, HD), axis=0)

    part = None
    for c in range(back + 1):
        at = slice(c * rows, (c + 1) * rows)
        term = dot(d_keys[at], wk, 1, 1) + dot(d_values[at], wv, 1, 1)
        if c == back:
            term = term + dot(d_query, wq, 1, 1)
        if part is not None:
            term = term + part
        if c < back:
            part = lax.ppermute(term.astype(BF16), "mp", down).astype(F32)
    d_first = term

    weighted_first = d_first * gain_attn
    cube_first = inv_first * inv_first * inv_first
    first_dots = jnp.sum(weighted_first * inputs, axis=1, keepdims=True)
    tokens_grad = (
        d_hidden + inv_first * weighted_first - inputs * cube_first / features * first_dots
    ).astype(BF16)

    grad_gain_attn = jnp.sum(d_first * inputs * inv_first, axis=0)
    grad_gain_mlp = jnp.sum(d_second * hidden * inv_second, axis=0)
    grad_b_up = jnp.sum(d_preact.astype(F32), axis=0)
    sums = jnp.concatenate(
        [grad_gain_mlp, jnp.sum(upstream, axis=0), grad_b_up, grad_gain_attn, scale_part]
    )
    sums = lax.psum(sums, ("dp", "mp"))
    sum_gain_mlp, sum_b_down, sum_b_up, sum_gain_attn, scale_total = jnp.split(
        sums, [features, 2 * features, 3 * features, 4 * features]
    )
    mine = b_up.shape[0]
    sum_b_up = lax.dynamic_slice_in_dim(sum_b_up, z * mine, mine, 0)
    grad_query_scale = scale_total * (LOG2E / math.sqrt(HD)) * jax.nn.sigmoid(query_scale)

    grads = (
        scatter_grad(dot(normed, d_query, 0, 0), "dp", "mp"),
        scatter_grad(dot(first, d_keys, 0, 0), "dp", "mp"),
        scatter_grad(dot(first, d_values, 0, 0), "dp", "mp"),
        scatter_grad(dot(mixed, d_attn, 0, 0), "mp", "dp"),
        scatter_grad(dot(second, d_preact, 0, 0), "dp", "mp"),
        scatter_grad(dot(active, cotangent, 0, 0), "mp", "dp"),
    )
    return (
        layer_out, tokens_grad, grads[0], grads[1], grads[2], grads[3], grads[4], sum_b_up,
        grads[5], sum_b_down, sum_gain_attn, sum_gain_mlp, grad_query_scale,
    )


def solution(mesh):
    tokens, rows_dp, rows_mp = P(("dp", "mp"), None), P("dp", "mp"), P("mp", "dp")
    return jax.shard_map(
        body,
        mesh=mesh,
        in_specs=(
            tokens, P("dp", None), rows_dp, rows_dp, rows_dp, rows_mp, rows_dp, P("mp"), rows_mp,
            P(), P(), P(), P(), tokens,
        ),
        out_specs=(
            tokens, tokens, rows_dp, rows_dp, rows_dp, rows_mp, rows_dp, P("mp"), rows_mp,
            P(), P(), P(), P(),
        ),
        check_vma=False,
    )
```

```python
import functools
import math

import jax
import jax.numpy as jnp
from jax import lax
from jax.experimental import pallas as pl
from jax.experimental.pallas import tpu as pltpu
from jax.sharding import PartitionSpec as P

HD = 80
LANES = 128
EPSILON = 1e-06
LOG2E = 1.442695
DOC_MAX = 1024
FAR = -1e30
F32 = jnp.float32
BF16 = jnp.bfloat16


def dot(a, b, ca, cb):
    return lax.dot_general(a, b, (((ca,), (cb,)), ((), ())), preferred_element_type=F32)


def row_inverse(values):
    return lax.rsqrt(jnp.mean(values * values, axis=1, keepdims=True) + EPSILON)


def spans(rows, width, block):
    own = width - rows
    out=[]
    for qb in range(rows//block):
        hi = own + (qb+1)*block
        lo = max(0, (own + qb*block - (DOC_MAX-1))//block*block)
        out.append((lo,hi))
    return out

def head_lanes(h, features):
    first = h*HD
    off = jnp.minimum(lax.div(first, LANES)*LANES, features-2*LANES)
    off = pl.multiple_of(off, LANES)
    lane = lax.broadcasted_iota(jnp.int32,(1,2*LANES),1) + (off-first)
    return pl.ds(off, 2*LANES), (lane>=0)&(lane<HD)

def fill_bias(seg_query, seg_key, bias, block, own):
    rows = seg_query.shape[1]; width=seg_key.shape[0]
    for kb in range(width//block):
        for qb in range(rows//block):
            row = seg_query[:, qb*block:(qb+1)*block]
            col = seg_key[kb*block:(kb+1)*block,:]
            ahead = (lax.broadcasted_iota(jnp.int32,(block,block),0)+(kb*block)) <= (lax.broadcasted_iota(jnp.int32,(block,block),1)+(own+qb*block))
            bias[kb*block:(kb+1)*block, qb*block:(qb+1)*block] = jnp.where((col==row)&ahead, 0.0, FAR)

def transpose_out(src, dst):
    for i in range(src.shape[0]//LANES):
        at = slice(i*LANES,(i+1)*LANES)
        dst[:, at] = src[at,:].T.astype(dst.dtype)

def forward_kernel(block, q_ref, k_ref, vt_ref, seg_query, seg_key, o_ref, lse_ref, ot, bias, scores, tops):
    rows, features = q_ref.shape; width=k_ref.shape[0]; own=width-rows
    fill_bias(seg_query, seg_key, bias, block, own)
    sp = spans(rows,width,block)
    heads = features//HD
    tiles=[]
    for kb in range(width//block):
        qs=[i for i,(lo,hi) in enumerate(sp) if lo<=kb*block<hi]
        if qs: tiles.append((kb,qs))
    def score(h, slot):
        lanes, mine = head_lanes(h, features)
        query = jnp.where(mine, q_ref[:, lanes], jnp.zeros((), BF16))
        top=[jnp.full((8,block),FAR,F32) for _ in sp]
        for kb,qs in tiles:
            qa, qz = qs[0]*block, (qs[-1]+1)*block
            at = slice(kb*block,(kb+1)*block)
            s = dot(k_ref[at,lanes], query[qa:qz],1,1) + bias[at,qa:qz]
            scores[slot, at, qa:qz] = s
            for i in qs:
                top[i] = jnp.maximum(top[i], jnp.max(s[:, i*block-qa:(i+1)*block-qa].reshape(block//8,8,block),axis=0))
        for i in range(len(sp)):
            tops[slot, :, i*block:(i+1)*block] = jnp.max(top[i],axis=0,keepdims=True)
    def head(h, carry):
        slot = lax.rem(h,2)
        score(h, slot)
        feats = pl.ds(pl.multiple_of(h*HD,16), HD)
        top = tops[slot]
        acc=[jnp.zeros((HD,block),F32) for _ in sp]; total=[jnp.zeros((8,block),F32) for _ in sp]
        for kb,qs in tiles:
            qa, qz = qs[0]*block, (qs[-1]+1)*block
            at = slice(kb*block,(kb+1)*block)
            p = jnp.exp(scores[slot, at, qa:qz] - top[:,qa:qz])
            part = dot(vt_ref[feats,at], p.astype(BF16), 1, 0)
            for i in qs:
                cut = slice(i*block-qa,(i+1)*block-qa)
                total[i] = total[i] + jnp.sum(p[:,cut].reshape(block//8,8,block),axis=0)
                acc[i] = acc[i] + part[:,cut]
        for i in range(len(sp)):
            at = slice(i*block,(i+1)*block)
            one = jnp.sum(total[i],axis=0,keepdims=True)
            ot[feats, at] = acc[i] / one
            lse_ref[pl.ds(h,1), at] = top[:,at] + jnp.log(one)
        return carry
    lax.fori_loop(0, heads, head, 0)
    transpose_out(ot, o_ref)

def attend_forward(q,k,vt,seg_q,seg_k,block):
    rows,features=q.shape; width=k.shape[0]
    return pl.pallas_call(functools.partial(forward_kernel, block),
        out_shape=[jax.ShapeDtypeStruct((rows,features),BF16), jax.ShapeDtypeStruct((features//HD,rows),F32)],
        scratch_shapes=[pltpu.VMEM((features,rows),F32), pltpu.VMEM((width,rows),F32), pltpu.VMEM((2,width,rows),F32), pltpu.VMEM((2,1,rows),F32)],
        compiler_params=pltpu.CompilerParams(vmem_limit_bytes=56<<20), name="attend_forward")(q,k,vt,seg_q,seg_k)

def backward_kernel(block, q_ref,k_ref,kt_ref,v_ref,g_ref,lse_ref,delta_ref,seg_query,seg_key,dq_ref,dk_ref,dv_ref,dqt,bias):
    rows, features = q_ref.shape; width=k_ref.shape[0]; own=width-rows
    fill_bias(seg_query, seg_key, bias, block, own)
    dk_ref[...] = jnp.zeros_like(dk_ref); dv_ref[...] = jnp.zeros_like(dv_ref)
    sp = spans(rows,width,block)
    def head(h, carry):
        lanes, mine = head_lanes(h, features)
        feats = pl.ds(pl.multiple_of(h*HD,16), HD)
        zero = jnp.zeros((), BF16)
        query = jnp.where(mine, q_ref[:, lanes], zero)
        grad = jnp.where(mine, g_ref[:, lanes], zero)
        lse = lse_ref[pl.ds(h,1),:]; delta=delta_ref[pl.ds(h,1),:]
        acc = [jnp.zeros((HD,block),F32) for _ in sp]
        for kb in range(width//block):
            qs=[i for i,(lo,hi) in enumerate(sp) if lo<=kb*block<hi]
            if not qs: continue
            qa, qz = qs[0]*block, (qs[-1]+1)*block
            at = slice(kb*block,(kb+1)*block)
            s = dot(k_ref[at,lanes], query[qa:qz],1,1) + bias[at,qa:qz]
            p = jnp.exp(s - lse[:,qa:qz])
            dp = dot(v_ref[at,lanes], grad[qa:qz],1,1)
            ds = (p*(dp-delta[:,qa:qz])).astype(BF16)
            dv_ref[at,lanes] += dot(p.astype(BF16), grad[qa:qz],1,0).astype(BF16)
            dk_ref[at,lanes] += dot(ds, query[qa:qz],1,0).astype(BF16)
            part = dot(kt_ref[feats,at], ds, 1, 0)
            for i in qs:
                acc[i] = acc[i] + part[:, i*block-qa:(i+1)*block-qa]
        for i in range(len(sp)):
            dqt[feats, i*block:(i+1)*block] = acc[i]
        return carry
    lax.fori_loop(0, features//HD, head, 0)
    transpose_out(dqt, dq_ref)

def attend_backward(q,k,kt,v,g,lse,delta,seg_q,seg_k,block):
    rows,features=q.shape; width=k.shape[0]
    return pl.pallas_call(functools.partial(backward_kernel, block),
        out_shape=[jax.ShapeDtypeStruct((rows,features),BF16), jax.ShapeDtypeStruct((width,features),BF16), jax.ShapeDtypeStruct((width,features),BF16)],
        scratch_shapes=[pltpu.VMEM((features,rows),F32), pltpu.VMEM((width,rows),F32)],
        compiler_params=pltpu.CompilerParams(vmem_limit_bytes=60<<20), name="attend_backward")(q,k,kt,v,g,lse,delta,seg_q,seg_k)

MESH = pl.DeviceIdType.MESH


def bit_of(index, b):
    return lax.rem(lax.div(index, 1 << b), 2)


def flipped(index, bits):
    for b in bits:
        index = index + (1 << b) * (1 - 2 * bit_of(index, b))
    return index


def split_order(count, turn):
    bits = list(range(count))
    rest = bits[1:][::-1]
    turn = turn % max(1, len(rest))
    return bits[:1] + rest[turn:] + rest[:turn]


def subsets(bits):
    out = [()]
    for b in bits:
        out = out + [s + (b,) for s in out]
    return out


def greet(dp_bits, stages, extra=()):
    d, z = lax.axis_index("dp"), lax.axis_index("mp")
    barrier = pltpu.get_barrier_semaphore()
    for b in range(dp_bits):
        pl.semaphore_signal(barrier, device_id={"dp": flipped(d, (b,))}, device_id_type=MESH)
    for step in range(1, stages):
        pl.semaphore_signal(
            barrier, device_id={"mp": lax.rem(z + step, stages)}, device_id_type=MESH
        )
    pl.semaphore_wait(barrier, dp_bits + stages - 1)
    return d, z


def gather_kernel(dp_bits, stages, back, *refs):
    weights, refs = refs[:6], refs[6:]
    bias, tokens, refs = refs[0], refs[1], refs[2:]
    fulls, refs = refs[:6], refs[6:]
    bias_all, window, refs = refs[0], refs[1], refs[2:]
    blocks, slab, blank, zs, zr, ds, dr, ls, xs, xr, bs, br, blank_sem = refs
    d, z = greet(dp_bits, stages)
    cols = weights[0].shape[1]

    def block_copy(w, step):
        return pltpu.make_async_remote_copy(
            src_ref=weights[w], dst_ref=blocks.at[w, step], send_sem=zs.at[w, step],
            recv_sem=zr.at[w, step], device_id={"mp": lax.rem(z + step, stages)},
            device_id_type=MESH,
        )

    def bias_copy(step):
        return pltpu.make_async_remote_copy(
            src_ref=bias, dst_ref=bias_all.at[step], send_sem=bs.at[step], recv_sem=br.at[step],
            device_id={"mp": lax.rem(z + step, stages)}, device_id_type=MESH,
        )

    def token_copy(hop):
        src = tokens if hop == 0 else window.at[hop - 1]
        return pltpu.make_async_remote_copy(
            src_ref=src, dst_ref=window.at[hop], send_sem=xs.at[hop], recv_sem=xr.at[hop],
            device_id={"mp": jnp.minimum(z + 1, stages - 1)}, device_id_type=MESH,
        )

    sent = []
    orders = [split_order(dp_bits, w)[::-1] for w in range(6)]

    def slab_copy(w, at, held, b, slot):
        which = flipped(d, held)
        src = slab.at[w] if not held else fulls[w].at[which]
        return pltpu.make_async_remote_copy(
            src_ref=src, dst_ref=fulls[w].at[which], send_sem=ds.at[w, slot],
            recv_sem=dr.at[w, which], device_id={"dp": flipped(d, (b,))}, device_id_type=MESH,
        )

    def slab_arrival(w, held, b, slot):
        which = flipped(d, held + (b,))
        return pltpu.make_async_remote_copy(
            src_ref=slab.at[w], dst_ref=fulls[w].at[which], send_sem=ds.at[w, slot],
            recv_sem=dr.at[w, which], device_id={"dp": flipped(d, (b,))}, device_id_type=MESH,
        )

    def start_blocks(w):
        for step in range(1, stages):
            copy = block_copy(w, step)
            copy.start()
            sent.append(copy)

    def own_copy(w):
        return pltpu.make_async_copy(slab.at[w], fulls[w].at[d], ls.at[w])

    def finish_blocks(w):
        blocks[w, 0] = weights[w][...]
        for step in range(1, stages):
            block_copy(w, step).wait_recv()
        for me in range(stages):

            @pl.when(z == me)
            def _():
                parts = [blocks[w, (me - s) % stages] for s in range(stages)]
                slab[w] = jnp.concatenate(parts, axis=1)

        own_copy(w).start()

    def start_round(w, k):
        order = orders[w]
        for slot, held in enumerate(subsets(order[:k])):
            copy = slab_copy(w, d, held, order[k], (1 << k) - 1 + slot)
            copy.start()
            sent.append(copy)

    def finish_round(w, k):
        order = orders[w]
        for slot, held in enumerate(subsets(order[:k])):
            slab_arrival(w, held, order[k], (1 << k) - 1 + slot).wait_recv()

    for w in range(3):
        start_blocks(w)
    for step in range(1, stages):
        copy = bias_copy(step)
        copy.start()
        sent.append(copy)

    @pl.when(z < stages - 1)
    def _():
        token_copy(0).start()

    for w in range(3, 6):
        start_blocks(w)
    blank[...] = jnp.zeros_like(blank)
    bias_all[0] = bias[...]

    def blank_copy(hop):
        return pltpu.make_async_copy(blank, window.at[hop], blank_sem.at[hop])

    for hop in range(back):

        @pl.when(z <= hop)
        def _():
            blank_copy(hop).start()

    for w in range(3):
        finish_blocks(w)
        start_round(w, 0)
    for k in range(1, dp_bits):
        for w in range(3):
            finish_round(w, k - 1)
            start_round(w, k)
    for hop in range(back):

        @pl.when(z > hop)
        def _():
            token_copy(hop).wait_recv()

        if hop + 1 < back:

            @pl.when((z > hop) & (z < stages - 1))
            def _():
                token_copy(hop + 1).start()

    for w in range(3, 6):
        finish_blocks(w)
        start_round(w, 0)
    for k in range(1, dp_bits):
        for w in range(3, 6):
            finish_round(w, k - 1)
            start_round(w, k)
    for w in range(6):
        finish_round(w, dp_bits - 1)
        own_copy(w).wait()
    for step in range(1, stages):
        bias_copy(step).wait_recv()
    for hop in range(back):

        @pl.when((z >= hop) & (z < stages - 1))
        def _():
            token_copy(hop).wait_send()

        @pl.when(z <= hop)
        def _():
            blank_copy(hop).wait()

    for copy in sent:
        copy.wait_send()


def gather_all(weights, bias, tokens, dp, stages, back):
    rows, cols = weights[0].shape
    held, features = tokens.shape
    dp_bits = dp.bit_length() - 1
    hbm = pl.BlockSpec(memory_space=pl.ANY)
    vmem = pl.BlockSpec(memory_space=pltpu.VMEM)
    dma = pltpu.SemaphoreType.DMA
    out = pl.pallas_call(
        functools.partial(gather_kernel, dp_bits, stages, back),
        in_specs=[vmem] * 7 + [hbm],
        out_specs=[hbm] * 6 + [vmem, hbm],
        out_shape=[jax.ShapeDtypeStruct((dp, rows, cols * stages), BF16)] * 6
        + [
            jax.ShapeDtypeStruct((stages,) + bias.shape, F32),
            jax.ShapeDtypeStruct((back, held, features), BF16),
        ],
        scratch_shapes=[
            pltpu.VMEM((6, stages, rows, cols), BF16),
            pltpu.VMEM((6, rows, cols * stages), BF16),
            pltpu.VMEM((held, features), BF16),
            dma((6, stages)), dma((6, stages)), dma((6, dp)), dma((6, dp)), dma((6,)),
            dma((back,)), dma((back,)), dma((stages,)), dma((stages,)), dma((back,)),
        ],
        compiler_params=pltpu.CompilerParams(
            collective_id=0, has_side_effects=True, vmem_limit_bytes=40 << 20
        ),
        name="gather_all",
    )(*weights, bias, tokens)
    fulls = [f.reshape(dp * rows, cols * stages) for f in out[:6]]
    return fulls, out[6], out[7]


def add_into(dst, src, count, chunk):
    rows = dst.shape[1]

    def step(index, carry):
        i, at = index // (rows // chunk), lax.rem(index, rows // chunk)
        at = pl.ds(pl.multiple_of(at * chunk, chunk), chunk)
        dst[i, at, :] = (dst[i, at, :].astype(F32) + src(i, at).astype(F32)).astype(BF16)
        return carry

    lax.fori_loop(0, count * (rows // chunk), step, 0)


def reduce_kernel(dp_bits, stages, *refs):
    grads, refs = refs[:6], refs[6:]
    sums, refs = refs[0], refs[1:]
    outs, refs = refs[:6], refs[6:]
    total, refs = refs[0], refs[1:]
    kept, got = refs[0], refs[1 : 1 + dp_bits]
    zsend, zgot, sgot, ks, rs, rr, zs, zr, ss, sr = refs[1 + dp_bits :]
    d, z = greet(dp_bits, stages)
    half = 1 << (dp_bits - 1)
    rows, features = kept.shape[2], kept.shape[3]
    chunk = 32 if rows % 32 == 0 else 8
    orders = [split_order(dp_bits, w) for w in range(6)]
    sent = []

    def place(w, slot, low):
        rest = orders[w][1:]
        at = low
        for i, b in enumerate(rest):
            if slot >> (len(rest) - 1 - i) & 1:
                at = at + (1 << b)
        return at

    def first_copy(w, slot):
        return pltpu.make_async_remote_copy(
            src_ref=grads[w].at[place(w, slot, 1 - bit_of(d, 0))], dst_ref=got[0].at[w, slot],
            send_sem=rs.at[w, slot], recv_sem=rr.at[w, slot],
            device_id={"dp": flipped(d, (0,))}, device_id_type=MESH,
        )

    def keep_copy(w, slot):
        return pltpu.make_async_copy(
            grads[w].at[place(w, slot, bit_of(d, 0))], kept.at[w, slot], ks.at[w, slot]
        )

    def round_copy(w, k):
        count = half >> k
        b = orders[w][k]
        other = 1 - bit_of(d, b)
        return pltpu.make_async_remote_copy(
            src_ref=got[k - 1].at[w, pl.ds(other * count, count)], dst_ref=got[k].at[w],
            send_sem=rs.at[w, half + k], recv_sem=rr.at[w, half + k],
            device_id={"dp": flipped(d, (b,))}, device_id_type=MESH,
        )

    def last_copy(w, step):
        to = lax.rem(z + step, stages)
        return pltpu.make_async_remote_copy(
            src_ref=zsend.at[w, to], dst_ref=zgot.at[w, step], send_sem=zs.at[w, step],
            recv_sem=zr.at[w, step], device_id={"mp": to}, device_id_type=MESH,
        )

    def sum_copy(k):
        if k < dp_bits:
            to = {"dp": flipped(d, (k,))}
        else:
            to = {"mp": flipped(z, (k - dp_bits,))}
        return pltpu.make_async_remote_copy(
            src_ref=total.at[k], dst_ref=sgot.at[k], send_sem=ss.at[k], recv_sem=sr.at[k],
            device_id=to, device_id_type=MESH,
        )

    def start(copy):
        copy.start()
        sent.append(copy)

    def begin_first(w):
        for slot in range(half):
            start(first_copy(w, slot))
            keep_copy(w, slot).start()

    def finish_first(w):
        for slot in range(half):
            keep_copy(w, slot).wait()
            first_copy(w, slot).wait_recv()
        add_into(got[0].at[w], lambda i, at: kept[w, i, at, :], half, chunk)

    def finish_round(w, k):
        count = half >> k
        round_copy(w, k).wait_recv()
        mine = bit_of(d, orders[w][k]) * count
        add_into(got[k].at[w], lambda i, at: got[k - 1][w, mine + i, at, :], count, chunk)

    def begin_last(w):
        cols = features // stages
        for s in range(stages):
            zsend[w, s] = got[dp_bits - 1][w, 0, :, s * cols : (s + 1) * cols]
        for step in range(1, stages):
            start(last_copy(w, step))

    def finish_last(w):
        value = zsend[w, z].astype(F32)
        for step in range(1, stages):
            last_copy(w, step).wait_recv()
            value = value + zgot[w, step].astype(F32)
        outs[w][...] = value

    levels = dp_bits + stages.bit_length() - 1
    total[0] = sums[...]
    start(sum_copy(0))
    for w in range(6):
        begin_first(w)

    def sum_step(k):
        sum_copy(k).wait_recv()
        total[k + 1] = total[k] + sgot[k]
        if k + 1 < levels:
            start(sum_copy(k + 1))

    for w in range(6):
        finish_first(w)
        start(round_copy(w, 1)) if dp_bits > 1 else begin_last(w)
        if w < levels:
            sum_step(w)
    for k in range(6, levels):
        sum_step(k)
    for k in range(1, dp_bits):
        for w in range(6):
            finish_round(w, k)
            start(round_copy(w, k + 1)) if k + 1 < dp_bits else begin_last(w)
    for w in range(6):
        finish_last(w)
    for copy in sent:
        copy.wait_send()


def reduce_all(grads, sums, dp, stages):
    features = grads[0].shape[1]
    rows, cols = grads[0].shape[0] // dp, features // stages
    dp_bits = dp.bit_length() - 1
    half = dp // 2
    levels = dp_bits + stages.bit_length() - 1
    hbm = pl.BlockSpec(memory_space=pl.ANY)
    vmem = pl.BlockSpec(memory_space=pltpu.VMEM)
    dma = pltpu.SemaphoreType.DMA
    lines = sums.shape[0]
    out = pl.pallas_call(
        functools.partial(reduce_kernel, dp_bits, stages),
        in_specs=[hbm] * 6 + [vmem],
        out_specs=[vmem] * 7,
        out_shape=[jax.ShapeDtypeStruct((rows, cols), F32)] * 6
        + [jax.ShapeDtypeStruct((levels + 1, lines, LANES), F32)],
        scratch_shapes=[pltpu.VMEM((6, half, rows, features), BF16)]
        + [pltpu.VMEM((6, half >> k, rows, features), BF16) for k in range(dp_bits)]
        + [
            pltpu.VMEM((6, stages, rows, cols), BF16),
            pltpu.VMEM((6, stages, rows, cols), BF16),
            pltpu.VMEM((levels, lines, LANES), F32),
            dma((6, half)), dma((6, half + dp_bits)), dma((6, half + dp_bits)),
            dma((6, stages)), dma((6, stages)), dma((levels,)), dma((levels,)),
        ],
        compiler_params=pltpu.CompilerParams(
            collective_id=1, has_side_effects=True, vmem_limit_bytes=56 << 20
        ),
        name="reduce_all",
    )(*[g.reshape(dp, rows, features) for g in grads], sums)
    return out[:6], out[6][levels]


def body(
    tokens, segments, w_query, w_key, w_value, w_output, w_up, b_up, w_down, b_down,
    gain_attn, gain_mlp, query_scale, cotangent,
):
    stages = lax.axis_size("mp")
    z = lax.axis_index("mp")
    seg = segments[0]
    rows, features = tokens.shape
    back = min(stages - 1, -(-(DOC_MAX - 1) // rows))
    own = back * rows
    block = min(256, rows)
    up = [(i, i + 1) for i in range(stages - 1)]
    down = [(i + 1, i) for i in range(stages - 1)]

    (wq, wk, wv, wu, wo, wd), b_all, before = gather_all(
        (w_query, w_key, w_value, w_up, w_output.T, w_down.T), b_up[None], tokens,
        lax.axis_size("dp"), stages, back,
    )
    b_full = b_all[(z - jnp.arange(stages)) % stages].reshape(-1)

    inputs = tokens.astype(F32)
    inv_first = row_inverse(inputs)
    normed = (inputs * inv_first * gain_attn).astype(BF16)
    others = before[::-1].reshape(own, features).astype(F32)
    first = jnp.concatenate(
        [(others * row_inverse(others) * gain_attn).astype(BF16), normed], axis=0
    )

    seg_wide = jnp.concatenate([jnp.full((own,), -1, jnp.int32), seg])
    seg_window = lax.dynamic_slice_in_dim(seg_wide, z * rows, own + rows, 0)
    seg_query = seg_window[own:]
    seg_query, seg_key = seg_query[None, :], seg_window[:, None]

    heads = features // HD
    factor = jax.nn.softplus(query_scale) * (LOG2E / math.sqrt(HD))
    factor_cols = jnp.tile(factor, heads)
    query_raw = jnp.dot(normed, wq, preferred_element_type=F32)
    scaled = (query_raw * factor_cols).astype(BF16)
    keys = jnp.dot(first, wk, preferred_element_type=F32).astype(BF16)
    values = jnp.dot(first, wv, preferred_element_type=F32).astype(BF16)
    mixed, lse = attend_forward(scaled, keys, values.T, seg_query, seg_key, block)

    hidden = inputs + dot(mixed, wo, 1, 1)
    inv_second = row_inverse(hidden)
    second = (hidden * inv_second * gain_mlp).astype(BF16)
    preact = jnp.dot(second, wu, preferred_element_type=F32) + b_full
    active = jax.nn.silu(preact).astype(BF16)
    layer_out = (hidden + dot(active, wd, 1, 1) + b_down).astype(BF16)

    upstream = cotangent.astype(F32)
    sigma = jax.nn.sigmoid(preact)
    d_active = dot(cotangent, wd, 1, 0)
    d_preact = (d_active * sigma * (1.0 + preact * (1.0 - sigma))).astype(BF16)
    d_second = dot(d_preact, wu, 1, 1)
    weighted = d_second * gain_mlp
    dots = jnp.sum(weighted * hidden, axis=1, keepdims=True)
    cube = inv_second * inv_second * inv_second
    d_hidden = upstream + inv_second * weighted - hidden * cube / features * dots
    d_attn = d_hidden.astype(BF16)
    d_mixed = dot(d_attn, wo, 1, 0).astype(BF16)

    owner = (jnp.arange(features)[None, :] // HD == jnp.arange(heads)[:, None]).astype(F32)
    delta = lax.dot_general(
        owner, d_mixed.astype(F32) * mixed.astype(F32), (((1,), (1,)), ((), ())),
        precision=lax.Precision.HIGHEST, preferred_element_type=F32,
    )
    d_scaled, d_keys, d_values = attend_backward(
        scaled, keys, keys.T, values, d_mixed, lse, delta, seg_query, seg_key, block
    )
    d_scaled_wide = d_scaled.astype(F32)
    d_query = (d_scaled_wide * factor_cols).astype(BF16)
    scale_part = jnp.sum(jnp.sum(d_scaled_wide * query_raw, axis=0).reshape(heads, HD), axis=0)

    part = None
    for c in range(back + 1):
        at = slice(c * rows, (c + 1) * rows)
        term = dot(d_keys[at], wk, 1, 1) + dot(d_values[at], wv, 1, 1)
        if c == back:
            term = term + dot(d_query, wq, 1, 1)
        if part is not None:
            term = term + part
        if c < back:
            part = lax.ppermute(term.astype(BF16), "mp", down).astype(F32)
    d_first = term

    weighted_first = d_first * gain_attn
    cube_first = inv_first * inv_first * inv_first
    first_dots = jnp.sum(weighted_first * inputs, axis=1, keepdims=True)
    tokens_grad = (
        d_hidden + inv_first * weighted_first - inputs * cube_first / features * first_dots
    ).astype(BF16)

    grad_gain_attn = jnp.sum(d_first * inputs * inv_first, axis=0)
    grad_gain_mlp = jnp.sum(d_second * hidden * inv_second, axis=0)
    grad_b_up = jnp.sum(d_preact.astype(F32), axis=0)
    sums = jnp.concatenate(
        [grad_gain_mlp, jnp.sum(upstream, axis=0), grad_b_up, grad_gain_attn, scale_part]
    )
    lines = -(-sums.shape[0] // (8 * LANES)) * 8
    grads, sums = reduce_all(
        [
            dot(normed, d_query, 0, 0).astype(BF16),
            dot(first, d_keys, 0, 0).astype(BF16),
            dot(first, d_values, 0, 0).astype(BF16),
            dot(second, d_preact, 0, 0).astype(BF16),
            dot(d_attn, mixed, 0, 0).astype(BF16),
            dot(cotangent, active, 0, 0).astype(BF16),
        ],
        jnp.pad(sums, (0, lines * LANES - sums.shape[0])).reshape(lines, LANES),
        lax.axis_size("dp"), stages,
    )
    sums = sums.reshape(-1)[: 4 * features + HD]
    sum_gain_mlp, sum_b_down, sum_b_up, sum_gain_attn, scale_total = jnp.split(
        sums, [features, 2 * features, 3 * features, 4 * features]
    )
    mine = b_up.shape[0]
    sum_b_up = lax.dynamic_slice_in_dim(sum_b_up, z * mine, mine, 0)
    grad_query_scale = scale_total * (LOG2E / math.sqrt(HD)) * jax.nn.sigmoid(query_scale)

    return (
        layer_out, tokens_grad, grads[0], grads[1], grads[2], grads[4].T, grads[3], sum_b_up,
        grads[5].T, sum_b_down, sum_gain_attn, sum_gain_mlp, grad_query_scale,
    )


def solution(mesh):
    tokens, rows_dp, rows_mp = P(("dp", "mp"), None), P("dp", "mp"), P("mp", "dp")
    return jax.shard_map(
        body,
        mesh=mesh,
        in_specs=(
            tokens, P("dp", None), rows_dp, rows_dp, rows_dp, rows_mp, rows_dp, P("mp"), rows_mp,
            P(), P(), P(), P(), tokens,
        ),
        out_specs=(
            tokens, tokens, rows_dp, rows_dp, rows_dp, rows_mp, rows_dp, P("mp"), rows_mp,
            P(), P(), P(), P(),
        ),
        check_vma=False,
    )
```

```python
import functools
import math

import jax
import jax.numpy as jnp
from jax import lax
from jax.experimental import pallas as pl
from jax.experimental.pallas import tpu as pltpu
from jax.sharding import PartitionSpec as P

HD = 80
LANES = 128
EPSILON = 1e-06
LOG2E = 1.442695
DOC_MAX = 1024
FAR = -1e30
F32 = jnp.float32
BF16 = jnp.bfloat16


def dot(a, b, ca, cb):
    return lax.dot_general(a, b, (((ca,), (cb,)), ((), ())), preferred_element_type=F32)


def row_inverse(values):
    return lax.rsqrt(jnp.mean(values * values, axis=1, keepdims=True) + EPSILON)


MESH = pl.DeviceIdType.MESH


def bit_of(index, b):
    return lax.rem(lax.div(index, 1 << b), 2)


def flipped(index, bits):
    for b in bits:
        index = index + (1 << b) * (1 - 2 * bit_of(index, b))
    return index


def split_order(count, turn):
    bits = list(range(count))
    rest = bits[1:][::-1]
    turn = turn % max(1, len(rest))
    return bits[:1] + rest[turn:] + rest[:turn]


def subsets(bits):
    out = [()]
    for b in bits:
        out = out + [s + (b,) for s in out]
    return out


def greet(dp_bits, stages, extra=()):
    d, z = lax.axis_index("dp"), lax.axis_index("mp")
    barrier = pltpu.get_barrier_semaphore()
    for b in range(dp_bits):
        pl.semaphore_signal(barrier, device_id={"dp": flipped(d, (b,))}, device_id_type=MESH)
    for step in range(1, stages):
        pl.semaphore_signal(
            barrier, device_id={"mp": lax.rem(z + step, stages)}, device_id_type=MESH
        )
    pl.semaphore_wait(barrier, dp_bits + stages - 1)
    return d, z


class Reduction:
    def __init__(self, dp_bits, stages, d, z, grads, outs, refs):
        self.dp_bits, self.stages, self.d, self.z = dp_bits, stages, d, z
        self.grads, self.outs = grads, outs
        self.pool = refs[0]
        self.kept, self.got = refs[0].at[0], refs[1 : 1 + dp_bits]
        self.zsend, self.zgot, self.ks, self.rs, self.rr, self.zs, self.zr = refs[1 + dp_bits :]
        self.half = 1 << (dp_bits - 1)
        self.parts = self.kept.shape[0] // len(outs)
        self.rows, self.features = self.kept.shape[2], self.kept.shape[3]
        self.sent = []

    def start(self, make, *args):
        make(*args).start()
        self.sent.append((make, args))

    def order(self, u):
        return split_order(self.dp_bits, u % self.parts)

    def place(self, u, slot, low):
        rest = self.order(u)[1:]
        at = low
        for i, b in enumerate(rest):
            if slot >> (len(rest) - 1 - i) & 1:
                at = at + (1 << b)
        return at

    def slot_of(self, u, index):
        rest = self.order(u)[1:]
        return sum(bit_of(index, b - 1) << (len(rest) - 1 - i) for i, b in enumerate(rest))

    def source(self, u, slot, low):
        cut = pl.ds(u % self.parts * self.rows, self.rows)
        return self.grads[u // self.parts].at[self.place(u, slot, low), cut]

    def first_copy(self, u, slot):
        return pltpu.make_async_remote_copy(
            src_ref=self.pool.at[1, u, slot]
            if self.grads is None
            else self.source(u, slot, 1 - bit_of(self.d, 0)),
            dst_ref=self.got[0].at[u, slot],
            send_sem=self.rs.at[u, slot], recv_sem=self.rr.at[u, slot],
            device_id={"dp": flipped(self.d, (0,))}, device_id_type=MESH,
        )

    def keep_copy(self, u, slot):
        return pltpu.make_async_copy(
            self.source(u, slot, bit_of(self.d, 0)), self.kept.at[u, slot], self.ks.at[u, slot]
        )

    def round_copy(self, u, k):
        count = self.half >> k
        b = self.order(u)[k]
        other = 1 - bit_of(self.d, b)
        return pltpu.make_async_remote_copy(
            src_ref=self.got[k - 1].at[u, pl.ds(other * count, count)],
            dst_ref=self.got[k].at[u],
            send_sem=self.rs.at[u, self.half + k], recv_sem=self.rr.at[u, self.half + k],
            device_id={"dp": flipped(self.d, (b,))}, device_id_type=MESH,
        )

    def last_copy(self, w, step):
        to = lax.rem(self.z + step, self.stages)
        return pltpu.make_async_remote_copy(
            src_ref=self.zsend.at[w, to], dst_ref=self.zgot.at[w, step],
            send_sem=self.zs.at[w, step], recv_sem=self.zr.at[w, step],
            device_id={"mp": to}, device_id_type=MESH,
        )

    def units(self, w):
        return range(w * self.parts, (w + 1) * self.parts)

    def begin(self, w):
        for u in self.units(w):
            for slot in range(self.half):
                self.start(self.first_copy, u, slot)
                if self.grads is not None:
                    self.keep_copy(u, slot).start()

    def add(self, dst, src, count):
        def step(i, carry):
            dst[i] = (dst[i].astype(F32) + src(i).astype(F32)).astype(BF16)
            return carry

        lax.fori_loop(0, count, step, 0)

    def advance(self, w, k):
        for u in self.units(w):
            count = self.half >> k
            if k == 0:
                for slot in range(self.half):
                    if self.grads is not None:
                        self.keep_copy(u, slot).wait()
                    self.first_copy(u, slot).wait_recv()
                self.add(self.got[0].at[u], lambda i: self.kept[u, i], count)
            else:
                self.round_copy(u, k).wait_recv()
                mine = bit_of(self.d, self.order(u)[k]) * count
                self.add(self.got[k].at[u], lambda i: self.got[k - 1][u, mine + i], count)
            if k + 1 < self.dp_bits:
                self.start(self.round_copy, u, k + 1)
        if k + 1 == self.dp_bits:
            self.begin_last(w)

    def begin_last(self, w):
        cols = self.features // self.stages
        for u in self.units(w):
            at = slice(u % self.parts * self.rows, (u % self.parts + 1) * self.rows)
            for s in range(self.stages):
                self.zsend[w, s, at, :] = self.got[self.dp_bits - 1][
                    u, 0, :, s * cols : (s + 1) * cols
                ]
        for step in range(1, self.stages):
            self.start(self.last_copy, w, step)

    def finish(self, w):
        value = self.zsend[w, self.z].astype(F32)
        for step in range(1, self.stages):
            self.last_copy(w, step).wait_recv()
            value = value + self.zgot[w, step].astype(F32)
        self.outs[w][...] = value

    def close(self):
        for make, args in self.sent:
            make(*args).wait_send()


def reduction_scratch(count, dp, stages, rows, features, local=False):
    dp_bits, half, cols = dp.bit_length() - 1, dp // 2, features // stages
    parts = 2 if rows % 32 == 0 else 1
    dma = pltpu.SemaphoreType.DMA
    units = count * parts
    return (
        [pltpu.VMEM((1 + local, units, half, rows // parts, features), BF16)]
        + [pltpu.VMEM((units, half >> k, rows // parts, features), BF16) for k in range(dp_bits)]
        + [pltpu.VMEM((count, stages, rows, cols), BF16)] * 2
        + [
            dma((units, half)), dma((units, half + dp_bits)), dma((units, half + dp_bits)),
            dma((count, stages)), dma((count, stages)),
        ]
    )


def spans(rows, width, block):
    own = width - rows
    out=[]
    for qb in range(rows//block):
        hi = own + (qb+1)*block
        lo = max(0, (own + qb*block - (DOC_MAX-1))//block*block)
        out.append((lo,hi))
    return out

def head_lanes(h, features):
    first = h*HD
    off = jnp.minimum(lax.div(first, LANES)*LANES, features-2*LANES)
    off = pl.multiple_of(off, LANES)
    lane = lax.broadcasted_iota(jnp.int32,(1,2*LANES),1) + (off-first)
    return pl.ds(off, 2*LANES), (lane>=0)&(lane<HD)

def fill_bias(seg_query, seg_key, bias, block, own):
    rows = seg_query.shape[1]; width=seg_key.shape[0]
    for kb in range(width//block):
        for qb in range(rows//block):
            row = seg_query[:, qb*block:(qb+1)*block]
            col = seg_key[kb*block:(kb+1)*block,:]
            ahead = (lax.broadcasted_iota(jnp.int32,(block,block),0)+(kb*block)) <= (lax.broadcasted_iota(jnp.int32,(block,block),1)+(own+qb*block))
            bias[kb*block:(kb+1)*block, qb*block:(qb+1)*block] = jnp.where((col==row)&ahead, 0.0, FAR)

def transpose_out(src, dst):
    for i in range(src.shape[0]//LANES):
        at = slice(i*LANES,(i+1)*LANES)
        dst[:, at] = src[at,:].T.astype(dst.dtype)

class Gathering:
    def __init__(self, dp_bits, stages, d, z, weights, homes, refs):
        self.dp_bits, self.stages, self.d, self.z = dp_bits, stages, d, z
        self.weights, self.homes = weights, homes
        self.blocks, self.slab, self.zs, self.zr, self.ds, self.dr, self.ls = refs
        self.rows, self.cols = weights[0].shape
        self.parts = self.ds.shape[0] // len(weights)
        self.cut = self.rows // self.parts
        self.sent = []

    def start(self, make, *args):
        make(*args).start()
        self.sent.append((make, args))

    def order(self, u):
        return split_order(self.dp_bits, u % self.parts)[::-1]

    def block_copy(self, w, step):
        return pltpu.make_async_remote_copy(
            src_ref=self.weights[w], dst_ref=self.blocks.at[w, step], send_sem=self.zs.at[w, step],
            recv_sem=self.zr.at[w, step], device_id={"mp": lax.rem(self.z + step, self.stages)},
            device_id_type=MESH,
        )

    def place(self, u, which):
        at = which * self.rows + u % self.parts * self.cut
        return self.homes[u // self.parts].at[pl.ds(pl.multiple_of(at, self.cut), self.cut)]

    def piece(self, u):
        at = u % self.parts * self.cut
        return self.slab.at[u // self.parts, pl.ds(at, self.cut)]

    def own_copy(self, u):
        return pltpu.make_async_copy(self.piece(u), self.place(u, self.d), self.ls.at[u])

    def round_copy(self, u, k, slot, held):
        which = flipped(self.d, held)
        return pltpu.make_async_remote_copy(
            src_ref=self.place(u, which) if held else self.piece(u),
            dst_ref=self.place(u, which),
            send_sem=self.ds.at[u, (1 << k) - 1 + slot], recv_sem=self.dr.at[u, which],
            device_id={"dp": flipped(self.d, self.order(u)[k : k + 1])}, device_id_type=MESH,
        )

    def arrival(self, u, k, held):
        which = flipped(self.d, held + tuple(self.order(u)[k : k + 1]))
        return pltpu.make_async_remote_copy(
            src_ref=self.piece(u), dst_ref=self.place(u, which),
            send_sem=self.ds.at[u, 0], recv_sem=self.dr.at[u, which],
            device_id={"dp": flipped(self.d, self.order(u)[k : k + 1])}, device_id_type=MESH,
        )

    def units(self, w):
        return range(w * self.parts, (w + 1) * self.parts)

    def begin(self, w):
        for step in range(1, self.stages):
            self.start(self.block_copy, w, step)

    def begin_round(self, w, k):
        for u in self.units(w):
            for slot, held in enumerate(subsets(self.order(u)[:k])):
                self.start(self.round_copy, u, k, slot, held)

    def collect(self, w):
        self.blocks[w, 0] = self.weights[w][...]
        for step in range(1, self.stages):
            self.block_copy(w, step).wait_recv()
        for me in range(self.stages):

            @pl.when(self.z == me)
            def _():
                self.slab[w] = jnp.concatenate(
                    [self.blocks[w, (me - s) % self.stages] for s in range(self.stages)], axis=1
                )

        for u in self.units(w):
            self.own_copy(u).start()
        self.begin_round(w, 0)

    def advance(self, w, k):
        for u in self.units(w):
            for held in subsets(self.order(u)[:k]):
                self.arrival(u, k, held).wait_recv()
        if k + 1 < self.dp_bits:
            self.begin_round(w, k + 1)
        else:
            for u in self.units(w):
                self.own_copy(u).wait()

    def close(self):
        for make, args in self.sent:
            make(*args).wait_send()


def gathering_scratch(count, dp, stages, rows, cols):
    parts = 2 if rows % 32 == 0 else 1
    dma = pltpu.SemaphoreType.DMA
    units = count * parts
    return [
        pltpu.VMEM((count, stages, rows, cols), BF16),
        pltpu.VMEM((count, rows, cols * stages), BF16),
        dma((count, stages)), dma((count, stages)), dma((units, dp)), dma((units, dp)), dma((units,)),
    ]


def forward_kernel(block, dp_bits, stages, back, *refs):
    weights, refs = refs[:6], refs[6:]
    bias_in, tokens, gain, factor, seg_query, seg_key = refs[:6]
    fulls, refs = refs[6:12], refs[12:]
    bias_all, raw_out, q_out, k_out, kt_out, v_out, nt_out, o_ref, lse_ref = refs[:9]
    refs = refs[9:]
    home, window, normed, nt, raw, q, k, kt, v, vt, ot, bias, scores = refs[:13]
    xs, xr, bs, br, os = refs[13:18]
    d, z = greet(dp_bits, stages)
    rows, features = tokens.shape
    width, heads = k.shape[0], features // HD
    own = width - rows
    tile = 2 * LANES
    homes = [home.at[w] for w in range(3)] + list(fulls[3:])
    work = Gathering(dp_bits, stages, d, z, weights, homes, refs[18:])

    def bias_copy(step):
        return pltpu.make_async_remote_copy(
            src_ref=bias_in, dst_ref=bias_all.at[step], send_sem=bs.at[step],
            recv_sem=br.at[step], device_id={"mp": lax.rem(z + step, stages)},
            device_id_type=MESH,
        )

    def token_copy(hop):
        return pltpu.make_async_remote_copy(
            src_ref=tokens if hop == 0 else window.at[hop - 1], dst_ref=window.at[hop],
            send_sem=xs.at[hop], recv_sem=xr.at[hop],
            device_id={"mp": jnp.minimum(z + 1, stages - 1)}, device_id_type=MESH,
        )

    kept = [
        (raw, raw_out), (q, q_out), (k, k_out), (kt, kt_out), (v, v_out), (nt, nt_out),
        (home.at[0], fulls[0]), (home.at[1], fulls[1]), (home.at[2], fulls[2]),
    ]

    def keep(i):
        return pltpu.make_async_copy(kept[i][0], kept[i][1], os.at[i])

    def norm(src, at):
        step_rows = 128

        def step(i, carry):
            part = pl.ds(pl.multiple_of(i * step_rows, step_rows), step_rows)
            x = src[part, :].astype(F32)
            value = (x * row_inverse(x) * gain[...]).astype(BF16)
            to = pl.ds(pl.multiple_of(at + i * step_rows, step_rows), step_rows)
            normed[to, :] = value
            return carry

        lax.fori_loop(0, rows // step_rows, step, 0)
        for c in range(features // tile):
            lanes = slice(c * tile, (c + 1) * tile)
            nt[lanes, at : at + rows] = normed[at : at + rows, lanes].T

    def project(w, at, out, out_t):
        def step(c, carry):
            lanes = pl.ds(pl.multiple_of(c * tile, tile), tile)
            value = dot(normed[at : at + rows, :], home[w, :, lanes], 1, 0).astype(BF16)
            out[at : at + rows, lanes] = value
            out_t[lanes, at : at + rows] = value.T
            return carry

        lax.fori_loop(0, features // tile, step, 0)

    for w in range(3):
        work.begin(w)
    for step in range(1, stages):
        work.start(bias_copy, step)

    @pl.when(z < stages - 1)
    def _():
        token_copy(0).start()

    bias_all[0] = bias_in[...]
    for hop in range(back):

        @pl.when(z <= hop)
        def _():
            window[hop] = jnp.zeros((rows, features), BF16)

    norm(tokens, own)
    fill_bias(seg_query, seg_key, bias, block, own)
    for w in range(3):
        work.collect(w)
    for r in range(dp_bits - 1):
        for w in range(3):
            work.advance(w, r)
    for w in range(3):
        work.advance(w, dp_bits - 1)
        keep(6 + w).start()
        if w == 0:

            def query(c, carry):
                lanes = pl.ds(pl.multiple_of(c * tile, tile), tile)
                value = dot(normed[own:, :], home[0, :, lanes], 1, 0)
                raw[:, lanes] = value
                q[:, lanes] = (value * factor[:, lanes]).astype(BF16)
                return carry

            lax.fori_loop(0, features // tile, query, 0)
            keep(0).start()
            keep(1).start()
        else:
            project(w, own, *((k, kt) if w == 1 else (v, vt)))
    for hop in range(back):

        @pl.when(z > hop)
        def _():
            token_copy(hop).wait_recv()

        if hop + 1 < back:

            @pl.when((z > hop) & (z < stages - 1))
            def _():
                token_copy(hop + 1).start()

        else:
            for w in range(3, 6):
                work.begin(w)
        at = own - (hop + 1) * rows
        norm(window.at[hop], at)
        project(1, at, k, kt)
        project(2, at, v, vt)
    for i in range(2, 6):
        keep(i).start()

    sp = spans(rows, width, block)
    tiles = []
    for kb in range(width // block):
        qs = [i for i, (lo, hi) in enumerate(sp) if lo <= kb * block < hi]
        if qs:
            tiles.append((kb, qs))
    due = {(w, r): min(heads - 1, 6 + 4 * (w - 3) + 4 * r) for w in range(3, 6) for r in range(2)}

    def head(h, carry):
        for at in sorted(set(due.values())):

            @pl.when(h == at)
            def _():
                for w, r in sorted(due, key=lambda e: (e[1], e[0])):
                    if due[w, r] == at:
                        if r == 0:
                            work.collect(w)
                        else:
                            work.advance(w, r - 1)

        lanes, mine = head_lanes(h, features)
        feats = pl.ds(pl.multiple_of(h * HD, 16), HD)
        query = jnp.where(mine, q[:, lanes], jnp.zeros((), BF16))
        top = [jnp.full((8, block), FAR, F32) for _ in sp]
        for kb, qs in tiles:
            qa, qz = qs[0] * block, (qs[-1] + 1) * block
            at = slice(kb * block, (kb + 1) * block)
            s = dot(k[at, lanes], query[qa:qz], 1, 1) + bias[at, qa:qz]
            scores[at, qa:qz] = s
            for i in qs:
                cut = s[:, i * block - qa : (i + 1) * block - qa]
                top[i] = jnp.maximum(top[i], jnp.max(cut.reshape(block // 8, 8, block), axis=0))
        top = jnp.concatenate([jnp.max(t, axis=0, keepdims=True) for t in top], axis=1)
        acc = [jnp.zeros((HD, block), F32) for _ in sp]
        total = [jnp.zeros((8, block), F32) for _ in sp]
        for kb, qs in tiles:
            qa, qz = qs[0] * block, (qs[-1] + 1) * block
            at = slice(kb * block, (kb + 1) * block)
            p = jnp.exp(scores[at, qa:qz] - top[:, qa:qz])
            part = dot(vt[feats, at], p.astype(BF16), 1, 0)
            for i in qs:
                cut = slice(i * block - qa, (i + 1) * block - qa)
                total[i] = total[i] + jnp.sum(p[:, cut].reshape(block // 8, 8, block), axis=0)
                acc[i] = acc[i] + part[:, cut]
        for i in range(len(sp)):
            at = slice(i * block, (i + 1) * block)
            one = jnp.sum(total[i], axis=0, keepdims=True)
            ot[feats, at] = acc[i] / one
            lse_ref[pl.ds(h, 1), at] = top[:, at] + jnp.log(one)
        return carry

    lax.fori_loop(0, heads, head, 0)
    transpose_out(ot, o_ref)
    for r in range(1, dp_bits):
        for w in range(3, 6):
            work.advance(w, r)
    for step in range(1, stages):
        bias_copy(step).wait_recv()
    for hop in range(back):

        @pl.when((z >= hop) & (z < stages - 1))
        def _():
            token_copy(hop).wait_send()

    for i in range(len(kept)):
        keep(i).wait()
    work.close()


def attend_forward(weights, bias, tokens, gain, factor, seg_q, seg_k, block, dp, stages, back):
    held, cols = weights[0].shape
    rows, features = tokens.shape
    width, heads = (back + 1) * rows, features // HD
    hbm = pl.BlockSpec(memory_space=pl.ANY)
    vmem = pl.BlockSpec(memory_space=pltpu.VMEM)
    dma = pltpu.SemaphoreType.DMA
    sds = jax.ShapeDtypeStruct
    return pl.pallas_call(
        functools.partial(forward_kernel, block, dp.bit_length() - 1, stages, back),
        in_specs=[vmem] * 12,
        out_specs=[hbm] * 6 + [vmem] + [hbm] * 6 + [vmem] * 2,
        out_shape=[sds((features, features), BF16)] * 6
        + [
            sds((stages,) + bias.shape, F32),
            sds((rows, features), F32),
            sds((rows, features), BF16),
            sds((width, features), BF16),
            sds((features, width), BF16),
            sds((width, features), BF16),
            sds((features, width), BF16),
            sds((rows, features), BF16),
            sds((heads, rows), F32),
        ],
        scratch_shapes=[
            pltpu.VMEM((3, features, features), BF16),
            pltpu.VMEM((back, rows, features), BF16),
            pltpu.VMEM((width, features), BF16),
            pltpu.VMEM((features, width), BF16),
            pltpu.VMEM((rows, features), F32),
            pltpu.VMEM((rows, features), BF16),
            pltpu.VMEM((width, features), BF16),
            pltpu.VMEM((features, width), BF16),
            pltpu.VMEM((width, features), BF16),
            pltpu.VMEM((features, width), BF16),
            pltpu.VMEM((features, rows), F32),
            pltpu.VMEM((width, rows), F32),
            pltpu.VMEM((width, rows), F32),
            dma((back,)), dma((back,)), dma((stages,)), dma((stages,)), dma((9,)),
        ]
        + gathering_scratch(6, dp, stages, held, cols),
        compiler_params=pltpu.CompilerParams(
            collective_id=0, has_side_effects=True, vmem_limit_bytes=62 << 20
        ),
        name="attend_forward",
    )(*weights, bias, tokens, gain, factor, seg_q, seg_k)


def backward_kernel(block, dp_bits, stages, count, *refs):
    q_ref, k_ref, kt_ref, v_ref, g_ref, lse_ref, delta_ref, seg_query, seg_key, wk, wv = refs[:11]
    grads, refs = refs[11 : 11 + count], refs[11 + count :]
    dq_ref, dk_ref, dv_ref, incoming = refs[:4]
    outs, refs = refs[4 : 4 + count], refs[4 + count :]
    dqt, bias, part, ps, pr, refs = refs[0], refs[1], refs[2], refs[3], refs[4], refs[5:]
    d, z = greet(dp_bits, stages)
    work = Reduction(dp_bits, stages, d, z, grads, outs, refs)
    for w in range(count):
        work.begin(w)
    rows, features = q_ref.shape
    heads, width = features // HD, k_ref.shape[0]
    back = width // rows - 1
    fill_bias(seg_query, seg_key, bias, block, width - rows)
    dk_ref[...] = jnp.zeros_like(dk_ref)
    dv_ref[...] = jnp.zeros_like(dv_ref)
    dqt[...] = jnp.zeros_like(dqt)
    sp = spans(rows, width, block)
    steps = heads * (back + 1)
    due = {}
    for w in range(count):
        for r, at in enumerate((0.16 + 0.08 * w, 0.56 + 0.25 * w, 0.74 + 0.25 * w)[:dp_bits]):
            if at < 1:
                due[w, r] = int(at * steps)

    def down():
        return pltpu.make_async_remote_copy(
            src_ref=part, dst_ref=incoming, send_sem=ps, recv_sem=pr,
            device_id={"mp": jnp.maximum(z - 1, 0)}, device_id_type=MESH,
        )

    for c in range(back + 1):

        def head(h, carry):
            for at in sorted(set(due.values())):
                if at // heads != c:
                    continue

                @pl.when(h == at % heads)
                def _():
                    for w, r in sorted(due, key=lambda e: (e[1], e[0])):
                        if due[w, r] == at:
                            work.advance(w, r)

            lanes, mine = head_lanes(h, features)
            feats = pl.ds(pl.multiple_of(h * HD, 16), HD)
            zero = jnp.zeros((), BF16)
            query = jnp.where(mine, q_ref[:, lanes], zero)
            grad = jnp.where(mine, g_ref[:, lanes], zero)
            lse = lse_ref[pl.ds(h, 1), :]
            delta = delta_ref[pl.ds(h, 1), :]
            acc = [None for _ in sp]
            for kb in range(c * rows // block, (c + 1) * rows // block):
                qs = [i for i, (lo, hi) in enumerate(sp) if lo <= kb * block < hi]
                if not qs:
                    continue
                qa, qz = qs[0] * block, (qs[-1] + 1) * block
                at = slice(kb * block, (kb + 1) * block)
                s = dot(k_ref[at, lanes], query[qa:qz], 1, 1) + bias[at, qa:qz]
                p = jnp.exp(s - lse[:, qa:qz])
                dp = dot(v_ref[at, lanes], grad[qa:qz], 1, 1)
                ds = (p * (dp - delta[:, qa:qz])).astype(BF16)
                dv_ref[at, lanes] += dot(p.astype(BF16), grad[qa:qz], 1, 0).astype(BF16)
                dk_ref[at, lanes] += dot(ds, query[qa:qz], 1, 0).astype(BF16)
                share = dot(kt_ref[feats, at], ds, 1, 0)
                for i in qs:
                    piece = share[:, i * block - qa : (i + 1) * block - qa]
                    acc[i] = piece if acc[i] is None else acc[i] + piece
            for i in range(len(sp)):
                if acc[i] is not None:
                    dqt[feats, i * block : (i + 1) * block] += acc[i]
            return carry

        lax.fori_loop(0, heads, head, 0)
        if c == 0 and back:
            back_project(part, ((dk_ref, wk), (dv_ref, wv)), 0, None)

            @pl.when(z >= back)
            def _():
                down().start()

    transpose_out(dqt, dq_ref)
    for r in range(dp_bits):
        for w in range(count):
            if (w, r) not in due:
                work.advance(w, r)
    for w in range(count):
        work.finish(w)
    if back:

        @pl.when((z + 1 >= back) & (z < stages - 1))
        def _():
            down().wait_recv()

        @pl.when(z >= back)
        def _():
            down().wait_send()

    work.close()


def back_project(out, pairs, at, more):
    rows, features = out.shape
    tile = 2 * LANES

    def step(c, carry):
        lanes = pl.ds(pl.multiple_of(c * tile, tile), tile)
        value = None
        for grad, weight in pairs:
            start = at if grad.shape[0] > rows else 0
            term = dot(grad[start : start + rows, :], weight[lanes, :], 1, 1)
            value = term if value is None else value + term
        if more is not None:
            value = value + more(lanes)
        out[:, lanes] = value.astype(out.dtype)
        return carry

    lax.fori_loop(0, features // tile, step, 0)


def attend_backward(q, k, kt, v, g, lse, delta, seg_q, seg_k, wk, wv, block, grads, dp, stages):
    rows, features = q.shape
    width, count = k.shape[0], len(grads)
    held, cols = grads[0].shape[0] // dp, features // stages
    hbm = pl.BlockSpec(memory_space=pl.ANY)
    vmem = pl.BlockSpec(memory_space=pltpu.VMEM)
    dma = pltpu.SemaphoreType.DMA
    sds = jax.ShapeDtypeStruct
    out = pl.pallas_call(
        functools.partial(backward_kernel, block, dp.bit_length() - 1, stages, count),
        in_specs=[vmem] * 11 + [hbm] * count,
        out_specs=[vmem] * 3 + [hbm] + [vmem] * count,
        out_shape=[
            sds((rows, features), BF16), sds((width, features), BF16), sds((width, features), BF16),
            sds((rows, features), BF16),
        ]
        + [sds((held, cols), F32)] * count,
        scratch_shapes=[
            pltpu.VMEM((features, rows), F32), pltpu.VMEM((width, rows), F32),
            pltpu.VMEM((rows, features), BF16), dma, dma,
        ]
        + reduction_scratch(count, dp, stages, held, features),
        compiler_params=pltpu.CompilerParams(
            collective_id=2, has_side_effects=True, vmem_limit_bytes=62 << 20
        ),
        name="attend_backward",
    )(
        q, k, kt, v, g, lse, delta, seg_q, seg_k, wk, wv,
        *[a.reshape(dp, held, features) for a in grads],
    )
    return out[:4], out[4:]


def input_kernel(dp_bits, stages, back, lead, *refs):
    nt, dq, dk, dv, wq, wk, wv, incoming, tokens, d_hidden, gain, sums = refs[:12]
    outs, tokens_grad, total, refs = refs[12:15], refs[15], refs[16], refs[17:]
    part, landed, d_first, sgot, ss, sr, ps, pr = refs[:8]
    d, z = greet(dp_bits, stages)
    work = Reduction(dp_bits, stages, d, z, None, outs, refs[8:])
    rows, features = tokens.shape
    own = back * rows
    levels = dp_bits + stages.bit_length() - 1
    held = features >> dp_bits
    grads = ((dv, 2, 0), (dk, 1, 0), (dq, 0, own))

    def down(hop):
        return pltpu.make_async_remote_copy(
            src_ref=part.at[hop - 1], dst_ref=landed.at[hop - 1], send_sem=ps.at[hop - 1],
            recv_sem=pr.at[hop - 1], device_id={"mp": jnp.maximum(z - 1, 0)}, device_id_type=MESH,
        )

    def arrived(hop):
        source = incoming if hop == 1 else landed.at[hop - 2]
        there = (z + 1 >= back - hop + 1) & (z < stages - 1)

        def take(lanes):
            return jnp.where(there, source[:, lanes].astype(F32), 0.0)

        return there, take

    def weight_grad(i):
        grad, w, at = grads[i]

        def step(t, carry):
            rows_at = pl.ds(pl.multiple_of(t * 2 * held, 2 * held), 2 * held)
            value = dot(nt[rows_at, at:], grad[...], 1, 0).astype(BF16)
            for low in range(2):
                which = lax.rem(bit_of(d, 0) + low, 2)
                for u in work.units(w):
                    cut = low * held + u % work.parts * work.rows
                    work.pool[which, u, work.slot_of(u, t)] = value[cut : cut + work.rows]
            return carry

        lax.fori_loop(0, 1 << (dp_bits - 1), step, 0)
        work.begin(w)

    def sum_copy(k):
        if k < dp_bits:
            to = {"dp": flipped(d, (k,))}
        else:
            to = {"mp": flipped(z, (k - dp_bits,))}
        return pltpu.make_async_remote_copy(
            src_ref=total.at[k], dst_ref=sgot.at[k], send_sem=ss.at[k], recv_sem=sr.at[k],
            device_id=to, device_id_type=MESH,
        )

    def sum_step(k):
        sum_copy(k).wait_recv()
        total[k + 1] = total[k] + sgot[k]
        if k + 1 < levels:
            work.start(sum_copy, k + 1)

    def pass_down(hop):
        there, take = arrived(hop)
        if hop > 1:

            @pl.when(there)
            def _():
                down(hop - 1).wait_recv()

        back_project(part.at[hop - 1], ((dk, wk), (dv, wv)), hop * rows, take)

        @pl.when(z >= back - hop)
        def _():
            down(hop).start()

    if back > 1:
        pass_down(1)
    weight_grad(0)
    weight_grad(1)
    work.advance(2, 0)
    weight_grad(2)
    work.advance(1, 0)
    for hop in range(2, back):
        pass_down(hop)
    back_project(d_first, ((dk, wk), (dv, wv), (dq, wq)), own, None)
    work.advance(0, 0)
    if dp_bits > 1:
        work.advance(2, 1)
    there, take = arrived(back) if back else (None, None)
    if back > 1:

        @pl.when(there)
        def _():
            down(back - 1).wait_recv()

    chunk = 64

    def finish(i, column):
        at = pl.ds(pl.multiple_of(i * chunk, chunk), chunk)
        x = tokens[at, :].astype(F32)
        grad = d_first[at, :]
        if back:
            source = incoming if back == 1 else landed.at[back - 2]
            grad = grad + jnp.where(there, source[at, :].astype(F32), 0.0)
        inverse = row_inverse(x)
        weighted = grad * gain[...]
        dots = jnp.sum(weighted * x, axis=1, keepdims=True)
        cube = inverse * inverse * inverse
        tokens_grad[at, :] = (
            d_hidden[at, :] + inverse * weighted - x * cube / features * dots
        ).astype(BF16)
        return column + jnp.sum(grad * x * inverse, axis=0, keepdims=True)

    column = lax.fori_loop(0, rows // chunk, finish, jnp.zeros((1, features), F32))
    total[0] = sums[...]
    for c in range(features // LANES):
        total[0, lead + c : lead + c + 1, :] = column[:, c * LANES : (c + 1) * LANES]
    work.start(sum_copy, 0)
    done = 0
    rest = [(w, k) for k in range(1, dp_bits) for w in (2, 1, 0) if (w, k) != (2, 1)]
    for w, k in rest:
        work.advance(w, k)
        if done < levels:
            sum_step(done)
            done += 1
    for k in range(done, levels):
        sum_step(k)
    for w in (2, 1, 0):
        work.finish(w)
    for hop in range(1, back):

        @pl.when(z >= back - hop)
        def _():
            down(hop).wait_send()

    work.close()


def input_gradients(
    nt, dq, dk, dv, wq, wk, wv, incoming, tokens, d_hidden, gain, sums, lead, dp, stages
):
    rows, features = tokens.shape
    back = dk.shape[0] // rows - 1
    held, cols = features // dp, features // stages
    dp_bits = dp.bit_length() - 1
    levels = dp_bits + stages.bit_length() - 1
    lines = sums.shape[0]
    vmem = pl.BlockSpec(memory_space=pltpu.VMEM)
    dma = pltpu.SemaphoreType.DMA
    hops = max(1, back - 1)
    out = pl.pallas_call(
        functools.partial(input_kernel, dp_bits, stages, back, lead),
        in_specs=[vmem] * 12,
        out_specs=[vmem] * 5,
        out_shape=[jax.ShapeDtypeStruct((held, cols), F32)] * 3
        + [
            jax.ShapeDtypeStruct((rows, features), BF16),
            jax.ShapeDtypeStruct((levels + 1, lines, LANES), F32),
        ],
        scratch_shapes=[
            pltpu.VMEM((hops, rows, features), BF16), pltpu.VMEM((hops, rows, features), BF16),
            pltpu.VMEM((rows, features), F32), pltpu.VMEM((levels, lines, LANES), F32),
            dma((levels,)), dma((levels,)), dma((hops,)), dma((hops,)),
        ]
        + reduction_scratch(3, dp, stages, held, features, True),
        compiler_params=pltpu.CompilerParams(
            collective_id=1, has_side_effects=True, vmem_limit_bytes=62 << 20
        ),
        name="input_gradients",
    )(nt, dq, dk, dv, wq, wk, wv, incoming, tokens, d_hidden, gain, sums)
    return out[:3], out[3], out[4][levels]


def body(
    tokens, segments, w_query, w_key, w_value, w_output, w_up, b_up, w_down, b_down,
    gain_attn, gain_mlp, query_scale, cotangent,
):
    stages = lax.axis_size("mp")
    z = lax.axis_index("mp")
    seg = segments[0]
    rows, features = tokens.shape
    back = min(stages - 1, -(-(DOC_MAX - 1) // rows))
    own = back * rows
    block = min(256, rows)

    inputs = tokens.astype(F32)
    inv_first = row_inverse(inputs)
    seg_wide = jnp.concatenate([jnp.full((own,), -1, jnp.int32), seg])
    seg_window = lax.dynamic_slice_in_dim(seg_wide, z * rows, own + rows, 0)
    seg_query = seg_window[own:]
    seg_query, seg_key = seg_query[None, :], seg_window[:, None]

    heads = features // HD
    factor = jax.nn.softplus(query_scale) * (LOG2E / math.sqrt(HD))
    factor_cols = jnp.tile(factor, heads)
    (
        wq, wk, wv, wu, wo, wd, b_all, query_raw, scaled, keys, keys_t, values, first_t, mixed, lse
    ) = attend_forward(
        (w_query, w_key, w_value, w_up, w_output.T, w_down.T), b_up[None], tokens,
        gain_attn[None], factor_cols[None], seg_query, seg_key, block,
        lax.axis_size("dp"), stages, back,
    )
    b_full = b_all[(z - jnp.arange(stages)) % stages].reshape(-1)

    hidden = inputs + dot(mixed, wo, 1, 1)
    inv_second = row_inverse(hidden)
    second = (hidden * inv_second * gain_mlp).astype(BF16)
    preact = jnp.dot(second, wu, preferred_element_type=F32) + b_full
    active = jax.nn.silu(preact).astype(BF16)
    layer_out = (hidden + dot(active, wd, 1, 1) + b_down).astype(BF16)

    upstream = cotangent.astype(F32)
    sigma = jax.nn.sigmoid(preact)
    d_active = dot(cotangent, wd, 1, 0)
    d_preact = (d_active * sigma * (1.0 + preact * (1.0 - sigma))).astype(BF16)
    d_second = dot(d_preact, wu, 1, 1)
    weighted = d_second * gain_mlp
    dots = jnp.sum(weighted * hidden, axis=1, keepdims=True)
    cube = inv_second * inv_second * inv_second
    d_hidden = upstream + inv_second * weighted - hidden * cube / features * dots
    d_attn = d_hidden.astype(BF16)
    d_mixed = dot(d_attn, wo, 1, 0).astype(BF16)

    owner = (jnp.arange(features)[None, :] // HD == jnp.arange(heads)[:, None]).astype(F32)
    delta = lax.dot_general(
        owner, d_mixed.astype(F32) * mixed.astype(F32), (((1,), (1,)), ((), ())),
        precision=lax.Precision.HIGHEST, preferred_element_type=F32,
    )
    (d_scaled, d_keys, d_values, incoming), mlp_grads = attend_backward(
        scaled, keys, keys_t, values, d_mixed, lse, delta, seg_query, seg_key, wk, wv, block,
        [
            dot(second, d_preact, 0, 0).astype(BF16),
            dot(d_attn, mixed, 0, 0).astype(BF16),
            dot(cotangent, active, 0, 0).astype(BF16),
        ],
        lax.axis_size("dp"), stages,
    )
    d_scaled_wide = d_scaled.astype(F32)
    d_query = (d_scaled_wide * factor_cols).astype(BF16)
    scale_part = jnp.sum(jnp.sum(d_scaled_wide * query_raw, axis=0).reshape(heads, HD), axis=0)

    grad_gain_mlp = jnp.sum(d_second * hidden * inv_second, axis=0)
    grad_b_up = jnp.sum(d_preact.astype(F32), axis=0)
    sums = jnp.concatenate(
        [
            grad_gain_mlp, jnp.sum(upstream, axis=0), grad_b_up, jnp.zeros((features,), F32),
            scale_part,
        ]
    )
    lines = -(-sums.shape[0] // (8 * LANES)) * 8
    grads, tokens_grad, sums = input_gradients(
        first_t, d_query, d_keys, d_values, wq, wk, wv, incoming, tokens, d_hidden,
        gain_attn[None],
        jnp.pad(sums, (0, lines * LANES - sums.shape[0])).reshape(lines, LANES),
        3 * features // LANES, lax.axis_size("dp"), stages,
    )
    sums = sums.reshape(-1)[: 4 * features + HD]
    sum_gain_mlp, sum_b_down, sum_b_up, sum_gain_attn, scale_total = jnp.split(
        sums, [features, 2 * features, 3 * features, 4 * features]
    )
    mine = b_up.shape[0]
    sum_b_up = lax.dynamic_slice_in_dim(sum_b_up, z * mine, mine, 0)
    grad_query_scale = scale_total * (LOG2E / math.sqrt(HD)) * jax.nn.sigmoid(query_scale)

    return (
        layer_out, tokens_grad, grads[0], grads[1], grads[2], mlp_grads[1].T, mlp_grads[0],
        sum_b_up, mlp_grads[2].T, sum_b_down, sum_gain_attn, sum_gain_mlp, grad_query_scale,
    )


def solution(mesh):
    tokens, rows_dp, rows_mp = P(("dp", "mp"), None), P("dp", "mp"), P("mp", "dp")
    return jax.shard_map(
        body,
        mesh=mesh,
        in_specs=(
            tokens, P("dp", None), rows_dp, rows_dp, rows_dp, rows_mp, rows_dp, P("mp"), rows_mp,
            P(), P(), P(), P(), tokens,
        ),
        out_specs=(
            tokens, tokens, rows_dp, rows_dp, rows_dp, rows_mp, rows_dp, P("mp"), rows_mp,
            P(), P(), P(), P(),
        ),
        check_vma=False,
    )
```

```python
import functools
import math

import jax
import jax.numpy as jnp
from jax import lax
from jax.experimental import pallas as pl
from jax.experimental.pallas import tpu as pltpu
from jax.sharding import PartitionSpec as P

HD = 80
LANES = 128
EPSILON = 1e-06
LOG2E = 1.442695
DOC_MAX = 1024
FAR = -1e30
F32 = jnp.float32
BF16 = jnp.bfloat16


def dot(a, b, ca, cb):
    return lax.dot_general(a, b, (((ca,), (cb,)), ((), ())), preferred_element_type=F32)


def row_inverse(values):
    return lax.rsqrt(jnp.mean(values * values, axis=1, keepdims=True) + EPSILON)


MESH = pl.DeviceIdType.MESH


def bit_of(index, b):
    return lax.rem(lax.div(index, 1 << b), 2)


def flipped(index, bits):
    for b in bits:
        index = index + (1 << b) * (1 - 2 * bit_of(index, b))
    return index


def split_order(count, turn):
    bits = list(range(count))
    rest = bits[1:][::-1]
    turn = turn % max(1, len(rest))
    return bits[:1] + rest[turn:] + rest[:turn]


def subsets(bits):
    out = [()]
    for b in bits:
        out = out + [s + (b,) for s in out]
    return out


def greet(dp_bits, stages, extra=()):
    d, z = lax.axis_index("dp"), lax.axis_index("mp")
    barrier = pltpu.get_barrier_semaphore()
    for b in range(dp_bits):
        pl.semaphore_signal(barrier, device_id={"dp": flipped(d, (b,))}, device_id_type=MESH)
    for step in range(1, stages):
        pl.semaphore_signal(
            barrier, device_id={"mp": lax.rem(z + step, stages)}, device_id_type=MESH
        )
    pl.semaphore_wait(barrier, dp_bits + stages - 1)
    return d, z


class Reduction:
    def __init__(self, dp_bits, stages, d, z, grads, outs, refs):
        self.dp_bits, self.stages, self.d, self.z = dp_bits, stages, d, z
        self.grads, self.outs = grads, outs
        self.pool = refs[0]
        self.kept, self.got = refs[0].at[0], refs[1 : 1 + dp_bits]
        self.zsend, self.zgot, self.ks, self.rs, self.rr, self.zs, self.zr = refs[1 + dp_bits :]
        self.half = 1 << (dp_bits - 1)
        self.parts = self.kept.shape[0] // len(outs)
        self.rows, self.features = self.kept.shape[2], self.kept.shape[3]
        self.sent = []

    def start(self, make, *args):
        make(*args).start()
        self.sent.append((make, args))

    def order(self, u):
        return split_order(self.dp_bits, u % self.parts)

    def place(self, u, slot, low):
        rest = self.order(u)[1:]
        at = low
        for i, b in enumerate(rest):
            if slot >> (len(rest) - 1 - i) & 1:
                at = at + (1 << b)
        return at

    def slot_of(self, u, index):
        rest = self.order(u)[1:]
        return sum(bit_of(index, b - 1) << (len(rest) - 1 - i) for i, b in enumerate(rest))

    def source(self, u, slot, low):
        cut = pl.ds(u % self.parts * self.rows, self.rows)
        return self.grads[u // self.parts].at[self.place(u, slot, low), cut]

    def first_copy(self, u, slot):
        return pltpu.make_async_remote_copy(
            src_ref=self.pool.at[1, u, slot]
            if self.grads is None
            else self.source(u, slot, 1 - bit_of(self.d, 0)),
            dst_ref=self.got[0].at[u, slot],
            send_sem=self.rs.at[u, slot], recv_sem=self.rr.at[u, slot],
            device_id={"dp": flipped(self.d, (0,))}, device_id_type=MESH,
        )

    def keep_copy(self, u, slot):
        return pltpu.make_async_copy(
            self.source(u, slot, bit_of(self.d, 0)), self.kept.at[u, slot], self.ks.at[u, slot]
        )

    def round_copy(self, u, k):
        count = self.half >> k
        b = self.order(u)[k]
        other = 1 - bit_of(self.d, b)
        return pltpu.make_async_remote_copy(
            src_ref=self.got[k - 1].at[u, pl.ds(other * count, count)],
            dst_ref=self.got[k].at[u],
            send_sem=self.rs.at[u, self.half + k], recv_sem=self.rr.at[u, self.half + k],
            device_id={"dp": flipped(self.d, (b,))}, device_id_type=MESH,
        )

    def last_copy(self, w, step):
        to = lax.rem(self.z + step, self.stages)
        return pltpu.make_async_remote_copy(
            src_ref=self.zsend.at[w, to], dst_ref=self.zgot.at[w, step],
            send_sem=self.zs.at[w, step], recv_sem=self.zr.at[w, step],
            device_id={"mp": to}, device_id_type=MESH,
        )

    def units(self, w):
        return range(w * self.parts, (w + 1) * self.parts)

    def begin(self, w):
        for u in self.units(w):
            for slot in range(self.half):
                self.start(self.first_copy, u, slot)
                if self.grads is not None:
                    self.keep_copy(u, slot).start()

    def add(self, dst, src, count):
        def step(i, carry):
            dst[i] = (dst[i].astype(F32) + src(i).astype(F32)).astype(BF16)
            return carry

        lax.fori_loop(0, count, step, 0)

    def advance(self, w, k):
        for u in self.units(w):
            count = self.half >> k
            if k == 0:
                for slot in range(self.half):
                    if self.grads is not None:
                        self.keep_copy(u, slot).wait()
                    self.first_copy(u, slot).wait_recv()
                self.add(self.got[0].at[u], lambda i: self.kept[u, i], count)
            else:
                self.round_copy(u, k).wait_recv()
                mine = bit_of(self.d, self.order(u)[k]) * count
                self.add(self.got[k].at[u], lambda i: self.got[k - 1][u, mine + i], count)
            if k + 1 < self.dp_bits:
                self.start(self.round_copy, u, k + 1)
        if k + 1 == self.dp_bits:
            self.begin_last(w)

    def begin_last(self, w):
        cols = self.features // self.stages
        whole = [self.got[self.dp_bits - 1][u, 0] for u in self.units(w)]
        for s in range(self.stages):
            self.zsend[w, s] = jnp.concatenate(
                [piece[:, s * cols : (s + 1) * cols] for piece in whole], axis=1
            )
        for step in range(1, self.stages):
            self.start(self.last_copy, w, step)

    def finish(self, w):
        value = self.zsend[w, self.z].astype(F32)
        for step in range(1, self.stages):
            self.last_copy(w, step).wait_recv()
            value = value + self.zgot[w, step].astype(F32)
        cols = self.features // self.stages
        for p in range(self.parts):
            at = slice(p * self.rows, (p + 1) * self.rows)
            self.outs[w][at, :] = value[:, p * cols : (p + 1) * cols]

    def close(self):
        for make, args in self.sent:
            make(*args).wait_send()


def reduction_scratch(count, dp, stages, rows, features, local=False):
    dp_bits, half, cols = dp.bit_length() - 1, dp // 2, features // stages
    parts = 2 if rows % 32 == 0 else 1
    dma = pltpu.SemaphoreType.DMA
    units = count * parts
    return (
        [pltpu.VMEM((1 + local, units, half, rows // parts, features), BF16)]
        + [pltpu.VMEM((units, half >> k, rows // parts, features), BF16) for k in range(dp_bits)]
        + [pltpu.VMEM((count, stages, rows // parts, cols * parts), BF16)] * 2
        + [
            dma((units, half)), dma((units, half + dp_bits)), dma((units, half + dp_bits)),
            dma((count, stages)), dma((count, stages)),
        ]
    )


def spans(rows, width, block):
    own = width - rows
    out=[]
    for qb in range(rows//block):
        hi = own + (qb+1)*block
        lo = max(0, (own + qb*block - (DOC_MAX-1))//block*block)
        out.append((lo,hi))
    return out

def head_lanes(h, features):
    first = h*HD
    off = jnp.minimum(lax.div(first, LANES)*LANES, features-2*LANES)
    off = pl.multiple_of(off, LANES)
    lane = lax.broadcasted_iota(jnp.int32,(1,2*LANES),1) + (off-first)
    return pl.ds(off, 2*LANES), (lane>=0)&(lane<HD)

def fill_bias(seg_query, seg_key, bias, block, own):
    rows = seg_query.shape[1]; width=seg_key.shape[0]
    for kb in range(width//block):
        for qb in range(rows//block):
            row = seg_query[:, qb*block:(qb+1)*block]
            col = seg_key[kb*block:(kb+1)*block,:]
            ahead = (lax.broadcasted_iota(jnp.int32,(block,block),0)+(kb*block)) <= (lax.broadcasted_iota(jnp.int32,(block,block),1)+(own+qb*block))
            bias[kb*block:(kb+1)*block, qb*block:(qb+1)*block] = jnp.where((col==row)&ahead, 0.0, FAR)

def transpose_out(src, dst):
    for i in range(src.shape[0]//LANES):
        at = slice(i*LANES,(i+1)*LANES)
        dst[:, at] = src[at,:].T.astype(dst.dtype)

class Gathering:
    def __init__(self, dp_bits, stages, d, z, weights, homes, refs):
        self.dp_bits, self.stages, self.d, self.z = dp_bits, stages, d, z
        self.weights, self.homes = weights, homes
        self.blocks, self.slab, self.zs, self.zr, self.ds, self.dr, self.ls = refs
        self.rows, self.cols = weights[0].shape
        self.parts = self.ds.shape[0] // len(weights)
        self.cut = self.rows // self.parts
        self.sent = []

    def start(self, make, *args):
        make(*args).start()
        self.sent.append((make, args, None))

    def order(self, u):
        return split_order(self.dp_bits, u % self.parts)[::-1]

    def hop_copy(self, w, j, way):
        at = lax.rem(self.z - way * j + self.stages, self.stages)
        to = lax.rem(self.z + way + self.stages, self.stages)
        return pltpu.make_async_remote_copy(
            src_ref=self.blocks.at[w, at], dst_ref=self.blocks.at[w, at],
            send_sem=self.zs.at[w, 2 * j + (way + 1) // 2], recv_sem=self.zr.at[w, at],
            device_id={"mp": to}, device_id_type=MESH,
        )

    def there(self, j, way):
        return self.z >= j if way == 1 else self.z < self.stages - j

    def pack(self, w):
        pieces = [self.weights[w][p * self.cut : (p + 1) * self.cut] for p in range(self.parts)]
        self.blocks[w, self.z] = jnp.concatenate(pieces, axis=1)

    def take(self, w, j):
        for way in (1, -1):

            @pl.when(self.there(j, way))
            def _():
                self.hop_copy(w, j, way).wait_recv()

    def hop(self, w, j):
        if j:
            self.take(w, j)
        for way in (1, -1):
            sends = self.there(j, way) & self.there(1, -way)

            @pl.when(sends)
            def _():
                self.hop_copy(w, j, way).start()

            self.sent.append((self.hop_copy, (w, j, way), sends))

    def place(self, u, which):
        at = which * self.rows + u % self.parts * self.cut
        return self.homes[u // self.parts].at[pl.ds(pl.multiple_of(at, self.cut), self.cut)]

    def piece(self, u):
        at = u % self.parts * self.cut
        return self.slab.at[u // self.parts, pl.ds(at, self.cut)]

    def own_copy(self, u):
        return pltpu.make_async_copy(self.piece(u), self.place(u, self.d), self.ls.at[u])

    def round_copy(self, u, k, slot, held):
        which = flipped(self.d, held)
        return pltpu.make_async_remote_copy(
            src_ref=self.place(u, which) if held else self.piece(u),
            dst_ref=self.place(u, which),
            send_sem=self.ds.at[u, (1 << k) - 1 + slot], recv_sem=self.dr.at[u, which],
            device_id={"dp": flipped(self.d, self.order(u)[k : k + 1])}, device_id_type=MESH,
        )

    def arrival(self, u, k, held):
        which = flipped(self.d, held + tuple(self.order(u)[k : k + 1]))
        return pltpu.make_async_remote_copy(
            src_ref=self.piece(u), dst_ref=self.place(u, which),
            send_sem=self.ds.at[u, 0], recv_sem=self.dr.at[u, which],
            device_id={"dp": flipped(self.d, self.order(u)[k : k + 1])}, device_id_type=MESH,
        )

    def units(self, w):
        return range(w * self.parts, (w + 1) * self.parts)

    def begin_round(self, w, k):
        for u in self.units(w):
            for slot, held in enumerate(subsets(self.order(u)[:k])):
                self.start(self.round_copy, u, k, slot, held)

    def collect(self, w):
        self.take(w, self.stages - 1)
        for p in range(self.parts):
            lanes = slice(p * self.cols, (p + 1) * self.cols)
            self.slab[w, p * self.cut : (p + 1) * self.cut] = jnp.concatenate(
                [self.blocks[w, s, :, lanes] for s in range(self.stages)], axis=1
            )
        for u in self.units(w):
            self.own_copy(u).start()

    def advance(self, w, k):
        for u in self.units(w):
            for held in subsets(self.order(u)[:k]):
                self.arrival(u, k, held).wait_recv()
        if k + 1 < self.dp_bits:
            self.begin_round(w, k + 1)
        else:
            for u in self.units(w):
                self.own_copy(u).wait()

    def close(self):
        for make, args, sends in self.sent:
            if sends is None:
                make(*args).wait_send()
            else:

                @pl.when(sends)
                def _():
                    make(*args).wait_send()


def gathering_scratch(count, dp, stages, rows, cols):
    parts = 2 if rows % 32 == 0 else 1
    dma = pltpu.SemaphoreType.DMA
    units = count * parts
    return [
        pltpu.VMEM((count, stages, rows // parts, cols * parts), BF16),
        pltpu.VMEM((count, rows, cols * stages), BF16),
        dma((count, 2 * stages)), dma((count, stages)), dma((units, dp)), dma((units, dp)), dma((units,)),
    ]


def forward_kernel(block, dp_bits, stages, back, *refs):
    weights, refs = refs[:6], refs[6:]
    bias_in, tokens, gain, factor, seg_query, seg_key = refs[:6]
    fulls, refs = refs[6:12], refs[12:]
    bias_all, raw_out, q_out, k_out, kt_out, v_out, nt_out, o_ref, lse_ref = refs[:9]
    refs = refs[9:]
    home, window, normed, nt, raw, q, k, kt, v, vt, ot, bias, scores, tops, totals = refs[:15]
    xs, xr, bs, br, os = refs[15:20]
    d, z = greet(dp_bits, stages)
    rows, features = tokens.shape
    width, heads = k.shape[0], features // HD
    own = width - rows
    tile = 2 * LANES
    homes = [home.at[w] for w in range(3)] + list(fulls[3:])
    work = Gathering(dp_bits, stages, d, z, weights, homes, refs[20:])

    def bias_copy(step):
        return pltpu.make_async_remote_copy(
            src_ref=bias_in, dst_ref=bias_all.at[step], send_sem=bs.at[step],
            recv_sem=br.at[step], device_id={"mp": lax.rem(z + step, stages)},
            device_id_type=MESH,
        )

    def token_copy(hop):
        return pltpu.make_async_remote_copy(
            src_ref=tokens if hop == 0 else window.at[hop - 1], dst_ref=window.at[hop],
            send_sem=xs.at[hop], recv_sem=xr.at[hop],
            device_id={"mp": jnp.minimum(z + 1, stages - 1)}, device_id_type=MESH,
        )

    kept = [
        (raw, raw_out), (q, q_out), (k, k_out), (kt, kt_out), (v, v_out), (nt, nt_out),
        (home.at[0], fulls[0]), (home.at[1], fulls[1]), (home.at[2], fulls[2]),
    ]

    def keep(i):
        return pltpu.make_async_copy(kept[i][0], kept[i][1], os.at[i])

    def norm(src, at):
        step_rows = 128

        def step(i, carry):
            part = pl.ds(pl.multiple_of(i * step_rows, step_rows), step_rows)
            x = src[part, :].astype(F32)
            value = (x * row_inverse(x) * gain[...]).astype(BF16)
            to = pl.ds(pl.multiple_of(at + i * step_rows, step_rows), step_rows)
            normed[to, :] = value
            return carry

        lax.fori_loop(0, rows // step_rows, step, 0)
        for c in range(features // tile):
            lanes = slice(c * tile, (c + 1) * tile)
            nt[lanes, at : at + rows] = normed[at : at + rows, lanes].T

    def project(w, at, out, out_t):
        def step(c, carry):
            lanes = pl.ds(pl.multiple_of(c * tile, tile), tile)
            value = dot(normed[at : at + rows, :], home[w, :, lanes], 1, 0).astype(BF16)
            out[at : at + rows, lanes] = value
            out_t[lanes, at : at + rows] = value.T
            return carry

        lax.fori_loop(0, features // tile, step, 0)

    first, rest = range(3), range(3, 6)
    for w in range(6):
        work.pack(w)
    for w in first:
        work.hop(w, 0)
    for step in range(1, stages):
        work.start(bias_copy, step)
    bias_all[0] = bias_in[...]
    for hop in range(back):

        @pl.when(z <= hop)
        def _():
            window[hop] = jnp.zeros((rows, features), BF16)

    norm(tokens, own)
    fill_bias(seg_query, seg_key, bias, block, own)
    for j in range(1, stages - 1):
        for w in first:
            work.hop(w, j)
    for w in rest:
        work.hop(w, 0)
    for w in first:
        work.collect(w)
        work.begin_round(w, 0)
    for j in range(1, stages - 1):
        if j <= 3 and dp_bits > 1:
            work.advance(j - 1, 0)
        for w in rest:
            work.hop(w, j)

    @pl.when(z < stages - 1)
    def _():
        token_copy(0).start()

    if dp_bits > 1:
        for w in range(max(0, min(stages - 2, 3)), 3):
            work.advance(w, 0)
    for w in rest:
        work.collect(w)
    for r in range(1, dp_bits - 1):
        for w in first:
            work.advance(w, r)
    for w in rest:
        work.begin_round(w, 0)
    for w in first:
        work.advance(w, dp_bits - 1)
        keep(6 + w).start()
        if w == 0:

            def query(c, carry):
                lanes = pl.ds(pl.multiple_of(c * tile, tile), tile)
                value = dot(normed[own:, :], home[0, :, lanes], 1, 0)
                raw[:, lanes] = value
                q[:, lanes] = (value * factor[:, lanes]).astype(BF16)
                return carry

            lax.fori_loop(0, features // tile, query, 0)
            keep(0).start()
            keep(1).start()
        else:
            project(w, own, *((k, kt) if w == 1 else (v, vt)))

    sp = spans(rows, width, block)

    def attend(low, high, fresh, last, due):
        tiles = []
        for kb in range(low // block, high // block):
            qs = [i for i, (lo, hi) in enumerate(sp) if lo <= kb * block < hi]
            if qs:
                tiles.append((kb, qs))

        def head(h, carry):
            for at in sorted(set(due.values())):

                @pl.when(h == at)
                def _():
                    for w, r in due:
                        if due[w, r] == at:
                            work.advance(w, r)

            lanes, mine = head_lanes(h, features)
            feats = pl.ds(pl.multiple_of(h * HD, 16), HD)
            query = jnp.where(mine, q[:, lanes], jnp.zeros((), BF16))
            top = [jnp.full((8, block), FAR, F32) for _ in sp]
            for kb, qs in tiles:
                qa, qz = qs[0] * block, (qs[-1] + 1) * block
                at = slice(kb * block, (kb + 1) * block)
                s = dot(k[at, lanes], query[qa:qz], 1, 1) + bias[at, qa:qz]
                scores[at, qa:qz] = s
                for i in qs:
                    cut = s[:, i * block - qa : (i + 1) * block - qa]
                    top[i] = jnp.maximum(top[i], jnp.max(cut.reshape(block // 8, 8, block), axis=0))
            top = jnp.concatenate([jnp.max(t, axis=0, keepdims=True) for t in top], axis=1)
            if not fresh:
                before = tops[pl.ds(h, 1), :]
                top = jnp.maximum(top, before)
                scale = jnp.exp(before - top)
            acc = [jnp.zeros((HD, block), F32) for _ in sp]
            total = [jnp.zeros((8, block), F32) for _ in sp]
            for kb, qs in tiles:
                qa, qz = qs[0] * block, (qs[-1] + 1) * block
                at = slice(kb * block, (kb + 1) * block)
                p = jnp.exp(scores[at, qa:qz] - top[:, qa:qz])
                part = dot(vt[feats, at], p.astype(BF16), 1, 0)
                for i in qs:
                    cut = slice(i * block - qa, (i + 1) * block - qa)
                    total[i] = total[i] + jnp.sum(p[:, cut].reshape(block // 8, 8, block), axis=0)
                    acc[i] = acc[i] + part[:, cut]
            for i in range(len(sp)):
                at = slice(i * block, (i + 1) * block)
                one = jnp.sum(total[i], axis=0, keepdims=True)
                out = acc[i]
                if not fresh:
                    one = one + totals[pl.ds(h, 1), at] * scale[:, at]
                    out = out + ot[feats, at] * scale[:, at]
                if last:
                    ot[feats, at] = out / one
                    lse_ref[pl.ds(h, 1), at] = top[:, at] + jnp.log(one)
                else:
                    ot[feats, at] = out
                    totals[pl.ds(h, 1), at] = one
                    tops[pl.ds(h, 1), at] = top[:, at]
            return carry

        lax.fori_loop(0, heads, head, 0)

    inside = {}
    if back and dp_bits > 2:
        inside = {(3, 0): 0, (4, 0): heads // 4, (5, 0): heads // 2, (3, 1): heads * 3 // 4}
    for hop in range(back):
        if hop + 1 == back:
            attend(rows, width, True, False, inside)

        @pl.when(z > hop)
        def _():
            token_copy(hop).wait_recv()

        if hop + 1 < back:

            @pl.when((z > hop) & (z < stages - 1))
            def _():
                token_copy(hop + 1).start()

        at = own - (hop + 1) * rows
        norm(window.at[hop], at)
        project(1, at, k, kt)
        project(2, at, v, vt)
    for i in range(2, 6):
        keep(i).start()
    attend(0, rows if back else width, not back, True, {})
    transpose_out(ot, o_ref)
    for r in range(dp_bits):
        for w in rest:
            if (w, r) not in inside:
                work.advance(w, r)
    for step in range(1, stages):
        bias_copy(step).wait_recv()
    for hop in range(back):

        @pl.when((z >= hop) & (z < stages - 1))
        def _():
            token_copy(hop).wait_send()

    for i in range(len(kept)):
        keep(i).wait()
    work.close()


def attend_forward(weights, bias, tokens, gain, factor, seg_q, seg_k, block, dp, stages, back):
    held, cols = weights[0].shape
    rows, features = tokens.shape
    width, heads = (back + 1) * rows, features // HD
    hbm = pl.BlockSpec(memory_space=pl.ANY)
    vmem = pl.BlockSpec(memory_space=pltpu.VMEM)
    dma = pltpu.SemaphoreType.DMA
    sds = jax.ShapeDtypeStruct
    return pl.pallas_call(
        functools.partial(forward_kernel, block, dp.bit_length() - 1, stages, back),
        in_specs=[vmem] * 12,
        out_specs=[hbm] * 6 + [vmem] + [hbm] * 6 + [vmem] * 2,
        out_shape=[sds((features, features), BF16)] * 6
        + [
            sds((stages,) + bias.shape, F32),
            sds((rows, features), F32),
            sds((rows, features), BF16),
            sds((width, features), BF16),
            sds((features, width), BF16),
            sds((width, features), BF16),
            sds((features, width), BF16),
            sds((rows, features), BF16),
            sds((heads, rows), F32),
        ],
        scratch_shapes=[
            pltpu.VMEM((3, features, features), BF16),
            pltpu.VMEM((back, rows, features), BF16),
            pltpu.VMEM((width, features), BF16),
            pltpu.VMEM((features, width), BF16),
            pltpu.VMEM((rows, features), F32),
            pltpu.VMEM((rows, features), BF16),
            pltpu.VMEM((width, features), BF16),
            pltpu.VMEM((features, width), BF16),
            pltpu.VMEM((width, features), BF16),
            pltpu.VMEM((features, width), BF16),
            pltpu.VMEM((features, rows), F32),
            pltpu.VMEM((width, rows), F32),
            pltpu.VMEM((width, rows), F32),
            pltpu.VMEM((heads, rows), F32),
            pltpu.VMEM((heads, rows), F32),
            dma((back,)), dma((back,)), dma((stages,)), dma((stages,)), dma((9,)),
        ]
        + gathering_scratch(6, dp, stages, held, cols),
        compiler_params=pltpu.CompilerParams(
            collective_id=0, has_side_effects=True, vmem_limit_bytes=62 << 20
        ),
        name="attend_forward",
    )(*weights, bias, tokens, gain, factor, seg_q, seg_k)


def backward_kernel(block, dp_bits, stages, count, *refs):
    q_ref, k_ref, kt_ref, v_ref, g_ref, lse_ref, delta_ref, seg_query, seg_key, wk, wv = refs[:11]
    grads, refs = refs[11 : 11 + count], refs[11 + count :]
    dq_ref, dk_ref, dv_ref, incoming = refs[:4]
    outs, refs = refs[4 : 4 + count], refs[4 + count :]
    dqt, bias, part, ps, pr, refs = refs[0], refs[1], refs[2], refs[3], refs[4], refs[5:]
    d, z = greet(dp_bits, stages)
    work = Reduction(dp_bits, stages, d, z, grads, outs, refs)
    for w in range(count):
        work.begin(w)
    rows, features = q_ref.shape
    heads, width = features // HD, k_ref.shape[0]
    back = width // rows - 1
    fill_bias(seg_query, seg_key, bias, block, width - rows)
    dk_ref[...] = jnp.zeros_like(dk_ref)
    dv_ref[...] = jnp.zeros_like(dv_ref)
    dqt[...] = jnp.zeros_like(dqt)
    sp = spans(rows, width, block)
    steps = heads * (back + 1)
    due = {}
    for w in range(count):
        for r, at in enumerate((0.16 + 0.08 * w, 0.56 + 0.25 * w, 0.74 + 0.25 * w)[:dp_bits]):
            if at < 1:
                due[w, r] = int(at * steps)

    def down():
        return pltpu.make_async_remote_copy(
            src_ref=part, dst_ref=incoming, send_sem=ps, recv_sem=pr,
            device_id={"mp": jnp.maximum(z - 1, 0)}, device_id_type=MESH,
        )

    for c in range(back + 1):

        def head(h, carry):
            for at in sorted(set(due.values())):
                if at // heads != c:
                    continue

                @pl.when(h == at % heads)
                def _():
                    for w, r in sorted(due, key=lambda e: (e[1], e[0])):
                        if due[w, r] == at:
                            work.advance(w, r)

            lanes, mine = head_lanes(h, features)
            feats = pl.ds(pl.multiple_of(h * HD, 16), HD)
            zero = jnp.zeros((), BF16)
            query = jnp.where(mine, q_ref[:, lanes], zero)
            grad = jnp.where(mine, g_ref[:, lanes], zero)
            lse = lse_ref[pl.ds(h, 1), :]
            delta = delta_ref[pl.ds(h, 1), :]
            acc = [None for _ in sp]
            for kb in range(c * rows // block, (c + 1) * rows // block):
                qs = [i for i, (lo, hi) in enumerate(sp) if lo <= kb * block < hi]
                if not qs:
                    continue
                qa, qz = qs[0] * block, (qs[-1] + 1) * block
                at = slice(kb * block, (kb + 1) * block)
                s = dot(k_ref[at, lanes], query[qa:qz], 1, 1) + bias[at, qa:qz]
                p = jnp.exp(s - lse[:, qa:qz])
                dp = dot(v_ref[at, lanes], grad[qa:qz], 1, 1)
                ds = (p * (dp - delta[:, qa:qz])).astype(BF16)
                dv_ref[at, lanes] += dot(p.astype(BF16), grad[qa:qz], 1, 0).astype(BF16)
                dk_ref[at, lanes] += dot(ds, query[qa:qz], 1, 0).astype(BF16)
                share = dot(kt_ref[feats, at], ds, 1, 0)
                for i in qs:
                    piece = share[:, i * block - qa : (i + 1) * block - qa]
                    acc[i] = piece if acc[i] is None else acc[i] + piece
            for i in range(len(sp)):
                if acc[i] is not None:
                    dqt[feats, i * block : (i + 1) * block] += acc[i]
            return carry

        lax.fori_loop(0, heads, head, 0)
        if c == 0 and back:
            back_project(part, ((dk_ref, wk), (dv_ref, wv)), 0, None)

            @pl.when(z >= back)
            def _():
                down().start()

    transpose_out(dqt, dq_ref)
    for w in range(count):
        for r in range(dp_bits):
            if (w, r) not in due:
                work.advance(w, r)
    for w in range(count):
        work.finish(w)
    if back:

        @pl.when((z + 1 >= back) & (z < stages - 1))
        def _():
            down().wait_recv()

        @pl.when(z >= back)
        def _():
            down().wait_send()

    work.close()


def back_project(out, pairs, at, more):
    rows, features = out.shape
    tile = 2 * LANES

    def step(c, carry):
        lanes = pl.ds(pl.multiple_of(c * tile, tile), tile)
        value = None
        for grad, weight in pairs:
            start = at if grad.shape[0] > rows else 0
            term = dot(grad[start : start + rows, :], weight[lanes, :], 1, 1)
            value = term if value is None else value + term
        if more is not None:
            value = value + more(lanes)
        out[:, lanes] = value.astype(out.dtype)
        return carry

    lax.fori_loop(0, features // tile, step, 0)


def attend_backward(q, k, kt, v, g, lse, delta, seg_q, seg_k, wk, wv, block, grads, dp, stages):
    rows, features = q.shape
    width, count = k.shape[0], len(grads)
    held, cols = grads[0].shape[0] // dp, features // stages
    hbm = pl.BlockSpec(memory_space=pl.ANY)
    vmem = pl.BlockSpec(memory_space=pltpu.VMEM)
    dma = pltpu.SemaphoreType.DMA
    sds = jax.ShapeDtypeStruct
    out = pl.pallas_call(
        functools.partial(backward_kernel, block, dp.bit_length() - 1, stages, count),
        in_specs=[vmem] * 11 + [hbm] * count,
        out_specs=[vmem] * 3 + [hbm] + [vmem] * count,
        out_shape=[
            sds((rows, features), BF16), sds((width, features), BF16), sds((width, features), BF16),
            sds((rows, features), BF16),
        ]
        + [sds((held, cols), F32)] * count,
        scratch_shapes=[
            pltpu.VMEM((features, rows), F32), pltpu.VMEM((width, rows), F32),
            pltpu.VMEM((rows, features), BF16), dma, dma,
        ]
        + reduction_scratch(count, dp, stages, held, features),
        compiler_params=pltpu.CompilerParams(
            collective_id=2, has_side_effects=True, vmem_limit_bytes=62 << 20
        ),
        name="attend_backward",
    )(
        q, k, kt, v, g, lse, delta, seg_q, seg_k, wk, wv,
        *[a.reshape(dp, held, features) for a in grads],
    )
    return out[:4], out[4:]


def input_kernel(dp_bits, stages, back, lead, *refs):
    nt, dq, dk, dv, wq, wk, wv, incoming, tokens, d_hidden, gain, sums = refs[:12]
    outs, tokens_grad, total, refs = refs[12:15], refs[15], refs[16], refs[17:]
    part, landed, d_first, sgot, ss, sr, ps, pr = refs[:8]
    d, z = greet(dp_bits, stages)
    work = Reduction(dp_bits, stages, d, z, None, outs, refs[8:])
    rows, features = tokens.shape
    own = back * rows
    levels = dp_bits + stages.bit_length() - 1
    held = features >> dp_bits
    grads = ((dv, 2, 0), (dk, 1, 0), (dq, 0, own))

    def down(hop):
        return pltpu.make_async_remote_copy(
            src_ref=part.at[hop - 1], dst_ref=landed.at[hop - 1], send_sem=ps.at[hop - 1],
            recv_sem=pr.at[hop - 1], device_id={"mp": jnp.maximum(z - 1, 0)}, device_id_type=MESH,
        )

    def arrived(hop):
        source = incoming if hop == 1 else landed.at[hop - 2]
        there = (z + 1 >= back - hop + 1) & (z < stages - 1)

        def take(lanes):
            return jnp.where(there, source[:, lanes].astype(F32), 0.0)

        return there, take

    def weight_grad(i):
        grad, w, at = grads[i]

        def step(t, carry):
            rows_at = pl.ds(pl.multiple_of(t * 2 * held, 2 * held), 2 * held)
            value = dot(nt[rows_at, at:], grad[...], 1, 0).astype(BF16)
            for low in range(2):
                which = lax.rem(bit_of(d, 0) + low, 2)
                for u in work.units(w):
                    cut = low * held + u % work.parts * work.rows
                    work.pool[which, u, work.slot_of(u, t)] = value[cut : cut + work.rows]
            return carry

        lax.fori_loop(0, 1 << (dp_bits - 1), step, 0)
        work.begin(w)

    def sum_copy(k):
        if k < dp_bits:
            to = {"dp": flipped(d, (k,))}
        else:
            to = {"mp": flipped(z, (k - dp_bits,))}
        return pltpu.make_async_remote_copy(
            src_ref=total.at[k], dst_ref=sgot.at[k], send_sem=ss.at[k], recv_sem=sr.at[k],
            device_id=to, device_id_type=MESH,
        )

    def sum_step(k):
        sum_copy(k).wait_recv()
        total[k + 1] = total[k] + sgot[k]
        if k + 1 < levels:
            work.start(sum_copy, k + 1)

    def pass_down(hop):
        there, take = arrived(hop)
        if hop > 1:

            @pl.when(there)
            def _():
                down(hop - 1).wait_recv()

        back_project(part.at[hop - 1], ((dk, wk), (dv, wv)), hop * rows, take)

        @pl.when(z >= back - hop)
        def _():
            down(hop).start()

    if back > 1:
        pass_down(1)
    weight_grad(0)
    weight_grad(1)
    work.advance(2, 0)
    weight_grad(2)
    work.advance(1, 0)
    for hop in range(2, back):
        pass_down(hop)
    back_project(d_first, ((dk, wk), (dv, wv), (dq, wq)), own, None)
    work.advance(0, 0)
    if dp_bits > 1:
        work.advance(2, 1)
    there, take = arrived(back) if back else (None, None)
    if back > 1:

        @pl.when(there)
        def _():
            down(back - 1).wait_recv()

    chunk = 64

    def finish(i, column):
        at = pl.ds(pl.multiple_of(i * chunk, chunk), chunk)
        x = tokens[at, :].astype(F32)
        grad = d_first[at, :]
        if back:
            source = incoming if back == 1 else landed.at[back - 2]
            grad = grad + jnp.where(there, source[at, :].astype(F32), 0.0)
        inverse = row_inverse(x)
        weighted = grad * gain[...]
        dots = jnp.sum(weighted * x, axis=1, keepdims=True)
        cube = inverse * inverse * inverse
        tokens_grad[at, :] = (
            d_hidden[at, :] + inverse * weighted - x * cube / features * dots
        ).astype(BF16)
        return column + jnp.sum(grad * x * inverse, axis=0, keepdims=True)

    column = lax.fori_loop(0, rows // chunk, finish, jnp.zeros((1, features), F32))
    total[0] = sums[...]
    for c in range(features // LANES):
        total[0, lead + c : lead + c + 1, :] = column[:, c * LANES : (c + 1) * LANES]
    work.start(sum_copy, 0)
    done = 0
    rest = [(w, k) for w in (2, 1, 0) for k in range(1, dp_bits) if (w, k) != (2, 1)]
    for w, k in rest:
        work.advance(w, k)
        if done < levels:
            sum_step(done)
            done += 1
    for k in range(done, levels):
        sum_step(k)
    for w in (2, 1, 0):
        work.finish(w)
    for hop in range(1, back):

        @pl.when(z >= back - hop)
        def _():
            down(hop).wait_send()

    work.close()


def input_gradients(
    nt, dq, dk, dv, wq, wk, wv, incoming, tokens, d_hidden, gain, sums, lead, dp, stages
):
    rows, features = tokens.shape
    back = dk.shape[0] // rows - 1
    held, cols = features // dp, features // stages
    dp_bits = dp.bit_length() - 1
    levels = dp_bits + stages.bit_length() - 1
    lines = sums.shape[0]
    vmem = pl.BlockSpec(memory_space=pltpu.VMEM)
    dma = pltpu.SemaphoreType.DMA
    hops = max(1, back - 1)
    out = pl.pallas_call(
        functools.partial(input_kernel, dp_bits, stages, back, lead),
        in_specs=[vmem] * 12,
        out_specs=[vmem] * 5,
        out_shape=[jax.ShapeDtypeStruct((held, cols), F32)] * 3
        + [
            jax.ShapeDtypeStruct((rows, features), BF16),
            jax.ShapeDtypeStruct((levels + 1, lines, LANES), F32),
        ],
        scratch_shapes=[
            pltpu.VMEM((hops, rows, features), BF16), pltpu.VMEM((hops, rows, features), BF16),
            pltpu.VMEM((rows, features), F32), pltpu.VMEM((levels, lines, LANES), F32),
            dma((levels,)), dma((levels,)), dma((hops,)), dma((hops,)),
        ]
        + reduction_scratch(3, dp, stages, held, features, True),
        compiler_params=pltpu.CompilerParams(
            collective_id=1, has_side_effects=True, vmem_limit_bytes=62 << 20
        ),
        name="input_gradients",
    )(nt, dq, dk, dv, wq, wk, wv, incoming, tokens, d_hidden, gain, sums)
    return out[:3], out[3], out[4][levels]


def body(
    tokens, segments, w_query, w_key, w_value, w_output, w_up, b_up, w_down, b_down,
    gain_attn, gain_mlp, query_scale, cotangent,
):
    stages = lax.axis_size("mp")
    z = lax.axis_index("mp")
    seg = segments[0]
    rows, features = tokens.shape
    back = min(stages - 1, -(-(DOC_MAX - 1) // rows))
    own = back * rows
    block = min(256, rows)

    inputs = tokens.astype(F32)
    inv_first = row_inverse(inputs)
    seg_wide = jnp.concatenate([jnp.full((own,), -1, jnp.int32), seg])
    seg_window = lax.dynamic_slice_in_dim(seg_wide, z * rows, own + rows, 0)
    seg_query = seg_window[own:]
    seg_query, seg_key = seg_query[None, :], seg_window[:, None]

    heads = features // HD
    factor = jax.nn.softplus(query_scale) * (LOG2E / math.sqrt(HD))
    factor_cols = jnp.tile(factor, heads)
    (
        wq, wk, wv, wu, wo, wd, b_all, query_raw, scaled, keys, keys_t, values, first_t, mixed, lse
    ) = attend_forward(
        (w_query, w_key, w_value, w_up, w_output.T, w_down.T), b_up[None], tokens,
        gain_attn[None], factor_cols[None], seg_query, seg_key, block,
        lax.axis_size("dp"), stages, back,
    )
    b_full = b_all[(z - jnp.arange(stages)) % stages].reshape(-1)

    hidden = inputs + dot(mixed, wo, 1, 1)
    inv_second = row_inverse(hidden)
    second = (hidden * inv_second * gain_mlp).astype(BF16)
    preact = jnp.dot(second, wu, preferred_element_type=F32) + b_full
    active = jax.nn.silu(preact).astype(BF16)
    layer_out = (hidden + dot(active, wd, 1, 1) + b_down).astype(BF16)

    upstream = cotangent.astype(F32)
    sigma = jax.nn.sigmoid(preact)
    d_active = dot(cotangent, wd, 1, 0)
    d_preact = (d_active * sigma * (1.0 + preact * (1.0 - sigma))).astype(BF16)
    d_second = dot(d_preact, wu, 1, 1)
    weighted = d_second * gain_mlp
    dots = jnp.sum(weighted * hidden, axis=1, keepdims=True)
    cube = inv_second * inv_second * inv_second
    d_hidden = upstream + inv_second * weighted - hidden * cube / features * dots
    d_attn = d_hidden.astype(BF16)
    d_mixed = dot(d_attn, wo, 1, 0).astype(BF16)

    owner = (jnp.arange(features)[None, :] // HD == jnp.arange(heads)[:, None]).astype(F32)
    delta = lax.dot_general(
        owner, d_mixed.astype(F32) * mixed.astype(F32), (((1,), (1,)), ((), ())),
        precision=lax.Precision.HIGHEST, preferred_element_type=F32,
    )
    (d_scaled, d_keys, d_values, incoming), mlp_grads = attend_backward(
        scaled, keys, keys_t, values, d_mixed, lse, delta, seg_query, seg_key, wk, wv, block,
        [
            dot(second, d_preact, 0, 0).astype(BF16),
            dot(d_attn, mixed, 0, 0).astype(BF16),
            dot(cotangent, active, 0, 0).astype(BF16),
        ],
        lax.axis_size("dp"), stages,
    )
    d_scaled_wide = d_scaled.astype(F32)
    d_query = (d_scaled_wide * factor_cols).astype(BF16)
    scale_part = jnp.sum(jnp.sum(d_scaled_wide * query_raw, axis=0).reshape(heads, HD), axis=0)

    grad_gain_mlp = jnp.sum(d_second * hidden * inv_second, axis=0)
    grad_b_up = jnp.sum(d_preact.astype(F32), axis=0)
    sums = jnp.concatenate(
        [
            grad_gain_mlp, jnp.sum(upstream, axis=0), grad_b_up, jnp.zeros((features,), F32),
            scale_part,
        ]
    )
    lines = -(-sums.shape[0] // (8 * LANES)) * 8
    grads, tokens_grad, sums = input_gradients(
        first_t, d_query, d_keys, d_values, wq, wk, wv, incoming, tokens, d_hidden,
        gain_attn[None],
        jnp.pad(sums, (0, lines * LANES - sums.shape[0])).reshape(lines, LANES),
        3 * features // LANES, lax.axis_size("dp"), stages,
    )
    sums = sums.reshape(-1)[: 4 * features + HD]
    sum_gain_mlp, sum_b_down, sum_b_up, sum_gain_attn, scale_total = jnp.split(
        sums, [features, 2 * features, 3 * features, 4 * features]
    )
    mine = b_up.shape[0]
    sum_b_up = lax.dynamic_slice_in_dim(sum_b_up, z * mine, mine, 0)
    grad_query_scale = scale_total * (LOG2E / math.sqrt(HD)) * jax.nn.sigmoid(query_scale)

    return (
        layer_out, tokens_grad, grads[0], grads[1], grads[2], mlp_grads[1].T, mlp_grads[0],
        sum_b_up, mlp_grads[2].T, sum_b_down, sum_gain_attn, sum_gain_mlp, grad_query_scale,
    )


def solution(mesh):
    tokens, rows_dp, rows_mp = P(("dp", "mp"), None), P("dp", "mp"), P("mp", "dp")
    return jax.shard_map(
        body,
        mesh=mesh,
        in_specs=(
            tokens, P("dp", None), rows_dp, rows_dp, rows_dp, rows_mp, rows_dp, P("mp"), rows_mp,
            P(), P(), P(), P(), tokens,
        ),
        out_specs=(
            tokens, tokens, rows_dp, rows_dp, rows_dp, rows_mp, rows_dp, P("mp"), rows_mp,
            P(), P(), P(), P(),
        ),
        check_vma=False,
    )
```

```python
import functools
import math

import jax
import jax.numpy as jnp
from jax import lax
from jax.experimental import pallas as pl
from jax.experimental.pallas import tpu as pltpu
from jax.sharding import PartitionSpec as P

HD = 80
LANES = 128
EPSILON = 1e-06
LOG2E = 1.442695
DOC_MAX = 1024
FAR = -1e30
EVENTS = (0.04, 0.1, 0.25, 0.32, 0.46, 0.6, 0.75)
F32 = jnp.float32
BF16 = jnp.bfloat16


def dot(a, b, ca, cb):
    return lax.dot_general(a, b, (((ca,), (cb,)), ((), ())), preferred_element_type=F32)


def row_inverse(values):
    return lax.rsqrt(jnp.mean(values * values, axis=1, keepdims=True) + EPSILON)


MESH = pl.DeviceIdType.MESH


def bit_of(index, b):
    return lax.rem(lax.div(index, 1 << b), 2)


def flipped(index, bits):
    for b in bits:
        index = index + (1 << b) * (1 - 2 * bit_of(index, b))
    return index


def split_order(count, turn):
    bits = list(range(count))
    rest = bits[1:][::-1]
    turn = turn % max(1, len(rest))
    return bits[:1] + rest[turn:] + rest[:turn]


def subsets(bits):
    out = [()]
    for b in bits:
        out = out + [s + (b,) for s in out]
    return out


def greet(dp_bits, stages, extra=()):
    d, z = lax.axis_index("dp"), lax.axis_index("mp")
    barrier = pltpu.get_barrier_semaphore()
    for b in range(dp_bits):
        pl.semaphore_signal(barrier, device_id={"dp": flipped(d, (b,))}, device_id_type=MESH)
    for step in range(1, stages):
        pl.semaphore_signal(
            barrier, device_id={"mp": lax.rem(z + step, stages)}, device_id_type=MESH
        )
    pl.semaphore_wait(barrier, dp_bits + stages - 1)
    return d, z


class Loads:
    def __init__(self, pairs, sems):
        self.pairs, self.sems = pairs, sems

    def copy(self, i):
        return pltpu.make_async_copy(self.pairs[i][0], self.pairs[i][1], self.sems.at[i])

    def start(self, *which):
        for i in which:
            self.copy(i).start()

    def wait(self, *which):
        for i in which:
            self.copy(i).wait()


class Reduction:
    def __init__(self, dp_bits, stages, d, z, grads, outs, refs):
        self.dp_bits, self.stages, self.d, self.z = dp_bits, stages, d, z
        self.grads, self.outs = grads, outs
        self.pool = refs[0]
        self.kept, self.got = refs[0].at[0], refs[1 : 1 + dp_bits]
        self.zsend, self.zgot, self.ks, self.rs, self.rr, self.zs, self.zr = refs[1 + dp_bits :]
        self.half = 1 << (dp_bits - 1)
        self.parts = self.kept.shape[0] // len(outs)
        self.rows, self.features = self.kept.shape[2], self.kept.shape[3]
        self.sent = []

    def start(self, make, *args):
        make(*args).start()
        self.sent.append((make, args))

    def order(self, u):
        return split_order(self.dp_bits, u % self.parts)

    def place(self, u, slot, low):
        rest = self.order(u)[1:]
        at = low
        for i, b in enumerate(rest):
            if slot >> (len(rest) - 1 - i) & 1:
                at = at + (1 << b)
        return at

    def slot_of(self, u, index):
        rest = self.order(u)[1:]
        return sum(bit_of(index, b - 1) << (len(rest) - 1 - i) for i, b in enumerate(rest))

    def source(self, u, slot, low):
        cut = pl.ds(u % self.parts * self.rows, self.rows)
        return self.grads[u // self.parts].at[self.place(u, slot, low), cut]

    def first_copy(self, u, slot):
        return pltpu.make_async_remote_copy(
            src_ref=self.pool.at[1, u, slot]
            if self.grads is None
            else self.source(u, slot, 1 - bit_of(self.d, 0)),
            dst_ref=self.got[0].at[u, slot],
            send_sem=self.rs.at[u, slot], recv_sem=self.rr.at[u, slot],
            device_id={"dp": flipped(self.d, (0,))}, device_id_type=MESH,
        )

    def keep_copy(self, u, slot):
        return pltpu.make_async_copy(
            self.source(u, slot, bit_of(self.d, 0)), self.kept.at[u, slot], self.ks.at[u, slot]
        )

    def round_copy(self, u, k):
        count = self.half >> k
        b = self.order(u)[k]
        other = 1 - bit_of(self.d, b)
        return pltpu.make_async_remote_copy(
            src_ref=self.got[k - 1].at[u, pl.ds(other * count, count)],
            dst_ref=self.got[k].at[u],
            send_sem=self.rs.at[u, self.half + k], recv_sem=self.rr.at[u, self.half + k],
            device_id={"dp": flipped(self.d, (b,))}, device_id_type=MESH,
        )

    def last_copy(self, w, step):
        to = lax.rem(self.z + step, self.stages)
        return pltpu.make_async_remote_copy(
            src_ref=self.zsend.at[w, to], dst_ref=self.zgot.at[w, step],
            send_sem=self.zs.at[w, step], recv_sem=self.zr.at[w, step],
            device_id={"mp": to}, device_id_type=MESH,
        )

    def units(self, w):
        return range(w * self.parts, (w + 1) * self.parts)

    def begin(self, w):
        for u in self.units(w):
            for slot in range(self.half):
                self.start(self.first_copy, u, slot)
                if self.grads is not None:
                    self.keep_copy(u, slot).start()

    def add(self, dst, src, count):
        def step(i, carry):
            dst[i] = (dst[i].astype(F32) + src(i).astype(F32)).astype(BF16)
            return carry

        lax.fori_loop(0, count, step, 0)

    def take(self, w, k):
        for u in self.units(w):
            count = self.half >> k
            if k == 0:
                for slot in range(self.half):
                    if self.grads is not None:
                        self.keep_copy(u, slot).wait()
                    self.first_copy(u, slot).wait_recv()
                self.add(self.got[0].at[u], lambda i: self.kept[u, i], count)
            else:
                self.round_copy(u, k).wait_recv()
                mine = bit_of(self.d, self.order(u)[k]) * count
                self.add(self.got[k].at[u], lambda i: self.got[k - 1][u, mine + i], count)

    def send(self, w, k):
        for u in self.units(w):
            self.start(self.round_copy, u, k)

    def schedule(self, order):
        events = []
        ahead = 2

        def event(w, k, starts):
            def run():
                self.take(w, k)
                if k and k + 1 < self.dp_bits:
                    self.send(w, k + 1)
                for other in starts:
                    self.send(other, 1)
                if k + 1 == self.dp_bits:
                    self.begin_last(w)

            return run

        for i, w in enumerate(order):
            starts = [w] if i < ahead and self.dp_bits > 1 else []
            events.append(event(w, 0, starts))
        for i, w in enumerate(order):
            for k in range(1, self.dp_bits):
                starts = [order[i + ahead]] if k == 1 and i + ahead < len(order) else []
                events.append(event(w, k, starts))
        return events

    def put(self, w, index, value):
        held = self.parts * self.rows
        for low in range(2):
            which = lax.rem(bit_of(self.d, 0) + low, 2)
            for u in self.units(w):
                cut = low * held + u % self.parts * self.rows
                self.pool[which, u, self.slot_of(u, index)] = value[cut : cut + self.rows]

    def weight_grad(self, w, left, right):
        held = self.parts * self.rows

        def step(t, carry):
            at = pl.ds(pl.multiple_of(t * 2 * held, 2 * held), 2 * held)
            self.put(w, t, dot(left(at), right(), 1, 0).astype(BF16))
            return carry

        lax.fori_loop(0, 1 << (self.dp_bits - 1), step, 0)
        self.begin(w)

    def begin_last(self, w):
        cols = self.features // self.stages
        whole = [self.got[self.dp_bits - 1][u, 0] for u in self.units(w)]
        for s in range(self.stages):
            self.zsend[w, s] = jnp.concatenate(
                [piece[:, s * cols : (s + 1) * cols] for piece in whole], axis=1
            )
        for step in range(1, self.stages):
            self.start(self.last_copy, w, step)

    def finish(self, w):
        value = self.zsend[w, self.z].astype(F32)
        for step in range(1, self.stages):
            self.last_copy(w, step).wait_recv()
            value = value + self.zgot[w, step].astype(F32)
        cols = self.features // self.stages
        for p in range(self.parts):
            at = slice(p * self.rows, (p + 1) * self.rows)
            self.outs[w][at, :] = value[:, p * cols : (p + 1) * cols]

    def close(self):
        for make, args in self.sent:
            make(*args).wait_send()


def reduction_scratch(count, dp, stages, rows, features, local=False):
    dp_bits, half, cols = dp.bit_length() - 1, dp // 2, features // stages
    parts = 2 if rows % 32 == 0 else 1
    dma = pltpu.SemaphoreType.DMA
    units = count * parts
    return (
        [pltpu.VMEM((1 + local, units, half, rows // parts, features), BF16)]
        + [pltpu.VMEM((units, half >> k, rows // parts, features), BF16) for k in range(dp_bits)]
        + [pltpu.VMEM((count, stages, rows // parts, cols * parts), BF16)] * 2
        + [
            dma((units, half)), dma((units, half + dp_bits)), dma((units, half + dp_bits)),
            dma((count, stages)), dma((count, stages)),
        ]
    )


def spans(rows, width, block):
    own = width - rows
    out=[]
    for qb in range(rows//block):
        hi = own + (qb+1)*block
        lo = max(0, (own + qb*block - (DOC_MAX-1))//block*block)
        out.append((lo,hi))
    return out

def head_lanes(h, features):
    first = h*HD
    off = jnp.minimum(lax.div(first, LANES)*LANES, features-2*LANES)
    off = pl.multiple_of(off, LANES)
    lane = lax.broadcasted_iota(jnp.int32,(1,2*LANES),1) + (off-first)
    return pl.ds(off, 2*LANES), (lane>=0)&(lane<HD)

def fill_bias(seg_query, seg_key, bias, block, own):
    rows = seg_query.shape[1]; width=seg_key.shape[0]
    for kb in range(width//block):
        for qb in range(rows//block):
            row = seg_query[:, qb*block:(qb+1)*block]
            col = seg_key[kb*block:(kb+1)*block,:]
            ahead = (lax.broadcasted_iota(jnp.int32,(block,block),0)+(kb*block)) <= (lax.broadcasted_iota(jnp.int32,(block,block),1)+(own+qb*block))
            bias[kb*block:(kb+1)*block, qb*block:(qb+1)*block] = jnp.where((col==row)&ahead, 0.0, FAR)

def transpose_out(src, dst):
    for i in range(src.shape[0]//LANES):
        at = slice(i*LANES,(i+1)*LANES)
        dst[:, at] = src[at,:].T.astype(dst.dtype)

class Gathering:
    def __init__(self, dp_bits, stages, d, z, weights, homes, refs):
        self.dp_bits, self.stages, self.d, self.z = dp_bits, stages, d, z
        self.weights, self.homes = weights, homes
        self.blocks, self.slab, self.zs, self.zr, self.ds, self.dr, self.ls = refs
        self.rows, self.cols = weights[0].shape
        self.parts = self.ds.shape[0] // len(weights)
        self.cut = self.rows // self.parts
        self.sent = []

    def start(self, make, *args):
        make(*args).start()
        self.sent.append((make, args, None))

    def order(self, u):
        return split_order(self.dp_bits, u % self.parts)[::-1]

    def hop_copy(self, w, j, way):
        at = lax.rem(self.z - way * j + self.stages, self.stages)
        to = lax.rem(self.z + way + self.stages, self.stages)
        return pltpu.make_async_remote_copy(
            src_ref=self.blocks.at[w, at], dst_ref=self.blocks.at[w, at],
            send_sem=self.zs.at[w, 2 * j + (way + 1) // 2], recv_sem=self.zr.at[w, at],
            device_id={"mp": to}, device_id_type=MESH,
        )

    def there(self, j, way):
        return self.z >= j if way == 1 else self.z < self.stages - j

    def pack(self, w):
        pieces = [self.weights[w][p * self.cut : (p + 1) * self.cut] for p in range(self.parts)]
        self.blocks[w, self.z] = jnp.concatenate(pieces, axis=1)

    def take(self, w, j):
        for way in (1, -1):

            @pl.when(self.there(j, way))
            def _():
                self.hop_copy(w, j, way).wait_recv()

    def hop(self, w, j):
        if j:
            self.take(w, j)
        for way in (1, -1):
            sends = self.there(j, way) & self.there(1, -way)

            @pl.when(sends)
            def _():
                self.hop_copy(w, j, way).start()

            self.sent.append((self.hop_copy, (w, j, way), sends))

    def place(self, u, which):
        at = which * self.rows + u % self.parts * self.cut
        return self.homes[u // self.parts].at[pl.ds(pl.multiple_of(at, self.cut), self.cut)]

    def piece(self, u):
        at = u % self.parts * self.cut
        return self.slab.at[u // self.parts, pl.ds(at, self.cut)]

    def own_copy(self, u):
        return pltpu.make_async_copy(self.piece(u), self.place(u, self.d), self.ls.at[u])

    def round_copy(self, u, k, slot, held):
        which = flipped(self.d, held)
        return pltpu.make_async_remote_copy(
            src_ref=self.place(u, which) if held else self.piece(u),
            dst_ref=self.place(u, which),
            send_sem=self.ds.at[u, (1 << k) - 1 + slot], recv_sem=self.dr.at[u, which],
            device_id={"dp": flipped(self.d, self.order(u)[k : k + 1])}, device_id_type=MESH,
        )

    def arrival(self, u, k, held):
        which = flipped(self.d, held + tuple(self.order(u)[k : k + 1]))
        return pltpu.make_async_remote_copy(
            src_ref=self.piece(u), dst_ref=self.place(u, which),
            send_sem=self.ds.at[u, 0], recv_sem=self.dr.at[u, which],
            device_id={"dp": flipped(self.d, self.order(u)[k : k + 1])}, device_id_type=MESH,
        )

    def units(self, w):
        return range(w * self.parts, (w + 1) * self.parts)

    def begin_round(self, w, k):
        for u in self.units(w):
            for slot, held in enumerate(subsets(self.order(u)[:k])):
                self.start(self.round_copy, u, k, slot, held)

    def collect(self, w):
        self.take(w, self.stages - 1)
        for p in range(self.parts):
            lanes = slice(p * self.cols, (p + 1) * self.cols)
            self.slab[w, p * self.cut : (p + 1) * self.cut] = jnp.concatenate(
                [self.blocks[w, s, :, lanes] for s in range(self.stages)], axis=1
            )
        for u in self.units(w):
            self.own_copy(u).start()

    def advance(self, w, k):
        for u in self.units(w):
            for held in subsets(self.order(u)[:k]):
                self.arrival(u, k, held).wait_recv()
        if k + 1 < self.dp_bits:
            self.begin_round(w, k + 1)
        else:
            for u in self.units(w):
                self.own_copy(u).wait()

    def close(self):
        for make, args, sends in self.sent:
            if sends is None:
                make(*args).wait_send()
            else:

                @pl.when(sends)
                def _():
                    make(*args).wait_send()


def gathering_scratch(count, dp, stages, rows, cols):
    parts = 2 if rows % 32 == 0 else 1
    dma = pltpu.SemaphoreType.DMA
    units = count * parts
    return [
        pltpu.VMEM((count, stages, rows // parts, cols * parts), BF16),
        pltpu.VMEM((count, rows, cols * stages), BF16),
        dma((count, 2 * stages)), dma((count, stages)), dma((units, dp)), dma((units, dp)), dma((units,)),
    ]


def forward_kernel(block, dp_bits, stages, back, *refs):
    weights, refs = refs[:6], refs[6:]
    bias_in, tokens, gain, factor, seg_query, seg_key = refs[:6]
    fulls, refs = refs[6:12], refs[12:]
    bias_full, raw_out, q_out, k_out, v_out, nt_out, o_ref, lse_ref = refs[:8]
    refs = refs[8:]
    home, window, normed, nt, raw, q, k, v, vt, ot, bias, scores, tops, totals, bias_all = refs[:15]
    xs, xr, bs, br, os = refs[15:20]
    d, z = greet(dp_bits, stages)
    rows, features = tokens.shape
    width, heads = k.shape[0], features // HD
    own = width - rows
    tile = 2 * LANES
    homes = [home.at[w] for w in range(3)] + list(fulls[3:])
    work = Gathering(dp_bits, stages, d, z, weights, homes, refs[20:])

    def bias_copy(step):
        return pltpu.make_async_remote_copy(
            src_ref=bias_in, dst_ref=bias_all.at[step], send_sem=bs.at[step],
            recv_sem=br.at[step], device_id={"mp": lax.rem(z + step, stages)},
            device_id_type=MESH,
        )

    def token_copy(hop):
        return pltpu.make_async_remote_copy(
            src_ref=tokens if hop == 0 else window.at[hop - 1], dst_ref=window.at[hop],
            send_sem=xs.at[hop], recv_sem=xr.at[hop],
            device_id={"mp": jnp.minimum(z + 1, stages - 1)}, device_id_type=MESH,
        )

    kept = [
        (raw, raw_out), (q, q_out), (k, k_out), (v, v_out), (nt, nt_out),
        (home.at[0], fulls[0]), (home.at[1], fulls[1]), (home.at[2], fulls[2]),
    ]

    def keep(i):
        return pltpu.make_async_copy(kept[i][0], kept[i][1], os.at[i])

    def norm(src, at):
        step_rows = 128

        def step(i, carry):
            part = pl.ds(pl.multiple_of(i * step_rows, step_rows), step_rows)
            x = src[part, :].astype(F32)
            value = (x * row_inverse(x) * gain[...]).astype(BF16)
            to = pl.ds(pl.multiple_of(at + i * step_rows, step_rows), step_rows)
            normed[to, :] = value
            return carry

        lax.fori_loop(0, rows // step_rows, step, 0)
        for c in range(features // tile):
            lanes = slice(c * tile, (c + 1) * tile)
            nt[lanes, at : at + rows] = normed[at : at + rows, lanes].T

    def project(w, at, out, out_t):
        def step(c, carry):
            lanes = pl.ds(pl.multiple_of(c * tile, tile), tile)
            value = dot(normed[at : at + rows, :], home[w, :, lanes], 1, 0).astype(BF16)
            out[at : at + rows, lanes] = value
            if out_t is not None:
                out_t[lanes, at : at + rows] = value.T
            return carry

        lax.fori_loop(0, features // tile, step, 0)

    first, rest = range(3), range(3, 6)
    for w in range(6):
        work.pack(w)
    for w in first:
        work.hop(w, 0)
    for step in range(1, stages):
        work.start(bias_copy, step)
    bias_all[0] = bias_in[...]
    for hop in range(back):

        @pl.when(z <= hop)
        def _():
            window[hop] = jnp.zeros((rows, features), BF16)

    norm(tokens, own)
    fill_bias(seg_query, seg_key, bias, block, own)
    for j in range(1, stages - 1):
        for w in first:
            work.hop(w, j)
    for w in rest:
        work.hop(w, 0)
    for w in first:
        work.collect(w)
        work.begin_round(w, 0)
    for j in range(1, stages - 1):
        if j <= 3 and dp_bits > 1:
            work.advance(j - 1, 0)
        for w in rest:
            work.hop(w, j)

    @pl.when(z < stages - 1)
    def _():
        token_copy(0).start()

    if dp_bits > 1:
        for w in range(max(0, min(stages - 2, 3)), 3):
            work.advance(w, 0)
    for w in rest:
        work.collect(w)
    for r in range(1, dp_bits - 1):
        for w in first:
            work.advance(w, r)
    for w in rest:
        work.begin_round(w, 0)
    for w in first:
        work.advance(w, dp_bits - 1)
        keep(5 + w).start()
        if w == 0:

            def query(c, carry):
                lanes = pl.ds(pl.multiple_of(c * tile, tile), tile)
                value = dot(normed[own:, :], home[0, :, lanes], 1, 0)
                raw[:, lanes] = value
                q[:, lanes] = (value * factor[:, lanes]).astype(BF16)
                return carry

            lax.fori_loop(0, features // tile, query, 0)
            keep(0).start()
            keep(1).start()
        else:
            project(w, own, *((k, None) if w == 1 else (v, vt)))

    sp = spans(rows, width, block)

    def attend(low, high, fresh, last, due):
        tiles = []
        for kb in range(low // block, high // block):
            qs = [i for i, (lo, hi) in enumerate(sp) if lo <= kb * block < hi]
            if qs:
                tiles.append((kb, qs))

        def head(h, carry):
            for at in sorted(set(due.values())):

                @pl.when(h == at)
                def _():
                    for w, r in due:
                        if due[w, r] == at:
                            work.advance(w, r)

            lanes, mine = head_lanes(h, features)
            feats = pl.ds(pl.multiple_of(h * HD, 16), HD)
            query = jnp.where(mine, q[:, lanes], jnp.zeros((), BF16))
            top = [jnp.full((8, block), FAR, F32) for _ in sp]
            for kb, qs in tiles:
                qa, qz = qs[0] * block, (qs[-1] + 1) * block
                at = slice(kb * block, (kb + 1) * block)
                s = dot(k[at, lanes], query[qa:qz], 1, 1) + bias[at, qa:qz]
                scores[at, qa:qz] = s
                for i in qs:
                    cut = s[:, i * block - qa : (i + 1) * block - qa]
                    top[i] = jnp.maximum(top[i], jnp.max(cut.reshape(block // 8, 8, block), axis=0))
            top = jnp.concatenate([jnp.max(t, axis=0, keepdims=True) for t in top], axis=1)
            if not fresh:
                before = tops[pl.ds(h, 1), :]
                top = jnp.maximum(top, before)
                scale = jnp.exp(before - top)
            acc = [jnp.zeros((HD, block), F32) for _ in sp]
            total = [jnp.zeros((8, block), F32) for _ in sp]
            for kb, qs in tiles:
                qa, qz = qs[0] * block, (qs[-1] + 1) * block
                at = slice(kb * block, (kb + 1) * block)
                p = jnp.exp(scores[at, qa:qz] - top[:, qa:qz])
                part = dot(vt[feats, at], p.astype(BF16), 1, 0)
                for i in qs:
                    cut = slice(i * block - qa, (i + 1) * block - qa)
                    total[i] = total[i] + jnp.sum(p[:, cut].reshape(block // 8, 8, block), axis=0)
                    acc[i] = acc[i] + part[:, cut]
            for i in range(len(sp)):
                at = slice(i * block, (i + 1) * block)
                one = jnp.sum(total[i], axis=0, keepdims=True)
                out = acc[i]
                if not fresh:
                    one = one + totals[pl.ds(h, 1), at] * scale[:, at]
                    out = out + ot[feats, at] * scale[:, at]
                if last:
                    ot[feats, at] = out / one
                    lse_ref[pl.ds(h, 1), at] = top[:, at] + jnp.log(one)
                else:
                    ot[feats, at] = out
                    totals[pl.ds(h, 1), at] = one
                    tops[pl.ds(h, 1), at] = top[:, at]
            return carry

        lax.fori_loop(0, heads, head, 0)

    inside = {}
    if back and dp_bits > 2:
        inside = {(3, 0): 0, (4, 0): heads // 4, (5, 0): heads // 2, (3, 1): heads * 3 // 4}
    for hop in range(back):
        if hop + 1 == back:
            attend(rows, width, True, False, inside)

        @pl.when(z > hop)
        def _():
            token_copy(hop).wait_recv()

        if hop + 1 < back:

            @pl.when((z > hop) & (z < stages - 1))
            def _():
                token_copy(hop + 1).start()

        at = own - (hop + 1) * rows
        norm(window.at[hop], at)
        project(1, at, k, None)
        project(2, at, v, vt)
    for i in range(2, 5):
        keep(i).start()
    attend(0, rows if back else width, not back, True, {})
    transpose_out(ot, o_ref)
    for r in range(dp_bits):
        for w in rest:
            if (w, r) not in inside:
                work.advance(w, r)
    for step in range(1, stages):
        bias_copy(step).wait_recv()
    bias_full[...] = jnp.concatenate(
        [bias_all[lax.rem(z - s + stages, stages)] for s in range(stages)], axis=1
    )
    for hop in range(back):

        @pl.when((z >= hop) & (z < stages - 1))
        def _():
            token_copy(hop).wait_send()

    for i in range(len(kept)):
        keep(i).wait()
    work.close()


def attend_forward(weights, bias, tokens, gain, factor, seg_q, seg_k, block, dp, stages, back):
    held, cols = weights[0].shape
    rows, features = tokens.shape
    width, heads = (back + 1) * rows, features // HD
    hbm = pl.BlockSpec(memory_space=pl.ANY)
    vmem = pl.BlockSpec(memory_space=pltpu.VMEM)
    dma = pltpu.SemaphoreType.DMA
    sds = jax.ShapeDtypeStruct
    return pl.pallas_call(
        functools.partial(forward_kernel, block, dp.bit_length() - 1, stages, back),
        in_specs=[vmem] * 12,
        out_specs=[hbm] * 6 + [vmem] + [hbm] * 5 + [vmem] * 2,
        out_shape=[sds((features, features), BF16)] * 6
        + [
            sds((1, features), F32),
            sds((rows, features), F32),
            sds((rows, features), BF16),
            sds((width, features), BF16),
            sds((width, features), BF16),
            sds((features, width), BF16),
            sds((rows, features), BF16),
            sds((heads, rows), F32),
        ],
        scratch_shapes=[
            pltpu.VMEM((3, features, features), BF16),
            pltpu.VMEM((back, rows, features), BF16),
            pltpu.VMEM((width, features), BF16),
            pltpu.VMEM((features, width), BF16),
            pltpu.VMEM((rows, features), F32),
            pltpu.VMEM((rows, features), BF16),
            pltpu.VMEM((width, features), BF16),
            pltpu.VMEM((width, features), BF16),
            pltpu.VMEM((features, width), BF16),
            pltpu.VMEM((features, rows), F32),
            pltpu.VMEM((width, rows), F32),
            pltpu.VMEM((width, rows), F32),
            pltpu.VMEM((heads, rows), F32),
            pltpu.VMEM((heads, rows), F32),
            pltpu.VMEM((stages,) + bias.shape, F32),
            dma((back,)), dma((back,)), dma((stages,)), dma((stages,)), dma((8,)),
        ]
        + gathering_scratch(6, dp, stages, held, cols),
        compiler_params=pltpu.CompilerParams(
            collective_id=0, has_side_effects=True, vmem_limit_bytes=62 << 20
        ),
        name="attend_forward",
    )(*weights, bias, tokens, gain, factor, seg_q, seg_k)


def middle_kernel(block, dp_bits, stages, *refs):
    sources, refs = refs[:12], refs[12:]
    b_up, b_down, gain, factor, lse_ref, seg_query, seg_key = refs[:7]
    results, incoming, outs, sums, refs = refs[7:12], refs[12], refs[13:16], refs[16], refs[17:]
    weights, hidden, wide, tmp, tr, keys, values, query_in, grad_in, bias, delta_ref = refs[:11]
    ps, pr, sems, refs = refs[11], refs[12], refs[13], refs[14:]
    d, z = greet(dp_bits, stages)
    work = Reduction(dp_bits, stages, d, z, None, outs, refs)
    rows, features = query_in.shape
    heads, width = features // HD, keys.shape[0]
    back = width // rows - 1
    tile = 2 * LANES
    w_out, w_up, w_down = weights.at[0], weights.at[1], weights.at[2]
    w_key, w_value = weights.at[2], weights.at[1]
    mixed, cot, x, second, active, d_pre, d_attn, spare = (tmp.at[i] for i in range(8))
    dk, dv = tmp.at[: back + 1], tmp.at[back + 1 : 2 * back + 2]
    dq, part = tmp.at[2 * back + 2], tmp.at[2 * back + 3]
    inside = (
        mixed, w_out, x, cot, w_up, w_down, keys, values, query_in, w_key, w_value, hidden,
    )
    outside = (spare, hidden, dq, dk, dv)
    loads = Loads(list(zip(sources, inside)) + list(zip(outside, results)), sems)
    loads.start(*range(9))
    fill_bias(seg_query, seg_key, bias, block, width - rows)

    def by_tile(body):
        def step(c, carry):
            body(pl.ds(pl.multiple_of(c * tile, tile), tile), c)
            return carry

        lax.fori_loop(0, features // tile, step, 0)

    def by_rows(body, start):
        def step(i, carry):
            return body(pl.ds(pl.multiple_of(i * 64, 64), 64), carry)

        return lax.fori_loop(0, rows // 64, step, start)

    def flip(src):
        for c in range(features // tile):
            lanes = slice(c * tile, (c + 1) * tile)
            tr[lanes, :] = src[:, lanes].T

    nothing = jnp.zeros((1, features), F32)

    def add_attention(lanes, c):
        hidden[:, lanes] = x[:, lanes].astype(F32) + dot(mixed[...], w_out[lanes, :], 1, 1)

    def norm(at, carry):
        h = hidden[at, :]
        second[at, :] = (h * row_inverse(h) * gain[...]).astype(BF16)
        return carry

    def activate(lanes, c):
        pre = dot(second[...], w_up[:, lanes], 1, 0) + b_up[:, lanes]
        sigma = 1.0 / (1.0 + jnp.exp(-pre))
        active[:, lanes] = (pre * sigma).astype(BF16)
        grad = dot(cot[...], w_down[:, lanes], 1, 0)
        grad = (grad * sigma * (1.0 + pre * (1.0 - sigma))).astype(BF16)
        d_pre[:, lanes] = grad
        sums[2:3, lanes] = jnp.sum(grad.astype(F32), axis=0, keepdims=True)

    def finish_layer(lanes, c):
        out = dot(active[...], w_down[lanes, :], 1, 1)
        spare[:, lanes] = (hidden[:, lanes] + out + b_down[:, lanes]).astype(BF16)
        sums[1:2, lanes] = jnp.sum(cot[:, lanes].astype(F32), axis=0, keepdims=True)

    def to_second(lanes, c):
        wide[:, lanes] = dot(d_pre[...], w_up[lanes, :], 1, 1)

    def to_hidden(at, column):
        h, grad = hidden[at, :], wide[at, :]
        inverse = row_inverse(h)
        weighted = grad * gain[...]
        dots = jnp.sum(weighted * h, axis=1, keepdims=True)
        cube = inverse * inverse * inverse
        d_hidden = cot[at, :].astype(F32) + inverse * weighted - h * cube / features * dots
        hidden[at, :] = d_hidden
        d_attn[at, :] = d_hidden.astype(BF16)
        return column + jnp.sum(grad * h * inverse, axis=0, keepdims=True)

    def to_mixed(lanes, c):
        grad = dot(d_attn[...], w_out[:, lanes], 1, 0).astype(BF16)
        grad_in[:, lanes] = grad
        both = grad.astype(F32) * mixed[:, lanes].astype(F32)
        lane = lax.broadcasted_iota(jnp.int32, (heads, tile), 1) + c * tile
        first = lax.broadcasted_iota(jnp.int32, (heads, tile), 0) * HD
        owner = jnp.where((lane >= first) & (lane < first + HD), 1.0, 0.0).astype(BF16)
        high = both.astype(BF16)
        rest = (both - high.astype(F32)).astype(BF16)
        delta_ref[...] += dot(owner, high, 1, 1) + dot(owner, rest, 1, 1)

    events = work.schedule(range(3))
    sums[3:8, :] = jnp.zeros((5, features), F32)
    delta_ref[...] = jnp.zeros_like(delta_ref)
    loads.wait(0, 1, 2)
    by_tile(add_attention)
    by_rows(norm, 0)
    loads.wait(3, 4, 5)
    by_tile(activate)
    flip(cot)
    work.weight_grad(0, lambda at: tr[at, :], lambda: active[...])
    by_tile(finish_layer)
    loads.start(12, 9)
    by_tile(to_second)
    loads.start(10)
    flip(second)
    work.weight_grad(1, lambda at: tr[at, :], lambda: d_pre[...])
    events[0]()
    sums[0:1, :] = by_rows(to_hidden, nothing)
    loads.start(13)
    by_tile(to_mixed)
    flip(d_attn)
    work.weight_grad(2, lambda at: tr[at, :], lambda: mixed[...])
    events[1]()
    loads.wait(12)
    for c in range(2 * back + 2):
        tmp[c] = jnp.zeros((rows, features), BF16)
    wide[...] = jnp.zeros_like(wide)
    loads.wait(6, 7, 8)
    sp = spans(rows, width, block)
    steps = heads * (back + 1)
    due = {i + 2: int(at * steps) // 2 * 2 for i, at in enumerate(EVENTS[: len(events) - 2])}

    def down():
        return pltpu.make_async_remote_copy(
            src_ref=part, dst_ref=incoming, send_sem=ps, recv_sem=pr,
            device_id={"mp": jnp.maximum(z - 1, 0)}, device_id_type=MESH,
        )

    for c in range(back + 1):

        def head(h):
            lanes, mine = head_lanes(h, features)
            zero = jnp.zeros((), BF16)
            query = jnp.where(mine, query_in[:, lanes], zero)
            grad = jnp.where(mine, grad_in[:, lanes], zero)
            lse = lse_ref[pl.ds(h, 1), :]
            delta = delta_ref[pl.ds(h, 1), :]
            for kb in range(c * rows // block, (c + 1) * rows // block):
                qs = [i for i, (lo, hi) in enumerate(sp) if lo <= kb * block < hi]
                if not qs:
                    continue
                qa, qz = qs[0] * block, (qs[-1] + 1) * block
                at = slice(kb * block, (kb + 1) * block)
                to = slice(kb * block - c * rows, (kb + 1) * block - c * rows)
                key = keys[at, lanes]
                s = dot(key, query[qa:qz], 1, 1) + bias[at, qa:qz]
                p = jnp.exp(s - lse[:, qa:qz])
                dp = dot(values[at, lanes], grad[qa:qz], 1, 1)
                ds = (p * (dp - delta[:, qa:qz])).astype(BF16)
                dv[c, to, lanes] += dot(p.astype(BF16), grad[qa:qz], 1, 0).astype(BF16)
                dk[c, to, lanes] += dot(ds, query[qa:qz], 1, 0).astype(BF16)
                wide[qa:qz, lanes] += dot(ds, jnp.where(mine, key, zero), 0, 0)

        def pair(i, carry):
            for at in sorted(set(due.values())):
                if at // heads != c:
                    continue

                @pl.when(2 * i == at % heads)
                def _():
                    for e in due:
                        if due[e] == at:
                            events[e]()

            head(2 * i)
            head(2 * i + 1)
            return carry

        lax.fori_loop(0, heads // 2, pair, 0)
        if c == 0:
            loads.wait(9, 10)
            if back:
                back_project(part, ((dk.at[0], w_key), (dv.at[0], w_value)), 0, None)

                @pl.when(z >= back)
                def _():
                    down().start()

            loads.wait(13)
            loads.start(11)

    loads.start(15, 16)
    loads.wait(11)

    def to_query(at, column):
        scaled = wide[at, :].astype(BF16).astype(F32)
        dq[at, :] = (scaled * factor[...]).astype(BF16)
        return column + jnp.sum(scaled * hidden[at, :], axis=0, keepdims=True)

    sums[4:5, :] = by_rows(to_query, nothing)
    loads.start(14)
    for i in range(2, len(events)):
        if i not in due:
            events[i]()
    for w in range(3):
        work.finish(w)
    loads.wait(14, 15, 16)
    if back:

        @pl.when((z + 1 >= back) & (z < stages - 1))
        def _():
            down().wait_recv()

        @pl.when(z >= back)
        def _():
            down().wait_send()

    work.close()


def back_project(out, pairs, at, more):
    rows, features = out.shape
    tile = 2 * LANES

    def step(c, carry):
        lanes = pl.ds(pl.multiple_of(c * tile, tile), tile)
        value = None
        for grad, weight in pairs:
            start = at if grad.shape[0] > rows else 0
            term = dot(grad[start : start + rows, :], weight[lanes, :], 1, 1)
            value = term if value is None else value + term
        if more is not None:
            value = value + more(lanes)
        out[:, lanes] = value.astype(out.dtype)
        return carry

    lax.fori_loop(0, features // tile, step, 0)


def middle(
    mixed, w_out, x, cot, w_up, w_down, k, v, q, w_key, w_value, raw, b_up, b_down, gain, factor,
    lse, seg_q, seg_k, block, dp, stages,
):
    rows, features = q.shape
    width, heads = k.shape[0], features // HD
    held, cols = features // dp, features // stages
    chunks = width // rows
    hbm = pl.BlockSpec(memory_space=pl.ANY)
    vmem = pl.BlockSpec(memory_space=pltpu.VMEM)
    dma = pltpu.SemaphoreType.DMA
    sds = jax.ShapeDtypeStruct
    low, high = sds((rows, features), BF16), sds((rows, features), F32)
    many = sds((chunks, rows, features), BF16)
    return pl.pallas_call(
        functools.partial(middle_kernel, block, dp.bit_length() - 1, stages),
        in_specs=[hbm] * 12 + [vmem] * 7,
        out_specs=[hbm] * 6 + [vmem] * 4,
        out_shape=[low, high, low, many, many, low]
        + [sds((held, cols), F32)] * 3
        + [sds((8, features), F32)],
        scratch_shapes=[
            pltpu.VMEM((3, features, features), BF16),
            pltpu.VMEM((rows, features), F32),
            pltpu.VMEM((rows, features), F32),
            pltpu.VMEM((max(8, 2 * chunks + 2), rows, features), BF16),
            pltpu.VMEM((features, rows), BF16),
            pltpu.VMEM((width, features), BF16),
            pltpu.VMEM((width, features), BF16),
            pltpu.VMEM((rows, features), BF16),
            pltpu.VMEM((rows, features), BF16),
            pltpu.VMEM((width, rows), F32),
            pltpu.VMEM((heads, rows), F32),
            dma, dma, dma((17,)),
        ]
        + reduction_scratch(3, dp, stages, held, features, True),
        compiler_params=pltpu.CompilerParams(
            collective_id=2, has_side_effects=True, vmem_limit_bytes=63 << 20
        ),
        name="middle",
    )(
        mixed, w_out, x, cot, w_up, w_down, k, v, q, w_key, w_value, raw, b_up, b_down, gain,
        factor, lse, seg_q, seg_k,
    )


def input_kernel(dp_bits, stages, back, *refs):
    sources, gain, sums, refs = refs[:10], refs[10], refs[11], refs[12:]
    outs, result, total, refs = refs[:3], refs[3], refs[4], refs[5:]
    inside, tokens_grad, refs = refs[:10], refs[10], refs[11:]
    dv, nt, dk, wk, wv, incoming, dq, wq, tokens, d_hidden = inside
    part, landed, d_first, sgot, ss, sr, ps, pr, sems = refs[:9]
    d, z = greet(dp_bits, stages)
    work = Reduction(dp_bits, stages, d, z, None, outs, refs[9:])
    loads = Loads(list(zip(sources, inside)) + [(tokens_grad, result)], sems)
    loads.start(*range(10))
    rows, features = tokens.shape
    own = back * rows
    levels = dp_bits + stages.bit_length() - 1
    held = features >> dp_bits
    grads = ((dv, 2, 0), (dk, 1, 0), (dq, 0, own))

    def down(hop):
        return pltpu.make_async_remote_copy(
            src_ref=part.at[hop - 1], dst_ref=landed.at[hop - 1], send_sem=ps.at[hop - 1],
            recv_sem=pr.at[hop - 1], device_id={"mp": jnp.maximum(z - 1, 0)}, device_id_type=MESH,
        )

    def arrived(hop):
        source = incoming if hop == 1 else landed.at[hop - 2]
        there = (z + 1 >= back - hop + 1) & (z < stages - 1)

        def take(lanes):
            return jnp.where(there, source[:, lanes].astype(F32), 0.0)

        return there, take

    def weight_grad(i):
        grad, w, at = grads[i]
        work.weight_grad(w, lambda rows_at: nt[rows_at, at:], lambda: grad[...])

    def sum_copy(k):
        if k < dp_bits:
            to = {"dp": flipped(d, (k,))}
        else:
            to = {"mp": flipped(z, (k - dp_bits,))}
        return pltpu.make_async_remote_copy(
            src_ref=total.at[k], dst_ref=sgot.at[k], send_sem=ss.at[k], recv_sem=sr.at[k],
            device_id=to, device_id_type=MESH,
        )

    def sum_step(k):
        sum_copy(k).wait_recv()
        total[k + 1] = total[k] + sgot[k]
        if k + 1 < levels:
            work.start(sum_copy, k + 1)

    def pass_down(hop):
        there, take = arrived(hop)
        if hop > 1:

            @pl.when(there)
            def _():
                down(hop - 1).wait_recv()

        back_project(part.at[hop - 1], ((dk, wk), (dv, wv)), hop * rows, take)

        @pl.when(z >= back - hop)
        def _():
            down(hop).start()

    events = work.schedule((2, 1, 0))
    loads.wait(0, 1)
    weight_grad(0)
    loads.wait(2, 3, 4, 5)
    if back > 1:
        pass_down(1)
    events[0]()
    weight_grad(1)
    loads.wait(6, 7)
    weight_grad(2)
    events[1]()
    for hop in range(2, back):
        pass_down(hop)
    events[2]()
    back_project(d_first, ((dk, wk), (dv, wv), (dq, wq)), own, None)
    early = 4 if dp_bits > 1 else 3
    for i in range(3, early):
        events[i]()
    loads.wait(8, 9)
    there, take = arrived(back) if back else (None, None)
    if back > 1:

        @pl.when(there)
        def _():
            down(back - 1).wait_recv()

    chunk = 64

    def finish(i, column):
        at = pl.ds(pl.multiple_of(i * chunk, chunk), chunk)
        x = tokens[at, :].astype(F32)
        grad = d_first[at, :]
        if back:
            source = incoming if back == 1 else landed.at[back - 2]
            grad = grad + jnp.where(there, source[at, :].astype(F32), 0.0)
        inverse = row_inverse(x)
        weighted = grad * gain[...]
        dots = jnp.sum(weighted * x, axis=1, keepdims=True)
        cube = inverse * inverse * inverse
        tokens_grad[at, :] = (
            d_hidden[at, :] + inverse * weighted - x * cube / features * dots
        ).astype(BF16)
        return column + jnp.sum(grad * x * inverse, axis=0, keepdims=True)

    column = lax.fori_loop(0, rows // chunk, finish, jnp.zeros((1, features), F32))
    total[0] = sums[...]
    total[0, 3:4, :] = column
    work.start(sum_copy, 0)
    loads.start(10)
    done = 0
    for event in events[early:]:
        event()
        if done < levels:
            sum_step(done)
            done += 1
    for k in range(done, levels):
        sum_step(k)
    for w in (2, 1, 0):
        work.finish(w)
    for hop in range(1, back):

        @pl.when(z >= back - hop)
        def _():
            down(hop).wait_send()

    loads.wait(10)
    work.close()


def input_gradients(
    nt, dq, dk, dv, wq, wk, wv, incoming, tokens, d_hidden, gain, sums, dp, stages
):
    rows, features = tokens.shape
    back = dk.shape[0] // rows - 1
    held, cols = features // dp, features // stages
    dp_bits = dp.bit_length() - 1
    levels = dp_bits + stages.bit_length() - 1
    hbm = pl.BlockSpec(memory_space=pl.ANY)
    vmem = pl.BlockSpec(memory_space=pltpu.VMEM)
    dma = pltpu.SemaphoreType.DMA
    hops = max(1, back - 1)
    sources = (dv, nt, dk, wk, wv, incoming, dq, wq, tokens, d_hidden)
    out = pl.pallas_call(
        functools.partial(input_kernel, dp_bits, stages, back),
        in_specs=[hbm] * 10 + [vmem] * 2,
        out_specs=[vmem] * 3 + [hbm, vmem],
        out_shape=[jax.ShapeDtypeStruct((held, cols), F32)] * 3
        + [
            jax.ShapeDtypeStruct((rows, features), BF16),
            jax.ShapeDtypeStruct((levels + 1,) + sums.shape, F32),
        ],
        scratch_shapes=[pltpu.VMEM(a.shape, a.dtype) for a in sources + (tokens,)]
        + [
            pltpu.VMEM((hops, rows, features), BF16), pltpu.VMEM((hops, rows, features), BF16),
            pltpu.VMEM((rows, features), F32), pltpu.VMEM((levels,) + sums.shape, F32),
            dma((levels,)), dma((levels,)), dma((hops,)), dma((hops,)), dma((11,)),
        ]
        + reduction_scratch(3, dp, stages, held, features, True),
        compiler_params=pltpu.CompilerParams(
            collective_id=1, has_side_effects=True, vmem_limit_bytes=62 << 20
        ),
        name="input_gradients",
    )(*sources, gain, sums)
    return out[:3], out[3], out[4][levels]


def body(
    tokens, segments, w_query, w_key, w_value, w_output, w_up, b_up, w_down, b_down,
    gain_attn, gain_mlp, query_scale, cotangent,
):
    stages = lax.axis_size("mp")
    z = lax.axis_index("mp")
    seg = segments[0]
    rows, features = tokens.shape
    back = min(stages - 1, -(-(DOC_MAX - 1) // rows))
    own = back * rows
    block = min(256, rows)

    seg_wide = jnp.concatenate([jnp.full((own,), -1, jnp.int32), seg])
    seg_window = lax.dynamic_slice_in_dim(seg_wide, z * rows, own + rows, 0)
    seg_query = seg_window[own:]
    seg_query, seg_key = seg_query[None, :], seg_window[:, None]

    heads = features // HD
    factor = jax.nn.softplus(query_scale) * (LOG2E / math.sqrt(HD))
    factor_cols = jnp.tile(factor, heads)
    dp = lax.axis_size("dp")
    (
        wq, wk, wv, wu, wo, wd, b_full, query_raw, scaled, keys, values, first_t, mixed, lse
    ) = attend_forward(
        (w_query, w_key, w_value, w_up, w_output.T, w_down.T), b_up[None], tokens,
        gain_attn[None], factor_cols[None], seg_query, seg_key, block, dp, stages, back,
    )
    layer_out, d_hidden, d_query, d_keys, d_values, incoming, *mlp, sums = middle(
        mixed, wo, tokens, cotangent, wu, wd, keys, values, scaled, wk, wv, query_raw,
        b_full, b_down[None], gain_mlp[None], factor_cols[None], lse, seg_query, seg_key,
        block, dp, stages,
    )
    grads, tokens_grad, sums = input_gradients(
        first_t, d_query, d_keys.reshape(own + rows, features),
        d_values.reshape(own + rows, features), wq, wk, wv, incoming, tokens, d_hidden,
        gain_attn[None], sums, dp, stages,
    )
    mine = b_up.shape[0]
    sum_b_up = lax.dynamic_slice_in_dim(sums[2], z * mine, mine, 0)
    scale_total = jnp.sum(sums[4].reshape(heads, HD), axis=0)
    grad_query_scale = scale_total * (LOG2E / math.sqrt(HD)) * jax.nn.sigmoid(query_scale)
    return (
        layer_out, tokens_grad, grads[0], grads[1], grads[2], mlp[2].T, mlp[1], sum_b_up,
        mlp[0].T, sums[1], sums[3], sums[0], grad_query_scale,
    )


def solution(mesh):
    tokens, rows_dp, rows_mp = P(("dp", "mp"), None), P("dp", "mp"), P("mp", "dp")
    return jax.shard_map(
        body,
        mesh=mesh,
        in_specs=(
            tokens, P("dp", None), rows_dp, rows_dp, rows_dp, rows_mp, rows_dp, P("mp"), rows_mp,
            P(), P(), P(), P(), tokens,
        ),
        out_specs=(
            tokens, tokens, rows_dp, rows_dp, rows_dp, rows_mp, rows_dp, P("mp"), rows_mp,
            P(), P(), P(), P(),
        ),
        check_vma=False,
    )
```

```python
import functools
import math

import jax
import jax.numpy as jnp
from jax import lax
from jax.experimental import pallas as pl
from jax.experimental.pallas import tpu as pltpu
from jax.sharding import PartitionSpec as P

HD = 80
LANES = 128
EPSILON = 1e-06
LOG2E = 1.442695
DOC_MAX = 1024
FAR = -1e30
EVENTS = (0.15, 0.3, 0.5, 0.6, 0.75, 0.9)
F32 = jnp.float32
BF16 = jnp.bfloat16


def dot(a, b, ca, cb):
    return lax.dot_general(a, b, (((ca,), (cb,)), ((), ())), preferred_element_type=F32)


def row_inverse(values):
    return lax.rsqrt(jnp.mean(values * values, axis=1, keepdims=True) + EPSILON)


MESH = pl.DeviceIdType.MESH


def bit_of(index, b):
    return lax.rem(lax.div(index, 1 << b), 2)


def flipped(index, bits):
    for b in bits:
        index = index + (1 << b) * (1 - 2 * bit_of(index, b))
    return index


def split_order(count, turn):
    bits = list(range(count))
    rest = bits[1:][::-1]
    turn = turn % max(1, len(rest))
    return bits[:1] + rest[turn:] + rest[:turn]


def subsets(bits):
    out = [()]
    for b in bits:
        out = out + [s + (b,) for s in out]
    return out


def greet(dp_bits, stages, extra=()):
    d, z = lax.axis_index("dp"), lax.axis_index("mp")
    barrier = pltpu.get_barrier_semaphore()
    for b in range(dp_bits):
        pl.semaphore_signal(barrier, device_id={"dp": flipped(d, (b,))}, device_id_type=MESH)
    for step in range(1, stages):
        pl.semaphore_signal(
            barrier, device_id={"mp": lax.rem(z + step, stages)}, device_id_type=MESH
        )
    pl.semaphore_wait(barrier, dp_bits + stages - 1)
    return d, z


class Loads:
    def __init__(self, pairs, sems):
        self.pairs, self.sems = pairs, sems

    def copy(self, i):
        return pltpu.make_async_copy(self.pairs[i][0], self.pairs[i][1], self.sems.at[i])

    def start(self, *which):
        for i in which:
            self.copy(i).start()

    def wait(self, *which):
        for i in which:
            self.copy(i).wait()


class Reduction:
    def __init__(self, dp_bits, stages, d, z, grads, outs, refs):
        self.dp_bits, self.stages, self.d, self.z = dp_bits, stages, d, z
        self.grads, self.outs = grads, outs
        self.pool = refs[0]
        self.kept, self.got = refs[0].at[0], refs[1 : 1 + dp_bits]
        self.zsend, self.zgot, self.ks, self.rs, self.rr, self.zs, self.zr = refs[1 + dp_bits :]
        self.half = 1 << (dp_bits - 1)
        self.parts = self.kept.shape[0] // len(outs)
        self.rows, self.features = self.kept.shape[2], self.kept.shape[3]
        self.sent = []

    def start(self, make, *args):
        make(*args).start()
        self.sent.append((make, args))

    def order(self, u):
        return split_order(self.dp_bits, u % self.parts)

    def place(self, u, slot, low):
        rest = self.order(u)[1:]
        at = low
        for i, b in enumerate(rest):
            if slot >> (len(rest) - 1 - i) & 1:
                at = at + (1 << b)
        return at

    def slot_of(self, u, index):
        rest = self.order(u)[1:]
        return sum(bit_of(index, b - 1) << (len(rest) - 1 - i) for i, b in enumerate(rest))

    def source(self, u, slot, low):
        cut = pl.ds(u % self.parts * self.rows, self.rows)
        return self.grads[u // self.parts].at[self.place(u, slot, low), cut]

    def first_copy(self, u, slot):
        return pltpu.make_async_remote_copy(
            src_ref=self.pool.at[1, u, slot]
            if self.grads is None
            else self.source(u, slot, 1 - bit_of(self.d, 0)),
            dst_ref=self.got[0].at[u, slot],
            send_sem=self.rs.at[u, slot], recv_sem=self.rr.at[u, slot],
            device_id={"dp": flipped(self.d, (0,))}, device_id_type=MESH,
        )

    def keep_copy(self, u, slot):
        return pltpu.make_async_copy(
            self.source(u, slot, bit_of(self.d, 0)), self.kept.at[u, slot], self.ks.at[u, slot]
        )

    def round_copy(self, u, k):
        count = self.half >> k
        b = self.order(u)[k]
        other = 1 - bit_of(self.d, b)
        return pltpu.make_async_remote_copy(
            src_ref=self.got[k - 1].at[u, pl.ds(other * count, count)],
            dst_ref=self.got[k].at[u],
            send_sem=self.rs.at[u, self.half + k], recv_sem=self.rr.at[u, self.half + k],
            device_id={"dp": flipped(self.d, (b,))}, device_id_type=MESH,
        )

    def last_copy(self, w, step):
        to = lax.rem(self.z + step, self.stages)
        return pltpu.make_async_remote_copy(
            src_ref=self.zsend.at[w, to], dst_ref=self.zgot.at[w, step],
            send_sem=self.zs.at[w, step], recv_sem=self.zr.at[w, step],
            device_id={"mp": to}, device_id_type=MESH,
        )

    def units(self, w):
        return range(w * self.parts, (w + 1) * self.parts)

    def begin(self, w):
        for u in self.units(w):
            for slot in range(self.half):
                self.start(self.first_copy, u, slot)
                if self.grads is not None:
                    self.keep_copy(u, slot).start()

    def add(self, dst, src, count):
        def step(i, carry):
            dst[i] = dst[i] + src(i)
            return carry

        lax.fori_loop(0, count, step, 0)

    def take(self, w, k):
        for u in self.units(w):
            count = self.half >> k
            if k == 0:
                for slot in range(self.half):
                    if self.grads is not None:
                        self.keep_copy(u, slot).wait()
                    self.first_copy(u, slot).wait_recv()
                self.add(self.got[0].at[u], lambda i: self.kept[u, i], count)
            else:
                self.round_copy(u, k).wait_recv()
                mine = bit_of(self.d, self.order(u)[k]) * count
                self.add(self.got[k].at[u], lambda i: self.got[k - 1][u, mine + i], count)

    def send(self, w, k):
        for u in self.units(w):
            self.start(self.round_copy, u, k)

    def advance(self, w, k):
        self.take(w, k)
        if k + 1 == self.dp_bits:
            self.begin_last(w)
        else:
            self.send(w, k + 1)

    def put(self, w, index, value):
        held = self.parts * self.rows
        for low in range(2):
            which = lax.rem(bit_of(self.d, 0) + low, 2)
            for u in self.units(w):
                cut = low * held + u % self.parts * self.rows
                self.pool[which, u, self.slot_of(u, index)] = value[cut : cut + self.rows]

    def weight_grad(self, w, left, right):
        held = self.parts * self.rows

        def step(t, carry):
            at = pl.ds(pl.multiple_of(t * 2 * held, 2 * held), 2 * held)
            self.put(w, t, dot(left(at), right(), 1, 0).astype(BF16))
            return carry

        lax.fori_loop(0, 1 << (self.dp_bits - 1), step, 0)
        self.begin(w)

    def begin_last(self, w):
        cols = self.features // self.stages
        whole = [self.got[self.dp_bits - 1][u, 0] for u in self.units(w)]
        for s in range(self.stages):
            self.zsend[w, s] = jnp.concatenate(
                [piece[:, s * cols : (s + 1) * cols] for piece in whole], axis=1
            )
        for step in range(1, self.stages):
            self.start(self.last_copy, w, step)

    def finish(self, w):
        value = self.zsend[w, self.z].astype(F32)
        for step in range(1, self.stages):
            self.last_copy(w, step).wait_recv()
            value = value + self.zgot[w, step].astype(F32)
        cols = self.features // self.stages
        for p in range(self.parts):
            at = slice(p * self.rows, (p + 1) * self.rows)
            self.outs[w][at, :] = value[:, p * cols : (p + 1) * cols]

    def close(self):
        for make, args in self.sent:
            make(*args).wait_send()


def reduction_scratch(count, dp, stages, rows, features, local=False):
    dp_bits, half, cols = dp.bit_length() - 1, dp // 2, features // stages
    parts = 2 if rows % 32 == 0 else 1
    dma = pltpu.SemaphoreType.DMA
    units = count * parts
    return (
        [pltpu.VMEM((1 + local, units, half, rows // parts, features), BF16)]
        + [pltpu.VMEM((units, half >> k, rows // parts, features), BF16) for k in range(dp_bits)]
        + [pltpu.VMEM((count, stages, rows // parts, cols * parts), BF16)] * 2
        + [
            dma((units, half)), dma((units, half + dp_bits)), dma((units, half + dp_bits)),
            dma((count, stages)), dma((count, stages)),
        ]
    )


def spans(rows, width, block):
    own = width - rows
    out=[]
    for qb in range(rows//block):
        hi = own + (qb+1)*block
        lo = max(0, (own + qb*block - (DOC_MAX-1))//block*block)
        out.append((lo,hi))
    return out

def head_lanes(h, features):
    first = h*HD
    off = jnp.minimum(lax.div(first, LANES)*LANES, features-2*LANES)
    off = pl.multiple_of(off, LANES)
    lane = lax.broadcasted_iota(jnp.int32,(1,2*LANES),1) + (off-first)
    return pl.ds(off, 2*LANES), (lane>=0)&(lane<HD)

def fill_bias(seg_query, seg_key, bias, block, own):
    rows = seg_query.shape[1]; width=seg_key.shape[0]
    for kb in range(width//block):
        for qb in range(rows//block):
            row = seg_query[:, qb*block:(qb+1)*block]
            col = seg_key[kb*block:(kb+1)*block,:]
            ahead = (lax.broadcasted_iota(jnp.int32,(block,block),0)+(kb*block)) <= (lax.broadcasted_iota(jnp.int32,(block,block),1)+(own+qb*block))
            bias[kb*block:(kb+1)*block, qb*block:(qb+1)*block] = jnp.where((col==row)&ahead, 0.0, FAR)

def transpose_out(src, dst):
    for i in range(src.shape[0]//LANES):
        at = slice(i*LANES,(i+1)*LANES)
        dst[:, at] = src[at,:].T.astype(dst.dtype)

class Gathering:
    def __init__(self, dp_bits, stages, d, z, weights, homes, refs):
        self.dp_bits, self.stages, self.d, self.z = dp_bits, stages, d, z
        self.weights, self.homes = weights, homes
        self.blocks, self.slab, self.zs, self.zr, self.ds, self.dr, self.ls = refs
        self.rows, self.cols = weights[0].shape
        self.parts = self.ds.shape[0] // len(weights)
        self.cut = self.rows // self.parts
        self.sent = []

    def start(self, make, *args):
        make(*args).start()
        self.sent.append((make, args, None))

    def order(self, u):
        return split_order(self.dp_bits, u % self.parts)[::-1]

    def hop_copy(self, w, j, way):
        at = lax.rem(self.z - way * j + self.stages, self.stages)
        to = lax.rem(self.z + way + self.stages, self.stages)
        return pltpu.make_async_remote_copy(
            src_ref=self.blocks.at[w, at], dst_ref=self.blocks.at[w, at],
            send_sem=self.zs.at[w, 2 * j + (way + 1) // 2], recv_sem=self.zr.at[w, at],
            device_id={"mp": to}, device_id_type=MESH,
        )

    def there(self, j, way):
        return self.z >= j if way == 1 else self.z < self.stages - j

    def pack(self, w):
        pieces = [self.weights[w][p * self.cut : (p + 1) * self.cut] for p in range(self.parts)]
        self.blocks[w, self.z] = jnp.concatenate(pieces, axis=1)

    def take(self, w, j):
        for way in (1, -1):

            @pl.when(self.there(j, way))
            def _():
                self.hop_copy(w, j, way).wait_recv()

    def hop(self, w, j):
        if j:
            self.take(w, j)
        for way in (1, -1):
            sends = self.there(j, way) & self.there(1, -way)

            @pl.when(sends)
            def _():
                self.hop_copy(w, j, way).start()

            self.sent.append((self.hop_copy, (w, j, way), sends))

    def place(self, u, which):
        at = which * self.rows + u % self.parts * self.cut
        return self.homes[u // self.parts].at[pl.ds(pl.multiple_of(at, self.cut), self.cut)]

    def piece(self, u):
        at = u % self.parts * self.cut
        return self.slab.at[u // self.parts, pl.ds(at, self.cut)]

    def own_copy(self, u):
        return pltpu.make_async_copy(self.piece(u), self.place(u, self.d), self.ls.at[u])

    def round_copy(self, u, k, slot, held):
        which = flipped(self.d, held)
        return pltpu.make_async_remote_copy(
            src_ref=self.place(u, which) if held else self.piece(u),
            dst_ref=self.place(u, which),
            send_sem=self.ds.at[u, (1 << k) - 1 + slot], recv_sem=self.dr.at[u, which],
            device_id={"dp": flipped(self.d, self.order(u)[k : k + 1])}, device_id_type=MESH,
        )

    def arrival(self, u, k, held):
        which = flipped(self.d, held + tuple(self.order(u)[k : k + 1]))
        return pltpu.make_async_remote_copy(
            src_ref=self.piece(u), dst_ref=self.place(u, which),
            send_sem=self.ds.at[u, 0], recv_sem=self.dr.at[u, which],
            device_id={"dp": flipped(self.d, self.order(u)[k : k + 1])}, device_id_type=MESH,
        )

    def units(self, w):
        return range(w * self.parts, (w + 1) * self.parts)

    def begin_round(self, w, k):
        for u in self.units(w):
            for slot, held in enumerate(subsets(self.order(u)[:k])):
                self.start(self.round_copy, u, k, slot, held)

    def collect(self, w):
        self.take(w, self.stages - 1)
        for p in range(self.parts):
            lanes = slice(p * self.cols, (p + 1) * self.cols)
            self.slab[w, p * self.cut : (p + 1) * self.cut] = jnp.concatenate(
                [self.blocks[w, s, :, lanes] for s in range(self.stages)], axis=1
            )
        for u in self.units(w):
            self.own_copy(u).start()

    def advance(self, w, k):
        for u in self.units(w):
            for held in subsets(self.order(u)[:k]):
                self.arrival(u, k, held).wait_recv()
        if k + 1 < self.dp_bits:
            self.begin_round(w, k + 1)
        else:
            for u in self.units(w):
                self.own_copy(u).wait()

    def close(self):
        for make, args, sends in self.sent:
            if sends is None:
                make(*args).wait_send()
            else:

                @pl.when(sends)
                def _():
                    make(*args).wait_send()


def gathering_scratch(count, dp, stages, rows, cols):
    parts = 2 if rows % 32 == 0 else 1
    dma = pltpu.SemaphoreType.DMA
    units = count * parts
    return [
        pltpu.VMEM((count, stages, rows // parts, cols * parts), BF16),
        pltpu.VMEM((count, rows, cols * stages), BF16),
        dma((count, 2 * stages)), dma((count, stages)), dma((units, dp)), dma((units, dp)), dma((units,)),
    ]


def forward_kernel(block, dp_bits, stages, back, *refs):
    weights, refs = refs[:6], refs[6:]
    bias_in, tokens, vectors, seg_query, seg_key = refs[:5]
    gain, factor = vectors.at[0:1], vectors.at[1:2]
    fulls, refs = refs[5:11], refs[11:]
    bias_full, raw_out, q_out, k_out, v_out, nt_out, o_ref, lse_ref = refs[:8]
    refs = refs[8:]
    home, window, normed, nt, raw, q, k, v, vt, ot, bias, scores, tops, totals, bias_all = refs[:15]
    xs, xr, bs, br, os = refs[15:20]
    d, z = greet(dp_bits, stages)
    rows, features = tokens.shape
    width, heads = k.shape[0], features // HD
    own = width - rows
    tile = 2 * LANES
    homes = [home.at[w] for w in range(3)] + list(fulls[3:])
    work = Gathering(dp_bits, stages, d, z, weights, homes, refs[20:])

    def bias_copy(step):
        return pltpu.make_async_remote_copy(
            src_ref=bias_in, dst_ref=bias_all.at[step], send_sem=bs.at[step],
            recv_sem=br.at[step], device_id={"mp": lax.rem(z + step, stages)},
            device_id_type=MESH,
        )

    def token_copy(hop):
        return pltpu.make_async_remote_copy(
            src_ref=tokens if hop == 0 else window.at[hop - 1], dst_ref=window.at[hop],
            send_sem=xs.at[hop], recv_sem=xr.at[hop],
            device_id={"mp": jnp.minimum(z + 1, stages - 1)}, device_id_type=MESH,
        )

    kept = [
        (raw, raw_out), (q, q_out), (k, k_out), (v, v_out), (nt, nt_out),
        (home.at[0], fulls[0]), (home.at[1], fulls[1]), (home.at[2], fulls[2]),
    ]

    def keep(i):
        return pltpu.make_async_copy(kept[i][0], kept[i][1], os.at[i])

    def norm(src, at):
        step_rows = 128

        def step(i, carry):
            part = pl.ds(pl.multiple_of(i * step_rows, step_rows), step_rows)
            x = src[part, :].astype(F32)
            value = (x * row_inverse(x) * gain[...]).astype(BF16)
            to = pl.ds(pl.multiple_of(at + i * step_rows, step_rows), step_rows)
            normed[to, :] = value
            return carry

        lax.fori_loop(0, rows // step_rows, step, 0)
        for c in range(features // tile):
            lanes = slice(c * tile, (c + 1) * tile)
            nt[lanes, at : at + rows] = normed[at : at + rows, lanes].T

    def project(w, at, out, out_t):
        def step(c, carry):
            lanes = pl.ds(pl.multiple_of(c * tile, tile), tile)
            value = dot(normed[at : at + rows, :], home[w, :, lanes], 1, 0).astype(BF16)
            out[at : at + rows, lanes] = value
            if out_t is not None:
                out_t[lanes, at : at + rows] = value.T
            return carry

        lax.fori_loop(0, features // tile, step, 0)

    first, rest = range(3), range(3, 6)
    for w in range(6):
        work.pack(w)
    for w in first:
        work.hop(w, 0)
    for step in range(1, stages):
        work.start(bias_copy, step)
    bias_all[0] = bias_in[...]
    for hop in range(back):

        @pl.when(z <= hop)
        def _():
            window[hop] = jnp.zeros((rows, features), BF16)

    norm(tokens, own)
    fill_bias(seg_query, seg_key, bias, block, own)
    for j in range(1, stages - 1):
        for w in first:
            work.hop(w, j)
    for w in rest:
        work.hop(w, 0)
    for w in first:
        work.collect(w)
        work.begin_round(w, 0)
    for j in range(1, stages - 1):
        if j <= 3 and dp_bits > 1:
            work.advance(j - 1, 0)
        for w in rest:
            work.hop(w, j)

    @pl.when(z < stages - 1)
    def _():
        token_copy(0).start()

    if dp_bits > 1:
        for w in range(max(0, min(stages - 2, 3)), 3):
            work.advance(w, 0)
    for w in rest:
        work.collect(w)
    for r in range(1, dp_bits - 1):
        for w in first:
            work.advance(w, r)
    for w in rest:
        work.begin_round(w, 0)
    for w in first:
        work.advance(w, dp_bits - 1)
        keep(5 + w).start()
        if w == 0:

            def query(c, carry):
                lanes = pl.ds(pl.multiple_of(c * tile, tile), tile)
                value = dot(normed[own:, :], home[0, :, lanes], 1, 0)
                raw[:, lanes] = value
                q[:, lanes] = (value * factor[:, lanes]).astype(BF16)
                return carry

            lax.fori_loop(0, features // tile, query, 0)
            keep(0).start()
            keep(1).start()
        else:
            project(w, own, *((k, None) if w == 1 else (v, vt)))

    sp = spans(rows, width, block)

    def attend(low, high, fresh, last, due):
        tiles = []
        for kb in range(low // block, high // block):
            qs = [i for i, (lo, hi) in enumerate(sp) if lo <= kb * block < hi]
            if qs:
                tiles.append((kb, qs))

        def head(h, carry):
            for at in sorted(set(due.values())):

                @pl.when(h == at)
                def _():
                    for w, r in due:
                        if due[w, r] == at:
                            work.advance(w, r)

            lanes, mine = head_lanes(h, features)
            feats = pl.ds(pl.multiple_of(h * HD, 16), HD)
            query = jnp.where(mine, q[:, lanes], jnp.zeros((), BF16))
            top = [jnp.full((8, block), FAR, F32) for _ in sp]
            for kb, qs in tiles:
                qa, qz = qs[0] * block, (qs[-1] + 1) * block
                at = slice(kb * block, (kb + 1) * block)
                s = dot(k[at, lanes], query[qa:qz], 1, 1) + bias[at, qa:qz]
                scores[at, qa:qz] = s
                for i in qs:
                    cut = s[:, i * block - qa : (i + 1) * block - qa]
                    top[i] = jnp.maximum(top[i], jnp.max(cut.reshape(block // 8, 8, block), axis=0))
            top = jnp.concatenate([jnp.max(t, axis=0, keepdims=True) for t in top], axis=1)
            if not fresh:
                before = tops[pl.ds(h, 1), :]
                top = jnp.maximum(top, before)
                scale = jnp.exp(before - top)
            acc = [jnp.zeros((HD, block), F32) for _ in sp]
            total = [jnp.zeros((8, block), F32) for _ in sp]
            for kb, qs in tiles:
                qa, qz = qs[0] * block, (qs[-1] + 1) * block
                at = slice(kb * block, (kb + 1) * block)
                p = jnp.exp(scores[at, qa:qz] - top[:, qa:qz])
                part = dot(vt[feats, at], p.astype(BF16), 1, 0)
                for i in qs:
                    cut = slice(i * block - qa, (i + 1) * block - qa)
                    total[i] = total[i] + jnp.sum(p[:, cut].reshape(block // 8, 8, block), axis=0)
                    acc[i] = acc[i] + part[:, cut]
            for i in range(len(sp)):
                at = slice(i * block, (i + 1) * block)
                one = jnp.sum(total[i], axis=0, keepdims=True)
                out = acc[i]
                if not fresh:
                    one = one + totals[pl.ds(h, 1), at] * scale[:, at]
                    out = out + ot[feats, at] * scale[:, at]
                if last:
                    ot[feats, at] = out / one
                    lse_ref[pl.ds(h, 1), at] = top[:, at] + jnp.log(one)
                else:
                    ot[feats, at] = out
                    totals[pl.ds(h, 1), at] = one
                    tops[pl.ds(h, 1), at] = top[:, at]
            return carry

        lax.fori_loop(0, heads, head, 0)

    inside = {}
    if back and dp_bits > 2:
        inside = {(3, 0): 0, (4, 0): heads // 4, (5, 0): heads // 2, (3, 1): heads * 3 // 4}
    for hop in range(back):
        if hop + 1 == back:
            attend(rows, width, True, False, inside)

        @pl.when(z > hop)
        def _():
            token_copy(hop).wait_recv()

        if hop + 1 < back:

            @pl.when((z > hop) & (z < stages - 1))
            def _():
                token_copy(hop + 1).start()

        at = own - (hop + 1) * rows
        norm(window.at[hop], at)
        project(1, at, k, None)
        project(2, at, v, vt)
    for i in range(2, 5):
        keep(i).start()
    attend(0, rows if back else width, not back, True, {})
    transpose_out(ot, o_ref)
    for r in range(dp_bits):
        for w in rest:
            if (w, r) not in inside:
                work.advance(w, r)
    for step in range(1, stages):
        bias_copy(step).wait_recv()
    bias_full[...] = jnp.concatenate(
        [bias_all[lax.rem(z - s + stages, stages)] for s in range(stages)], axis=1
    )
    for hop in range(back):

        @pl.when((z >= hop) & (z < stages - 1))
        def _():
            token_copy(hop).wait_send()

    for i in range(len(kept)):
        keep(i).wait()
    work.close()


def attend_forward(weights, bias, tokens, vectors, seg_q, seg_k, block, dp, stages, back):
    held, cols = weights[0].shape
    rows, features = tokens.shape
    width, heads = (back + 1) * rows, features // HD
    hbm = pl.BlockSpec(memory_space=pl.ANY)
    vmem = pl.BlockSpec(memory_space=pltpu.VMEM)
    dma = pltpu.SemaphoreType.DMA
    sds = jax.ShapeDtypeStruct
    return pl.pallas_call(
        functools.partial(forward_kernel, block, dp.bit_length() - 1, stages, back),
        in_specs=[vmem] * 11,
        out_specs=[hbm] * 6 + [vmem] + [hbm] * 5 + [vmem] * 2,
        out_shape=[sds((features, features), BF16)] * 6
        + [
            sds((1, features), F32),
            sds((rows, features), F32),
            sds((rows, features), BF16),
            sds((width, features), BF16),
            sds((width, features), BF16),
            sds((features, width), BF16),
            sds((rows, features), BF16),
            sds((heads, rows), F32),
        ],
        scratch_shapes=[
            pltpu.VMEM((3, features, features), BF16),
            pltpu.VMEM((back, rows, features), BF16),
            pltpu.VMEM((width, features), BF16),
            pltpu.VMEM((features, width), BF16),
            pltpu.VMEM((rows, features), F32),
            pltpu.VMEM((rows, features), BF16),
            pltpu.VMEM((width, features), BF16),
            pltpu.VMEM((width, features), BF16),
            pltpu.VMEM((features, width), BF16),
            pltpu.VMEM((features, rows), F32),
            pltpu.VMEM((width, rows), F32),
            pltpu.VMEM((width, rows), F32),
            pltpu.VMEM((heads, rows), F32),
            pltpu.VMEM((heads, rows), F32),
            pltpu.VMEM((stages,) + bias.shape, F32),
            dma((back,)), dma((back,)), dma((stages,)), dma((stages,)), dma((8,)),
        ]
        + gathering_scratch(6, dp, stages, held, cols),
        compiler_params=pltpu.CompilerParams(
            collective_id=0, has_side_effects=True, vmem_limit_bytes=62 << 20
        ),
        name="attend_forward",
    )(*weights, bias, tokens, vectors, seg_q, seg_k)


def middle_kernel(block, dp_bits, stages, *refs):
    sources, refs = refs[:12], refs[12:]
    b_up, vectors, lse_ref, seg_query, seg_key = refs[:5]
    factor, gain, b_down = (vectors.at[i : i + 1] for i in (1, 2, 3))
    results, incoming, outs, sums, refs = refs[5:11], refs[11], refs[12:15], refs[15], refs[16:]
    weights, hidden, wide, tmp, tr, keys, values, query_in, grad_in, bias, delta_ref = refs[:11]
    ps, pr, sems, refs = refs[11], refs[12], refs[13], refs[14:]
    d, z = greet(dp_bits, stages)
    work = Reduction(dp_bits, stages, d, z, None, outs, refs)
    rows, features = query_in.shape
    heads, width = features // HD, keys.shape[0]
    back = width // rows - 1
    tile = 2 * LANES
    w_out, w_up, w_down = weights.at[0], weights.at[1], weights.at[2]
    w_key, w_value = weights.at[2], weights.at[1]
    mixed, cot, x, second, active, d_pre, d_attn, spare = (tmp.at[i] for i in range(8))
    dk, dv = tmp.at[: back + 1], tmp.at[back + 1 : 2 * back + 2]
    dq, part = tmp.at[2 * back + 2], tmp.at[2 * back + 3]
    inside = (
        mixed, w_out, x, cot, w_up, w_down, keys, values, query_in, w_key, w_value, hidden,
    )
    half = rows // 2
    outside = (spare, hidden, dq, dk, dv, part.at[half:])
    loads = Loads(list(zip(sources, inside)) + list(zip(outside, results)), sems)
    loads.start(*range(9))
    fill_bias(seg_query, seg_key, bias, block, width - rows)

    def by_tile(body):
        for c in range(features // tile):
            body(slice(c * tile, (c + 1) * tile), c)

    def by_rows(body, start):
        def step(i, carry):
            return body(pl.ds(pl.multiple_of(i * 64, 64), 64), carry)

        return lax.fori_loop(0, rows // 64, step, start)

    def flip(src):
        for c in range(features // tile):
            lanes = slice(c * tile, (c + 1) * tile)
            tr[lanes, :] = src[:, lanes].T

    nothing = jnp.zeros((1, features), F32)

    def add_attention(lanes, c):
        hidden[:, lanes] = x[:, lanes].astype(F32) + dot(mixed[...], w_out[lanes, :], 1, 1)

    def norm(at, carry):
        h = hidden[at, :]
        second[at, :] = (h * row_inverse(h) * gain[...]).astype(BF16)
        return carry

    def activate(lanes, c):
        pre = dot(second[...], w_up[:, lanes], 1, 0) + b_up[:, lanes]
        sigma = 1.0 / (1.0 + jnp.exp(-pre))
        active[:, lanes] = (pre * sigma).astype(BF16)
        grad = dot(cot[...], w_down[:, lanes], 1, 0)
        grad = (grad * sigma * (1.0 + pre * (1.0 - sigma))).astype(BF16)
        d_pre[:, lanes] = grad
        sums[2:3, lanes] = jnp.sum(grad.astype(F32), axis=0, keepdims=True)

    def finish_layer(lanes, c):
        out = dot(active[...], w_down[lanes, :], 1, 1)
        spare[:, lanes] = (hidden[:, lanes] + out + b_down[:, lanes]).astype(BF16)
        sums[1:2, lanes] = jnp.sum(cot[:, lanes].astype(F32), axis=0, keepdims=True)

    def to_second(lanes, c):
        wide[:, lanes] = dot(d_pre[...], w_up[lanes, :], 1, 1)

    def to_hidden(at, column):
        h, grad = hidden[at, :], wide[at, :]
        inverse = row_inverse(h)
        weighted = grad * gain[...]
        dots = jnp.sum(weighted * h, axis=1, keepdims=True)
        cube = inverse * inverse * inverse
        d_hidden = cot[at, :].astype(F32) + inverse * weighted - h * cube / features * dots
        hidden[at, :] = d_hidden
        d_attn[at, :] = d_hidden.astype(BF16)
        return column + jnp.sum(grad * h * inverse, axis=0, keepdims=True)

    def to_mixed(lanes, c):
        grad = dot(d_attn[...], w_out[:, lanes], 1, 0).astype(BF16)
        grad_in[:, lanes] = grad
        both = grad.astype(F32) * mixed[:, lanes].astype(F32)
        lane = lax.broadcasted_iota(jnp.int32, (heads, tile), 1) + c * tile
        first = lax.broadcasted_iota(jnp.int32, (heads, tile), 0) * HD
        owner = jnp.where((lane >= first) & (lane < first + HD), 1.0, 0.0).astype(BF16)
        high = both.astype(BF16)
        rest = (both - high.astype(F32)).astype(BF16)
        delta_ref[...] += dot(owner, high, 1, 1) + dot(owner, rest, 1, 1)

    sums[3:8, :] = jnp.zeros((5, features), F32)
    delta_ref[...] = jnp.zeros_like(delta_ref)
    loads.wait(0, 1, 2)
    by_tile(add_attention)
    by_rows(norm, 0)
    loads.wait(3, 4, 5)
    by_tile(activate)
    flip(cot)
    work.weight_grad(0, lambda at: tr[at, :], lambda: active[...])
    by_tile(finish_layer)
    loads.start(12, 9)
    by_tile(to_second)
    loads.start(10)
    flip(second)
    work.weight_grad(1, lambda at: tr[at, :], lambda: d_pre[...])
    work.advance(0, 0)
    sums[0:1, :] = by_rows(to_hidden, nothing)
    loads.start(13)
    by_tile(to_mixed)
    flip(d_attn)
    work.weight_grad(2, lambda at: tr[at, :], lambda: mixed[...])
    work.advance(1, 0)
    if dp_bits > 1:
        work.advance(0, 1)
    loads.wait(12)
    for c in range(2 * back + 2):
        tmp[c] = jnp.zeros((rows, features), BF16)
    wide[...] = jnp.zeros_like(wide)
    loads.wait(6, 7, 8)
    sp = spans(rows, width, block)
    steps = heads * (back + 1)
    events = [(2, 0)] + [(w, k) for w in range(3) for k in range(1, dp_bits) if (w, k) != (0, 1)]
    due = {i: int(at * steps) // 2 * 2 for i, at in enumerate(EVENTS[: len(events)])}

    def down():
        return pltpu.make_async_remote_copy(
            src_ref=part.at[:half], dst_ref=incoming, send_sem=ps, recv_sem=pr,
            device_id={"mp": jnp.maximum(z - 1, 0)}, device_id_type=MESH,
        )

    for c in range(back + 1):

        def head(h):
            lanes, mine = head_lanes(h, features)
            zero = jnp.zeros((), BF16)
            query = jnp.where(mine, query_in[:, lanes], zero)
            grad = jnp.where(mine, grad_in[:, lanes], zero)
            lse = lse_ref[pl.ds(h, 1), :]
            delta = delta_ref[pl.ds(h, 1), :]
            for kb in range(c * rows // block, (c + 1) * rows // block):
                qs = [i for i, (lo, hi) in enumerate(sp) if lo <= kb * block < hi]
                if not qs:
                    continue
                qa, qz = qs[0] * block, (qs[-1] + 1) * block
                at = slice(kb * block, (kb + 1) * block)
                to = slice(kb * block - c * rows, (kb + 1) * block - c * rows)
                key = keys[at, lanes]
                s = dot(key, query[qa:qz], 1, 1) + bias[at, qa:qz]
                p = jnp.exp(s - lse[:, qa:qz])
                dp = dot(values[at, lanes], grad[qa:qz], 1, 1)
                ds = (p * (dp - delta[:, qa:qz])).astype(BF16)
                dv[c, to, lanes] += dot(p.astype(BF16), grad[qa:qz], 1, 0).astype(BF16)
                dk[c, to, lanes] += dot(ds, query[qa:qz], 1, 0).astype(BF16)
                wide[qa:qz, lanes] += dot(ds, jnp.where(mine, key, zero), 0, 0)

        def pair(i, carry):
            for at in sorted(set(due.values())):
                if at // heads != c:
                    continue

                @pl.when(2 * i == at % heads)
                def _():
                    for e in due:
                        if due[e] == at:
                            work.advance(*events[e])

            head(2 * i)
            head(2 * i + 1)
            return carry

        lax.fori_loop(0, heads // 2, pair, 0)
        if c == 0:
            loads.wait(9, 10)
            if back:
                back_project(part, ((dk.at[0], w_key), (dv.at[0], w_value)), 0, None)
                loads.start(17)

                @pl.when(z >= back)
                def _():
                    down().start()

            loads.wait(13)
            loads.start(11)

    loads.start(15, 16)
    loads.wait(11)

    def to_query(at, column):
        scaled = wide[at, :].astype(BF16).astype(F32)
        dq[at, :] = (scaled * factor[...]).astype(BF16)
        return column + jnp.sum(scaled * hidden[at, :], axis=0, keepdims=True)

    sums[4:5, :] = by_rows(to_query, nothing)
    loads.start(14)
    for i in range(len(due), len(events)):
        work.advance(*events[i])
    for w in range(3):
        work.finish(w)
    loads.wait(14, 15, 16)
    if back:
        loads.wait(17)

        @pl.when((z + 1 >= back) & (z < stages - 1))
        def _():
            down().wait_recv()

        @pl.when(z >= back)
        def _():
            down().wait_send()

    work.close()


def back_project(out, pairs, at, more):
    rows, features = out.shape
    tile = 2 * LANES

    def step(c, carry):
        lanes = pl.ds(pl.multiple_of(c * tile, tile), tile)
        value = None
        for grad, weight in pairs:
            start = at if grad.shape[0] > rows else 0
            term = dot(grad[start : start + rows, :], weight[lanes, :], 1, 1)
            value = term if value is None else value + term
        if more is not None:
            value = value + more(lanes)
        out[:, lanes] = value.astype(out.dtype)
        return carry

    lax.fori_loop(0, features // tile, step, 0)


def middle(
    mixed, w_out, x, cot, w_up, w_down, k, v, q, w_key, w_value, raw, b_up, vectors,
    lse, seg_q, seg_k, block, dp, stages,
):
    rows, features = q.shape
    width, heads = k.shape[0], features // HD
    held, cols = features // dp, features // stages
    chunks = width // rows
    hbm = pl.BlockSpec(memory_space=pl.ANY)
    vmem = pl.BlockSpec(memory_space=pltpu.VMEM)
    dma = pltpu.SemaphoreType.DMA
    sds = jax.ShapeDtypeStruct
    low, high = sds((rows, features), BF16), sds((rows, features), F32)
    many, part = sds((chunks, rows, features), BF16), sds((rows // 2, features), BF16)
    return pl.pallas_call(
        functools.partial(middle_kernel, block, dp.bit_length() - 1, stages),
        in_specs=[hbm] * 12 + [vmem] * 5,
        out_specs=[hbm] * 7 + [vmem] * 4,
        out_shape=[low, high, low, many, many, part, part]
        + [sds((held, cols), F32)] * 3
        + [sds((8, features), F32)],
        scratch_shapes=[
            pltpu.VMEM((3, features, features), BF16),
            pltpu.VMEM((rows, features), F32),
            pltpu.VMEM((rows, features), F32),
            pltpu.VMEM((max(8, 2 * chunks + 2), rows, features), BF16),
            pltpu.VMEM((features, rows), BF16),
            pltpu.VMEM((width, features), BF16),
            pltpu.VMEM((width, features), BF16),
            pltpu.VMEM((rows, features), BF16),
            pltpu.VMEM((rows, features), BF16),
            pltpu.VMEM((width, rows), F32),
            pltpu.VMEM((heads, rows), F32),
            dma, dma, dma((18,)),
        ]
        + reduction_scratch(3, dp, stages, held, features, True),
        compiler_params=pltpu.CompilerParams(
            collective_id=2, has_side_effects=True, vmem_limit_bytes=63 << 20
        ),
        name="middle",
    )(
        mixed, w_out, x, cot, w_up, w_down, k, v, q, w_key, w_value, raw, b_up, vectors,
        lse, seg_q, seg_k,
    )


def input_kernel(dp_bits, stages, back, *refs):
    sources, farther, vectors, sums, refs = refs[:10], refs[10], refs[11], refs[12], refs[13:]
    gain = vectors.at[0:1]
    outs, result, total, refs = refs[:3], refs[3], refs[4], refs[5:]
    inside, tokens_grad, refs = refs[:10], refs[10], refs[11:]
    dv, nt, dk, wk, wv, incoming, dq, wq, tokens, d_hidden = inside
    part, landed, d_first, sgot, ss, sr, ps, pr, sems = refs[:9]
    d, z = greet(dp_bits, stages)
    work = Reduction(dp_bits, stages, d, z, None, outs, refs[9:])
    rows, features = tokens.shape
    own, half = back * rows, rows // 2
    inside = inside[:5] + (incoming.at[:half],) + inside[6:]
    loads = Loads(list(zip(sources, inside)) + [(tokens_grad, result)], sems)
    levels = dp_bits + stages.bit_length() - 1
    held = features >> dp_bits
    grads = ((dv, 2, 0), (dk, 1, 0), (dq, 0, own))

    def down(hop):
        return pltpu.make_async_remote_copy(
            src_ref=part.at[hop - 1] if hop else farther,
            dst_ref=landed.at[hop - 1] if hop else incoming.at[half:],
            send_sem=ps.at[hop], recv_sem=pr.at[hop],
            device_id={"mp": jnp.maximum(z - 1, 0)}, device_id_type=MESH,
        )

    if back:

        @pl.when(z >= back)
        def _():
            down(0).start()

    loads.start(*range(10))

    def arrived(hop):
        source = incoming if hop == 1 else landed.at[hop - 2]
        there = (z + 1 >= back - hop + 1) & (z < stages - 1)

        def take(lanes):
            return jnp.where(there, source[:, lanes].astype(F32), 0.0)

        return there, take

    def weight_grad(i):
        grad, w, at = grads[i]
        work.weight_grad(w, lambda rows_at: nt[rows_at, at:], lambda: grad[...])

    def sum_copy(k):
        if k < dp_bits:
            to = {"dp": flipped(d, (k,))}
        else:
            to = {"mp": flipped(z, (k - dp_bits,))}
        return pltpu.make_async_remote_copy(
            src_ref=total.at[k], dst_ref=sgot.at[k], send_sem=ss.at[k], recv_sem=sr.at[k],
            device_id=to, device_id_type=MESH,
        )

    def sum_step(k):
        sum_copy(k).wait_recv()
        total[k + 1] = total[k] + sgot[k]
        if k + 1 < levels:
            work.start(sum_copy, k + 1)

    def pass_down(hop):
        there, take = arrived(hop)

        @pl.when(there)
        def _():
            down(hop - 1).wait_recv()

        back_project(part.at[hop - 1], ((dk, wk), (dv, wv)), hop * rows, take)

        @pl.when(z >= back - hop)
        def _():
            down(hop).start()

    loads.wait(0, 1)
    weight_grad(0)
    loads.wait(2)
    weight_grad(1)
    work.advance(2, 0)
    loads.wait(3, 4, 5)
    if back > 1:
        pass_down(1)
    work.advance(1, 0)
    loads.wait(6, 7)
    weight_grad(2)
    for hop in range(2, back):
        pass_down(hop)
    work.advance(0, 0)
    back_project(d_first, ((dk, wk), (dv, wv), (dq, wq)), own, None)
    events = [(w, k) for w in (2, 1, 0) for k in range(1, dp_bits)]
    for event in events[:1]:
        work.advance(*event)
    loads.wait(8, 9)
    there, take = arrived(back) if back else (None, None)
    if back:

        @pl.when(there)
        def _():
            down(back - 1).wait_recv()

    chunk = 64

    def finish(i, column):
        at = pl.ds(pl.multiple_of(i * chunk, chunk), chunk)
        x = tokens[at, :].astype(F32)
        grad = d_first[at, :]
        if back:
            source = incoming if back == 1 else landed.at[back - 2]
            grad = grad + jnp.where(there, source[at, :].astype(F32), 0.0)
        inverse = row_inverse(x)
        weighted = grad * gain[...]
        dots = jnp.sum(weighted * x, axis=1, keepdims=True)
        cube = inverse * inverse * inverse
        tokens_grad[at, :] = (
            d_hidden[at, :] + inverse * weighted - x * cube / features * dots
        ).astype(BF16)
        return column + jnp.sum(grad * x * inverse, axis=0, keepdims=True)

    column = lax.fori_loop(0, rows // chunk, finish, jnp.zeros((1, features), F32))
    total[0] = sums[...]
    total[0, 3:4, :] = column
    work.start(sum_copy, 0)
    loads.start(10)
    done = 0
    for event in events[1:]:
        work.advance(*event)
        if done < levels:
            sum_step(done)
            done += 1
    for k in range(done, levels):
        sum_step(k)
    for w in (2, 1, 0):
        work.finish(w)
    for hop in range(back):

        @pl.when(z >= back - hop)
        def _():
            down(hop).wait_send()

    loads.wait(10)
    work.close()


def input_gradients(
    nt, dq, dk, dv, wq, wk, wv, incoming, farther, tokens, d_hidden, vectors, sums, dp, stages
):
    rows, features = tokens.shape
    back = dk.shape[0] // rows - 1
    held, cols = features // dp, features // stages
    dp_bits = dp.bit_length() - 1
    levels = dp_bits + stages.bit_length() - 1
    hbm = pl.BlockSpec(memory_space=pl.ANY)
    vmem = pl.BlockSpec(memory_space=pltpu.VMEM)
    dma = pltpu.SemaphoreType.DMA
    hops = max(1, back - 1)
    sources = (dv, nt, dk, wk, wv, incoming, dq, wq, tokens, d_hidden)
    out = pl.pallas_call(
        functools.partial(input_kernel, dp_bits, stages, back),
        in_specs=[hbm] * 11 + [vmem] * 2,
        out_specs=[vmem] * 3 + [hbm, vmem],
        out_shape=[jax.ShapeDtypeStruct((held, cols), F32)] * 3
        + [
            jax.ShapeDtypeStruct((rows, features), BF16),
            jax.ShapeDtypeStruct((levels + 1,) + sums.shape, F32),
        ],
        scratch_shapes=[pltpu.VMEM(tokens.shape if a is incoming else a.shape, a.dtype) for a in sources + (tokens,)]
        + [
            pltpu.VMEM((hops, rows, features), BF16), pltpu.VMEM((hops, rows, features), BF16),
            pltpu.VMEM((rows, features), F32), pltpu.VMEM((levels,) + sums.shape, F32),
            dma((levels,)), dma((levels,)), dma((hops + 1,)), dma((hops + 1,)), dma((11,)),
        ]
        + reduction_scratch(3, dp, stages, held, features, True),
        compiler_params=pltpu.CompilerParams(
            collective_id=1, has_side_effects=True, vmem_limit_bytes=62 << 20
        ),
        name="input_gradients",
    )(*sources, farther, vectors, sums)
    return out[:3], out[3], out[4][levels]


def body(
    tokens, segments, w_query, w_key, w_value, w_output, w_up, b_up, w_down, b_down,
    gain_attn, gain_mlp, query_scale, cotangent,
):
    stages = lax.axis_size("mp")
    z = lax.axis_index("mp")
    seg = segments[0]
    rows, features = tokens.shape
    back = min(stages - 1, -(-(DOC_MAX - 1) // rows))
    own = back * rows
    block = min(256, rows)

    seg_wide = jnp.concatenate([jnp.full((own,), -1, jnp.int32), seg])
    seg_window = lax.dynamic_slice_in_dim(seg_wide, z * rows, own + rows, 0)
    seg_query = seg_window[own:]
    seg_query, seg_key = seg_query[None, :], seg_window[:, None]

    heads = features // HD
    factor = jax.nn.softplus(query_scale) * (LOG2E / math.sqrt(HD))
    vectors = jnp.stack([gain_attn, jnp.tile(factor, heads), gain_mlp, b_down])
    dp = lax.axis_size("dp")
    (
        wq, wk, wv, wu, wo, wd, b_full, query_raw, scaled, keys, values, first_t, mixed, lse
    ) = attend_forward(
        (w_query, w_key, w_value, w_up, w_output.T, w_down.T), b_up[None], tokens,
        vectors, seg_query, seg_key, block, dp, stages, back,
    )
    layer_out, d_hidden, d_query, d_keys, d_values, farther, incoming, *mlp, sums = middle(
        mixed, wo, tokens, cotangent, wu, wd, keys, values, scaled, wk, wv, query_raw,
        b_full, vectors, lse, seg_query, seg_key, block, dp, stages,
    )
    grads, tokens_grad, sums = input_gradients(
        first_t, d_query, d_keys.reshape(own + rows, features),
        d_values.reshape(own + rows, features), wq, wk, wv, incoming, farther, tokens,
        d_hidden, vectors, sums, dp, stages,
    )
    mine = b_up.shape[0]
    sum_b_up = lax.dynamic_slice_in_dim(sums[2], z * mine, mine, 0)
    scale_total = jnp.sum(sums[4].reshape(heads, HD), axis=0)
    grad_query_scale = scale_total * (LOG2E / math.sqrt(HD)) * jax.nn.sigmoid(query_scale)
    return (
        layer_out, tokens_grad, grads[0], grads[1], grads[2], mlp[2].T, mlp[1], sum_b_up,
        mlp[0].T, sums[1], sums[3], sums[0], grad_query_scale,
    )


def solution(mesh):
    tokens, rows_dp, rows_mp = P(("dp", "mp"), None), P("dp", "mp"), P("mp", "dp")
    return jax.shard_map(
        body,
        mesh=mesh,
        in_specs=(
            tokens, P("dp", None), rows_dp, rows_dp, rows_dp, rows_mp, rows_dp, P("mp"), rows_mp,
            P(), P(), P(), P(), tokens,
        ),
        out_specs=(
            tokens, tokens, rows_dp, rows_dp, rows_dp, rows_mp, rows_dp, P("mp"), rows_mp,
            P(), P(), P(), P(),
        ),
        check_vma=False,
    )
```

```python
import functools
import math

import jax
import jax.numpy as jnp
from jax import lax
from jax.experimental import pallas as pl
from jax.experimental.pallas import tpu as pltpu
from jax.sharding import PartitionSpec as P

HD = 80
LANES = 128
EPSILON = 1e-06
LOG2E = 1.442695
DOC_MAX = 1024
FAR = -1e30
EVENTS = (0.15, 0.3, 0.5, 0.6, 0.75, 0.9)
F32 = jnp.float32
BF16 = jnp.bfloat16


def dot(a, b, ca, cb):
    return lax.dot_general(a, b, (((ca,), (cb,)), ((), ())), preferred_element_type=F32)


def row_inverse(values):
    return lax.rsqrt(jnp.mean(values * values, axis=1, keepdims=True) + EPSILON)


MESH = pl.DeviceIdType.MESH


def bit_of(index, b):
    return lax.rem(lax.div(index, 1 << b), 2)


def flipped(index, bits):
    for b in bits:
        index = index + (1 << b) * (1 - 2 * bit_of(index, b))
    return index


def split_order(count, turn):
    bits = list(range(count))
    rest = bits[1:][::-1]
    turn = turn % max(1, len(rest))
    return bits[:1] + rest[turn:] + rest[:turn]


def subsets(bits):
    out = [()]
    for b in bits:
        out = out + [s + (b,) for s in out]
    return out


def greet(dp_bits, stages, extra=()):
    d, z = lax.axis_index("dp"), lax.axis_index("mp")
    barrier = pltpu.get_barrier_semaphore()
    for b in range(dp_bits):
        pl.semaphore_signal(barrier, device_id={"dp": flipped(d, (b,))}, device_id_type=MESH)
    for step in range(1, stages):
        pl.semaphore_signal(
            barrier, device_id={"mp": lax.rem(z + step, stages)}, device_id_type=MESH
        )
    pl.semaphore_wait(barrier, dp_bits + stages - 1)
    return d, z


class Loads:
    def __init__(self, pairs, sems):
        self.pairs, self.sems = pairs, sems

    def copy(self, i):
        return pltpu.make_async_copy(self.pairs[i][0], self.pairs[i][1], self.sems.at[i])

    def start(self, *which):
        for i in which:
            self.copy(i).start()

    def wait(self, *which):
        for i in which:
            self.copy(i).wait()


class Reduction:
    def __init__(self, dp_bits, stages, d, z, grads, outs, refs):
        self.dp_bits, self.stages, self.d, self.z = dp_bits, stages, d, z
        self.grads, self.outs = grads, outs
        self.pool = refs[0]
        self.kept, self.got = refs[0].at[0], refs[1 : 1 + dp_bits]
        self.zsend, self.zgot, self.ks, self.rs, self.rr, self.zs, self.zr = refs[1 + dp_bits :]
        self.half = 1 << (dp_bits - 1)
        self.parts = self.kept.shape[0] // len(outs)
        self.rows, self.features = self.kept.shape[2], self.kept.shape[3]
        self.sent = []

    def start(self, make, *args):
        make(*args).start()
        self.sent.append((make, args))

    def order(self, u):
        return split_order(self.dp_bits, u % self.parts)

    def place(self, u, slot, low):
        rest = self.order(u)[1:]
        at = low
        for i, b in enumerate(rest):
            if slot >> (len(rest) - 1 - i) & 1:
                at = at + (1 << b)
        return at

    def slot_of(self, u, index):
        rest = self.order(u)[1:]
        return sum(bit_of(index, b - 1) << (len(rest) - 1 - i) for i, b in enumerate(rest))

    def source(self, u, slot, low):
        cut = pl.ds(u % self.parts * self.rows, self.rows)
        return self.grads[u // self.parts].at[self.place(u, slot, low), cut]

    def first_copy(self, u, slot):
        return pltpu.make_async_remote_copy(
            src_ref=self.pool.at[1, u, slot]
            if self.grads is None
            else self.source(u, slot, 1 - bit_of(self.d, 0)),
            dst_ref=self.got[0].at[u, slot],
            send_sem=self.rs.at[u, slot], recv_sem=self.rr.at[u, slot],
            device_id={"dp": flipped(self.d, (0,))}, device_id_type=MESH,
        )

    def keep_copy(self, u, slot):
        return pltpu.make_async_copy(
            self.source(u, slot, bit_of(self.d, 0)), self.kept.at[u, slot], self.ks.at[u, slot]
        )

    def round_copy(self, u, k):
        count = self.half >> k
        b = self.order(u)[k]
        other = 1 - bit_of(self.d, b)
        return pltpu.make_async_remote_copy(
            src_ref=self.got[k - 1].at[u, pl.ds(other * count, count)],
            dst_ref=self.got[k].at[u],
            send_sem=self.rs.at[u, self.half + k], recv_sem=self.rr.at[u, self.half + k],
            device_id={"dp": flipped(self.d, (b,))}, device_id_type=MESH,
        )

    def last_copy(self, w, step):
        to = lax.rem(self.z + step, self.stages)
        return pltpu.make_async_remote_copy(
            src_ref=self.zsend.at[w, to], dst_ref=self.zgot.at[w, step],
            send_sem=self.zs.at[w, step], recv_sem=self.zr.at[w, step],
            device_id={"mp": to}, device_id_type=MESH,
        )

    def units(self, w):
        return range(w * self.parts, (w + 1) * self.parts)

    def begin(self, w):
        for u in self.units(w):
            for slot in range(self.half):
                self.start(self.first_copy, u, slot)
                if self.grads is not None:
                    self.keep_copy(u, slot).start()

    def add(self, dst, src, count):
        def step(i, carry):
            dst[i] = dst[i] + src(i)
            return carry

        lax.fori_loop(0, count, step, 0)

    def take(self, w, k):
        for u in self.units(w):
            count = self.half >> k
            if k == 0:
                for slot in range(self.half):
                    if self.grads is not None:
                        self.keep_copy(u, slot).wait()
                    self.first_copy(u, slot).wait_recv()
                self.add(self.got[0].at[u], lambda i: self.kept[u, i], count)
            else:
                self.round_copy(u, k).wait_recv()
                mine = bit_of(self.d, self.order(u)[k]) * count
                self.add(self.got[k].at[u], lambda i: self.got[k - 1][u, mine + i], count)

    def send(self, w, k):
        for u in self.units(w):
            self.start(self.round_copy, u, k)

    def advance(self, w, k):
        self.take(w, k)
        if k + 1 == self.dp_bits:
            self.begin_last(w)
        else:
            self.send(w, k + 1)

    def put(self, w, index, value):
        held = self.parts * self.rows
        for low in range(2):
            which = lax.rem(bit_of(self.d, 0) + low, 2)
            for u in self.units(w):
                cut = low * held + u % self.parts * self.rows
                self.pool[which, u, self.slot_of(u, index)] = value[cut : cut + self.rows]

    def weight_grad(self, w, left, right):
        held = self.parts * self.rows

        def step(t, carry):
            at = pl.ds(pl.multiple_of(t * 2 * held, 2 * held), 2 * held)
            self.put(w, t, dot(left(at), right(), 1, 0).astype(BF16))
            return carry

        lax.fori_loop(0, 1 << (self.dp_bits - 1), step, 0)
        self.begin(w)

    def begin_last(self, w):
        cols = self.features // self.stages
        whole = [self.got[self.dp_bits - 1][u, 0] for u in self.units(w)]
        for s in range(self.stages):
            self.zsend[w, s] = jnp.concatenate(
                [piece[:, s * cols : (s + 1) * cols] for piece in whole], axis=1
            )
        for step in range(1, self.stages):
            self.start(self.last_copy, w, step)

    def finish(self, w):
        value = self.zsend[w, self.z].astype(F32)
        for step in range(1, self.stages):
            self.last_copy(w, step).wait_recv()
            value = value + self.zgot[w, step].astype(F32)
        cols = self.features // self.stages
        for p in range(self.parts):
            at = slice(p * self.rows, (p + 1) * self.rows)
            self.outs[w][at, :] = value[:, p * cols : (p + 1) * cols]

    def close(self):
        for make, args in self.sent:
            make(*args).wait_send()


def reduction_scratch(count, dp, stages, rows, features, local=False):
    dp_bits, half, cols = dp.bit_length() - 1, dp // 2, features // stages
    parts = 2 if rows % 32 == 0 else 1
    dma = pltpu.SemaphoreType.DMA
    units = count * parts
    return (
        [pltpu.VMEM((1 + local, units, half, rows // parts, features), BF16)]
        + [pltpu.VMEM((units, half >> k, rows // parts, features), BF16) for k in range(dp_bits)]
        + [pltpu.VMEM((count, stages, rows // parts, cols * parts), BF16)] * 2
        + [
            dma((units, half)), dma((units, half + dp_bits)), dma((units, half + dp_bits)),
            dma((count, stages)), dma((count, stages)),
        ]
    )


def spans(rows, width, block):
    own = width - rows
    out=[]
    for qb in range(rows//block):
        hi = own + (qb+1)*block
        lo = max(0, (own + qb*block - (DOC_MAX-1))//block*block)
        out.append((lo,hi))
    return out

def head_lanes(h, features):
    first = h*HD
    off = jnp.minimum(lax.div(first, LANES)*LANES, features-2*LANES)
    off = pl.multiple_of(off, LANES)
    lane = lax.broadcasted_iota(jnp.int32,(1,2*LANES),1) + (off-first)
    return pl.ds(off, 2*LANES), (lane>=0)&(lane<HD)

def fill_bias(segments, z, bias, block, own):
    width, rows = bias.shape
    first = z * rows
    for kb in range(width // block):
        start = first + (kb * block - own)
        at = pl.ds(pl.multiple_of(jnp.maximum(start, 0), block), block)
        col = jnp.broadcast_to(segments[:, at], (block, block)).T
        sub = lax.broadcasted_iota(jnp.int32, (block, block), 0) + kb * block
        for qb in range(rows // block):
            row = segments[:, pl.ds(pl.multiple_of(first + qb * block, block), block)]
            last = lax.broadcasted_iota(jnp.int32, (block, block), 1) + (own + qb * block)
            allowed = (col == row) & (sub <= last) & (start >= 0)
            bias[kb * block : (kb + 1) * block, qb * block : (qb + 1) * block] = jnp.where(
                allowed, 0.0, FAR
            )


def transpose_out(src, dst):
    for i in range(src.shape[0]//LANES):
        at = slice(i*LANES,(i+1)*LANES)
        dst[:, at] = src[at,:].T.astype(dst.dtype)

class Gathering:
    def __init__(self, dp_bits, stages, d, z, weights, homes, refs):
        self.dp_bits, self.stages, self.d, self.z = dp_bits, stages, d, z
        self.weights, self.homes = weights, homes
        self.blocks, self.slab, self.zs, self.zr, self.ds, self.dr, self.ls = refs
        self.rows, self.cols = weights[0].shape
        self.parts = self.ds.shape[0] // len(weights)
        self.cut = self.rows // self.parts
        self.sent = []

    def start(self, make, *args):
        make(*args).start()
        self.sent.append((make, args, None))

    def order(self, u):
        return split_order(self.dp_bits, u % self.parts)[::-1]

    def hop_copy(self, w, j, way):
        at = lax.rem(self.z - way * j + self.stages, self.stages)
        to = lax.rem(self.z + way + self.stages, self.stages)
        return pltpu.make_async_remote_copy(
            src_ref=self.blocks.at[w, at], dst_ref=self.blocks.at[w, at],
            send_sem=self.zs.at[w, 2 * j + (way + 1) // 2], recv_sem=self.zr.at[w, at],
            device_id={"mp": to}, device_id_type=MESH,
        )

    def there(self, j, way):
        return self.z >= j if way == 1 else self.z < self.stages - j

    def pack(self, w):
        pieces = [self.weights[w][p * self.cut : (p + 1) * self.cut] for p in range(self.parts)]
        self.blocks[w, self.z] = jnp.concatenate(pieces, axis=1)

    def take(self, w, j):
        for way in (1, -1):

            @pl.when(self.there(j, way))
            def _():
                self.hop_copy(w, j, way).wait_recv()

    def hop(self, w, j):
        if j:
            self.take(w, j)
        for way in (1, -1):
            sends = self.there(j, way) & self.there(1, -way)

            @pl.when(sends)
            def _():
                self.hop_copy(w, j, way).start()

            self.sent.append((self.hop_copy, (w, j, way), sends))

    def place(self, u, which):
        at = which * self.rows + u % self.parts * self.cut
        return self.homes[u // self.parts].at[pl.ds(pl.multiple_of(at, self.cut), self.cut)]

    def piece(self, u):
        at = u % self.parts * self.cut
        return self.slab.at[u // self.parts, pl.ds(at, self.cut)]

    def own_copy(self, u):
        return pltpu.make_async_copy(self.piece(u), self.place(u, self.d), self.ls.at[u])

    def round_copy(self, u, k, slot, held):
        which = flipped(self.d, held)
        return pltpu.make_async_remote_copy(
            src_ref=self.place(u, which) if held else self.piece(u),
            dst_ref=self.place(u, which),
            send_sem=self.ds.at[u, (1 << k) - 1 + slot], recv_sem=self.dr.at[u, which],
            device_id={"dp": flipped(self.d, self.order(u)[k : k + 1])}, device_id_type=MESH,
        )

    def arrival(self, u, k, held):
        which = flipped(self.d, held + tuple(self.order(u)[k : k + 1]))
        return pltpu.make_async_remote_copy(
            src_ref=self.piece(u), dst_ref=self.place(u, which),
            send_sem=self.ds.at[u, 0], recv_sem=self.dr.at[u, which],
            device_id={"dp": flipped(self.d, self.order(u)[k : k + 1])}, device_id_type=MESH,
        )

    def units(self, w):
        return range(w * self.parts, (w + 1) * self.parts)

    def begin_round(self, w, k):
        for u in self.units(w):
            for slot, held in enumerate(subsets(self.order(u)[:k])):
                self.start(self.round_copy, u, k, slot, held)

    def collect(self, w):
        self.take(w, self.stages - 1)
        for p in range(self.parts):
            lanes = slice(p * self.cols, (p + 1) * self.cols)
            self.slab[w, p * self.cut : (p + 1) * self.cut] = jnp.concatenate(
                [self.blocks[w, s, :, lanes] for s in range(self.stages)], axis=1
            )
        for u in self.units(w):
            self.own_copy(u).start()

    def advance(self, w, k):
        for u in self.units(w):
            for held in subsets(self.order(u)[:k]):
                self.arrival(u, k, held).wait_recv()
        if k + 1 < self.dp_bits:
            self.begin_round(w, k + 1)
        else:
            for u in self.units(w):
                self.own_copy(u).wait()

    def close(self):
        for make, args, sends in self.sent:
            if sends is None:
                make(*args).wait_send()
            else:

                @pl.when(sends)
                def _():
                    make(*args).wait_send()


def gathering_scratch(count, dp, stages, rows, cols):
    parts = 2 if rows % 32 == 0 else 1
    dma = pltpu.SemaphoreType.DMA
    units = count * parts
    return [
        pltpu.VMEM((count, stages, rows // parts, cols * parts), BF16),
        pltpu.VMEM((count, rows, cols * stages), BF16),
        dma((count, 2 * stages)), dma((count, stages)), dma((units, dp)), dma((units, dp)), dma((units,)),
    ]


def forward_kernel(block, dp_bits, stages, back, *refs):
    weights, refs = refs[:6], refs[6:]
    tokens, vectors, segments = refs[:3]
    gain, factor = vectors.at[0:1], vectors.at[1:2]
    fulls, refs = refs[3:9], refs[9:]
    bias_full, raw_out, q_out, k_out, v_out, nt_out, o_ref, lse_ref = refs[:8]
    refs = refs[8:]
    home, window, normed, nt, raw, q, k, v, vt, ot, bias, scores, tops, totals, bias_in, bias_all = refs[:16]
    xs, xr, bs, br, os = refs[16:21]
    d, z = greet(dp_bits, stages)
    rows, features = tokens.shape
    width, heads = k.shape[0], features // HD
    own = width - rows
    tile = 2 * LANES
    homes = [home.at[w] for w in range(3)] + list(fulls[3:])
    work = Gathering(dp_bits, stages, d, z, weights, homes, refs[21:])

    def bias_copy(step):
        return pltpu.make_async_remote_copy(
            src_ref=bias_in, dst_ref=bias_all.at[step], send_sem=bs.at[step],
            recv_sem=br.at[step], device_id={"mp": lax.rem(z + step, stages)},
            device_id_type=MESH,
        )

    def token_copy(hop):
        return pltpu.make_async_remote_copy(
            src_ref=tokens if hop == 0 else window.at[hop - 1], dst_ref=window.at[hop],
            send_sem=xs.at[hop], recv_sem=xr.at[hop],
            device_id={"mp": jnp.minimum(z + 1, stages - 1)}, device_id_type=MESH,
        )

    kept = [
        (raw, raw_out), (q, q_out), (k, k_out), (v, v_out), (nt, nt_out),
        (home.at[0], fulls[0]), (home.at[1], fulls[1]), (home.at[2], fulls[2]),
    ]

    def keep(i):
        return pltpu.make_async_copy(kept[i][0], kept[i][1], os.at[i])

    def norm(src, at):
        step_rows = 128

        def step(i, carry):
            part = pl.ds(pl.multiple_of(i * step_rows, step_rows), step_rows)
            x = src[part, :].astype(F32)
            value = (x * row_inverse(x) * gain[...]).astype(BF16)
            to = pl.ds(pl.multiple_of(at + i * step_rows, step_rows), step_rows)
            normed[to, :] = value
            return carry

        lax.fori_loop(0, rows // step_rows, step, 0)
        for c in range(features // tile):
            lanes = slice(c * tile, (c + 1) * tile)
            nt[lanes, at : at + rows] = normed[at : at + rows, lanes].T

    def project(w, at, out, out_t):
        def step(c, carry):
            lanes = pl.ds(pl.multiple_of(c * tile, tile), tile)
            value = dot(normed[at : at + rows, :], home[w, :, lanes], 1, 0).astype(BF16)
            out[at : at + rows, lanes] = value
            if out_t is not None:
                out_t[lanes, at : at + rows] = value.T
            return carry

        lax.fori_loop(0, features // tile, step, 0)

    first, rest = range(3), range(3, 6)
    for w in range(6):
        work.pack(w)
    for w in first:
        work.hop(w, 0)
    bias_in[...] = vectors[4:5, : features // stages]
    for step in range(1, stages):
        work.start(bias_copy, step)
    bias_all[0] = bias_in[...]
    for hop in range(back):

        @pl.when(z <= hop)
        def _():
            window[hop] = jnp.zeros((rows, features), BF16)

    norm(tokens, own)
    fill_bias(segments, z, bias, block, own)
    for j in range(1, stages - 1):
        for w in first:
            work.hop(w, j)
    for w in rest:
        work.hop(w, 0)
    for w in first:
        work.collect(w)
        work.begin_round(w, 0)
    for j in range(1, stages - 1):
        if j <= 3 and dp_bits > 1:
            work.advance(j - 1, 0)
        for w in rest:
            work.hop(w, j)

    @pl.when(z < stages - 1)
    def _():
        token_copy(0).start()

    if dp_bits > 1:
        for w in range(max(0, min(stages - 2, 3)), 3):
            work.advance(w, 0)
    for w in rest:
        work.collect(w)
    for r in range(1, dp_bits - 1):
        for w in first:
            work.advance(w, r)
    for w in rest:
        work.begin_round(w, 0)
    for w in first:
        work.advance(w, dp_bits - 1)
        keep(5 + w).start()
        if w == 0:

            def query(c, carry):
                lanes = pl.ds(pl.multiple_of(c * tile, tile), tile)
                value = dot(normed[own:, :], home[0, :, lanes], 1, 0)
                raw[:, lanes] = value
                q[:, lanes] = (value * factor[:, lanes]).astype(BF16)
                return carry

            lax.fori_loop(0, features // tile, query, 0)
            keep(0).start()
            keep(1).start()
        else:
            project(w, own, *((k, None) if w == 1 else (v, vt)))

    sp = spans(rows, width, block)

    def attend(low, high, fresh, last, due):
        tiles = []
        for kb in range(low // block, high // block):
            qs = [i for i, (lo, hi) in enumerate(sp) if lo <= kb * block < hi]
            if qs:
                tiles.append((kb, qs))

        def head(h, carry):
            for at in sorted(set(due.values())):

                @pl.when(h == at)
                def _():
                    for w, r in due:
                        if due[w, r] == at:
                            work.advance(w, r)

            lanes, mine = head_lanes(h, features)
            feats = pl.ds(pl.multiple_of(h * HD, 16), HD)
            query = jnp.where(mine, q[:, lanes], jnp.zeros((), BF16))
            top = [jnp.full((8, block), FAR, F32) for _ in sp]
            for kb, qs in tiles:
                qa, qz = qs[0] * block, (qs[-1] + 1) * block
                at = slice(kb * block, (kb + 1) * block)
                s = dot(k[at, lanes], query[qa:qz], 1, 1) + bias[at, qa:qz]
                scores[at, qa:qz] = s
                for i in qs:
                    cut = s[:, i * block - qa : (i + 1) * block - qa]
                    top[i] = jnp.maximum(top[i], jnp.max(cut.reshape(block // 8, 8, block), axis=0))
            top = jnp.concatenate([jnp.max(t, axis=0, keepdims=True) for t in top], axis=1)
            if not fresh:
                before = tops[pl.ds(h, 1), :]
                top = jnp.maximum(top, before)
                scale = jnp.exp(before - top)
            acc = [jnp.zeros((HD, block), F32) for _ in sp]
            total = [jnp.zeros((8, block), F32) for _ in sp]
            for kb, qs in tiles:
                qa, qz = qs[0] * block, (qs[-1] + 1) * block
                at = slice(kb * block, (kb + 1) * block)
                p = jnp.exp(scores[at, qa:qz] - top[:, qa:qz])
                part = dot(vt[feats, at], p.astype(BF16), 1, 0)
                for i in qs:
                    cut = slice(i * block - qa, (i + 1) * block - qa)
                    total[i] = total[i] + jnp.sum(p[:, cut].reshape(block // 8, 8, block), axis=0)
                    acc[i] = acc[i] + part[:, cut]
            for i in range(len(sp)):
                at = slice(i * block, (i + 1) * block)
                one = jnp.sum(total[i], axis=0, keepdims=True)
                out = acc[i]
                if not fresh:
                    one = one + totals[pl.ds(h, 1), at] * scale[:, at]
                    out = out + ot[feats, at] * scale[:, at]
                if last:
                    ot[feats, at] = out / one
                    lse_ref[pl.ds(h, 1), at] = top[:, at] + jnp.log(one)
                else:
                    ot[feats, at] = out
                    totals[pl.ds(h, 1), at] = one
                    tops[pl.ds(h, 1), at] = top[:, at]
            return carry

        lax.fori_loop(0, heads, head, 0)

    inside, ready = {}, []
    if back and dp_bits > 2:
        inside = {(3, 1): heads * 3 // 8, (4, 1): heads * 5 // 8, (5, 1): heads * 7 // 8}
        ready = [(3, 0), (4, 0), (5, 0)]
    for pair in ready[:1]:
        work.advance(*pair)
    for hop in range(back):
        if hop + 1 == back:
            for pair in ready[1:]:
                work.advance(*pair)
            attend(rows, width, True, False, inside)

        @pl.when(z > hop)
        def _():
            token_copy(hop).wait_recv()

        if hop + 1 < back:

            @pl.when((z > hop) & (z < stages - 1))
            def _():
                token_copy(hop + 1).start()

        at = own - (hop + 1) * rows
        norm(window.at[hop], at)
        project(1, at, k, None)
        project(2, at, v, vt)
    for i in range(2, 5):
        keep(i).start()
    attend(0, rows if back else width, not back, True, {})
    transpose_out(ot, o_ref)
    for r in range(dp_bits):
        for w in rest:
            if (w, r) not in inside and (w, r) not in ready:
                work.advance(w, r)
    for step in range(1, stages):
        bias_copy(step).wait_recv()
    bias_full[...] = jnp.concatenate(
        [bias_all[lax.rem(z - s + stages, stages)] for s in range(stages)], axis=1
    )
    for hop in range(back):

        @pl.when((z >= hop) & (z < stages - 1))
        def _():
            token_copy(hop).wait_send()

    for i in range(len(kept)):
        keep(i).wait()
    work.close()


def attend_forward(weights, tokens, vectors, segments, block, dp, stages, back):
    held, cols = weights[0].shape
    rows, features = tokens.shape
    width, heads = (back + 1) * rows, features // HD
    hbm = pl.BlockSpec(memory_space=pl.ANY)
    vmem = pl.BlockSpec(memory_space=pltpu.VMEM)
    dma = pltpu.SemaphoreType.DMA
    sds = jax.ShapeDtypeStruct
    return pl.pallas_call(
        functools.partial(forward_kernel, block, dp.bit_length() - 1, stages, back),
        in_specs=[vmem] * 9,
        out_specs=[hbm] * 6 + [vmem] + [hbm] * 5 + [vmem] * 2,
        out_shape=[sds((features, features), BF16)] * 6
        + [
            sds((1, features), F32),
            sds((rows, features), F32),
            sds((rows, features), BF16),
            sds((width, features), BF16),
            sds((width, features), BF16),
            sds((features, width), BF16),
            sds((rows, features), BF16),
            sds((heads, rows), F32),
        ],
        scratch_shapes=[
            pltpu.VMEM((3, features, features), BF16),
            pltpu.VMEM((back, rows, features), BF16),
            pltpu.VMEM((width, features), BF16),
            pltpu.VMEM((features, width), BF16),
            pltpu.VMEM((rows, features), F32),
            pltpu.VMEM((rows, features), BF16),
            pltpu.VMEM((width, features), BF16),
            pltpu.VMEM((width, features), BF16),
            pltpu.VMEM((features, width), BF16),
            pltpu.VMEM((features, rows), F32),
            pltpu.VMEM((width, rows), F32),
            pltpu.VMEM((width, rows), F32),
            pltpu.VMEM((heads, rows), F32),
            pltpu.VMEM((heads, rows), F32),
            pltpu.VMEM((1, features // stages), F32),
            pltpu.VMEM((stages, 1, features // stages), F32),
            dma((back,)), dma((back,)), dma((stages,)), dma((stages,)), dma((8,)),
        ]
        + gathering_scratch(6, dp, stages, held, cols),
        compiler_params=pltpu.CompilerParams(
            collective_id=0, has_side_effects=True, vmem_limit_bytes=62 << 20
        ),
        name="attend_forward",
    )(*weights, tokens, vectors, segments)


def middle_kernel(block, dp_bits, stages, *refs):
    sources, refs = refs[:12], refs[12:]
    b_up, vectors, lse_ref, segments = refs[:4]
    factor, gain, b_down = (vectors.at[i : i + 1] for i in (1, 2, 3))
    results, incoming, outs, sums, refs = refs[4:10], refs[10], refs[11:14], refs[14], refs[15:]
    weights, hidden, wide, tmp, tr, keys, values, query_in, grad_in, bias, delta_ref = refs[:11]
    ps, pr, sems, refs = refs[11], refs[12], refs[13], refs[14:]
    d, z = greet(dp_bits, stages)
    work = Reduction(dp_bits, stages, d, z, None, outs, refs)
    rows, features = query_in.shape
    heads, width = features // HD, keys.shape[0]
    back = width // rows - 1
    tile = 2 * LANES
    w_out, w_up, w_down = weights.at[0], weights.at[1], weights.at[2]
    w_key, w_value = weights.at[2], weights.at[1]
    mixed, cot, x, second, active, d_pre, d_attn, spare = (tmp.at[i] for i in range(8))
    dk, dv = tmp.at[: back + 1], tmp.at[back + 1 : 2 * back + 2]
    dq, part = tmp.at[2 * back + 2], tmp.at[2 * back + 3]
    inside = (
        mixed, w_out, x, cot, w_up, w_down, keys, values, query_in, w_key, w_value, hidden,
    )
    half = rows // 2
    outside = (spare, hidden, dq, dk, dv, part.at[half:])
    loads = Loads(list(zip(sources, inside)) + list(zip(outside, results)), sems)
    loads.start(*range(9))
    fill_bias(segments, z, bias, block, width - rows)

    def by_tile(body):
        for c in range(features // tile):
            body(slice(c * tile, (c + 1) * tile), c)

    def by_rows(body, start):
        def step(i, carry):
            return body(pl.ds(pl.multiple_of(i * 64, 64), 64), carry)

        return lax.fori_loop(0, rows // 64, step, start)

    def flip(src):
        for c in range(features // tile):
            lanes = slice(c * tile, (c + 1) * tile)
            tr[lanes, :] = src[:, lanes].T

    nothing = jnp.zeros((1, features), F32)

    def add_attention(lanes, c):
        hidden[:, lanes] = x[:, lanes].astype(F32) + dot(mixed[...], w_out[lanes, :], 1, 1)

    def norm(at, carry):
        h = hidden[at, :]
        second[at, :] = (h * row_inverse(h) * gain[...]).astype(BF16)
        return carry

    def activate(lanes, c):
        pre = dot(second[...], w_up[:, lanes], 1, 0) + b_up[:, lanes]
        sigma = 1.0 / (1.0 + jnp.exp(-pre))
        active[:, lanes] = (pre * sigma).astype(BF16)
        grad = dot(cot[...], w_down[:, lanes], 1, 0)
        grad = (grad * sigma * (1.0 + pre * (1.0 - sigma))).astype(BF16)
        d_pre[:, lanes] = grad
        sums[2:3, lanes] = jnp.sum(grad.astype(F32), axis=0, keepdims=True)

    def finish_layer(lanes, c):
        out = dot(active[...], w_down[lanes, :], 1, 1)
        spare[:, lanes] = (hidden[:, lanes] + out + b_down[:, lanes]).astype(BF16)
        sums[1:2, lanes] = jnp.sum(cot[:, lanes].astype(F32), axis=0, keepdims=True)

    def to_second(lanes, c):
        wide[:, lanes] = dot(d_pre[...], w_up[lanes, :], 1, 1)

    def to_hidden(at, column):
        h, grad = hidden[at, :], wide[at, :]
        inverse = row_inverse(h)
        weighted = grad * gain[...]
        dots = jnp.sum(weighted * h, axis=1, keepdims=True)
        cube = inverse * inverse * inverse
        d_hidden = cot[at, :].astype(F32) + inverse * weighted - h * cube / features * dots
        hidden[at, :] = d_hidden
        d_attn[at, :] = d_hidden.astype(BF16)
        return column + jnp.sum(grad * h * inverse, axis=0, keepdims=True)

    def to_mixed(lanes, c):
        grad = dot(d_attn[...], w_out[:, lanes], 1, 0).astype(BF16)
        grad_in[:, lanes] = grad
        both = grad.astype(F32) * mixed[:, lanes].astype(F32)
        lane = lax.broadcasted_iota(jnp.int32, (heads, tile), 1) + c * tile
        first = lax.broadcasted_iota(jnp.int32, (heads, tile), 0) * HD
        owner = jnp.where((lane >= first) & (lane < first + HD), 1.0, 0.0).astype(BF16)
        high = both.astype(BF16)
        rest = (both - high.astype(F32)).astype(BF16)
        delta_ref[...] += dot(owner, high, 1, 1) + dot(owner, rest, 1, 1)

    sums[3:8, :] = jnp.zeros((5, features), F32)
    delta_ref[...] = jnp.zeros_like(delta_ref)
    loads.wait(0, 1, 2)
    by_tile(add_attention)
    by_rows(norm, 0)
    loads.wait(3, 4, 5)
    by_tile(activate)
    flip(cot)
    work.weight_grad(0, lambda at: tr[at, :], lambda: active[...])
    by_tile(finish_layer)
    loads.start(12, 9)
    by_tile(to_second)
    loads.start(10)
    flip(second)
    work.weight_grad(1, lambda at: tr[at, :], lambda: d_pre[...])
    work.advance(0, 0)
    sums[0:1, :] = by_rows(to_hidden, nothing)
    loads.start(13)
    by_tile(to_mixed)
    flip(d_attn)
    work.weight_grad(2, lambda at: tr[at, :], lambda: mixed[...])
    work.advance(1, 0)
    if dp_bits > 1:
        work.advance(0, 1)
    loads.wait(12)
    for c in range(2 * back + 2):
        tmp[c] = jnp.zeros((rows, features), BF16)
    wide[...] = jnp.zeros_like(wide)
    loads.wait(6, 7, 8)
    sp = spans(rows, width, block)
    steps = heads * (back + 1)
    events = [(2, 0)] + [(w, k) for w in range(3) for k in range(1, dp_bits) if (w, k) != (0, 1)]
    due = {i: int(at * steps) // 2 * 2 for i, at in enumerate(EVENTS[: len(events)])}

    def down():
        return pltpu.make_async_remote_copy(
            src_ref=part.at[:half], dst_ref=incoming, send_sem=ps, recv_sem=pr,
            device_id={"mp": jnp.maximum(z - 1, 0)}, device_id_type=MESH,
        )

    for c in range(back + 1):

        def head(h):
            lanes, mine = head_lanes(h, features)
            zero = jnp.zeros((), BF16)
            query = jnp.where(mine, query_in[:, lanes], zero)
            grad = jnp.where(mine, grad_in[:, lanes], zero)
            lse = lse_ref[pl.ds(h, 1), :]
            delta = delta_ref[pl.ds(h, 1), :]
            for kb in range(c * rows // block, (c + 1) * rows // block):
                qs = [i for i, (lo, hi) in enumerate(sp) if lo <= kb * block < hi]
                if not qs:
                    continue
                qa, qz = qs[0] * block, (qs[-1] + 1) * block
                at = slice(kb * block, (kb + 1) * block)
                to = slice(kb * block - c * rows, (kb + 1) * block - c * rows)
                key = keys[at, lanes]
                s = dot(key, query[qa:qz], 1, 1) + bias[at, qa:qz]
                p = jnp.exp(s - lse[:, qa:qz])
                dp = dot(values[at, lanes], grad[qa:qz], 1, 1)
                ds = (p * (dp - delta[:, qa:qz])).astype(BF16)
                dv[c, to, lanes] += dot(p.astype(BF16), grad[qa:qz], 1, 0).astype(BF16)
                dk[c, to, lanes] += dot(ds, query[qa:qz], 1, 0).astype(BF16)
                wide[qa:qz, lanes] += dot(ds, jnp.where(mine, key, zero), 0, 0)

        def pair(i, carry):
            for at in sorted(set(due.values())):
                if at // heads != c:
                    continue

                @pl.when(2 * i == at % heads)
                def _():
                    for e in due:
                        if due[e] == at:
                            work.advance(*events[e])

            head(2 * i)
            head(2 * i + 1)
            return carry

        lax.fori_loop(0, heads // 2, pair, 0)
        if c == 0:
            loads.wait(9, 10)
            if back:
                back_project(part, ((dk.at[0], w_key), (dv.at[0], w_value)), 0, None)
                loads.start(17)

                @pl.when(z >= back)
                def _():
                    down().start()

            loads.wait(13)
            loads.start(11)

    loads.start(15, 16)
    loads.wait(11)

    def to_query(at, column):
        scaled = wide[at, :].astype(BF16).astype(F32)
        dq[at, :] = (scaled * factor[...]).astype(BF16)
        return column + jnp.sum(scaled * hidden[at, :], axis=0, keepdims=True)

    sums[4:5, :] = by_rows(to_query, nothing)
    loads.start(14)
    for i in range(len(due), len(events)):
        work.advance(*events[i])
    for w in range(3):
        work.finish(w)
    loads.wait(14, 15, 16)
    if back:
        loads.wait(17)

        @pl.when((z + 1 >= back) & (z < stages - 1))
        def _():
            down().wait_recv()

        @pl.when(z >= back)
        def _():
            down().wait_send()

    work.close()


def back_project(out, pairs, at, more):
    rows, features = out.shape
    tile = 2 * LANES

    def step(c, carry):
        lanes = pl.ds(pl.multiple_of(c * tile, tile), tile)
        value = None
        for grad, weight in pairs:
            start = at if grad.shape[0] > rows else 0
            term = dot(grad[start : start + rows, :], weight[lanes, :], 1, 1)
            value = term if value is None else value + term
        if more is not None:
            value = value + more(lanes)
        out[:, lanes] = value.astype(out.dtype)
        return carry

    lax.fori_loop(0, features // tile, step, 0)


def middle(
    mixed, w_out, x, cot, w_up, w_down, k, v, q, w_key, w_value, raw, b_up, vectors,
    lse, segments, block, dp, stages,
):
    rows, features = q.shape
    width, heads = k.shape[0], features // HD
    held, cols = features // dp, features // stages
    chunks = width // rows
    hbm = pl.BlockSpec(memory_space=pl.ANY)
    vmem = pl.BlockSpec(memory_space=pltpu.VMEM)
    dma = pltpu.SemaphoreType.DMA
    sds = jax.ShapeDtypeStruct
    low, high = sds((rows, features), BF16), sds((rows, features), F32)
    many, part = sds((chunks, rows, features), BF16), sds((rows // 2, features), BF16)
    return pl.pallas_call(
        functools.partial(middle_kernel, block, dp.bit_length() - 1, stages),
        in_specs=[hbm] * 12 + [vmem] * 4,
        out_specs=[hbm] * 7 + [vmem] * 4,
        out_shape=[low, high, low, many, many, part, part]
        + [sds((held, cols), F32)] * 3
        + [sds((8, features), F32)],
        scratch_shapes=[
            pltpu.VMEM((3, features, features), BF16),
            pltpu.VMEM((rows, features), F32),
            pltpu.VMEM((rows, features), F32),
            pltpu.VMEM((max(8, 2 * chunks + 2), rows, features), BF16),
            pltpu.VMEM((features, rows), BF16),
            pltpu.VMEM((width, features), BF16),
            pltpu.VMEM((width, features), BF16),
            pltpu.VMEM((rows, features), BF16),
            pltpu.VMEM((rows, features), BF16),
            pltpu.VMEM((width, rows), F32),
            pltpu.VMEM((heads, rows), F32),
            dma, dma, dma((18,)),
        ]
        + reduction_scratch(3, dp, stages, held, features, True),
        compiler_params=pltpu.CompilerParams(
            collective_id=2, has_side_effects=True, vmem_limit_bytes=63 << 20
        ),
        name="middle",
    )(
        mixed, w_out, x, cot, w_up, w_down, k, v, q, w_key, w_value, raw, b_up, vectors,
        lse, segments,
    )


def input_kernel(dp_bits, stages, back, *refs):
    sources, farther, vectors, sums, refs = refs[:10], refs[10], refs[11], refs[12], refs[13:]
    gain = vectors.at[0:1]
    outs, result, total, refs = refs[:3], refs[3], refs[4], refs[5:]
    inside, tokens_grad, refs = refs[:10], refs[10], refs[11:]
    dv, nt, dk, wk, wv, incoming, dq, wq, tokens, d_hidden = inside
    part, landed, d_first, sgot, ss, sr, ps, pr, sems = refs[:9]
    d, z = greet(dp_bits, stages)
    work = Reduction(dp_bits, stages, d, z, None, outs, refs[9:])
    rows, features = tokens.shape
    own, half = back * rows, rows // 2
    inside = inside[:5] + (incoming.at[:half],) + inside[6:]
    loads = Loads(list(zip(sources, inside)) + [(tokens_grad, result)], sems)
    levels = dp_bits + stages.bit_length() - 1
    held = features >> dp_bits
    grads = ((dv, 2, 0), (dk, 1, 0), (dq, 0, own))

    def down(hop):
        return pltpu.make_async_remote_copy(
            src_ref=part.at[hop - 1] if hop else farther,
            dst_ref=landed.at[hop - 1] if hop else incoming.at[half:],
            send_sem=ps.at[hop], recv_sem=pr.at[hop],
            device_id={"mp": jnp.maximum(z - 1, 0)}, device_id_type=MESH,
        )

    if back:

        @pl.when(z >= back)
        def _():
            down(0).start()

    loads.start(*range(10))

    def arrived(hop):
        source = incoming if hop == 1 else landed.at[hop - 2]
        there = (z + 1 >= back - hop + 1) & (z < stages - 1)

        def take(lanes):
            return jnp.where(there, source[:, lanes].astype(F32), 0.0)

        return there, take

    def weight_grad(i):
        grad, w, at = grads[i]
        work.weight_grad(w, lambda rows_at: nt[rows_at, at:], lambda: grad[...])

    def sum_copy(k):
        if k < dp_bits:
            to = {"dp": flipped(d, (k,))}
        else:
            to = {"mp": flipped(z, (k - dp_bits,))}
        return pltpu.make_async_remote_copy(
            src_ref=total.at[k], dst_ref=sgot.at[k], send_sem=ss.at[k], recv_sem=sr.at[k],
            device_id=to, device_id_type=MESH,
        )

    def sum_step(k):
        sum_copy(k).wait_recv()
        total[k + 1] = total[k] + sgot[k]
        if k + 1 < levels:
            work.start(sum_copy, k + 1)

    def pass_down(hop):
        there, take = arrived(hop)

        @pl.when(there)
        def _():
            down(hop - 1).wait_recv()

        back_project(part.at[hop - 1], ((dk, wk), (dv, wv)), hop * rows, take)

        @pl.when(z >= back - hop)
        def _():
            down(hop).start()

    loads.wait(0, 1)
    weight_grad(0)
    loads.wait(2)
    weight_grad(1)
    work.advance(2, 0)
    loads.wait(3, 4, 5)
    if back > 1:
        pass_down(1)
    work.advance(1, 0)
    loads.wait(6, 7)
    weight_grad(2)
    for hop in range(2, back):
        pass_down(hop)
    work.advance(0, 0)
    back_project(d_first, ((dk, wk), (dv, wv), (dq, wq)), own, None)
    events = [(w, k) for w in (2, 1, 0) for k in range(1, dp_bits)]
    for event in events[:1]:
        work.advance(*event)
    loads.wait(8, 9)
    there, take = arrived(back) if back else (None, None)
    if back:

        @pl.when(there)
        def _():
            down(back - 1).wait_recv()

    chunk = 64

    def finish(i, column):
        at = pl.ds(pl.multiple_of(i * chunk, chunk), chunk)
        x = tokens[at, :].astype(F32)
        grad = d_first[at, :]
        if back:
            source = incoming if back == 1 else landed.at[back - 2]
            grad = grad + jnp.where(there, source[at, :].astype(F32), 0.0)
        inverse = row_inverse(x)
        weighted = grad * gain[...]
        dots = jnp.sum(weighted * x, axis=1, keepdims=True)
        cube = inverse * inverse * inverse
        tokens_grad[at, :] = (
            d_hidden[at, :] + inverse * weighted - x * cube / features * dots
        ).astype(BF16)
        return column + jnp.sum(grad * x * inverse, axis=0, keepdims=True)

    column = lax.fori_loop(0, rows // chunk, finish, jnp.zeros((1, features), F32))
    total[0] = sums[...]
    total[0, 3:4, :] = column
    work.start(sum_copy, 0)
    loads.start(10)
    done = 0
    for event in events[1:]:
        work.advance(*event)
        if done < levels:
            sum_step(done)
            done += 1
    for k in range(done, levels):
        sum_step(k)
    for w in (2, 1, 0):
        work.finish(w)
    for hop in range(back):

        @pl.when(z >= back - hop)
        def _():
            down(hop).wait_send()

    loads.wait(10)
    work.close()


def input_gradients(
    nt, dq, dk, dv, wq, wk, wv, incoming, farther, tokens, d_hidden, vectors, sums, dp, stages
):
    rows, features = tokens.shape
    back = dk.shape[0] // rows - 1
    held, cols = features // dp, features // stages
    dp_bits = dp.bit_length() - 1
    levels = dp_bits + stages.bit_length() - 1
    hbm = pl.BlockSpec(memory_space=pl.ANY)
    vmem = pl.BlockSpec(memory_space=pltpu.VMEM)
    dma = pltpu.SemaphoreType.DMA
    hops = max(1, back - 1)
    sources = (dv, nt, dk, wk, wv, incoming, dq, wq, tokens, d_hidden)
    out = pl.pallas_call(
        functools.partial(input_kernel, dp_bits, stages, back),
        in_specs=[hbm] * 11 + [vmem] * 2,
        out_specs=[vmem] * 3 + [hbm, vmem],
        out_shape=[jax.ShapeDtypeStruct((held, cols), F32)] * 3
        + [
            jax.ShapeDtypeStruct((rows, features), BF16),
            jax.ShapeDtypeStruct((levels + 1,) + sums.shape, F32),
        ],
        scratch_shapes=[pltpu.VMEM(tokens.shape if a is incoming else a.shape, a.dtype) for a in sources + (tokens,)]
        + [
            pltpu.VMEM((hops, rows, features), BF16), pltpu.VMEM((hops, rows, features), BF16),
            pltpu.VMEM((rows, features), F32), pltpu.VMEM((levels,) + sums.shape, F32),
            dma((levels,)), dma((levels,)), dma((hops + 1,)), dma((hops + 1,)), dma((11,)),
        ]
        + reduction_scratch(3, dp, stages, held, features, True),
        compiler_params=pltpu.CompilerParams(
            collective_id=1, has_side_effects=True, vmem_limit_bytes=62 << 20
        ),
        name="input_gradients",
    )(*sources, farther, vectors, sums)
    return out[:3], out[3], out[4][levels]


def hand_over_kernel(count, *refs):
    half = (len(refs) - 1) // 2
    sources, results, sems = refs[:half], refs[half : 2 * half], refs[-1]
    loads = Loads(list(zip(sources[:count], results[:count])), sems)
    loads.start(*range(count))
    for source, result in zip(sources[count:], results[count:]):
        result[...] = source[...].T
    loads.wait(*range(count))


def hand_over(plain, turned):
    hbm = pl.BlockSpec(memory_space=pl.ANY)
    vmem = pl.BlockSpec(memory_space=pltpu.VMEM)
    sds = jax.ShapeDtypeStruct
    return pl.pallas_call(
        functools.partial(hand_over_kernel, len(plain)),
        in_specs=[hbm] * len(plain) + [vmem] * len(turned),
        out_specs=[hbm] * len(plain) + [vmem] * len(turned),
        out_shape=[sds(a.shape, a.dtype) for a in plain]
        + [sds(a.shape[::-1], a.dtype) for a in turned],
        scratch_shapes=[pltpu.SemaphoreType.DMA((len(plain),))],
        name="hand_over",
    )(*plain, *turned)


def body(
    tokens, segments, w_query, w_key, w_value, w_output, w_up, b_up, w_down, b_down,
    gain_attn, gain_mlp, query_scale, cotangent,
):
    stages = lax.axis_size("mp")
    z = lax.axis_index("mp")
    rows, features = tokens.shape
    back = min(stages - 1, -(-(DOC_MAX - 1) // rows))
    own = back * rows
    block = min(256, rows)
    heads = features // HD
    dp = lax.axis_size("dp")
    factor = jax.nn.softplus(query_scale) * (LOG2E / math.sqrt(HD))
    mine = b_up.shape[0]
    vectors = jnp.zeros((8, features), F32)
    row = lax.broadcasted_iota(jnp.int32, (8, features), 0)
    given = (gain_attn, jnp.tile(factor, heads), gain_mlp, b_down, jnp.pad(b_up, (0, features - mine)))
    for i, value in enumerate(given):
        vectors = jnp.where(row == i, value[None], vectors)
    (
        wq, wk, wv, wu, wo, wd, b_full, query_raw, scaled, keys, values, first_t, mixed, lse
    ) = attend_forward(
        (w_query, w_key, w_value, w_up, w_output.T, w_down.T), tokens, vectors, segments,
        block, dp, stages, back,
    )
    layer_out, d_hidden, d_query, d_keys, d_values, farther, incoming, *mlp, sums = middle(
        mixed, wo, tokens, cotangent, wu, wd, keys, values, scaled, wk, wv, query_raw,
        b_full, vectors, lse, segments, block, dp, stages,
    )
    grads, tokens_grad, sums = input_gradients(
        first_t, d_query, d_keys.reshape(own + rows, features),
        d_values.reshape(own + rows, features), wq, wk, wv, incoming, farther, tokens,
        d_hidden, vectors, sums, dp, stages,
    )
    sum_b_up = lax.dynamic_slice_in_dim(sums[2], z * mine, mine, 0)
    scale_total = jnp.sum(sums[4].reshape(heads, HD), axis=0)
    grad_query_scale = scale_total * (LOG2E / math.sqrt(HD)) * jax.nn.sigmoid(query_scale)
    layer_out, tokens_grad, g_query, g_key, g_value, g_up, g_output, g_down = hand_over(
        (layer_out, tokens_grad, *grads, mlp[1]), (mlp[2], mlp[0])
    )
    return (
        layer_out, tokens_grad, g_query, g_key, g_value, g_output, g_up, sum_b_up,
        g_down, sums[1], sums[3], sums[0], grad_query_scale,
    )


def solution(mesh):
    tokens, rows_dp, rows_mp = P(("dp", "mp"), None), P("dp", "mp"), P("mp", "dp")
    return jax.shard_map(
        body,
        mesh=mesh,
        in_specs=(
            tokens, P("dp", None), rows_dp, rows_dp, rows_dp, rows_mp, rows_dp, P("mp"), rows_mp,
            P(), P(), P(), P(), tokens,
        ),
        out_specs=(
            tokens, tokens, rows_dp, rows_dp, rows_dp, rows_mp, rows_dp, P("mp"), rows_mp,
            P(), P(), P(), P(),
        ),
        check_vma=False,
    )
```

```python
import functools
import math

import jax
import jax.numpy as jnp
from jax import lax
from jax.experimental import pallas as pl
from jax.experimental.pallas import tpu as pltpu
from jax.sharding import PartitionSpec as P

HD = 80
LANES = 128
EPSILON = 1e-06
LOG2E = 1.442695
DOC_MAX = 1024
FAR = -1e30
EVENTS = (0.15, 0.3, 0.5, 0.6, 0.75, 0.9)
F32 = jnp.float32
BF16 = jnp.bfloat16


def dot(a, b, ca, cb):
    return lax.dot_general(a, b, (((ca,), (cb,)), ((), ())), preferred_element_type=F32)


def row_inverse(values):
    return lax.rsqrt(jnp.mean(values * values, axis=1, keepdims=True) + EPSILON)


MESH = pl.DeviceIdType.MESH


def bit_of(index, b):
    return lax.rem(lax.div(index, 1 << b), 2)


def flipped(index, bits):
    for b in bits:
        index = index + (1 << b) * (1 - 2 * bit_of(index, b))
    return index


def split_order(count, turn):
    bits = list(range(count))
    rest = bits[1:][::-1]
    turn = turn % max(1, len(rest))
    return bits[:1] + rest[turn:] + rest[:turn]


def subsets(bits):
    out = [()]
    for b in bits:
        out = out + [s + (b,) for s in out]
    return out


def greet(dp_bits, stages, extra=()):
    d, z = lax.axis_index("dp"), lax.axis_index("mp")
    barrier = pltpu.get_barrier_semaphore()
    for b in range(dp_bits):
        pl.semaphore_signal(barrier, device_id={"dp": flipped(d, (b,))}, device_id_type=MESH)
    for step in range(1, stages):
        pl.semaphore_signal(
            barrier, device_id={"mp": lax.rem(z + step, stages)}, device_id_type=MESH
        )
    pl.semaphore_wait(barrier, dp_bits + stages - 1)
    return d, z


class Loads:
    def __init__(self, pairs, sems):
        self.pairs, self.sems = pairs, sems

    def copy(self, i):
        return pltpu.make_async_copy(self.pairs[i][0], self.pairs[i][1], self.sems.at[i])

    def start(self, *which):
        for i in which:
            self.copy(i).start()

    def wait(self, *which):
        for i in which:
            self.copy(i).wait()


class Reduction:
    def __init__(self, dp_bits, stages, d, z, grads, outs, refs):
        self.dp_bits, self.stages, self.d, self.z = dp_bits, stages, d, z
        self.grads, self.outs = grads, outs
        self.pool = refs[0]
        self.kept, self.got = refs[0].at[0], refs[1 : 1 + dp_bits]
        self.zsend, self.zgot, self.ks, self.rs, self.rr, self.zs, self.zr = refs[1 + dp_bits :]
        self.half = 1 << (dp_bits - 1)
        self.parts = self.kept.shape[0] // len(outs)
        self.rows, self.features = self.kept.shape[2], self.kept.shape[3]
        self.sent = []

    def start(self, make, *args):
        make(*args).start()
        self.sent.append((make, args))

    def order(self, u):
        return split_order(self.dp_bits, u % self.parts)

    def place(self, u, slot, low):
        rest = self.order(u)[1:]
        at = low
        for i, b in enumerate(rest):
            if slot >> (len(rest) - 1 - i) & 1:
                at = at + (1 << b)
        return at

    def slot_of(self, u, index):
        rest = self.order(u)[1:]
        return sum(bit_of(index, b - 1) << (len(rest) - 1 - i) for i, b in enumerate(rest))

    def source(self, u, slot, low):
        cut = pl.ds(u % self.parts * self.rows, self.rows)
        return self.grads[u // self.parts].at[self.place(u, slot, low), cut]

    def first_copy(self, u, slot):
        return pltpu.make_async_remote_copy(
            src_ref=self.pool.at[1, u, slot]
            if self.grads is None
            else self.source(u, slot, 1 - bit_of(self.d, 0)),
            dst_ref=self.got[0].at[u, slot],
            send_sem=self.rs.at[u, slot], recv_sem=self.rr.at[u, slot],
            device_id={"dp": flipped(self.d, (0,))}, device_id_type=MESH,
        )

    def keep_copy(self, u, slot):
        return pltpu.make_async_copy(
            self.source(u, slot, bit_of(self.d, 0)), self.kept.at[u, slot], self.ks.at[u, slot]
        )

    def round_copy(self, u, k):
        count = self.half >> k
        b = self.order(u)[k]
        other = 1 - bit_of(self.d, b)
        return pltpu.make_async_remote_copy(
            src_ref=self.got[k - 1].at[u, pl.ds(other * count, count)],
            dst_ref=self.got[k].at[u],
            send_sem=self.rs.at[u, self.half + k], recv_sem=self.rr.at[u, self.half + k],
            device_id={"dp": flipped(self.d, (b,))}, device_id_type=MESH,
        )

    def last_copy(self, w, step):
        to = lax.rem(self.z + step, self.stages)
        return pltpu.make_async_remote_copy(
            src_ref=self.zsend.at[w, to], dst_ref=self.zgot.at[w, step],
            send_sem=self.zs.at[w, step], recv_sem=self.zr.at[w, step],
            device_id={"mp": to}, device_id_type=MESH,
        )

    def units(self, w):
        return range(w * self.parts, (w + 1) * self.parts)

    def begin(self, w):
        for u in self.units(w):
            for slot in range(self.half):
                self.start(self.first_copy, u, slot)
                if self.grads is not None:
                    self.keep_copy(u, slot).start()

    def add(self, dst, src, count):
        def step(i, carry):
            dst[i] = dst[i] + src(i)
            return carry

        lax.fori_loop(0, count, step, 0)

    def take(self, w, k):
        for u in self.units(w):
            count = self.half >> k
            if k == 0:
                for slot in range(self.half):
                    if self.grads is not None:
                        self.keep_copy(u, slot).wait()
                    self.first_copy(u, slot).wait_recv()
                self.add(self.got[0].at[u], lambda i: self.kept[u, i], count)
            else:
                self.round_copy(u, k).wait_recv()
                mine = bit_of(self.d, self.order(u)[k]) * count
                self.add(self.got[k].at[u], lambda i: self.got[k - 1][u, mine + i], count)

    def send(self, w, k):
        for u in self.units(w):
            self.start(self.round_copy, u, k)

    def advance(self, w, k):
        self.take(w, k)
        if k + 1 == self.dp_bits:
            self.begin_last(w)
        else:
            self.send(w, k + 1)

    def put(self, w, index, value):
        held = self.parts * self.rows
        for low in range(2):
            which = lax.rem(bit_of(self.d, 0) + low, 2)
            for u in self.units(w):
                cut = low * held + u % self.parts * self.rows
                self.pool[which, u, self.slot_of(u, index)] = value[cut : cut + self.rows]

    def weight_grad(self, w, left, right):
        held = self.parts * self.rows

        def step(t, carry):
            at = pl.ds(pl.multiple_of(t * 2 * held, 2 * held), 2 * held)
            self.put(w, t, dot(left(at), right(), 1, 0).astype(BF16))
            return carry

        lax.fori_loop(0, 1 << (self.dp_bits - 1), step, 0)
        self.begin(w)

    def begin_last(self, w):
        cols = self.features // self.stages
        whole = [self.got[self.dp_bits - 1][u, 0] for u in self.units(w)]
        for s in range(self.stages):
            self.zsend[w, s] = jnp.concatenate(
                [piece[:, s * cols : (s + 1) * cols] for piece in whole], axis=1
            )
        for step in range(1, self.stages):
            self.start(self.last_copy, w, step)

    def finish(self, w):
        value = self.zsend[w, self.z].astype(F32)
        for step in range(1, self.stages):
            self.last_copy(w, step).wait_recv()
            value = value + self.zgot[w, step].astype(F32)
        cols = self.features // self.stages
        for p in range(self.parts):
            at = slice(p * self.rows, (p + 1) * self.rows)
            self.outs[w][at, :] = value[:, p * cols : (p + 1) * cols]

    def close(self):
        for make, args in self.sent:
            make(*args).wait_send()


def reduction_scratch(count, dp, stages, rows, features, local=False):
    dp_bits, half, cols = dp.bit_length() - 1, dp // 2, features // stages
    parts = 2 if rows % 32 == 0 else 1
    dma = pltpu.SemaphoreType.DMA
    units = count * parts
    return (
        [pltpu.VMEM((1 + local, units, half, rows // parts, features), BF16)]
        + [pltpu.VMEM((units, half >> k, rows // parts, features), BF16) for k in range(dp_bits)]
        + [pltpu.VMEM((count, stages, rows // parts, cols * parts), BF16)] * 2
        + [
            dma((units, half)), dma((units, half + dp_bits)), dma((units, half + dp_bits)),
            dma((count, stages)), dma((count, stages)),
        ]
    )


def spans(rows, width, block):
    own = width - rows
    out=[]
    for qb in range(rows//block):
        hi = own + (qb+1)*block
        lo = max(0, (own + qb*block - (DOC_MAX-1))//block*block)
        out.append((lo,hi))
    return out

def head_lanes(h, features):
    first = h*HD
    off = jnp.minimum(lax.div(first, LANES)*LANES, features-2*LANES)
    off = pl.multiple_of(off, LANES)
    lane = lax.broadcasted_iota(jnp.int32,(1,2*LANES),1) + (off-first)
    return pl.ds(off, 2*LANES), (lane>=0)&(lane<HD)

def fill_bias(segments, z, bias, block, own):
    width, rows = bias.shape
    first = z * rows
    for kb in range(width // block):
        start = first + (kb * block - own)
        at = pl.ds(pl.multiple_of(jnp.maximum(start, 0), block), block)
        col = jnp.broadcast_to(segments[:, at], (block, block)).T
        sub = lax.broadcasted_iota(jnp.int32, (block, block), 0) + kb * block
        for qb in range(rows // block):
            row = segments[:, pl.ds(pl.multiple_of(first + qb * block, block), block)]
            last = lax.broadcasted_iota(jnp.int32, (block, block), 1) + (own + qb * block)
            allowed = (col == row) & (sub <= last) & (start >= 0)
            bias[kb * block : (kb + 1) * block, qb * block : (qb + 1) * block] = jnp.where(
                allowed, 0.0, FAR
            )


def transpose_out(src, dst):
    for i in range(src.shape[0]//LANES):
        at = slice(i*LANES,(i+1)*LANES)
        dst[:, at] = src[at,:].T.astype(dst.dtype)

class Gathering:
    def __init__(self, dp_bits, stages, d, z, weights, homes, refs):
        self.dp_bits, self.stages, self.d, self.z = dp_bits, stages, d, z
        self.weights, self.homes = weights, homes
        self.blocks, self.slab, self.zs, self.zr, self.ds, self.dr, self.ls = refs
        self.rows, self.cols = weights[0].shape
        self.parts = self.ds.shape[0] // len(weights)
        self.cut = self.rows // self.parts
        self.sent = []

    def start(self, make, *args):
        make(*args).start()
        self.sent.append((make, args, None))

    def order(self, u):
        return split_order(self.dp_bits, u % self.parts)[::-1]

    def hop_copy(self, w, j, way):
        at = lax.rem(self.z - way * j + self.stages, self.stages)
        to = lax.rem(self.z + way + self.stages, self.stages)
        return pltpu.make_async_remote_copy(
            src_ref=self.blocks.at[w, at], dst_ref=self.blocks.at[w, at],
            send_sem=self.zs.at[w, 2 * j + (way + 1) // 2], recv_sem=self.zr.at[w, at],
            device_id={"mp": to}, device_id_type=MESH,
        )

    def there(self, j, way):
        return self.z >= j if way == 1 else self.z < self.stages - j

    def pack(self, w):
        pieces = [self.weights[w][p * self.cut : (p + 1) * self.cut] for p in range(self.parts)]
        self.blocks[w, self.z] = jnp.concatenate(pieces, axis=1)

    def take(self, w, j):
        for way in (1, -1):

            @pl.when(self.there(j, way))
            def _():
                self.hop_copy(w, j, way).wait_recv()

    def hop(self, w, j):
        if j:
            self.take(w, j)
        for way in (1, -1):
            sends = self.there(j, way) & self.there(1, -way)

            @pl.when(sends)
            def _():
                self.hop_copy(w, j, way).start()

            self.sent.append((self.hop_copy, (w, j, way), sends))

    def place(self, u, which):
        at = which * self.rows + u % self.parts * self.cut
        return self.homes[u // self.parts].at[pl.ds(pl.multiple_of(at, self.cut), self.cut)]

    def piece(self, u):
        at = u % self.parts * self.cut
        return self.slab.at[u // self.parts, pl.ds(at, self.cut)]

    def own_copy(self, u):
        return pltpu.make_async_copy(self.piece(u), self.place(u, self.d), self.ls.at[u])

    def round_copy(self, u, k, slot, held):
        which = flipped(self.d, held)
        return pltpu.make_async_remote_copy(
            src_ref=self.place(u, which) if held else self.piece(u),
            dst_ref=self.place(u, which),
            send_sem=self.ds.at[u, (1 << k) - 1 + slot], recv_sem=self.dr.at[u, which],
            device_id={"dp": flipped(self.d, self.order(u)[k : k + 1])}, device_id_type=MESH,
        )

    def arrival(self, u, k, held):
        which = flipped(self.d, held + tuple(self.order(u)[k : k + 1]))
        return pltpu.make_async_remote_copy(
            src_ref=self.piece(u), dst_ref=self.place(u, which),
            send_sem=self.ds.at[u, 0], recv_sem=self.dr.at[u, which],
            device_id={"dp": flipped(self.d, self.order(u)[k : k + 1])}, device_id_type=MESH,
        )

    def units(self, w):
        return range(w * self.parts, (w + 1) * self.parts)

    def begin_round(self, w, k):
        for u in self.units(w):
            for slot, held in enumerate(subsets(self.order(u)[:k])):
                self.start(self.round_copy, u, k, slot, held)

    def collect(self, w):
        self.take(w, self.stages - 1)
        for p in range(self.parts):
            lanes = slice(p * self.cols, (p + 1) * self.cols)
            self.slab[w, p * self.cut : (p + 1) * self.cut] = jnp.concatenate(
                [self.blocks[w, s, :, lanes] for s in range(self.stages)], axis=1
            )
        for u in self.units(w):
            self.own_copy(u).start()

    def advance(self, w, k):
        for u in self.units(w):
            for held in subsets(self.order(u)[:k]):
                self.arrival(u, k, held).wait_recv()
        if k + 1 < self.dp_bits:
            self.begin_round(w, k + 1)
        else:
            for u in self.units(w):
                self.own_copy(u).wait()

    def close(self):
        for make, args, sends in self.sent:
            if sends is None:
                make(*args).wait_send()
            else:

                @pl.when(sends)
                def _():
                    make(*args).wait_send()


def gathering_scratch(count, dp, stages, rows, cols):
    parts = 2 if rows % 32 == 0 else 1
    dma = pltpu.SemaphoreType.DMA
    units = count * parts
    return [
        pltpu.VMEM((count, stages, rows // parts, cols * parts), BF16),
        pltpu.VMEM((count, rows, cols * stages), BF16),
        dma((count, 2 * stages)), dma((count, stages)), dma((units, dp)), dma((units, dp)), dma((units,)),
    ]


def forward_kernel(block, dp_bits, stages, back, *refs):
    weights, refs = refs[:6], refs[6:]
    tokens, vectors, segments = refs[:3]
    gain, factor = vectors.at[0:1], vectors.at[1:2]
    fulls, refs = refs[3:9], refs[9:]
    bias_full, raw_out, q_out, k_out, v_out, nt_out, o_ref, lse_ref = refs[:8]
    refs = refs[8:]
    home, window, normed, nt, raw, q, k, v, vt, ot, bias, scores, tops, totals, bias_in, bias_all = refs[:16]
    xs, xr, bs, br, os = refs[16:21]
    d, z = greet(dp_bits, stages)
    rows, features = tokens.shape
    width, heads = k.shape[0], features // HD
    own = width - rows
    tile = 2 * LANES
    homes = [home.at[w] for w in range(3)] + list(fulls[3:])
    work = Gathering(dp_bits, stages, d, z, weights, homes, refs[21:])

    def bias_copy(step):
        return pltpu.make_async_remote_copy(
            src_ref=bias_in, dst_ref=bias_all.at[step], send_sem=bs.at[step],
            recv_sem=br.at[step], device_id={"mp": lax.rem(z + step, stages)},
            device_id_type=MESH,
        )

    def token_copy(hop):
        return pltpu.make_async_remote_copy(
            src_ref=tokens if hop == 0 else window.at[hop - 1], dst_ref=window.at[hop],
            send_sem=xs.at[hop], recv_sem=xr.at[hop],
            device_id={"mp": jnp.minimum(z + 1, stages - 1)}, device_id_type=MESH,
        )

    kept = [
        (raw, raw_out), (q, q_out), (k, k_out), (v, v_out), (nt, nt_out),
        (home.at[0], fulls[0]), (home.at[1], fulls[1]), (home.at[2], fulls[2]),
    ]

    def keep(i):
        return pltpu.make_async_copy(kept[i][0], kept[i][1], os.at[i])

    def norm(src, at):
        step_rows = 128

        def step(i, carry):
            part = pl.ds(pl.multiple_of(i * step_rows, step_rows), step_rows)
            x = src[part, :].astype(F32)
            value = (x * row_inverse(x) * gain[...]).astype(BF16)
            to = pl.ds(pl.multiple_of(at + i * step_rows, step_rows), step_rows)
            normed[to, :] = value
            return carry

        lax.fori_loop(0, rows // step_rows, step, 0)
        for c in range(features // tile):
            lanes = slice(c * tile, (c + 1) * tile)
            nt[lanes, at : at + rows] = normed[at : at + rows, lanes].T

    def project(w, at, out, out_t):
        def step(c, carry):
            lanes = pl.ds(pl.multiple_of(c * tile, tile), tile)
            value = dot(normed[at : at + rows, :], home[w, :, lanes], 1, 0).astype(BF16)
            out[at : at + rows, lanes] = value
            if out_t is not None:
                out_t[lanes, at : at + rows] = value.T
            return carry

        lax.fori_loop(0, features // tile, step, 0)

    first, rest = range(3), range(3, 6)
    for w in range(6):
        work.pack(w)
    for w in first:
        work.hop(w, 0)
    bias_in[...] = vectors[4:5, : features // stages]
    for step in range(1, stages):
        work.start(bias_copy, step)
    bias_all[0] = bias_in[...]
    for hop in range(back):

        @pl.when(z <= hop)
        def _():
            window[hop] = jnp.zeros((rows, features), BF16)

    norm(tokens, own)
    fill_bias(segments, z, bias, block, own)
    for j in range(1, stages - 1):
        for w in first:
            work.hop(w, j)
    for w in rest:
        work.hop(w, 0)
    for w in first:
        work.collect(w)
        work.begin_round(w, 0)
    for j in range(1, stages - 1):
        if j <= 3 and dp_bits > 1:
            work.advance(j - 1, 0)
        for w in rest:
            work.hop(w, j)

    @pl.when(z < stages - 1)
    def _():
        token_copy(0).start()

    if dp_bits > 1:
        for w in range(max(0, min(stages - 2, 3)), 3):
            work.advance(w, 0)
    for w in rest:
        work.collect(w)
    for r in range(1, dp_bits - 1):
        for w in first:
            work.advance(w, r)
    for w in rest:
        work.begin_round(w, 0)
    for w in first:
        work.advance(w, dp_bits - 1)
        keep(5 + w).start()
        if w == 0:

            def query(c, carry):
                lanes = pl.ds(pl.multiple_of(c * tile, tile), tile)
                value = dot(normed[own:, :], home[0, :, lanes], 1, 0)
                raw[:, lanes] = value
                q[:, lanes] = (value * factor[:, lanes]).astype(BF16)
                return carry

            lax.fori_loop(0, features // tile, query, 0)
            keep(0).start()
            keep(1).start()
        else:
            project(w, own, *((k, None) if w == 1 else (v, vt)))

    sp = spans(rows, width, block)

    def attend(low, high, fresh, last, due):
        tiles = []
        for kb in range(low // block, high // block):
            qs = [i for i, (lo, hi) in enumerate(sp) if lo <= kb * block < hi]
            if qs:
                tiles.append((kb, qs))

        def head(h, carry):
            for at in sorted(set(due.values())):

                @pl.when(h == at)
                def _():
                    for w, r in due:
                        if due[w, r] == at:
                            work.advance(w, r)

            lanes, mine = head_lanes(h, features)
            feats = pl.ds(pl.multiple_of(h * HD, 16), HD)
            query = jnp.where(mine, q[:, lanes], jnp.zeros((), BF16))
            top = [jnp.full((8, block), FAR, F32) for _ in sp]
            for kb, qs in tiles:
                qa, qz = qs[0] * block, (qs[-1] + 1) * block
                at = slice(kb * block, (kb + 1) * block)
                s = dot(k[at, lanes], query[qa:qz], 1, 1) + bias[at, qa:qz]
                scores[at, qa:qz] = s
                for i in qs:
                    cut = s[:, i * block - qa : (i + 1) * block - qa]
                    top[i] = jnp.maximum(top[i], jnp.max(cut.reshape(block // 8, 8, block), axis=0))
            top = jnp.concatenate([jnp.max(t, axis=0, keepdims=True) for t in top], axis=1)
            if not fresh:
                before = tops[pl.ds(h, 1), :]
                top = jnp.maximum(top, before)
                scale = jnp.exp(before - top)
            acc = [jnp.zeros((HD, block), F32) for _ in sp]
            total = [jnp.zeros((8, block), F32) for _ in sp]
            for kb, qs in tiles:
                qa, qz = qs[0] * block, (qs[-1] + 1) * block
                at = slice(kb * block, (kb + 1) * block)
                p = jnp.exp(scores[at, qa:qz] - top[:, qa:qz])
                part = dot(vt[feats, at], p.astype(BF16), 1, 0)
                for i in qs:
                    cut = slice(i * block - qa, (i + 1) * block - qa)
                    total[i] = total[i] + jnp.sum(p[:, cut].reshape(block // 8, 8, block), axis=0)
                    acc[i] = acc[i] + part[:, cut]
            for i in range(len(sp)):
                at = slice(i * block, (i + 1) * block)
                one = jnp.sum(total[i], axis=0, keepdims=True)
                out = acc[i]
                if not fresh:
                    one = one + totals[pl.ds(h, 1), at] * scale[:, at]
                    out = out + ot[feats, at] * scale[:, at]
                if last:
                    ot[feats, at] = out / one
                    lse_ref[pl.ds(h, 1), at] = top[:, at] + jnp.log(one)
                else:
                    ot[feats, at] = out
                    totals[pl.ds(h, 1), at] = one
                    tops[pl.ds(h, 1), at] = top[:, at]
            return carry

        lax.fori_loop(0, heads, head, 0)

    inside, ready = {}, []
    if back and dp_bits > 2:
        inside = {(3, 1): heads * 3 // 8, (4, 1): heads * 5 // 8, (5, 1): heads * 7 // 8}
        ready = [(3, 0), (4, 0), (5, 0)]
    for pair in ready[:1]:
        work.advance(*pair)
    for hop in range(back):
        if hop + 1 == back:
            for pair in ready[1:]:
                work.advance(*pair)
            attend(rows, width, True, False, inside)

        @pl.when(z > hop)
        def _():
            token_copy(hop).wait_recv()

        if hop + 1 < back:

            @pl.when((z > hop) & (z < stages - 1))
            def _():
                token_copy(hop + 1).start()

        at = own - (hop + 1) * rows
        norm(window.at[hop], at)
        project(1, at, k, None)
        project(2, at, v, vt)
    for i in range(2, 5):
        keep(i).start()
    attend(0, rows if back else width, not back, True, {})
    transpose_out(ot, o_ref)
    for r in range(dp_bits):
        for w in rest:
            if (w, r) not in inside and (w, r) not in ready:
                work.advance(w, r)
    for step in range(1, stages):
        bias_copy(step).wait_recv()
    bias_full[...] = jnp.concatenate(
        [bias_all[lax.rem(z - s + stages, stages)] for s in range(stages)], axis=1
    )
    for hop in range(back):

        @pl.when((z >= hop) & (z < stages - 1))
        def _():
            token_copy(hop).wait_send()

    for i in range(len(kept)):
        keep(i).wait()
    work.close()


def attend_forward(weights, tokens, vectors, segments, block, dp, stages, back):
    held, cols = weights[0].shape
    rows, features = tokens.shape
    width, heads = (back + 1) * rows, features // HD
    hbm = pl.BlockSpec(memory_space=pl.ANY)
    vmem = pl.BlockSpec(memory_space=pltpu.VMEM)
    dma = pltpu.SemaphoreType.DMA
    sds = jax.ShapeDtypeStruct
    return pl.pallas_call(
        functools.partial(forward_kernel, block, dp.bit_length() - 1, stages, back),
        in_specs=[vmem] * 9,
        out_specs=[hbm] * 6 + [vmem] + [hbm] * 5 + [vmem] * 2,
        out_shape=[sds((features, features), BF16)] * 6
        + [
            sds((1, features), F32),
            sds((rows, features), F32),
            sds((rows, features), BF16),
            sds((width, features), BF16),
            sds((width, features), BF16),
            sds((features, width), BF16),
            sds((rows, features), BF16),
            sds((heads, rows), F32),
        ],
        scratch_shapes=[
            pltpu.VMEM((3, features, features), BF16),
            pltpu.VMEM((back, rows, features), BF16),
            pltpu.VMEM((width, features), BF16),
            pltpu.VMEM((features, width), BF16),
            pltpu.VMEM((rows, features), F32),
            pltpu.VMEM((rows, features), BF16),
            pltpu.VMEM((width, features), BF16),
            pltpu.VMEM((width, features), BF16),
            pltpu.VMEM((features, width), BF16),
            pltpu.VMEM((features, rows), F32),
            pltpu.VMEM((width, rows), F32),
            pltpu.VMEM((width, rows), F32),
            pltpu.VMEM((heads, rows), F32),
            pltpu.VMEM((heads, rows), F32),
            pltpu.VMEM((1, features // stages), F32),
            pltpu.VMEM((stages, 1, features // stages), F32),
            dma((back,)), dma((back,)), dma((stages,)), dma((stages,)), dma((8,)),
        ]
        + gathering_scratch(6, dp, stages, held, cols),
        compiler_params=pltpu.CompilerParams(
            collective_id=0, has_side_effects=True, vmem_limit_bytes=62 << 20
        ),
        name="attend_forward",
    )(*weights, tokens, vectors, segments)


def middle_kernel(block, dp_bits, stages, *refs):
    sources, refs = refs[:12], refs[12:]
    b_up, vectors, lse_ref, segments = refs[:4]
    factor, gain, b_down = (vectors.at[i : i + 1] for i in (1, 2, 3))
    results, incoming, outs, sums, refs = refs[4:10], refs[10], refs[11:14], refs[14], refs[15:]
    weights, hidden, wide, tmp, tr, keys, values, query_in, grad_in, bias, delta_ref = refs[:11]
    ps, pr, sems, refs = refs[11], refs[12], refs[13], refs[14:]
    d, z = greet(dp_bits, stages)
    work = Reduction(dp_bits, stages, d, z, None, outs, refs)
    rows, features = query_in.shape
    heads, width = features // HD, keys.shape[0]
    back = width // rows - 1
    tile = 2 * LANES
    w_out, w_up, w_down = weights.at[0], weights.at[1], weights.at[2]
    w_key, w_value = weights.at[2], weights.at[1]
    mixed, cot, x, second, active, d_pre, d_attn, spare = (tmp.at[i] for i in range(8))
    dk, dv = tmp.at[: back + 1], tmp.at[back + 1 : 2 * back + 2]
    dq, part = tmp.at[2 * back + 2], tmp.at[2 * back + 3]
    inside = (
        mixed, w_out, x, cot, w_up, w_down, keys, values, query_in, w_key, w_value, hidden,
    )
    half = rows // 2
    outside = (spare, hidden, dq, dk, dv, part.at[half:])
    loads = Loads(list(zip(sources, inside)) + list(zip(outside, results)), sems)
    loads.start(*range(9))
    fill_bias(segments, z, bias, block, width - rows)

    def by_tile(body):
        for c in range(features // tile):
            body(slice(c * tile, (c + 1) * tile), c)

    def by_rows(body, start):
        def step(i, carry):
            return body(pl.ds(pl.multiple_of(i * 64, 64), 64), carry)

        return lax.fori_loop(0, rows // 64, step, start)

    def flip(src):
        for c in range(features // tile):
            lanes = slice(c * tile, (c + 1) * tile)
            tr[lanes, :] = src[:, lanes].T

    nothing = jnp.zeros((1, features), F32)

    def add_attention(lanes, c):
        hidden[:, lanes] = x[:, lanes].astype(F32) + dot(mixed[...], w_out[lanes, :], 1, 1)

    def norm(at, carry):
        h = hidden[at, :]
        second[at, :] = (h * row_inverse(h) * gain[...]).astype(BF16)
        return carry

    def activate(lanes, c):
        pre = dot(second[...], w_up[:, lanes], 1, 0) + b_up[:, lanes]
        sigma = 1.0 / (1.0 + jnp.exp(-pre))
        active[:, lanes] = (pre * sigma).astype(BF16)
        grad = dot(cot[...], w_down[:, lanes], 1, 0)
        grad = (grad * sigma * (1.0 + pre * (1.0 - sigma))).astype(BF16)
        d_pre[:, lanes] = grad
        sums[2:3, lanes] = jnp.sum(grad.astype(F32), axis=0, keepdims=True)

    def finish_layer(lanes, c):
        out = dot(active[...], w_down[lanes, :], 1, 1)
        spare[:, lanes] = (hidden[:, lanes] + out + b_down[:, lanes]).astype(BF16)
        sums[1:2, lanes] = jnp.sum(cot[:, lanes].astype(F32), axis=0, keepdims=True)

    def to_second(lanes, c):
        wide[:, lanes] = dot(d_pre[...], w_up[lanes, :], 1, 1)

    def to_hidden(at, column):
        h, grad = hidden[at, :], wide[at, :]
        inverse = row_inverse(h)
        weighted = grad * gain[...]
        dots = jnp.sum(weighted * h, axis=1, keepdims=True)
        cube = inverse * inverse * inverse
        d_hidden = cot[at, :].astype(F32) + inverse * weighted - h * cube / features * dots
        hidden[at, :] = d_hidden
        d_attn[at, :] = d_hidden.astype(BF16)
        return column + jnp.sum(grad * h * inverse, axis=0, keepdims=True)

    def to_mixed(lanes, c):
        grad = dot(d_attn[...], w_out[:, lanes], 1, 0).astype(BF16)
        grad_in[:, lanes] = grad
        both = grad.astype(F32) * mixed[:, lanes].astype(F32)
        lane = lax.broadcasted_iota(jnp.int32, (heads, tile), 1) + c * tile
        first = lax.broadcasted_iota(jnp.int32, (heads, tile), 0) * HD
        owner = jnp.where((lane >= first) & (lane < first + HD), 1.0, 0.0).astype(BF16)
        high = both.astype(BF16)
        rest = (both - high.astype(F32)).astype(BF16)
        delta_ref[...] += dot(owner, high, 1, 1) + dot(owner, rest, 1, 1)

    sums[3:8, :] = jnp.zeros((5, features), F32)
    delta_ref[...] = jnp.zeros_like(delta_ref)
    loads.wait(0, 1, 2)
    by_tile(add_attention)
    by_rows(norm, 0)
    loads.wait(3, 4, 5)
    by_tile(activate)
    flip(cot)
    work.weight_grad(0, lambda at: tr[at, :], lambda: active[...])
    by_tile(finish_layer)
    loads.start(12, 9)
    by_tile(to_second)
    loads.start(10)
    flip(second)
    work.weight_grad(1, lambda at: tr[at, :], lambda: d_pre[...])
    work.advance(0, 0)
    sums[0:1, :] = by_rows(to_hidden, nothing)
    loads.start(13)
    by_tile(to_mixed)
    flip(d_attn)
    work.weight_grad(2, lambda at: tr[at, :], lambda: mixed[...])
    work.advance(1, 0)
    if dp_bits > 1:
        work.advance(0, 1)
    loads.wait(12)
    for c in range(2 * back + 2):
        tmp[c] = jnp.zeros((rows, features), BF16)
    wide[...] = jnp.zeros_like(wide)
    loads.wait(6, 7, 8)
    sp = spans(rows, width, block)
    steps = heads * (back + 1)
    events = [(2, 0)] + [(w, k) for w in range(3) for k in range(1, dp_bits) if (w, k) != (0, 1)]
    due = {i: int(at * steps) // 2 * 2 for i, at in enumerate(EVENTS[: len(events)])}

    def down():
        return pltpu.make_async_remote_copy(
            src_ref=part.at[:half], dst_ref=incoming, send_sem=ps, recv_sem=pr,
            device_id={"mp": jnp.maximum(z - 1, 0)}, device_id_type=MESH,
        )

    for c in range(back + 1):

        def head(h):
            lanes, mine = head_lanes(h, features)
            zero = jnp.zeros((), BF16)
            query = jnp.where(mine, query_in[:, lanes], zero)
            grad = jnp.where(mine, grad_in[:, lanes], zero)
            lse = lse_ref[pl.ds(h, 1), :]
            delta = delta_ref[pl.ds(h, 1), :]
            for kb in range(c * rows // block, (c + 1) * rows // block):
                qs = [i for i, (lo, hi) in enumerate(sp) if lo <= kb * block < hi]
                if not qs:
                    continue
                qa, qz = qs[0] * block, (qs[-1] + 1) * block
                at = slice(kb * block, (kb + 1) * block)
                to = slice(kb * block - c * rows, (kb + 1) * block - c * rows)
                key = keys[at, lanes]
                s = dot(key, query[qa:qz], 1, 1) + bias[at, qa:qz]
                p = jnp.exp(s - lse[:, qa:qz])
                dp = dot(values[at, lanes], grad[qa:qz], 1, 1)
                ds = (p * (dp - delta[:, qa:qz])).astype(BF16)
                dv[c, to, lanes] += dot(p.astype(BF16), grad[qa:qz], 1, 0).astype(BF16)
                dk[c, to, lanes] += dot(ds, query[qa:qz], 1, 0).astype(BF16)
                wide[qa:qz, lanes] += dot(ds, jnp.where(mine, key, zero), 0, 0)

        def pair(i, carry):
            for at in sorted(set(due.values())):
                if at // heads != c:
                    continue

                @pl.when(2 * i == at % heads)
                def _():
                    for e in due:
                        if due[e] == at:
                            work.advance(*events[e])

            head(2 * i)
            head(2 * i + 1)
            return carry

        lax.fori_loop(0, heads // 2, pair, 0)
        if c == 0:
            loads.wait(9, 10)
            if back:
                back_project(part, ((dk.at[0], w_key), (dv.at[0], w_value)), 0, None)
                loads.start(17)

                @pl.when(z >= back)
                def _():
                    down().start()

            loads.wait(13)
            loads.start(11)

    loads.start(15, 16)
    loads.wait(11)

    def to_query(at, column):
        scaled = wide[at, :].astype(BF16).astype(F32)
        dq[at, :] = (scaled * factor[...]).astype(BF16)
        return column + jnp.sum(scaled * hidden[at, :], axis=0, keepdims=True)

    sums[4:5, :] = by_rows(to_query, nothing)
    loads.start(14)
    for i in range(len(due), len(events)):
        work.advance(*events[i])
    for w in range(3):
        work.finish(w)
    loads.wait(14, 15, 16)
    if back:
        loads.wait(17)

        @pl.when((z + 1 >= back) & (z < stages - 1))
        def _():
            down().wait_recv()

        @pl.when(z >= back)
        def _():
            down().wait_send()

    work.close()


def back_project(out, pairs, at, more):
    rows, features = out.shape
    tile = 2 * LANES

    def step(c, carry):
        lanes = pl.ds(pl.multiple_of(c * tile, tile), tile)
        value = None
        for grad, weight in pairs:
            start = at if grad.shape[0] > rows else 0
            term = dot(grad[start : start + rows, :], weight[lanes, :], 1, 1)
            value = term if value is None else value + term
        if more is not None:
            value = value + more(lanes)
        out[:, lanes] = value.astype(out.dtype)
        return carry

    lax.fori_loop(0, features // tile, step, 0)


def middle(
    mixed, w_out, x, cot, w_up, w_down, k, v, q, w_key, w_value, raw, b_up, vectors,
    lse, segments, block, dp, stages,
):
    rows, features = q.shape
    width, heads = k.shape[0], features // HD
    held, cols = features // dp, features // stages
    chunks = width // rows
    hbm = pl.BlockSpec(memory_space=pl.ANY)
    vmem = pl.BlockSpec(memory_space=pltpu.VMEM)
    dma = pltpu.SemaphoreType.DMA
    sds = jax.ShapeDtypeStruct
    low, high = sds((rows, features), BF16), sds((rows, features), F32)
    many, part = sds((chunks, rows, features), BF16), sds((rows // 2, features), BF16)
    return pl.pallas_call(
        functools.partial(middle_kernel, block, dp.bit_length() - 1, stages),
        in_specs=[hbm] * 12 + [vmem] * 4,
        out_specs=[hbm] * 7 + [vmem] * 4,
        out_shape=[low, high, low, many, many, part, part]
        + [sds((held, cols), F32)] * 3
        + [sds((8, features), F32)],
        scratch_shapes=[
            pltpu.VMEM((3, features, features), BF16),
            pltpu.VMEM((rows, features), F32),
            pltpu.VMEM((rows, features), F32),
            pltpu.VMEM((max(8, 2 * chunks + 2), rows, features), BF16),
            pltpu.VMEM((features, rows), BF16),
            pltpu.VMEM((width, features), BF16),
            pltpu.VMEM((width, features), BF16),
            pltpu.VMEM((rows, features), BF16),
            pltpu.VMEM((rows, features), BF16),
            pltpu.VMEM((width, rows), F32),
            pltpu.VMEM((heads, rows), F32),
            dma, dma, dma((18,)),
        ]
        + reduction_scratch(3, dp, stages, held, features, True),
        compiler_params=pltpu.CompilerParams(
            collective_id=2, has_side_effects=True, vmem_limit_bytes=63 << 20
        ),
        name="middle",
    )(
        mixed, w_out, x, cot, w_up, w_down, k, v, q, w_key, w_value, raw, b_up, vectors,
        lse, segments,
    )


def input_kernel(dp_bits, stages, back, *refs):
    sources, farther, vectors, sums, refs = refs[:10], refs[10], refs[11], refs[12], refs[13:]
    gain = vectors.at[0:1]
    outs, result, total, refs = refs[:3], refs[3], refs[4], refs[5:]
    inside, tokens_grad, refs = refs[:10], refs[10], refs[11:]
    dv, nt, dk, wk, wv, incoming, dq, wq, tokens, d_hidden = inside
    part, landed, d_first, sgot, ss, sr, ps, pr, sems = refs[:9]
    d, z = greet(dp_bits, stages)
    work = Reduction(dp_bits, stages, d, z, None, outs, refs[9:])
    rows, features = tokens.shape
    own, half = back * rows, rows // 2
    inside = inside[:5] + (incoming.at[:half],) + inside[6:]
    loads = Loads(list(zip(sources, inside)) + [(tokens_grad, result)], sems)
    levels = dp_bits + stages.bit_length() - 1
    held = features >> dp_bits
    grads = ((dv, 2, 0), (dk, 1, 0), (dq, 0, own))

    def down(hop):
        return pltpu.make_async_remote_copy(
            src_ref=part.at[hop - 1] if hop else farther,
            dst_ref=landed.at[hop - 1] if hop else incoming.at[half:],
            send_sem=ps.at[hop], recv_sem=pr.at[hop],
            device_id={"mp": jnp.maximum(z - 1, 0)}, device_id_type=MESH,
        )

    if back:

        @pl.when(z >= back)
        def _():
            down(0).start()

    loads.start(*range(10))

    def arrived(hop):
        source = incoming if hop == 1 else landed.at[hop - 2]
        there = (z + 1 >= back - hop + 1) & (z < stages - 1)

        def take(lanes):
            return jnp.where(there, source[:, lanes].astype(F32), 0.0)

        return there, take

    def weight_grad(i):
        grad, w, at = grads[i]
        work.weight_grad(w, lambda rows_at: nt[rows_at, at:], lambda: grad[...])

    def sum_copy(k):
        if k < dp_bits:
            to = {"dp": flipped(d, (k,))}
        else:
            to = {"mp": flipped(z, (k - dp_bits,))}
        return pltpu.make_async_remote_copy(
            src_ref=total.at[k], dst_ref=sgot.at[k], send_sem=ss.at[k], recv_sem=sr.at[k],
            device_id=to, device_id_type=MESH,
        )

    def sum_step(k):
        sum_copy(k).wait_recv()
        total[k + 1] = total[k] + sgot[k]
        if k + 1 < levels:
            work.start(sum_copy, k + 1)

    def pass_down(hop):
        there, take = arrived(hop)

        @pl.when(there)
        def _():
            down(hop - 1).wait_recv()

        back_project(part.at[hop - 1], ((dk, wk), (dv, wv)), hop * rows, take)

        @pl.when(z >= back - hop)
        def _():
            down(hop).start()

    loads.wait(0, 1)
    weight_grad(0)
    loads.wait(2)
    weight_grad(1)
    work.advance(2, 0)
    loads.wait(3, 4, 5)
    if back > 1:
        pass_down(1)
    work.advance(1, 0)
    loads.wait(6, 7)
    weight_grad(2)
    for hop in range(2, back):
        pass_down(hop)
    work.advance(0, 0)
    back_project(d_first, ((dk, wk), (dv, wv), (dq, wq)), own, None)
    events = [(w, k) for w in (2, 1, 0) for k in range(1, dp_bits)]
    for event in events[:1]:
        work.advance(*event)
    loads.wait(8, 9)
    there, take = arrived(back) if back else (None, None)
    if back:

        @pl.when(there)
        def _():
            down(back - 1).wait_recv()

    chunk = 64

    def finish(i, column):
        at = pl.ds(pl.multiple_of(i * chunk, chunk), chunk)
        x = tokens[at, :].astype(F32)
        grad = d_first[at, :]
        if back:
            source = incoming if back == 1 else landed.at[back - 2]
            grad = grad + jnp.where(there, source[at, :].astype(F32), 0.0)
        inverse = row_inverse(x)
        weighted = grad * gain[...]
        dots = jnp.sum(weighted * x, axis=1, keepdims=True)
        cube = inverse * inverse * inverse
        tokens_grad[at, :] = (
            d_hidden[at, :] + inverse * weighted - x * cube / features * dots
        ).astype(BF16)
        return column + jnp.sum(grad * x * inverse, axis=0, keepdims=True)

    column = lax.fori_loop(0, rows // chunk, finish, jnp.zeros((1, features), F32))
    total[0] = sums[...]
    total[0, 3:4, :] = column
    work.start(sum_copy, 0)
    loads.start(10)
    done = 0
    for event in events[1:]:
        work.advance(*event)
        if done < levels:
            sum_step(done)
            done += 1
    for k in range(done, levels):
        sum_step(k)
    for w in (2, 1, 0):
        work.finish(w)
    for hop in range(back):

        @pl.when(z >= back - hop)
        def _():
            down(hop).wait_send()

    loads.wait(10)
    work.close()


def input_gradients(
    nt, dq, dk, dv, wq, wk, wv, incoming, farther, tokens, d_hidden, vectors, sums, dp, stages
):
    rows, features = tokens.shape
    back = dk.shape[0] // rows - 1
    held, cols = features // dp, features // stages
    dp_bits = dp.bit_length() - 1
    levels = dp_bits + stages.bit_length() - 1
    hbm = pl.BlockSpec(memory_space=pl.ANY)
    vmem = pl.BlockSpec(memory_space=pltpu.VMEM)
    dma = pltpu.SemaphoreType.DMA
    hops = max(1, back - 1)
    sources = (dv, nt, dk, wk, wv, incoming, dq, wq, tokens, d_hidden)
    out = pl.pallas_call(
        functools.partial(input_kernel, dp_bits, stages, back),
        in_specs=[hbm] * 11 + [vmem] * 2,
        out_specs=[vmem] * 3 + [hbm, vmem],
        out_shape=[jax.ShapeDtypeStruct((held, cols), F32)] * 3
        + [
            jax.ShapeDtypeStruct((rows, features), BF16),
            jax.ShapeDtypeStruct((levels + 1,) + sums.shape, F32),
        ],
        scratch_shapes=[pltpu.VMEM(tokens.shape if a is incoming else a.shape, a.dtype) for a in sources + (tokens,)]
        + [
            pltpu.VMEM((hops, rows, features), BF16), pltpu.VMEM((hops, rows, features), BF16),
            pltpu.VMEM((rows, features), F32), pltpu.VMEM((levels,) + sums.shape, F32),
            dma((levels,)), dma((levels,)), dma((hops + 1,)), dma((hops + 1,)), dma((11,)),
        ]
        + reduction_scratch(3, dp, stages, held, features, True),
        compiler_params=pltpu.CompilerParams(
            collective_id=1, has_side_effects=True, vmem_limit_bytes=62 << 20
        ),
        name="input_gradients",
    )(*sources, farther, vectors, sums)
    return out[:3], out[3], out[4][levels]


def hand_over_kernel(count, *refs):
    half = len(refs) // 2
    for i, (source, result) in enumerate(zip(refs[:half], refs[half:])):
        result[...] = source[...] if i < count else source[...].T


def hand_over(plain, turned):
    vmem = pl.BlockSpec(memory_space=pltpu.VMEM)
    sds = jax.ShapeDtypeStruct
    return pl.pallas_call(
        functools.partial(hand_over_kernel, len(plain)),
        in_specs=[vmem] * (len(plain) + len(turned)),
        out_specs=[vmem] * (len(plain) + len(turned)),
        out_shape=[sds(a.shape, a.dtype) for a in plain]
        + [sds(a.shape[::-1], a.dtype) for a in turned],
        name="hand_over",
    )(*plain, *turned)


def body(
    tokens, segments, w_query, w_key, w_value, w_output, w_up, b_up, w_down, b_down,
    gain_attn, gain_mlp, query_scale, cotangent,
):
    stages = lax.axis_size("mp")
    z = lax.axis_index("mp")
    rows, features = tokens.shape
    back = min(stages - 1, -(-(DOC_MAX - 1) // rows))
    own = back * rows
    block = min(256, rows)
    heads = features // HD
    dp = lax.axis_size("dp")
    factor = jax.nn.softplus(query_scale) * (LOG2E / math.sqrt(HD))
    mine = b_up.shape[0]
    vectors = jnp.zeros((8, features), F32)
    row = lax.broadcasted_iota(jnp.int32, (8, features), 0)
    given = (gain_attn, jnp.tile(factor, heads), gain_mlp, b_down, jnp.pad(b_up, (0, features - mine)))
    for i, value in enumerate(given):
        vectors = jnp.where(row == i, value[None], vectors)
    (
        wq, wk, wv, wu, wo, wd, b_full, query_raw, scaled, keys, values, first_t, mixed, lse
    ) = attend_forward(
        (w_query, w_key, w_value, w_up, w_output.T, w_down.T), tokens, vectors, segments,
        block, dp, stages, back,
    )
    layer_out, d_hidden, d_query, d_keys, d_values, farther, incoming, *mlp, sums = middle(
        mixed, wo, tokens, cotangent, wu, wd, keys, values, scaled, wk, wv, query_raw,
        b_full, vectors, lse, segments, block, dp, stages,
    )
    grads, tokens_grad, sums = input_gradients(
        first_t, d_query, d_keys.reshape(own + rows, features),
        d_values.reshape(own + rows, features), wq, wk, wv, incoming, farther, tokens,
        d_hidden, vectors, sums, dp, stages,
    )
    sum_b_up = lax.dynamic_slice_in_dim(sums[2], z * mine, mine, 0)
    scale_total = jnp.sum(sums[4].reshape(heads, HD), axis=0)
    grad_query_scale = scale_total * (LOG2E / math.sqrt(HD)) * jax.nn.sigmoid(query_scale)
    layer_out, tokens_grad, g_query, g_key, g_value, g_up, g_output, g_down = hand_over(
        (layer_out, tokens_grad, *grads, mlp[1]), (mlp[2], mlp[0])
    )
    return (
        layer_out, tokens_grad, g_query, g_key, g_value, g_output, g_up, sum_b_up,
        g_down, sums[1], sums[3], sums[0], grad_query_scale,
    )


def solution(mesh):
    tokens, rows_dp, rows_mp = P(("dp", "mp"), None), P("dp", "mp"), P("mp", "dp")
    return jax.shard_map(
        body,
        mesh=mesh,
        in_specs=(
            tokens, P("dp", None), rows_dp, rows_dp, rows_dp, rows_mp, rows_dp, P("mp"), rows_mp,
            P(), P(), P(), P(), tokens,
        ),
        out_specs=(
            tokens, tokens, rows_dp, rows_dp, rows_dp, rows_mp, rows_dp, P("mp"), rows_mp,
            P(), P(), P(), P(),
        ),
        check_vma=False,
    )
```

```python
import functools
import math

import jax
import jax.numpy as jnp
from jax import lax
from jax.experimental import pallas as pl
from jax.experimental.pallas import tpu as pltpu
from jax.sharding import PartitionSpec as P

HD = 80
LANES = 128
EPSILON = 1e-06
LOG2E = 1.442695
DOC_MAX = 1024
FAR = -1e30
EVENTS = (0.15, 0.3, 0.5, 0.6, 0.75, 0.9)
F32 = jnp.float32
BF16 = jnp.bfloat16


def dot(a, b, ca, cb):
    return lax.dot_general(a, b, (((ca,), (cb,)), ((), ())), preferred_element_type=F32)


def row_inverse(values):
    return lax.rsqrt(jnp.mean(values * values, axis=1, keepdims=True) + EPSILON)


MESH = pl.DeviceIdType.MESH


def bit_of(index, b):
    return lax.rem(lax.div(index, 1 << b), 2)


def flipped(index, bits):
    for b in bits:
        index = index + (1 << b) * (1 - 2 * bit_of(index, b))
    return index


def split_order(count, turn):
    bits = list(range(count))
    rest = bits[1:][::-1]
    turn = turn % max(1, len(rest))
    return bits[:1] + rest[turn:] + rest[:turn]


def subsets(bits):
    out = [()]
    for b in bits:
        out = out + [s + (b,) for s in out]
    return out


def greet(dp_bits, stages, extra=()):
    d, z = lax.axis_index("dp"), lax.axis_index("mp")
    barrier = pltpu.get_barrier_semaphore()
    for b in range(dp_bits):
        pl.semaphore_signal(barrier, device_id={"dp": flipped(d, (b,))}, device_id_type=MESH)
    for step in range(1, stages):
        pl.semaphore_signal(
            barrier, device_id={"mp": lax.rem(z + step, stages)}, device_id_type=MESH
        )
    pl.semaphore_wait(barrier, dp_bits + stages - 1)
    return d, z


class Loads:
    def __init__(self, pairs, sems):
        self.pairs, self.sems = pairs, sems

    def copy(self, i):
        return pltpu.make_async_copy(self.pairs[i][0], self.pairs[i][1], self.sems.at[i])

    def start(self, *which):
        for i in which:
            self.copy(i).start()

    def wait(self, *which):
        for i in which:
            self.copy(i).wait()


class Reduction:
    def __init__(self, dp_bits, stages, d, z, grads, outs, refs):
        self.dp_bits, self.stages, self.d, self.z = dp_bits, stages, d, z
        self.grads, self.outs = grads, outs
        self.pool = refs[0]
        self.kept, self.got = refs[0].at[0], refs[1 : 1 + dp_bits]
        self.zsend, self.zgot, self.ks, self.rs, self.rr, self.zs, self.zr = refs[1 + dp_bits :]
        self.half = 1 << (dp_bits - 1)
        self.parts = self.kept.shape[0] // len(outs)
        self.rows, self.features = self.kept.shape[2], self.kept.shape[3]
        self.sent = []

    def start(self, make, *args):
        make(*args).start()
        self.sent.append((make, args))

    def order(self, u):
        return split_order(self.dp_bits, u % self.parts)

    def place(self, u, slot, low):
        rest = self.order(u)[1:]
        at = low
        for i, b in enumerate(rest):
            if slot >> (len(rest) - 1 - i) & 1:
                at = at + (1 << b)
        return at

    def slot_of(self, u, index):
        rest = self.order(u)[1:]
        return sum(bit_of(index, b - 1) << (len(rest) - 1 - i) for i, b in enumerate(rest))

    def source(self, u, slot, low):
        cut = pl.ds(u % self.parts * self.rows, self.rows)
        return self.grads[u // self.parts].at[self.place(u, slot, low), cut]

    def first_copy(self, u, slot):
        return pltpu.make_async_remote_copy(
            src_ref=self.pool.at[1, u, slot]
            if self.grads is None
            else self.source(u, slot, 1 - bit_of(self.d, 0)),
            dst_ref=self.got[0].at[u, slot],
            send_sem=self.rs.at[u, slot], recv_sem=self.rr.at[u, slot],
            device_id={"dp": flipped(self.d, (0,))}, device_id_type=MESH,
        )

    def keep_copy(self, u, slot):
        return pltpu.make_async_copy(
            self.source(u, slot, bit_of(self.d, 0)), self.kept.at[u, slot], self.ks.at[u, slot]
        )

    def round_copy(self, u, k):
        count = self.half >> k
        b = self.order(u)[k]
        other = 1 - bit_of(self.d, b)
        return pltpu.make_async_remote_copy(
            src_ref=self.got[k - 1].at[u, pl.ds(other * count, count)],
            dst_ref=self.got[k].at[u],
            send_sem=self.rs.at[u, self.half + k], recv_sem=self.rr.at[u, self.half + k],
            device_id={"dp": flipped(self.d, (b,))}, device_id_type=MESH,
        )

    def last_copy(self, w, step):
        to = lax.rem(self.z + step, self.stages)
        return pltpu.make_async_remote_copy(
            src_ref=self.zsend.at[w, to], dst_ref=self.zgot.at[w, step],
            send_sem=self.zs.at[w, step], recv_sem=self.zr.at[w, step],
            device_id={"mp": to}, device_id_type=MESH,
        )

    def units(self, w):
        return range(w * self.parts, (w + 1) * self.parts)

    def begin(self, w):
        for u in self.units(w):
            for slot in range(self.half):
                self.start(self.first_copy, u, slot)
                if self.grads is not None:
                    self.keep_copy(u, slot).start()

    def add(self, dst, src, count):
        def step(i, carry):
            dst[i] = dst[i] + src(i)
            return carry

        lax.fori_loop(0, count, step, 0)

    def take(self, w, k):
        for u in self.units(w):
            count = self.half >> k
            if k == 0:
                for slot in range(self.half):
                    if self.grads is not None:
                        self.keep_copy(u, slot).wait()
                    self.first_copy(u, slot).wait_recv()
                self.add(self.got[0].at[u], lambda i: self.kept[u, i], count)
            else:
                self.round_copy(u, k).wait_recv()
                mine = bit_of(self.d, self.order(u)[k]) * count
                self.add(self.got[k].at[u], lambda i: self.got[k - 1][u, mine + i], count)

    def send(self, w, k):
        for u in self.units(w):
            self.start(self.round_copy, u, k)

    def advance(self, w, k):
        self.take(w, k)
        if k + 1 == self.dp_bits:
            self.begin_last(w)
        else:
            self.send(w, k + 1)

    def put(self, w, index, value):
        held = self.parts * self.rows
        for low in range(2):
            which = lax.rem(bit_of(self.d, 0) + low, 2)
            for u in self.units(w):
                cut = low * held + u % self.parts * self.rows
                self.pool[which, u, self.slot_of(u, index)] = value[cut : cut + self.rows]

    def weight_grad(self, w, left, right):
        held = self.parts * self.rows

        def step(t, carry):
            at = pl.ds(pl.multiple_of(t * 2 * held, 2 * held), 2 * held)
            self.put(w, t, dot(left(at), right(), 1, 0).astype(BF16))
            return carry

        lax.fori_loop(0, 1 << (self.dp_bits - 1), step, 0)
        self.begin(w)

    def begin_last(self, w):
        cols = self.features // self.stages
        whole = [self.got[self.dp_bits - 1][u, 0] for u in self.units(w)]
        for s in range(self.stages):
            self.zsend[w, s] = jnp.concatenate(
                [piece[:, s * cols : (s + 1) * cols] for piece in whole], axis=1
            )
        for step in range(1, self.stages):
            self.start(self.last_copy, w, step)

    def finish(self, w):
        value = self.zsend[w, self.z].astype(F32)
        for step in range(1, self.stages):
            self.last_copy(w, step).wait_recv()
            value = value + self.zgot[w, step].astype(F32)
        cols = self.features // self.stages
        for p in range(self.parts):
            at = slice(p * self.rows, (p + 1) * self.rows)
            self.outs[w][at, :] = value[:, p * cols : (p + 1) * cols]

    def close(self):
        for make, args in self.sent:
            make(*args).wait_send()


def reduction_scratch(count, dp, stages, rows, features, local=False):
    dp_bits, half, cols = dp.bit_length() - 1, dp // 2, features // stages
    parts = 2 if rows % 32 == 0 else 1
    dma = pltpu.SemaphoreType.DMA
    units = count * parts
    return (
        [pltpu.VMEM((1 + local, units, half, rows // parts, features), BF16)]
        + [pltpu.VMEM((units, half >> k, rows // parts, features), BF16) for k in range(dp_bits)]
        + [pltpu.VMEM((count, stages, rows // parts, cols * parts), BF16)] * 2
        + [
            dma((units, half)), dma((units, half + dp_bits)), dma((units, half + dp_bits)),
            dma((count, stages)), dma((count, stages)),
        ]
    )


def spans(rows, width, block):
    own = width - rows
    out=[]
    for qb in range(rows//block):
        hi = own + (qb+1)*block
        lo = max(0, (own + qb*block - (DOC_MAX-1))//block*block)
        out.append((lo,hi))
    return out

def head_lanes(h, features):
    first = h*HD
    off = jnp.minimum(lax.div(first, LANES)*LANES, features-2*LANES)
    off = pl.multiple_of(off, LANES)
    lane = lax.broadcasted_iota(jnp.int32,(1,2*LANES),1) + (off-first)
    return pl.ds(off, 2*LANES), (lane>=0)&(lane<HD)

def fill_bias(segments, z, bias, block, own):
    width, rows = bias.shape
    first = z * rows
    for kb in range(width // block):
        start = first + (kb * block - own)
        at = pl.ds(pl.multiple_of(jnp.maximum(start, 0), block), block)
        col = jnp.broadcast_to(segments[:, at], (block, block)).T
        sub = lax.broadcasted_iota(jnp.int32, (block, block), 0) + kb * block
        for qb in range(rows // block):
            row = segments[:, pl.ds(pl.multiple_of(first + qb * block, block), block)]
            last = lax.broadcasted_iota(jnp.int32, (block, block), 1) + (own + qb * block)
            allowed = (col == row) & (sub <= last) & (start >= 0)
            bias[kb * block : (kb + 1) * block, qb * block : (qb + 1) * block] = jnp.where(
                allowed, 0.0, FAR
            )


def transpose_out(src, dst):
    for i in range(src.shape[0]//LANES):
        at = slice(i*LANES,(i+1)*LANES)
        dst[:, at] = src[at,:].T.astype(dst.dtype)

class Gathering:
    def __init__(self, dp_bits, stages, d, z, weights, homes, refs):
        self.dp_bits, self.stages, self.d, self.z = dp_bits, stages, d, z
        self.weights, self.homes = weights, homes
        self.blocks, self.slab, self.zs, self.zr, self.ds, self.dr, self.ls = refs
        self.rows, self.cols = weights[0].shape
        self.parts = self.ds.shape[0] // len(weights)
        self.cut = self.rows // self.parts
        self.sent = []

    def start(self, make, *args):
        make(*args).start()
        self.sent.append((make, args, None))

    def order(self, u):
        return split_order(self.dp_bits, u % self.parts)[::-1]

    def hop_copy(self, w, j, way):
        at = lax.rem(self.z - way * j + self.stages, self.stages)
        to = lax.rem(self.z + way + self.stages, self.stages)
        return pltpu.make_async_remote_copy(
            src_ref=self.blocks.at[w, at], dst_ref=self.blocks.at[w, at],
            send_sem=self.zs.at[w, 2 * j + (way + 1) // 2], recv_sem=self.zr.at[w, at],
            device_id={"mp": to}, device_id_type=MESH,
        )

    def there(self, j, way):
        return self.z >= j if way == 1 else self.z < self.stages - j

    def pack(self, w):
        pieces = [self.weights[w][p * self.cut : (p + 1) * self.cut] for p in range(self.parts)]
        self.blocks[w, self.z] = jnp.concatenate(pieces, axis=1)

    def take(self, w, j):
        for way in (1, -1):

            @pl.when(self.there(j, way))
            def _():
                self.hop_copy(w, j, way).wait_recv()

    def hop(self, w, j):
        if j:
            self.take(w, j)
        for way in (1, -1):
            sends = self.there(j, way) & self.there(1, -way)

            @pl.when(sends)
            def _():
                self.hop_copy(w, j, way).start()

            self.sent.append((self.hop_copy, (w, j, way), sends))

    def place(self, u, which):
        at = which * self.rows + u % self.parts * self.cut
        return self.homes[u // self.parts].at[pl.ds(pl.multiple_of(at, self.cut), self.cut)]

    def piece(self, u):
        at = u % self.parts * self.cut
        return self.slab.at[u // self.parts, pl.ds(at, self.cut)]

    def own_copy(self, u):
        return pltpu.make_async_copy(self.piece(u), self.place(u, self.d), self.ls.at[u])

    def round_copy(self, u, k, slot, held):
        which = flipped(self.d, held)
        return pltpu.make_async_remote_copy(
            src_ref=self.place(u, which) if held else self.piece(u),
            dst_ref=self.place(u, which),
            send_sem=self.ds.at[u, (1 << k) - 1 + slot], recv_sem=self.dr.at[u, which],
            device_id={"dp": flipped(self.d, self.order(u)[k : k + 1])}, device_id_type=MESH,
        )

    def arrival(self, u, k, held):
        which = flipped(self.d, held + tuple(self.order(u)[k : k + 1]))
        return pltpu.make_async_remote_copy(
            src_ref=self.piece(u), dst_ref=self.place(u, which),
            send_sem=self.ds.at[u, 0], recv_sem=self.dr.at[u, which],
            device_id={"dp": flipped(self.d, self.order(u)[k : k + 1])}, device_id_type=MESH,
        )

    def units(self, w):
        return range(w * self.parts, (w + 1) * self.parts)

    def begin_round(self, w, k):
        for u in self.units(w):
            for slot, held in enumerate(subsets(self.order(u)[:k])):
                self.start(self.round_copy, u, k, slot, held)

    def collect(self, w):
        self.take(w, self.stages - 1)
        for p in range(self.parts):
            lanes = slice(p * self.cols, (p + 1) * self.cols)
            self.slab[w, p * self.cut : (p + 1) * self.cut] = jnp.concatenate(
                [self.blocks[w, s, :, lanes] for s in range(self.stages)], axis=1
            )
        for u in self.units(w):
            self.own_copy(u).start()

    def advance(self, w, k):
        for u in self.units(w):
            for held in subsets(self.order(u)[:k]):
                self.arrival(u, k, held).wait_recv()
        if k + 1 < self.dp_bits:
            self.begin_round(w, k + 1)
        else:
            for u in self.units(w):
                self.own_copy(u).wait()

    def close(self):
        for make, args, sends in self.sent:
            if sends is None:
                make(*args).wait_send()
            else:

                @pl.when(sends)
                def _():
                    make(*args).wait_send()


def gathering_scratch(count, dp, stages, rows, cols):
    parts = 2 if rows % 32 == 0 else 1
    dma = pltpu.SemaphoreType.DMA
    units = count * parts
    return [
        pltpu.VMEM((count, stages, rows // parts, cols * parts), BF16),
        pltpu.VMEM((count, rows, cols * stages), BF16),
        dma((count, 2 * stages)), dma((count, stages)), dma((units, dp)), dma((units, dp)), dma((units,)),
    ]


def forward_kernel(block, dp_bits, stages, back, *refs):
    weights, refs = refs[:6], refs[6:]
    tokens, vectors, segments = refs[:3]
    gain, factor = vectors.at[0:1], vectors.at[1:2]
    fulls, refs = refs[3:9], refs[9:]
    bias_full, raw_out, q_out, k_out, v_out, nt_out, o_ref, lse_ref = refs[:8]
    refs = refs[8:]
    home, window, normed, nt, raw, q, k, v, vt, ot, bias, scores, tops, totals, bias_in, bias_all = refs[:16]
    xs, xr, bs, br, os = refs[16:21]
    d, z = greet(dp_bits, stages)
    rows, features = tokens.shape
    width, heads = k.shape[0], features // HD
    own = width - rows
    tile = 2 * LANES
    homes = [home.at[w] for w in range(3)] + list(fulls[3:])
    work = Gathering(dp_bits, stages, d, z, weights, homes, refs[21:])

    def bias_copy(step):
        return pltpu.make_async_remote_copy(
            src_ref=bias_in, dst_ref=bias_all.at[step], send_sem=bs.at[step],
            recv_sem=br.at[step], device_id={"mp": lax.rem(z + step, stages)},
            device_id_type=MESH,
        )

    def token_copy(hop):
        return pltpu.make_async_remote_copy(
            src_ref=tokens if hop == 0 else window.at[hop - 1], dst_ref=window.at[hop],
            send_sem=xs.at[hop], recv_sem=xr.at[hop],
            device_id={"mp": jnp.minimum(z + 1, stages - 1)}, device_id_type=MESH,
        )

    kept = [
        (raw, raw_out), (q, q_out), (k, k_out), (v, v_out), (nt, nt_out),
        (home.at[0], fulls[0]), (home.at[1], fulls[1]), (home.at[2], fulls[2]),
    ]

    def keep(i):
        return pltpu.make_async_copy(kept[i][0], kept[i][1], os.at[i])

    def norm(src, at):
        step_rows = 128

        def step(i, carry):
            part = pl.ds(pl.multiple_of(i * step_rows, step_rows), step_rows)
            x = src[part, :].astype(F32)
            value = (x * row_inverse(x) * gain[...]).astype(BF16)
            to = pl.ds(pl.multiple_of(at + i * step_rows, step_rows), step_rows)
            normed[to, :] = value
            return carry

        lax.fori_loop(0, rows // step_rows, step, 0)
        for c in range(features // tile):
            lanes = slice(c * tile, (c + 1) * tile)
            nt[lanes, at : at + rows] = normed[at : at + rows, lanes].T

    def project(w, at, out, out_t):
        def step(c, carry):
            lanes = pl.ds(pl.multiple_of(c * tile, tile), tile)
            value = dot(normed[at : at + rows, :], home[w, :, lanes], 1, 0).astype(BF16)
            out[at : at + rows, lanes] = value
            if out_t is not None:
                out_t[lanes, at : at + rows] = value.T
            return carry

        lax.fori_loop(0, features // tile, step, 0)

    def project_both(at):
        def step(c, carry):
            lanes = pl.ds(pl.multiple_of(c * tile, tile), tile)
            source = normed[at : at + rows, :]
            k[at : at + rows, lanes] = dot(source, home[1, :, lanes], 1, 0).astype(BF16)
            value = dot(source, home[2, :, lanes], 1, 0).astype(BF16)
            v[at : at + rows, lanes] = value
            vt[lanes, at : at + rows] = value.T
            return carry

        lax.fori_loop(0, features // tile, step, 0)

    first, rest = range(3), range(3, 6)
    for w in range(6):
        work.pack(w)
    for w in first:
        work.hop(w, 0)
    bias_in[...] = vectors[4:5, : features // stages]
    for step in range(1, stages):
        work.start(bias_copy, step)
    bias_all[0] = bias_in[...]
    for hop in range(back):

        @pl.when(z <= hop)
        def _():
            window[hop] = jnp.zeros((rows, features), BF16)

    norm(tokens, own)
    fill_bias(segments, z, bias, block, own)
    for j in range(1, stages - 1):
        for w in first:
            work.hop(w, j)
    for w in rest:
        work.hop(w, 0)
    for w in first:
        work.collect(w)
        work.begin_round(w, 0)
    for j in range(1, stages - 1):
        if j <= 3 and dp_bits > 1:
            work.advance(j - 1, 0)
        for w in rest:
            work.hop(w, j)

    @pl.when(z < stages - 1)
    def _():
        token_copy(0).start()

    if dp_bits > 1:
        for w in range(max(0, min(stages - 2, 3)), 3):
            work.advance(w, 0)
    for w in rest:
        work.collect(w)
    for r in range(1, dp_bits - 1):
        for w in first:
            work.advance(w, r)
    for w in rest:
        work.begin_round(w, 0)
    for w in first:
        work.advance(w, dp_bits - 1)
        keep(5 + w).start()
        if w == 0:

            def query(c, carry):
                lanes = pl.ds(pl.multiple_of(c * tile, tile), tile)
                value = dot(normed[own:, :], home[0, :, lanes], 1, 0)
                raw[:, lanes] = value
                q[:, lanes] = (value * factor[:, lanes]).astype(BF16)
                return carry

            lax.fori_loop(0, features // tile, query, 0)
            keep(0).start()
            keep(1).start()
        else:
            project(w, own, *((k, None) if w == 1 else (v, vt)))

    sp = spans(rows, width, block)

    def attend(low, high, fresh, last, due):
        tiles = []
        for kb in range(low // block, high // block):
            qs = [i for i, (lo, hi) in enumerate(sp) if lo <= kb * block < hi]
            if qs:
                tiles.append((kb, qs))

        def head(h):
            lanes, mine = head_lanes(h, features)
            feats = pl.ds(pl.multiple_of(h * HD, 16), HD)
            query = jnp.where(mine, q[:, lanes], jnp.zeros((), BF16))
            top = [jnp.full((8, block), FAR, F32) for _ in sp]
            for kb, qs in tiles:
                qa, qz = qs[0] * block, (qs[-1] + 1) * block
                at = slice(kb * block, (kb + 1) * block)
                s = dot(k[at, lanes], query[qa:qz], 1, 1) + bias[at, qa:qz]
                scores[at, qa:qz] = s
                for i in qs:
                    cut = s[:, i * block - qa : (i + 1) * block - qa]
                    top[i] = jnp.maximum(top[i], jnp.max(cut.reshape(block // 8, 8, block), axis=0))
            top = jnp.concatenate([jnp.max(t, axis=0, keepdims=True) for t in top], axis=1)
            if not fresh:
                before = tops[pl.ds(h, 1), :]
                top = jnp.maximum(top, before)
                scale = jnp.exp(before - top)
            acc = [jnp.zeros((HD, block), F32) for _ in sp]
            total = [jnp.zeros((8, block), F32) for _ in sp]
            for kb, qs in tiles:
                qa, qz = qs[0] * block, (qs[-1] + 1) * block
                at = slice(kb * block, (kb + 1) * block)
                p = jnp.exp(scores[at, qa:qz] - top[:, qa:qz])
                part = dot(vt[feats, at], p.astype(BF16), 1, 0)
                for i in qs:
                    cut = slice(i * block - qa, (i + 1) * block - qa)
                    total[i] = total[i] + jnp.sum(p[:, cut].reshape(block // 8, 8, block), axis=0)
                    acc[i] = acc[i] + part[:, cut]
            for i in range(len(sp)):
                at = slice(i * block, (i + 1) * block)
                one = jnp.sum(total[i], axis=0, keepdims=True)
                out = acc[i]
                if not fresh:
                    one = one + totals[pl.ds(h, 1), at] * scale[:, at]
                    out = out + ot[feats, at] * scale[:, at]
                if last:
                    ot[feats, at] = out / one
                    lse_ref[pl.ds(h, 1), at] = top[:, at] + jnp.log(one)
                else:
                    ot[feats, at] = out
                    totals[pl.ds(h, 1), at] = one
                    tops[pl.ds(h, 1), at] = top[:, at]

        def pair(i, carry):
            for at in sorted(set(due.values())):

                @pl.when(2 * i == at)
                def _():
                    for w, r in due:
                        if due[w, r] == at:
                            work.advance(w, r)

            head(2 * i)
            head(2 * i + 1)
            return carry

        lax.fori_loop(0, heads // 2, pair, 0)

    inside, ready = {}, []
    if back and dp_bits > 2:
        inside = {(3, 1): heads * 3 // 8, (4, 1): heads * 5 // 8, (5, 1): heads * 7 // 8}
        ready = [(3, 0), (4, 0), (5, 0)]
    for pair in ready[:1]:
        work.advance(*pair)
    for hop in range(back):
        if hop + 1 == back:
            for pair in ready[1:]:
                work.advance(*pair)
            attend(rows, width, True, False, inside)

        @pl.when(z > hop)
        def _():
            token_copy(hop).wait_recv()

        if hop + 1 < back:

            @pl.when((z > hop) & (z < stages - 1))
            def _():
                token_copy(hop + 1).start()

        at = own - (hop + 1) * rows
        norm(window.at[hop], at)
        project_both(at)
    for i in range(2, 5):
        keep(i).start()
    attend(0, rows if back else width, not back, True, {})
    transpose_out(ot, o_ref)
    for r in range(dp_bits):
        for w in rest:
            if (w, r) not in inside and (w, r) not in ready:
                work.advance(w, r)
    for step in range(1, stages):
        bias_copy(step).wait_recv()
    bias_full[...] = jnp.concatenate(
        [bias_all[lax.rem(z - s + stages, stages)] for s in range(stages)], axis=1
    )
    for hop in range(back):

        @pl.when((z >= hop) & (z < stages - 1))
        def _():
            token_copy(hop).wait_send()

    for i in range(len(kept)):
        keep(i).wait()
    work.close()


def attend_forward(weights, tokens, vectors, segments, block, dp, stages, back):
    held, cols = weights[0].shape
    rows, features = tokens.shape
    width, heads = (back + 1) * rows, features // HD
    hbm = pl.BlockSpec(memory_space=pl.ANY)
    vmem = pl.BlockSpec(memory_space=pltpu.VMEM)
    dma = pltpu.SemaphoreType.DMA
    sds = jax.ShapeDtypeStruct
    return pl.pallas_call(
        functools.partial(forward_kernel, block, dp.bit_length() - 1, stages, back),
        in_specs=[vmem] * 9,
        out_specs=[hbm] * 6 + [vmem] + [hbm] * 5 + [vmem] * 2,
        out_shape=[sds((features, features), BF16)] * 6
        + [
            sds((1, features), F32),
            sds((rows, features), F32),
            sds((rows, features), BF16),
            sds((width, features), BF16),
            sds((width, features), BF16),
            sds((features, width), BF16),
            sds((rows, features), BF16),
            sds((heads, rows), F32),
        ],
        scratch_shapes=[
            pltpu.VMEM((3, features, features), BF16),
            pltpu.VMEM((back, rows, features), BF16),
            pltpu.VMEM((width, features), BF16),
            pltpu.VMEM((features, width), BF16),
            pltpu.VMEM((rows, features), F32),
            pltpu.VMEM((rows, features), BF16),
            pltpu.VMEM((width, features), BF16),
            pltpu.VMEM((width, features), BF16),
            pltpu.VMEM((features, width), BF16),
            pltpu.VMEM((features, rows), F32),
            pltpu.VMEM((width, rows), F32),
            pltpu.VMEM((width, rows), F32),
            pltpu.VMEM((heads, rows), F32),
            pltpu.VMEM((heads, rows), F32),
            pltpu.VMEM((1, features // stages), F32),
            pltpu.VMEM((stages, 1, features // stages), F32),
            dma((back,)), dma((back,)), dma((stages,)), dma((stages,)), dma((8,)),
        ]
        + gathering_scratch(6, dp, stages, held, cols),
        compiler_params=pltpu.CompilerParams(
            collective_id=0, has_side_effects=True, vmem_limit_bytes=62 << 20
        ),
        name="attend_forward",
    )(*weights, tokens, vectors, segments)


def middle_kernel(block, dp_bits, stages, *refs):
    sources, refs = refs[:12], refs[12:]
    b_up, vectors, lse_ref, segments = refs[:4]
    factor, gain, b_down = (vectors.at[i : i + 1] for i in (1, 2, 3))
    results, incoming, outs, sums, refs = refs[4:10], refs[10], refs[11:14], refs[14], refs[15:]
    weights, hidden, wide, tmp, tr, keys, values, query_in, grad_in, bias, delta_ref = refs[:11]
    ps, pr, sems, refs = refs[11], refs[12], refs[13], refs[14:]
    d, z = greet(dp_bits, stages)
    work = Reduction(dp_bits, stages, d, z, None, outs, refs)
    rows, features = query_in.shape
    heads, width = features // HD, keys.shape[0]
    back = width // rows - 1
    tile = 2 * LANES
    w_out, w_up, w_down = weights.at[0], weights.at[1], weights.at[2]
    w_key, w_value = weights.at[2], weights.at[1]
    mixed, cot, x, second, active, d_pre, d_attn, spare = (tmp.at[i] for i in range(8))
    dk, dv = tmp.at[: back + 1], tmp.at[back + 1 : 2 * back + 2]
    dq, part = tmp.at[2 * back + 2], tmp.at[2 * back + 3]
    inside = (
        mixed, w_out, x, cot, w_up, w_down, keys, values, query_in, w_key, w_value, hidden,
    )
    half = rows // 2
    outside = (spare, hidden, dq, dk, dv, part.at[half:])
    loads = Loads(list(zip(sources, inside)) + list(zip(outside, results)), sems)
    loads.start(*range(9))
    fill_bias(segments, z, bias, block, width - rows)

    def by_tile(body):
        for c in range(features // tile):
            body(slice(c * tile, (c + 1) * tile), c)

    def by_rows(body, start):
        def step(i, carry):
            return body(pl.ds(pl.multiple_of(i * 64, 64), 64), carry)

        return lax.fori_loop(0, rows // 64, step, start)

    def flip(src):
        for c in range(features // tile):
            lanes = slice(c * tile, (c + 1) * tile)
            tr[lanes, :] = src[:, lanes].T

    nothing = jnp.zeros((1, features), F32)

    def add_attention(lanes, c):
        hidden[:, lanes] = x[:, lanes].astype(F32) + dot(mixed[...], w_out[lanes, :], 1, 1)

    def norm(at, carry):
        h = hidden[at, :]
        second[at, :] = (h * row_inverse(h) * gain[...]).astype(BF16)
        return carry

    def activate(lanes, c):
        pre = dot(second[...], w_up[:, lanes], 1, 0) + b_up[:, lanes]
        sigma = 1.0 / (1.0 + jnp.exp(-pre))
        active[:, lanes] = (pre * sigma).astype(BF16)
        grad = dot(cot[...], w_down[:, lanes], 1, 0)
        grad = (grad * sigma * (1.0 + pre * (1.0 - sigma))).astype(BF16)
        d_pre[:, lanes] = grad
        sums[2:3, lanes] = jnp.sum(grad.astype(F32), axis=0, keepdims=True)

    def finish_layer(lanes, c):
        out = dot(active[...], w_down[lanes, :], 1, 1)
        spare[:, lanes] = (hidden[:, lanes] + out + b_down[:, lanes]).astype(BF16)
        sums[1:2, lanes] = jnp.sum(cot[:, lanes].astype(F32), axis=0, keepdims=True)

    def to_second(lanes, c):
        wide[:, lanes] = dot(d_pre[...], w_up[lanes, :], 1, 1)

    def to_hidden(at, column):
        h, grad = hidden[at, :], wide[at, :]
        inverse = row_inverse(h)
        weighted = grad * gain[...]
        dots = jnp.sum(weighted * h, axis=1, keepdims=True)
        cube = inverse * inverse * inverse
        d_hidden = cot[at, :].astype(F32) + inverse * weighted - h * cube / features * dots
        hidden[at, :] = d_hidden
        d_attn[at, :] = d_hidden.astype(BF16)
        return column + jnp.sum(grad * h * inverse, axis=0, keepdims=True)

    def to_mixed(lanes, c):
        grad = dot(d_attn[...], w_out[:, lanes], 1, 0).astype(BF16)
        grad_in[:, lanes] = grad
        both = grad.astype(F32) * mixed[:, lanes].astype(F32)
        lane = lax.broadcasted_iota(jnp.int32, (heads, tile), 1) + c * tile
        first = lax.broadcasted_iota(jnp.int32, (heads, tile), 0) * HD
        owner = jnp.where((lane >= first) & (lane < first + HD), 1.0, 0.0).astype(BF16)
        high = both.astype(BF16)
        rest = (both - high.astype(F32)).astype(BF16)
        delta_ref[...] += dot(owner, high, 1, 1) + dot(owner, rest, 1, 1)

    sums[3:8, :] = jnp.zeros((5, features), F32)
    delta_ref[...] = jnp.zeros_like(delta_ref)
    loads.wait(0, 1, 2)
    by_tile(add_attention)
    by_rows(norm, 0)
    loads.wait(3, 4, 5)
    by_tile(activate)
    flip(cot)
    work.weight_grad(0, lambda at: tr[at, :], lambda: active[...])
    by_tile(finish_layer)
    loads.start(12, 9)
    by_tile(to_second)
    loads.start(10)
    flip(second)
    work.weight_grad(1, lambda at: tr[at, :], lambda: d_pre[...])
    work.advance(0, 0)
    sums[0:1, :] = by_rows(to_hidden, nothing)
    loads.start(13)
    by_tile(to_mixed)
    flip(d_attn)
    work.weight_grad(2, lambda at: tr[at, :], lambda: mixed[...])
    work.advance(1, 0)
    if dp_bits > 1:
        work.advance(0, 1)
    loads.wait(12)
    for c in range(2 * back + 2):
        tmp[c] = jnp.zeros((rows, features), BF16)
    wide[...] = jnp.zeros_like(wide)
    loads.wait(6, 7, 8)
    sp = spans(rows, width, block)
    steps = heads * (back + 1)
    events = [(2, 0)] + [(w, k) for w in range(3) for k in range(1, dp_bits) if (w, k) != (0, 1)]
    due = {i: int(at * steps) // 2 * 2 for i, at in enumerate(EVENTS[: len(events)])}

    def down():
        return pltpu.make_async_remote_copy(
            src_ref=part.at[:half], dst_ref=incoming, send_sem=ps, recv_sem=pr,
            device_id={"mp": jnp.maximum(z - 1, 0)}, device_id_type=MESH,
        )

    for c in range(back + 1):

        def head(h):
            lanes, mine = head_lanes(h, features)
            zero = jnp.zeros((), BF16)
            query = jnp.where(mine, query_in[:, lanes], zero)
            grad = jnp.where(mine, grad_in[:, lanes], zero)
            lse = lse_ref[pl.ds(h, 1), :]
            delta = delta_ref[pl.ds(h, 1), :]
            for kb in range(c * rows // block, (c + 1) * rows // block):
                qs = [i for i, (lo, hi) in enumerate(sp) if lo <= kb * block < hi]
                if not qs:
                    continue
                qa, qz = qs[0] * block, (qs[-1] + 1) * block
                at = slice(kb * block, (kb + 1) * block)
                to = slice(kb * block - c * rows, (kb + 1) * block - c * rows)
                key = keys[at, lanes]
                s = dot(key, query[qa:qz], 1, 1) + bias[at, qa:qz]
                p = jnp.exp(s - lse[:, qa:qz])
                dp = dot(values[at, lanes], grad[qa:qz], 1, 1)
                ds = (p * (dp - delta[:, qa:qz])).astype(BF16)
                dv[c, to, lanes] += dot(p.astype(BF16), grad[qa:qz], 1, 0).astype(BF16)
                dk[c, to, lanes] += dot(ds, query[qa:qz], 1, 0).astype(BF16)
                wide[qa:qz, lanes] += dot(ds, jnp.where(mine, key, zero), 0, 0)

        def pair(i, carry):
            for at in sorted(set(due.values())):
                if at // heads != c:
                    continue

                @pl.when(2 * i == at % heads)
                def _():
                    for e in due:
                        if due[e] == at:
                            work.advance(*events[e])

            head(2 * i)
            head(2 * i + 1)
            return carry

        lax.fori_loop(0, heads // 2, pair, 0)
        if c == 0:
            loads.wait(9, 10)
            if back:
                back_project(part, ((dk.at[0], w_key), (dv.at[0], w_value)), 0, None)
                loads.start(17)

                @pl.when(z >= back)
                def _():
                    down().start()

            loads.wait(13)
            loads.start(11)

    loads.start(15, 16)
    loads.wait(11)

    def to_query(at, column):
        scaled = wide[at, :].astype(BF16).astype(F32)
        dq[at, :] = (scaled * factor[...]).astype(BF16)
        return column + jnp.sum(scaled * hidden[at, :], axis=0, keepdims=True)

    sums[4:5, :] = by_rows(to_query, nothing)
    loads.start(14)
    for i in range(len(due), len(events)):
        work.advance(*events[i])
    for w in range(3):
        work.finish(w)
    loads.wait(14, 15, 16)
    if back:
        loads.wait(17)

        @pl.when((z + 1 >= back) & (z < stages - 1))
        def _():
            down().wait_recv()

        @pl.when(z >= back)
        def _():
            down().wait_send()

    work.close()


def back_project(out, pairs, at, more):
    rows, features = out.shape
    tile = 2 * LANES

    def step(c, carry):
        lanes = pl.ds(pl.multiple_of(c * tile, tile), tile)
        value = None
        for grad, weight in pairs:
            start = at if grad.shape[0] > rows else 0
            term = dot(grad[start : start + rows, :], weight[lanes, :], 1, 1)
            value = term if value is None else value + term
        if more is not None:
            value = value + more(lanes)
        out[:, lanes] = value.astype(out.dtype)
        return carry

    lax.fori_loop(0, features // tile, step, 0)


def middle(
    mixed, w_out, x, cot, w_up, w_down, k, v, q, w_key, w_value, raw, b_up, vectors,
    lse, segments, block, dp, stages,
):
    rows, features = q.shape
    width, heads = k.shape[0], features // HD
    held, cols = features // dp, features // stages
    chunks = width // rows
    hbm = pl.BlockSpec(memory_space=pl.ANY)
    vmem = pl.BlockSpec(memory_space=pltpu.VMEM)
    dma = pltpu.SemaphoreType.DMA
    sds = jax.ShapeDtypeStruct
    low, high = sds((rows, features), BF16), sds((rows, features), F32)
    many, part = sds((chunks, rows, features), BF16), sds((rows // 2, features), BF16)
    return pl.pallas_call(
        functools.partial(middle_kernel, block, dp.bit_length() - 1, stages),
        in_specs=[hbm] * 12 + [vmem] * 4,
        out_specs=[hbm] * 7 + [vmem] * 4,
        out_shape=[low, high, low, many, many, part, part]
        + [sds((held, cols), F32)] * 3
        + [sds((8, features), F32)],
        scratch_shapes=[
            pltpu.VMEM((3, features, features), BF16),
            pltpu.VMEM((rows, features), F32),
            pltpu.VMEM((rows, features), F32),
            pltpu.VMEM((max(8, 2 * chunks + 2), rows, features), BF16),
            pltpu.VMEM((features, rows), BF16),
            pltpu.VMEM((width, features), BF16),
            pltpu.VMEM((width, features), BF16),
            pltpu.VMEM((rows, features), BF16),
            pltpu.VMEM((rows, features), BF16),
            pltpu.VMEM((width, rows), F32),
            pltpu.VMEM((heads, rows), F32),
            dma, dma, dma((18,)),
        ]
        + reduction_scratch(3, dp, stages, held, features, True),
        compiler_params=pltpu.CompilerParams(
            collective_id=2, has_side_effects=True, vmem_limit_bytes=63 << 20
        ),
        name="middle",
    )(
        mixed, w_out, x, cot, w_up, w_down, k, v, q, w_key, w_value, raw, b_up, vectors,
        lse, segments,
    )


def input_kernel(dp_bits, stages, back, *refs):
    sources, farther, vectors, sums, refs = refs[:10], refs[10], refs[11], refs[12], refs[13:]
    gain = vectors.at[0:1]
    outs, result, total, refs = refs[:3], refs[3], refs[4], refs[5:]
    inside, tokens_grad, refs = refs[:10], refs[10], refs[11:]
    dv, nt, dk, wk, wv, incoming, dq, wq, tokens, d_hidden = inside
    part, landed, d_first, sgot, ss, sr, ps, pr, sems = refs[:9]
    d, z = greet(dp_bits, stages)
    work = Reduction(dp_bits, stages, d, z, None, outs, refs[9:])
    rows, features = tokens.shape
    own, half = back * rows, rows // 2
    inside = inside[:5] + (incoming.at[:half],) + inside[6:]
    loads = Loads(list(zip(sources, inside)) + [(tokens_grad, result)], sems)
    levels = dp_bits + stages.bit_length() - 1
    held = features >> dp_bits
    grads = ((dv, 2, 0), (dk, 1, 0), (dq, 0, own))

    def down(hop):
        return pltpu.make_async_remote_copy(
            src_ref=part.at[hop - 1] if hop else farther,
            dst_ref=landed.at[hop - 1] if hop else incoming.at[half:],
            send_sem=ps.at[hop], recv_sem=pr.at[hop],
            device_id={"mp": jnp.maximum(z - 1, 0)}, device_id_type=MESH,
        )

    if back:

        @pl.when(z >= back)
        def _():
            down(0).start()

    loads.start(*range(10))

    def arrived(hop):
        source = incoming if hop == 1 else landed.at[hop - 2]
        there = (z + 1 >= back - hop + 1) & (z < stages - 1)

        def take(lanes):
            return jnp.where(there, source[:, lanes].astype(F32), 0.0)

        return there, take

    def weight_grad(i):
        grad, w, at = grads[i]
        work.weight_grad(w, lambda rows_at: nt[rows_at, at:], lambda: grad[...])

    def sum_copy(k):
        if k < dp_bits:
            to = {"dp": flipped(d, (k,))}
        else:
            to = {"mp": flipped(z, (k - dp_bits,))}
        return pltpu.make_async_remote_copy(
            src_ref=total.at[k], dst_ref=sgot.at[k], send_sem=ss.at[k], recv_sem=sr.at[k],
            device_id=to, device_id_type=MESH,
        )

    def sum_step(k):
        sum_copy(k).wait_recv()
        total[k + 1] = total[k] + sgot[k]
        if k + 1 < levels:
            work.start(sum_copy, k + 1)

    def pass_down(hop):
        there, take = arrived(hop)

        @pl.when(there)
        def _():
            down(hop - 1).wait_recv()

        back_project(part.at[hop - 1], ((dk, wk), (dv, wv)), hop * rows, take)

        @pl.when(z >= back - hop)
        def _():
            down(hop).start()

    loads.wait(0, 1)
    weight_grad(0)
    loads.wait(2)
    weight_grad(1)
    work.advance(2, 0)
    loads.wait(3, 4, 5)
    if back > 1:
        pass_down(1)
    work.advance(1, 0)
    loads.wait(6, 7)
    weight_grad(2)
    for hop in range(2, back):
        pass_down(hop)
    work.advance(0, 0)
    back_project(d_first, ((dk, wk), (dv, wv), (dq, wq)), own, None)
    events = [(w, k) for w in (2, 1, 0) for k in range(1, dp_bits)]
    for event in events[:1]:
        work.advance(*event)
    loads.wait(8, 9)
    there, take = arrived(back) if back else (None, None)
    if back:

        @pl.when(there)
        def _():
            down(back - 1).wait_recv()

    chunk = 64

    def finish(i, column):
        at = pl.ds(pl.multiple_of(i * chunk, chunk), chunk)
        x = tokens[at, :].astype(F32)
        grad = d_first[at, :]
        if back:
            source = incoming if back == 1 else landed.at[back - 2]
            grad = grad + jnp.where(there, source[at, :].astype(F32), 0.0)
        inverse = row_inverse(x)
        weighted = grad * gain[...]
        dots = jnp.sum(weighted * x, axis=1, keepdims=True)
        cube = inverse * inverse * inverse
        tokens_grad[at, :] = (
            d_hidden[at, :] + inverse * weighted - x * cube / features * dots
        ).astype(BF16)
        return column + jnp.sum(grad * x * inverse, axis=0, keepdims=True)

    column = lax.fori_loop(0, rows // chunk, finish, jnp.zeros((1, features), F32))
    total[0] = sums[...]
    total[0, 3:4, :] = column
    work.start(sum_copy, 0)
    loads.start(10)
    done = 0
    for event in events[1:]:
        work.advance(*event)
        if done < levels:
            sum_step(done)
            done += 1
    for k in range(done, levels):
        sum_step(k)
    for w in (2, 1, 0):
        work.finish(w)
    for hop in range(back):

        @pl.when(z >= back - hop)
        def _():
            down(hop).wait_send()

    loads.wait(10)
    work.close()


def input_gradients(
    nt, dq, dk, dv, wq, wk, wv, incoming, farther, tokens, d_hidden, vectors, sums, dp, stages
):
    rows, features = tokens.shape
    back = dk.shape[0] // rows - 1
    held, cols = features // dp, features // stages
    dp_bits = dp.bit_length() - 1
    levels = dp_bits + stages.bit_length() - 1
    hbm = pl.BlockSpec(memory_space=pl.ANY)
    vmem = pl.BlockSpec(memory_space=pltpu.VMEM)
    dma = pltpu.SemaphoreType.DMA
    hops = max(1, back - 1)
    sources = (dv, nt, dk, wk, wv, incoming, dq, wq, tokens, d_hidden)
    out = pl.pallas_call(
        functools.partial(input_kernel, dp_bits, stages, back),
        in_specs=[hbm] * 11 + [vmem] * 2,
        out_specs=[vmem] * 3 + [hbm, vmem],
        out_shape=[jax.ShapeDtypeStruct((held, cols), F32)] * 3
        + [
            jax.ShapeDtypeStruct((rows, features), BF16),
            jax.ShapeDtypeStruct((levels + 1,) + sums.shape, F32),
        ],
        scratch_shapes=[pltpu.VMEM(tokens.shape if a is incoming else a.shape, a.dtype) for a in sources + (tokens,)]
        + [
            pltpu.VMEM((hops, rows, features), BF16), pltpu.VMEM((hops, rows, features), BF16),
            pltpu.VMEM((rows, features), F32), pltpu.VMEM((levels,) + sums.shape, F32),
            dma((levels,)), dma((levels,)), dma((hops + 1,)), dma((hops + 1,)), dma((11,)),
        ]
        + reduction_scratch(3, dp, stages, held, features, True),
        compiler_params=pltpu.CompilerParams(
            collective_id=1, has_side_effects=True, vmem_limit_bytes=62 << 20
        ),
        name="input_gradients",
    )(*sources, farther, vectors, sums)
    return out[:3], out[3], out[4][levels]


def hand_over_kernel(*refs):
    half = len(refs) // 2
    for source, result in zip(refs[:half], refs[half:]):
        result[...] = source[...]


def hand_over(arrays):
    vmem = pl.BlockSpec(memory_space=pltpu.VMEM)
    return pl.pallas_call(
        hand_over_kernel,
        in_specs=[vmem] * len(arrays),
        out_specs=[vmem] * len(arrays),
        out_shape=[jax.ShapeDtypeStruct(a.shape, a.dtype) for a in arrays],
        name="hand_over",
    )(*arrays)


def body(
    tokens, segments, w_query, w_key, w_value, w_output, w_up, b_up, w_down, b_down,
    gain_attn, gain_mlp, query_scale, cotangent,
):
    stages = lax.axis_size("mp")
    z = lax.axis_index("mp")
    rows, features = tokens.shape
    back = min(stages - 1, -(-(DOC_MAX - 1) // rows))
    own = back * rows
    block = min(256, rows)
    heads = features // HD
    dp = lax.axis_size("dp")
    factor = jax.nn.softplus(query_scale) * (LOG2E / math.sqrt(HD))
    mine = b_up.shape[0]
    vectors = jnp.zeros((8, features), F32)
    row = lax.broadcasted_iota(jnp.int32, (8, features), 0)
    given = (gain_attn, jnp.tile(factor, heads), gain_mlp, b_down, jnp.pad(b_up, (0, features - mine)))
    for i, value in enumerate(given):
        vectors = jnp.where(row == i, value[None], vectors)
    (
        wq, wk, wv, wu, wo, wd, b_full, query_raw, scaled, keys, values, first_t, mixed, lse
    ) = attend_forward(
        (w_query, w_key, w_value, w_up, w_output.T, w_down.T), tokens, vectors, segments,
        block, dp, stages, back,
    )
    layer_out, d_hidden, d_query, d_keys, d_values, farther, incoming, *mlp, sums = middle(
        mixed, wo, tokens, cotangent, wu, wd, keys, values, scaled, wk, wv, query_raw,
        b_full, vectors, lse, segments, block, dp, stages,
    )
    grads, tokens_grad, sums = input_gradients(
        first_t, d_query, d_keys.reshape(own + rows, features),
        d_values.reshape(own + rows, features), wq, wk, wv, incoming, farther, tokens,
        d_hidden, vectors, sums, dp, stages,
    )
    sum_b_up = lax.dynamic_slice_in_dim(sums[2], z * mine, mine, 0)
    scale_total = jnp.sum(sums[4].reshape(heads, HD), axis=0)
    grad_query_scale = scale_total * (LOG2E / math.sqrt(HD)) * jax.nn.sigmoid(query_scale)
    layer_out, tokens_grad, g_query, g_key, g_value, g_up, g_output, g_down = hand_over(
        (layer_out, tokens_grad, *grads, mlp[1], mlp[2], mlp[0])
    )
    return (
        layer_out, tokens_grad, g_query, g_key, g_value, g_output.T, g_up, sum_b_up,
        g_down.T, sums[1], sums[3], sums[0], grad_query_scale,
    )


def solution(mesh):
    tokens, rows_dp, rows_mp = P(("dp", "mp"), None), P("dp", "mp"), P("mp", "dp")
    return jax.shard_map(
        body,
        mesh=mesh,
        in_specs=(
            tokens, P("dp", None), rows_dp, rows_dp, rows_dp, rows_mp, rows_dp, P("mp"), rows_mp,
            P(), P(), P(), P(), tokens,
        ),
        out_specs=(
            tokens, tokens, rows_dp, rows_dp, rows_dp, rows_mp, rows_dp, P("mp"), rows_mp,
            P(), P(), P(), P(),
        ),
        check_vma=False,
    )
```

```python
import functools
import math

import jax
import jax.numpy as jnp
from jax import lax
from jax.experimental import pallas as pl
from jax.experimental.pallas import tpu as pltpu
from jax.sharding import PartitionSpec as P

HD = 80
LANES = 128
EPSILON = 1e-06
LOG2E = 1.442695
DOC_MAX = 1024
FAR = -1e30
EVENTS = (0.15, 0.3, 0.5, 0.6, 0.75, 0.9)
F32 = jnp.float32
BF16 = jnp.bfloat16


def dot(a, b, ca, cb):
    return lax.dot_general(a, b, (((ca,), (cb,)), ((), ())), preferred_element_type=F32)


def row_inverse(values):
    return lax.rsqrt(jnp.mean(values * values, axis=1, keepdims=True) + EPSILON)


MESH = pl.DeviceIdType.MESH


def bit_of(index, b):
    return lax.rem(lax.div(index, 1 << b), 2)


def flipped(index, bits):
    for b in bits:
        index = index + (1 << b) * (1 - 2 * bit_of(index, b))
    return index


def split_order(count, turn):
    bits = list(range(count))
    rest = bits[1:][::-1]
    turn = turn % max(1, len(rest))
    return bits[:1] + rest[turn:] + rest[:turn]


def subsets(bits):
    out = [()]
    for b in bits:
        out = out + [s + (b,) for s in out]
    return out


def greet(dp_bits, stages, extra=()):
    d, z = lax.axis_index("dp"), lax.axis_index("mp")
    barrier = pltpu.get_barrier_semaphore()
    for b in range(dp_bits):
        pl.semaphore_signal(barrier, device_id={"dp": flipped(d, (b,))}, device_id_type=MESH)
    for step in range(1, stages):
        pl.semaphore_signal(
            barrier, device_id={"mp": lax.rem(z + step, stages)}, device_id_type=MESH
        )
    pl.semaphore_wait(barrier, dp_bits + stages - 1)
    return d, z


class Loads:
    def __init__(self, pairs, sems):
        self.pairs, self.sems = pairs, sems

    def copy(self, i):
        return pltpu.make_async_copy(self.pairs[i][0], self.pairs[i][1], self.sems.at[i])

    def start(self, *which):
        for i in which:
            self.copy(i).start()

    def wait(self, *which):
        for i in which:
            self.copy(i).wait()


class Reduction:
    def __init__(self, dp_bits, stages, d, z, grads, outs, refs):
        self.dp_bits, self.stages, self.d, self.z = dp_bits, stages, d, z
        self.grads, self.outs = grads, outs
        self.pool = refs[0]
        self.kept, self.got = refs[0].at[0], refs[1 : 1 + dp_bits]
        self.zsend, self.zgot, self.ks, self.rs, self.rr, self.zs, self.zr = refs[1 + dp_bits :]
        self.half = 1 << (dp_bits - 1)
        self.parts = self.kept.shape[0] // len(outs)
        self.rows, self.features = self.kept.shape[2], self.kept.shape[3]
        self.sent = []

    def start(self, make, *args):
        make(*args).start()
        self.sent.append((make, args))

    def order(self, u):
        return split_order(self.dp_bits, u % self.parts)

    def place(self, u, slot, low):
        rest = self.order(u)[1:]
        at = low
        for i, b in enumerate(rest):
            if slot >> (len(rest) - 1 - i) & 1:
                at = at + (1 << b)
        return at

    def slot_of(self, u, index):
        rest = self.order(u)[1:]
        return sum(bit_of(index, b - 1) << (len(rest) - 1 - i) for i, b in enumerate(rest))

    def source(self, u, slot, low):
        cut = pl.ds(u % self.parts * self.rows, self.rows)
        return self.grads[u // self.parts].at[self.place(u, slot, low), cut]

    def first_copy(self, u, slot):
        return pltpu.make_async_remote_copy(
            src_ref=self.pool.at[1, u, slot]
            if self.grads is None
            else self.source(u, slot, 1 - bit_of(self.d, 0)),
            dst_ref=self.got[0].at[u, slot],
            send_sem=self.rs.at[u, slot], recv_sem=self.rr.at[u, slot],
            device_id={"dp": flipped(self.d, (0,))}, device_id_type=MESH,
        )

    def keep_copy(self, u, slot):
        return pltpu.make_async_copy(
            self.source(u, slot, bit_of(self.d, 0)), self.kept.at[u, slot], self.ks.at[u, slot]
        )

    def round_copy(self, u, k):
        count = self.half >> k
        b = self.order(u)[k]
        other = 1 - bit_of(self.d, b)
        return pltpu.make_async_remote_copy(
            src_ref=self.got[k - 1].at[u, pl.ds(other * count, count)],
            dst_ref=self.got[k].at[u],
            send_sem=self.rs.at[u, self.half + k], recv_sem=self.rr.at[u, self.half + k],
            device_id={"dp": flipped(self.d, (b,))}, device_id_type=MESH,
        )

    def last_copy(self, w, step):
        to = lax.rem(self.z + step, self.stages)
        return pltpu.make_async_remote_copy(
            src_ref=self.zsend.at[w, to], dst_ref=self.zgot.at[w, step],
            send_sem=self.zs.at[w, step], recv_sem=self.zr.at[w, step],
            device_id={"mp": to}, device_id_type=MESH,
        )

    def units(self, w):
        return range(w * self.parts, (w + 1) * self.parts)

    def begin(self, w):
        for u in self.units(w):
            for slot in range(self.half):
                self.start(self.first_copy, u, slot)
                if self.grads is not None:
                    self.keep_copy(u, slot).start()

    def add(self, dst, src, count):
        def step(i, carry):
            dst[i] = dst[i] + src(i)
            return carry

        lax.fori_loop(0, count, step, 0)

    def take(self, w, k):
        for u in self.units(w):
            count = self.half >> k
            if k == 0:
                for slot in range(self.half):
                    if self.grads is not None:
                        self.keep_copy(u, slot).wait()
                    self.first_copy(u, slot).wait_recv()
                self.add(self.got[0].at[u], lambda i: self.kept[u, i], count)
            else:
                self.round_copy(u, k).wait_recv()
                mine = bit_of(self.d, self.order(u)[k]) * count
                self.add(self.got[k].at[u], lambda i: self.got[k - 1][u, mine + i], count)

    def send(self, w, k):
        for u in self.units(w):
            self.start(self.round_copy, u, k)

    def advance(self, w, k):
        self.take(w, k)
        if k + 1 == self.dp_bits:
            self.begin_last(w)
        else:
            self.send(w, k + 1)

    def put(self, w, index, value):
        held = self.parts * self.rows
        for low in range(2):
            which = lax.rem(bit_of(self.d, 0) + low, 2)
            for u in self.units(w):
                cut = low * held + u % self.parts * self.rows
                self.pool[which, u, self.slot_of(u, index)] = value[cut : cut + self.rows]

    def weight_grad(self, w, left, right):
        held = self.parts * self.rows

        def step(t, carry):
            at = pl.ds(pl.multiple_of(t * 2 * held, 2 * held), 2 * held)
            self.put(w, t, dot(left(at), right(), 1, 0).astype(BF16))
            return carry

        lax.fori_loop(0, 1 << (self.dp_bits - 1), step, 0)
        self.begin(w)

    def begin_last(self, w):
        cols = self.features // self.stages
        whole = [self.got[self.dp_bits - 1][u, 0] for u in self.units(w)]
        for s in range(self.stages):
            self.zsend[w, s] = jnp.concatenate(
                [piece[:, s * cols : (s + 1) * cols] for piece in whole], axis=1
            )
        for step in range(1, self.stages):
            self.start(self.last_copy, w, step)

    def finish(self, w):
        value = self.zsend[w, self.z].astype(F32)
        for step in range(1, self.stages):
            self.last_copy(w, step).wait_recv()
            value = value + self.zgot[w, step].astype(F32)
        cols = self.features // self.stages
        for p in range(self.parts):
            at = slice(p * self.rows, (p + 1) * self.rows)
            self.outs[w][at, :] = value[:, p * cols : (p + 1) * cols]

    def close(self):
        for make, args in self.sent:
            make(*args).wait_send()


def reduction_scratch(count, dp, stages, rows, features, local=False):
    dp_bits, half, cols = dp.bit_length() - 1, dp // 2, features // stages
    parts = 2 if rows % 32 == 0 else 1
    dma = pltpu.SemaphoreType.DMA
    units = count * parts
    return (
        [pltpu.VMEM((1 + local, units, half, rows // parts, features), BF16)]
        + [pltpu.VMEM((units, half >> k, rows // parts, features), BF16) for k in range(dp_bits)]
        + [pltpu.VMEM((count, stages, rows // parts, cols * parts), BF16)] * 2
        + [
            dma((units, half)), dma((units, half + dp_bits)), dma((units, half + dp_bits)),
            dma((count, stages)), dma((count, stages)),
        ]
    )


def spans(rows, width, block):
    own = width - rows
    out=[]
    for qb in range(rows//block):
        hi = own + (qb+1)*block
        lo = max(0, (own + qb*block - (DOC_MAX-1))//block*block)
        out.append((lo,hi))
    return out

def head_lanes(h, features):
    first = h*HD
    off = jnp.minimum(lax.div(first, LANES)*LANES, features-2*LANES)
    off = pl.multiple_of(off, LANES)
    lane = lax.broadcasted_iota(jnp.int32,(1,2*LANES),1) + (off-first)
    return pl.ds(off, 2*LANES), (lane>=0)&(lane<HD)

def fill_bias(segments, z, bias, block, own):
    width, rows = bias.shape
    first = z * rows
    for kb in range(width // block):
        start = first + (kb * block - own)
        at = pl.ds(pl.multiple_of(jnp.maximum(start, 0), block), block)
        col = jnp.broadcast_to(segments[:, at], (block, block)).T
        sub = lax.broadcasted_iota(jnp.int32, (block, block), 0) + kb * block
        for qb in range(rows // block):
            row = segments[:, pl.ds(pl.multiple_of(first + qb * block, block), block)]
            last = lax.broadcasted_iota(jnp.int32, (block, block), 1) + (own + qb * block)
            allowed = (col == row) & (sub <= last) & (start >= 0)
            bias[kb * block : (kb + 1) * block, qb * block : (qb + 1) * block] = jnp.where(
                allowed, 0.0, FAR
            )


def transpose_out(src, dst):
    for i in range(src.shape[0]//LANES):
        at = slice(i*LANES,(i+1)*LANES)
        dst[:, at] = src[at,:].T.astype(dst.dtype)

class Gathering:
    def __init__(self, dp_bits, stages, d, z, weights, homes, refs):
        self.dp_bits, self.stages, self.d, self.z = dp_bits, stages, d, z
        self.weights, self.homes = weights, homes
        self.blocks, self.slab, self.zs, self.zr, self.ds, self.dr, self.ls = refs
        self.rows, self.cols = weights[0].shape
        self.parts = self.ds.shape[0] // len(weights)
        self.cut = self.rows // self.parts
        self.sent = []

    def start(self, make, *args):
        make(*args).start()
        self.sent.append((make, args, None))

    def order(self, u):
        return split_order(self.dp_bits, u % self.parts)[::-1]

    def hop_copy(self, w, j, way):
        at = lax.rem(self.z - way * j + self.stages, self.stages)
        to = lax.rem(self.z + way + self.stages, self.stages)
        return pltpu.make_async_remote_copy(
            src_ref=self.blocks.at[w, at], dst_ref=self.blocks.at[w, at],
            send_sem=self.zs.at[w, 2 * j + (way + 1) // 2], recv_sem=self.zr.at[w, at],
            device_id={"mp": to}, device_id_type=MESH,
        )

    def there(self, j, way):
        return self.z >= j if way == 1 else self.z < self.stages - j

    def pack(self, w):
        pieces = [self.weights[w][p * self.cut : (p + 1) * self.cut] for p in range(self.parts)]
        self.blocks[w, self.z] = jnp.concatenate(pieces, axis=1)

    def take(self, w, j):
        for way in (1, -1):

            @pl.when(self.there(j, way))
            def _():
                self.hop_copy(w, j, way).wait_recv()

    def hop(self, w, j):
        if j:
            self.take(w, j)
        for way in (1, -1):
            sends = self.there(j, way) & self.there(1, -way)

            @pl.when(sends)
            def _():
                self.hop_copy(w, j, way).start()

            self.sent.append((self.hop_copy, (w, j, way), sends))

    def place(self, u, which):
        at = which * self.rows + u % self.parts * self.cut
        return self.homes[u // self.parts].at[pl.ds(pl.multiple_of(at, self.cut), self.cut)]

    def piece(self, u):
        at = u % self.parts * self.cut
        return self.slab.at[u // self.parts, pl.ds(at, self.cut)]

    def own_copy(self, u):
        return pltpu.make_async_copy(self.piece(u), self.place(u, self.d), self.ls.at[u])

    def round_copy(self, u, k, slot, held):
        which = flipped(self.d, held)
        return pltpu.make_async_remote_copy(
            src_ref=self.place(u, which) if held else self.piece(u),
            dst_ref=self.place(u, which),
            send_sem=self.ds.at[u, (1 << k) - 1 + slot], recv_sem=self.dr.at[u, which],
            device_id={"dp": flipped(self.d, self.order(u)[k : k + 1])}, device_id_type=MESH,
        )

    def arrival(self, u, k, held):
        which = flipped(self.d, held + tuple(self.order(u)[k : k + 1]))
        return pltpu.make_async_remote_copy(
            src_ref=self.piece(u), dst_ref=self.place(u, which),
            send_sem=self.ds.at[u, 0], recv_sem=self.dr.at[u, which],
            device_id={"dp": flipped(self.d, self.order(u)[k : k + 1])}, device_id_type=MESH,
        )

    def units(self, w):
        return range(w * self.parts, (w + 1) * self.parts)

    def begin_round(self, w, k):
        for u in self.units(w):
            for slot, held in enumerate(subsets(self.order(u)[:k])):
                self.start(self.round_copy, u, k, slot, held)

    def collect(self, w):
        self.take(w, self.stages - 1)
        for p in range(self.parts):
            lanes = slice(p * self.cols, (p + 1) * self.cols)
            self.slab[w, p * self.cut : (p + 1) * self.cut] = jnp.concatenate(
                [self.blocks[w, s, :, lanes] for s in range(self.stages)], axis=1
            )
        for u in self.units(w):
            self.own_copy(u).start()

    def advance(self, w, k):
        for u in self.units(w):
            for held in subsets(self.order(u)[:k]):
                self.arrival(u, k, held).wait_recv()
        if k + 1 < self.dp_bits:
            self.begin_round(w, k + 1)
        else:
            for u in self.units(w):
                self.own_copy(u).wait()

    def close(self):
        for make, args, sends in self.sent:
            if sends is None:
                make(*args).wait_send()
            else:

                @pl.when(sends)
                def _():
                    make(*args).wait_send()


def gathering_scratch(count, dp, stages, rows, cols):
    parts = 2 if rows % 32 == 0 else 1
    dma = pltpu.SemaphoreType.DMA
    units = count * parts
    return [
        pltpu.VMEM((count, stages, rows // parts, cols * parts), BF16),
        pltpu.VMEM((count, rows, cols * stages), BF16),
        dma((count, 2 * stages)), dma((count, stages)), dma((units, dp)), dma((units, dp)), dma((units,)),
    ]


def forward_kernel(block, dp_bits, stages, back, *refs):
    weights, refs = refs[:6], refs[6:]
    tokens, vectors, segments = refs[:3]
    gain, factor = vectors.at[0:1], vectors.at[1:2]
    fulls, refs = refs[3:9], refs[9:]
    bias_full, raw_out, q_out, k_out, v_out, nt_out, o_ref, lse_ref = refs[:8]
    refs = refs[8:]
    home, window, normed, nt, raw, q, k, v, vt, ot, bias, scores, tops, totals, bias_in, bias_all = refs[:16]
    xs, xr, bs, br, os = refs[16:21]
    d, z = greet(dp_bits, stages)
    rows, features = tokens.shape
    width, heads = k.shape[0], features // HD
    own = width - rows
    tile = 2 * LANES
    homes = [home.at[w] for w in range(3)] + list(fulls[3:])
    work = Gathering(dp_bits, stages, d, z, weights, homes, refs[21:])

    def bias_copy(step):
        return pltpu.make_async_remote_copy(
            src_ref=bias_in, dst_ref=bias_all.at[step], send_sem=bs.at[step],
            recv_sem=br.at[step], device_id={"mp": lax.rem(z + step, stages)},
            device_id_type=MESH,
        )

    def token_copy(hop):
        return pltpu.make_async_remote_copy(
            src_ref=tokens if hop == 0 else window.at[hop - 1], dst_ref=window.at[hop],
            send_sem=xs.at[hop], recv_sem=xr.at[hop],
            device_id={"mp": jnp.minimum(z + 1, stages - 1)}, device_id_type=MESH,
        )

    kept = [
        (raw, raw_out), (q, q_out), (k, k_out), (v, v_out), (nt, nt_out),
        (home.at[0], fulls[0]), (home.at[1], fulls[1]), (home.at[2], fulls[2]),
    ]

    def keep(i):
        return pltpu.make_async_copy(kept[i][0], kept[i][1], os.at[i])

    def norm(src, at):
        step_rows = 128

        def step(i, carry):
            part = pl.ds(pl.multiple_of(i * step_rows, step_rows), step_rows)
            x = src[part, :].astype(F32)
            value = (x * row_inverse(x) * gain[...]).astype(BF16)
            to = pl.ds(pl.multiple_of(at + i * step_rows, step_rows), step_rows)
            normed[to, :] = value
            return carry

        lax.fori_loop(0, rows // step_rows, step, 0)
        for c in range(features // tile):
            lanes = slice(c * tile, (c + 1) * tile)
            nt[lanes, at : at + rows] = normed[at : at + rows, lanes].T

    def project_both(at):
        def step(c, carry):
            lanes = pl.ds(pl.multiple_of(c * tile, tile), tile)
            source = normed[at : at + rows, :]
            k[at : at + rows, lanes] = dot(source, home[1, :, lanes], 1, 0).astype(BF16)
            value = dot(source, home[2, :, lanes], 1, 0).astype(BF16)
            v[at : at + rows, lanes] = value
            vt[lanes, at : at + rows] = value.T
            return carry

        lax.fori_loop(0, features // tile, step, 0)

    first, rest = range(3), range(3, 6)
    for w in range(6):
        work.pack(w)
    for w in first:
        work.hop(w, 0)
    bias_in[...] = vectors[4:5, : features // stages]
    for step in range(1, stages):
        work.start(bias_copy, step)
    bias_all[0] = bias_in[...]
    for hop in range(back):

        @pl.when(z <= hop)
        def _():
            window[hop] = jnp.zeros((rows, features), BF16)

    norm(tokens, own)
    fill_bias(segments, z, bias, block, own)
    for j in range(1, stages - 1):
        for w in first:
            work.hop(w, j)
    for w in rest:
        work.hop(w, 0)
    for w in first:
        work.collect(w)
        work.begin_round(w, 0)
    for j in range(1, stages - 1):
        if j <= 3 and dp_bits > 1:
            work.advance(j - 1, 0)
        for w in rest:
            work.hop(w, j)

    @pl.when(z < stages - 1)
    def _():
        token_copy(0).start()

    if dp_bits > 1:
        for w in range(max(0, min(stages - 2, 3)), 3):
            work.advance(w, 0)
    for w in rest:
        work.collect(w)
    for r in range(1, dp_bits - 1):
        for w in first:
            work.advance(w, r)
    for w in rest:
        work.begin_round(w, 0)
    for w in first:
        work.advance(w, dp_bits - 1)
        keep(5 + w).start()
        if w == 0:

            def query(c, carry):
                lanes = pl.ds(pl.multiple_of(c * tile, tile), tile)
                value = dot(normed[own:, :], home[0, :, lanes], 1, 0)
                raw[:, lanes] = value
                q[:, lanes] = (value * factor[:, lanes]).astype(BF16)
                return carry

            lax.fori_loop(0, features // tile, query, 0)
            keep(0).start()
            keep(1).start()
        elif w == 2:
            project_both(own)

    sp = spans(rows, width, block)

    def attend(low, high, fresh, last, due):
        tiles = []
        for kb in range(low // block, high // block):
            qs = [i for i, (lo, hi) in enumerate(sp) if lo <= kb * block < hi]
            if qs:
                tiles.append((kb, qs))

        def head(h, scores):
            lanes, mine = head_lanes(h, features)
            feats = pl.ds(pl.multiple_of(h * HD, 16), HD)
            query = jnp.where(mine, q[:, lanes], jnp.zeros((), BF16))
            top = [jnp.full((8, block), FAR, F32) for _ in sp]
            for kb, qs in tiles:
                qa, qz = qs[0] * block, (qs[-1] + 1) * block
                at = slice(kb * block, (kb + 1) * block)
                s = dot(k[at, lanes], query[qa:qz], 1, 1) + bias[at, qa:qz]
                scores[at, qa:qz] = s
                for i in qs:
                    cut = s[:, i * block - qa : (i + 1) * block - qa]
                    top[i] = jnp.maximum(top[i], jnp.max(cut.reshape(block // 8, 8, block), axis=0))
            top = jnp.concatenate([jnp.max(t, axis=0, keepdims=True) for t in top], axis=1)
            if not fresh:
                before = tops[pl.ds(h, 1), :]
                top = jnp.maximum(top, before)
                scale = jnp.exp(before - top)
            acc = [jnp.zeros((HD, block), F32) for _ in sp]
            total = [jnp.zeros((8, block), F32) for _ in sp]
            for kb, qs in tiles:
                qa, qz = qs[0] * block, (qs[-1] + 1) * block
                at = slice(kb * block, (kb + 1) * block)
                p = jnp.exp(scores[at, qa:qz] - top[:, qa:qz])
                part = dot(vt[feats, at], p.astype(BF16), 1, 0)
                for i in qs:
                    cut = slice(i * block - qa, (i + 1) * block - qa)
                    total[i] = total[i] + jnp.sum(p[:, cut].reshape(block // 8, 8, block), axis=0)
                    acc[i] = acc[i] + part[:, cut]
            for i in range(len(sp)):
                at = slice(i * block, (i + 1) * block)
                one = jnp.sum(total[i], axis=0, keepdims=True)
                out = acc[i]
                if not fresh:
                    one = one + totals[pl.ds(h, 1), at] * scale[:, at]
                    out = out + ot[feats, at] * scale[:, at]
                if last:
                    ot[feats, at] = out / one
                    lse_ref[pl.ds(h, 1), at] = top[:, at] + jnp.log(one)
                else:
                    ot[feats, at] = out
                    totals[pl.ds(h, 1), at] = one
                    tops[pl.ds(h, 1), at] = top[:, at]

        def pair(i, carry):
            for at in sorted(set(due.values())):

                @pl.when(2 * i == at)
                def _():
                    for w, r in due:
                        if due[w, r] == at:
                            work.advance(w, r)

            head(2 * i, scores.at[0])
            head(2 * i + 1, scores.at[1])
            return carry

        lax.fori_loop(0, heads // 2, pair, 0)

    inside, ready = {}, []
    if back and dp_bits > 2:
        inside = {(3, 1): heads * 3 // 8, (4, 1): heads * 5 // 8, (5, 1): heads * 7 // 8}
        ready = [(3, 0), (4, 0), (5, 0)]
    for pair in ready[:1]:
        work.advance(*pair)
    for hop in range(back):
        if hop + 1 == back:
            for pair in ready[1:]:
                work.advance(*pair)
            attend(rows, width, True, False, inside)

        @pl.when(z > hop)
        def _():
            token_copy(hop).wait_recv()

        if hop + 1 < back:

            @pl.when((z > hop) & (z < stages - 1))
            def _():
                token_copy(hop + 1).start()

        at = own - (hop + 1) * rows
        norm(window.at[hop], at)
        project_both(at)
    for i in range(2, 5):
        keep(i).start()
    attend(0, rows if back else width, not back, True, {})
    transpose_out(ot, o_ref)
    for r in range(dp_bits):
        for w in rest:
            if (w, r) not in inside and (w, r) not in ready:
                work.advance(w, r)
    for step in range(1, stages):
        bias_copy(step).wait_recv()
    bias_full[...] = jnp.concatenate(
        [bias_all[lax.rem(z - s + stages, stages)] for s in range(stages)], axis=1
    )
    for hop in range(back):

        @pl.when((z >= hop) & (z < stages - 1))
        def _():
            token_copy(hop).wait_send()

    for i in range(len(kept)):
        keep(i).wait()
    work.close()


def attend_forward(weights, tokens, vectors, segments, block, dp, stages, back):
    held, cols = weights[0].shape
    rows, features = tokens.shape
    width, heads = (back + 1) * rows, features // HD
    hbm = pl.BlockSpec(memory_space=pl.ANY)
    vmem = pl.BlockSpec(memory_space=pltpu.VMEM)
    dma = pltpu.SemaphoreType.DMA
    sds = jax.ShapeDtypeStruct
    return pl.pallas_call(
        functools.partial(forward_kernel, block, dp.bit_length() - 1, stages, back),
        in_specs=[vmem] * 9,
        out_specs=[hbm] * 6 + [vmem] + [hbm] * 5 + [vmem] * 2,
        out_shape=[sds((features, features), BF16)] * 6
        + [
            sds((1, features), F32),
            sds((rows, features), F32),
            sds((rows, features), BF16),
            sds((width, features), BF16),
            sds((width, features), BF16),
            sds((features, width), BF16),
            sds((rows, features), BF16),
            sds((heads, rows), F32),
        ],
        scratch_shapes=[
            pltpu.VMEM((3, features, features), BF16),
            pltpu.VMEM((back, rows, features), BF16),
            pltpu.VMEM((width, features), BF16),
            pltpu.VMEM((features, width), BF16),
            pltpu.VMEM((rows, features), F32),
            pltpu.VMEM((rows, features), BF16),
            pltpu.VMEM((width, features), BF16),
            pltpu.VMEM((width, features), BF16),
            pltpu.VMEM((features, width), BF16),
            pltpu.VMEM((features, rows), F32),
            pltpu.VMEM((width, rows), F32),
            pltpu.VMEM((2, width, rows), F32),
            pltpu.VMEM((heads, rows), F32),
            pltpu.VMEM((heads, rows), F32),
            pltpu.VMEM((1, features // stages), F32),
            pltpu.VMEM((stages, 1, features // stages), F32),
            dma((back,)), dma((back,)), dma((stages,)), dma((stages,)), dma((8,)),
        ]
        + gathering_scratch(6, dp, stages, held, cols),
        compiler_params=pltpu.CompilerParams(
            collective_id=0, has_side_effects=True, vmem_limit_bytes=62 << 20
        ),
        name="attend_forward",
    )(*weights, tokens, vectors, segments)


def middle_kernel(block, dp_bits, stages, *refs):
    sources, refs = refs[:12], refs[12:]
    b_up, vectors, lse_ref, segments = refs[:4]
    factor, gain, b_down = (vectors.at[i : i + 1] for i in (1, 2, 3))
    results, incoming, outs, sums, refs = refs[4:10], refs[10], refs[11:14], refs[14], refs[15:]
    weights, hidden, wide, tmp, tr, keys, values, query_in, grad_in, bias, delta_ref = refs[:11]
    ps, pr, sems, refs = refs[11], refs[12], refs[13], refs[14:]
    d, z = greet(dp_bits, stages)
    work = Reduction(dp_bits, stages, d, z, None, outs, refs)
    rows, features = query_in.shape
    heads, width = features // HD, keys.shape[0]
    back = width // rows - 1
    tile = 2 * LANES
    w_out, w_up, w_down = weights.at[0], weights.at[1], weights.at[2]
    w_key, w_value = weights.at[2], weights.at[1]
    mixed, cot, x, second, active, d_pre, d_attn, spare = (tmp.at[i] for i in range(8))
    dk, dv = tmp.at[: back + 1], tmp.at[back + 1 : 2 * back + 2]
    dq, part = tmp.at[2 * back + 2], tmp.at[2 * back + 3]
    inside = (
        mixed, w_out, x, cot, w_up, w_down, keys, values, query_in, w_key, w_value, hidden,
    )
    half = rows // 2
    outside = (spare, hidden, dq, dk, dv, part.at[half:])
    loads = Loads(list(zip(sources, inside)) + list(zip(outside, results)), sems)
    loads.start(0, 1, 2)
    fill_bias(segments, z, bias, block, width - rows)

    def by_tile(body):
        for c in range(features // tile):
            body(slice(c * tile, (c + 1) * tile), c)

    def by_rows(body, start):
        def step(i, carry):
            return body(pl.ds(pl.multiple_of(i * 64, 64), 64), carry)

        return lax.fori_loop(0, rows // 64, step, start)

    def flip(src):
        for c in range(features // tile):
            lanes = slice(c * tile, (c + 1) * tile)
            tr[lanes, :] = src[:, lanes].T

    nothing = jnp.zeros((1, features), F32)

    def add_attention(lanes, c):
        hidden[:, lanes] = x[:, lanes].astype(F32) + dot(mixed[...], w_out[lanes, :], 1, 1)

    def norm(at, carry):
        h = hidden[at, :]
        second[at, :] = (h * row_inverse(h) * gain[...]).astype(BF16)
        return carry

    def activate(lanes, c):
        pre = dot(second[...], w_up[:, lanes], 1, 0) + b_up[:, lanes]
        sigma = 1.0 / (1.0 + jnp.exp(-pre))
        active[:, lanes] = (pre * sigma).astype(BF16)
        grad = dot(cot[...], w_down[:, lanes], 1, 0)
        grad = (grad * sigma * (1.0 + pre * (1.0 - sigma))).astype(BF16)
        d_pre[:, lanes] = grad
        sums[2:3, lanes] = jnp.sum(grad.astype(F32), axis=0, keepdims=True)

    def finish_layer(lanes, c):
        out = dot(active[...], w_down[lanes, :], 1, 1)
        spare[:, lanes] = (hidden[:, lanes] + out + b_down[:, lanes]).astype(BF16)
        sums[1:2, lanes] = jnp.sum(cot[:, lanes].astype(F32), axis=0, keepdims=True)

    def to_second(lanes, c):
        wide[:, lanes] = dot(d_pre[...], w_up[lanes, :], 1, 1)

    def to_hidden(at, column):
        h, grad = hidden[at, :], wide[at, :]
        inverse = row_inverse(h)
        weighted = grad * gain[...]
        dots = jnp.sum(weighted * h, axis=1, keepdims=True)
        cube = inverse * inverse * inverse
        d_hidden = cot[at, :].astype(F32) + inverse * weighted - h * cube / features * dots
        hidden[at, :] = d_hidden
        d_attn[at, :] = d_hidden.astype(BF16)
        return column + jnp.sum(grad * h * inverse, axis=0, keepdims=True)

    def to_mixed(lanes, c):
        grad = dot(d_attn[...], w_out[:, lanes], 1, 0).astype(BF16)
        grad_in[:, lanes] = grad
        both = grad.astype(F32) * mixed[:, lanes].astype(F32)
        lane = lax.broadcasted_iota(jnp.int32, (heads, tile), 1) + c * tile
        first = lax.broadcasted_iota(jnp.int32, (heads, tile), 0) * HD
        owner = jnp.where((lane >= first) & (lane < first + HD), 1.0, 0.0).astype(BF16)
        high = both.astype(BF16)
        rest = (both - high.astype(F32)).astype(BF16)
        delta_ref[...] += dot(owner, high, 1, 1) + dot(owner, rest, 1, 1)

    sums[3:8, :] = jnp.zeros((5, features), F32)
    delta_ref[...] = jnp.zeros_like(delta_ref)
    loads.wait(0, 1, 2)
    loads.start(3, 4, 5)
    by_tile(add_attention)
    by_rows(norm, 0)
    loads.wait(3, 4, 5)
    loads.start(6, 7, 8)
    by_tile(activate)
    flip(cot)
    work.weight_grad(0, lambda at: tr[at, :], lambda: active[...])
    by_tile(finish_layer)
    loads.start(12, 9)
    by_tile(to_second)
    loads.start(10)
    flip(second)
    work.weight_grad(1, lambda at: tr[at, :], lambda: d_pre[...])
    work.advance(0, 0)
    sums[0:1, :] = by_rows(to_hidden, nothing)
    loads.start(13)
    by_tile(to_mixed)
    flip(d_attn)
    work.weight_grad(2, lambda at: tr[at, :], lambda: mixed[...])
    work.advance(1, 0)
    if dp_bits > 1:
        work.advance(0, 1)
    loads.wait(12)
    for c in range(2 * back + 2):
        tmp[c] = jnp.zeros((rows, features), BF16)
    wide[...] = jnp.zeros_like(wide)
    loads.wait(6, 7, 8)
    sp = spans(rows, width, block)
    steps = heads * (back + 1)
    events = [(2, 0)] + [(w, k) for w in range(3) for k in range(1, dp_bits) if (w, k) != (0, 1)]
    due = {i: int(at * steps) // 2 * 2 for i, at in enumerate(EVENTS[: len(events)])}

    def down():
        return pltpu.make_async_remote_copy(
            src_ref=part.at[:half], dst_ref=incoming, send_sem=ps, recv_sem=pr,
            device_id={"mp": jnp.maximum(z - 1, 0)}, device_id_type=MESH,
        )

    for c in range(back + 1):

        def head(h):
            lanes, mine = head_lanes(h, features)
            zero = jnp.zeros((), BF16)
            query = jnp.where(mine, query_in[:, lanes], zero)
            grad = jnp.where(mine, grad_in[:, lanes], zero)
            lse = lse_ref[pl.ds(h, 1), :]
            delta = delta_ref[pl.ds(h, 1), :]
            for kb in range(c * rows // block, (c + 1) * rows // block):
                qs = [i for i, (lo, hi) in enumerate(sp) if lo <= kb * block < hi]
                if not qs:
                    continue
                qa, qz = qs[0] * block, (qs[-1] + 1) * block
                at = slice(kb * block, (kb + 1) * block)
                to = slice(kb * block - c * rows, (kb + 1) * block - c * rows)
                key = keys[at, lanes]
                s = dot(key, query[qa:qz], 1, 1) + bias[at, qa:qz]
                p = jnp.exp(s - lse[:, qa:qz])
                dp = dot(values[at, lanes], grad[qa:qz], 1, 1)
                ds = (p * (dp - delta[:, qa:qz])).astype(BF16)
                dv[c, to, lanes] += dot(p.astype(BF16), grad[qa:qz], 1, 0).astype(BF16)
                dk[c, to, lanes] += dot(ds, query[qa:qz], 1, 0).astype(BF16)
                wide[qa:qz, lanes] += dot(ds, jnp.where(mine, key, zero), 0, 0)

        def pair(i, carry):
            for at in sorted(set(due.values())):
                if at // heads != c:
                    continue

                @pl.when(2 * i == at % heads)
                def _():
                    for e in due:
                        if due[e] == at:
                            work.advance(*events[e])

            head(2 * i)
            head(2 * i + 1)
            return carry

        lax.fori_loop(0, heads // 2, pair, 0)
        if c == 0:
            loads.wait(9, 10)
            if back:
                back_project(part, ((dk.at[0], w_key), (dv.at[0], w_value)), 0, None)
                loads.start(17)

                @pl.when(z >= back)
                def _():
                    down().start()

            loads.wait(13)
            loads.start(11)

    loads.start(15, 16)
    loads.wait(11)

    def to_query(at, column):
        scaled = wide[at, :].astype(BF16).astype(F32)
        dq[at, :] = (scaled * factor[...]).astype(BF16)
        return column + jnp.sum(scaled * hidden[at, :], axis=0, keepdims=True)

    sums[4:5, :] = by_rows(to_query, nothing)
    loads.start(14)
    for i in range(len(due), len(events)):
        work.advance(*events[i])
    for w in range(3):
        work.finish(w)
    loads.wait(14, 15, 16)
    if back:
        loads.wait(17)

        @pl.when((z + 1 >= back) & (z < stages - 1))
        def _():
            down().wait_recv()

        @pl.when(z >= back)
        def _():
            down().wait_send()

    work.close()


def back_project(out, pairs, at, more):
    rows, features = out.shape
    tile = 2 * LANES

    def step(c, carry):
        lanes = pl.ds(pl.multiple_of(c * tile, tile), tile)
        value = None
        for grad, weight in pairs:
            start = at if grad.shape[0] > rows else 0
            term = dot(grad[start : start + rows, :], weight[lanes, :], 1, 1)
            value = term if value is None else value + term
        if more is not None:
            value = value + more(lanes)
        out[:, lanes] = value.astype(out.dtype)
        return carry

    lax.fori_loop(0, features // tile, step, 0)


def middle(
    mixed, w_out, x, cot, w_up, w_down, k, v, q, w_key, w_value, raw, b_up, vectors,
    lse, segments, block, dp, stages,
):
    rows, features = q.shape
    width, heads = k.shape[0], features // HD
    held, cols = features // dp, features // stages
    chunks = width // rows
    hbm = pl.BlockSpec(memory_space=pl.ANY)
    vmem = pl.BlockSpec(memory_space=pltpu.VMEM)
    dma = pltpu.SemaphoreType.DMA
    sds = jax.ShapeDtypeStruct
    low, high = sds((rows, features), BF16), sds((rows, features), F32)
    many, part = sds((chunks, rows, features), BF16), sds((rows // 2, features), BF16)
    return pl.pallas_call(
        functools.partial(middle_kernel, block, dp.bit_length() - 1, stages),
        in_specs=[hbm] * 12 + [vmem] * 4,
        out_specs=[hbm] * 7 + [vmem] * 4,
        out_shape=[low, high, low, many, many, part, part]
        + [sds((held, cols), F32)] * 3
        + [sds((8, features), F32)],
        scratch_shapes=[
            pltpu.VMEM((3, features, features), BF16),
            pltpu.VMEM((rows, features), F32),
            pltpu.VMEM((rows, features), F32),
            pltpu.VMEM((max(8, 2 * chunks + 2), rows, features), BF16),
            pltpu.VMEM((features, rows), BF16),
            pltpu.VMEM((width, features), BF16),
            pltpu.VMEM((width, features), BF16),
            pltpu.VMEM((rows, features), BF16),
            pltpu.VMEM((rows, features), BF16),
            pltpu.VMEM((width, rows), F32),
            pltpu.VMEM((heads, rows), F32),
            dma, dma, dma((18,)),
        ]
        + reduction_scratch(3, dp, stages, held, features, True),
        compiler_params=pltpu.CompilerParams(
            collective_id=2, has_side_effects=True, vmem_limit_bytes=63 << 20
        ),
        name="middle",
    )(
        mixed, w_out, x, cot, w_up, w_down, k, v, q, w_key, w_value, raw, b_up, vectors,
        lse, segments,
    )


def input_kernel(dp_bits, stages, back, *refs):
    sources, farther, vectors, sums, refs = refs[:10], refs[10], refs[11], refs[12], refs[13:]
    gain = vectors.at[0:1]
    outs, result, total, refs = refs[:3], refs[3], refs[4], refs[5:]
    inside, tokens_grad, refs = refs[:10], refs[10], refs[11:]
    dv, nt, dk, wk, wv, incoming, dq, wq, tokens, d_hidden = inside
    part, landed, d_first, sgot, ss, sr, ps, pr, sems = refs[:9]
    d, z = greet(dp_bits, stages)
    work = Reduction(dp_bits, stages, d, z, None, outs, refs[9:])
    rows, features = tokens.shape
    own, half = back * rows, rows // 2
    inside = inside[:5] + (incoming.at[:half],) + inside[6:]
    loads = Loads(list(zip(sources, inside)) + [(tokens_grad, result)], sems)
    levels = dp_bits + stages.bit_length() - 1
    held = features >> dp_bits
    grads = ((dv, 2, 0), (dk, 1, 0), (dq, 0, own))

    def down(hop):
        return pltpu.make_async_remote_copy(
            src_ref=part.at[hop - 1] if hop else farther,
            dst_ref=landed.at[hop - 1] if hop else incoming.at[half:],
            send_sem=ps.at[hop], recv_sem=pr.at[hop],
            device_id={"mp": jnp.maximum(z - 1, 0)}, device_id_type=MESH,
        )

    if back:

        @pl.when(z >= back)
        def _():
            down(0).start()

    loads.start(0, 1)

    def arrived(hop):
        source = incoming if hop == 1 else landed.at[hop - 2]
        there = (z + 1 >= back - hop + 1) & (z < stages - 1)

        def take(lanes):
            return jnp.where(there, source[:, lanes].astype(F32), 0.0)

        return there, take

    def weight_grad(i):
        grad, w, at = grads[i]
        work.weight_grad(w, lambda rows_at: nt[rows_at, at:], lambda: grad[...])

    def sum_copy(k):
        if k < dp_bits:
            to = {"dp": flipped(d, (k,))}
        else:
            to = {"mp": flipped(z, (k - dp_bits,))}
        return pltpu.make_async_remote_copy(
            src_ref=total.at[k], dst_ref=sgot.at[k], send_sem=ss.at[k], recv_sem=sr.at[k],
            device_id=to, device_id_type=MESH,
        )

    def sum_step(k):
        sum_copy(k).wait_recv()
        total[k + 1] = total[k] + sgot[k]
        if k + 1 < levels:
            work.start(sum_copy, k + 1)

    def pass_down(hop):
        there, take = arrived(hop)

        @pl.when(there)
        def _():
            down(hop - 1).wait_recv()

        back_project(part.at[hop - 1], ((dk, wk), (dv, wv)), hop * rows, take)

        @pl.when(z >= back - hop)
        def _():
            down(hop).start()

    loads.wait(0, 1)
    loads.start(2, 3, 4, 5)
    weight_grad(0)
    loads.start(6, 7, 8, 9)
    loads.wait(2)
    weight_grad(1)
    work.advance(2, 0)
    loads.wait(3, 4, 5)
    if back > 1:
        pass_down(1)
    work.advance(1, 0)
    loads.wait(6, 7)
    weight_grad(2)
    for hop in range(2, back):
        pass_down(hop)
    work.advance(0, 0)
    back_project(d_first, ((dk, wk), (dv, wv), (dq, wq)), own, None)
    events = [(w, k) for w in (2, 1, 0) for k in range(1, dp_bits)]
    for event in events[:1]:
        work.advance(*event)
    loads.wait(8, 9)
    there, take = arrived(back) if back else (None, None)
    if back:

        @pl.when(there)
        def _():
            down(back - 1).wait_recv()

    chunk = 64

    def finish(i, column):
        at = pl.ds(pl.multiple_of(i * chunk, chunk), chunk)
        x = tokens[at, :].astype(F32)
        grad = d_first[at, :]
        if back:
            source = incoming if back == 1 else landed.at[back - 2]
            grad = grad + jnp.where(there, source[at, :].astype(F32), 0.0)
        inverse = row_inverse(x)
        weighted = grad * gain[...]
        dots = jnp.sum(weighted * x, axis=1, keepdims=True)
        cube = inverse * inverse * inverse
        tokens_grad[at, :] = (
            d_hidden[at, :] + inverse * weighted - x * cube / features * dots
        ).astype(BF16)
        return column + jnp.sum(grad * x * inverse, axis=0, keepdims=True)

    column = lax.fori_loop(0, rows // chunk, finish, jnp.zeros((1, features), F32))
    total[0] = sums[...]
    total[0, 3:4, :] = column
    work.start(sum_copy, 0)
    loads.start(10)
    done = 0
    for event in events[1:]:
        work.advance(*event)
        if done < levels:
            sum_step(done)
            done += 1
    for k in range(done, levels):
        sum_step(k)
    for w in (2, 1, 0):
        work.finish(w)
    for hop in range(back):

        @pl.when(z >= back - hop)
        def _():
            down(hop).wait_send()

    loads.wait(10)
    work.close()


def input_gradients(
    nt, dq, dk, dv, wq, wk, wv, incoming, farther, tokens, d_hidden, vectors, sums, dp, stages
):
    rows, features = tokens.shape
    back = dk.shape[0] // rows - 1
    held, cols = features // dp, features // stages
    dp_bits = dp.bit_length() - 1
    levels = dp_bits + stages.bit_length() - 1
    hbm = pl.BlockSpec(memory_space=pl.ANY)
    vmem = pl.BlockSpec(memory_space=pltpu.VMEM)
    dma = pltpu.SemaphoreType.DMA
    hops = max(1, back - 1)
    sources = (dv, nt, dk, wk, wv, incoming, dq, wq, tokens, d_hidden)
    out = pl.pallas_call(
        functools.partial(input_kernel, dp_bits, stages, back),
        in_specs=[hbm] * 11 + [vmem] * 2,
        out_specs=[vmem] * 3 + [hbm, vmem],
        out_shape=[jax.ShapeDtypeStruct((held, cols), F32)] * 3
        + [
            jax.ShapeDtypeStruct((rows, features), BF16),
            jax.ShapeDtypeStruct((levels + 1,) + sums.shape, F32),
        ],
        scratch_shapes=[pltpu.VMEM(tokens.shape if a is incoming else a.shape, a.dtype) for a in sources + (tokens,)]
        + [
            pltpu.VMEM((hops, rows, features), BF16), pltpu.VMEM((hops, rows, features), BF16),
            pltpu.VMEM((rows, features), F32), pltpu.VMEM((levels,) + sums.shape, F32),
            dma((levels,)), dma((levels,)), dma((hops + 1,)), dma((hops + 1,)), dma((11,)),
        ]
        + reduction_scratch(3, dp, stages, held, features, True),
        compiler_params=pltpu.CompilerParams(
            collective_id=1, has_side_effects=True, vmem_limit_bytes=62 << 20
        ),
        name="input_gradients",
    )(*sources, farther, vectors, sums)
    return out[:3], out[3], out[4][levels]


def hand_over_kernel(*refs):
    half = len(refs) // 2
    for source, result in zip(refs[:half], refs[half:]):
        result[...] = source[...]


def hand_over(arrays):
    steps = 4 if all(a.shape[0] % 64 == 0 or (a.shape[0] % 32 == 0 and a.dtype == F32) for a in arrays) else 1
    specs = [pl.BlockSpec((a.shape[0] // steps, a.shape[1]), lambda i: (i, 0)) for a in arrays]
    return pl.pallas_call(
        hand_over_kernel,
        grid=(steps,),
        in_specs=specs,
        out_specs=specs,
        out_shape=[jax.ShapeDtypeStruct(a.shape, a.dtype) for a in arrays],
        name="hand_over",
    )(*arrays)


def body(
    tokens, segments, w_query, w_key, w_value, w_output, w_up, b_up, w_down, b_down,
    gain_attn, gain_mlp, query_scale, cotangent,
):
    stages = lax.axis_size("mp")
    z = lax.axis_index("mp")
    rows, features = tokens.shape
    back = min(stages - 1, -(-(DOC_MAX - 1) // rows))
    own = back * rows
    block = min(256, rows)
    heads = features // HD
    dp = lax.axis_size("dp")
    factor = jax.nn.softplus(query_scale) * (LOG2E / math.sqrt(HD))
    mine = b_up.shape[0]
    vectors = jnp.zeros((8, features), F32)
    row = lax.broadcasted_iota(jnp.int32, (8, features), 0)
    given = (gain_attn, jnp.tile(factor, heads), gain_mlp, b_down, jnp.pad(b_up, (0, features - mine)))
    for i, value in enumerate(given):
        vectors = jnp.where(row == i, value[None], vectors)
    (
        wq, wk, wv, wu, wo, wd, b_full, query_raw, scaled, keys, values, first_t, mixed, lse
    ) = attend_forward(
        (w_query, w_key, w_value, w_up, w_output.T, w_down.T), tokens, vectors, segments,
        block, dp, stages, back,
    )
    layer_out, d_hidden, d_query, d_keys, d_values, farther, incoming, *mlp, sums = middle(
        mixed, wo, tokens, cotangent, wu, wd, keys, values, scaled, wk, wv, query_raw,
        b_full, vectors, lse, segments, block, dp, stages,
    )
    grads, tokens_grad, sums = input_gradients(
        first_t, d_query, d_keys.reshape(own + rows, features),
        d_values.reshape(own + rows, features), wq, wk, wv, incoming, farther, tokens,
        d_hidden, vectors, sums, dp, stages,
    )
    sum_b_up = lax.dynamic_slice_in_dim(sums[2], z * mine, mine, 0)
    scale_total = jnp.sum(sums[4].reshape(heads, HD), axis=0)
    grad_query_scale = scale_total * (LOG2E / math.sqrt(HD)) * jax.nn.sigmoid(query_scale)
    layer_out, tokens_grad, g_query, g_key, g_value, g_up, g_output, g_down = hand_over(
        (layer_out, tokens_grad, *grads, mlp[1], mlp[2], mlp[0])
    )
    return (
        layer_out, tokens_grad, g_query, g_key, g_value, g_output.T, g_up, sum_b_up,
        g_down.T, sums[1], sums[3], sums[0], grad_query_scale,
    )


def solution(mesh):
    tokens, rows_dp, rows_mp = P(("dp", "mp"), None), P("dp", "mp"), P("mp", "dp")
    return jax.shard_map(
        body,
        mesh=mesh,
        in_specs=(
            tokens, P("dp", None), rows_dp, rows_dp, rows_dp, rows_mp, rows_dp, P("mp"), rows_mp,
            P(), P(), P(), P(), tokens,
        ),
        out_specs=(
            tokens, tokens, rows_dp, rows_dp, rows_dp, rows_mp, rows_dp, P("mp"), rows_mp,
            P(), P(), P(), P(),
        ),
        check_vma=False,
    )
```

```python
import functools
import math

import jax
import jax.numpy as jnp
from jax import lax
from jax.experimental import pallas as pl
from jax.experimental.pallas import tpu as pltpu
from jax.sharding import PartitionSpec as P

HD = 80
LANES = 128
EPSILON = 1e-06
LOG2E = 1.442695
DOC_MAX = 1024
FAR = -1e30
EVENTS = (0.15, 0.3, 0.5, 0.6, 0.75, 0.9)
F32 = jnp.float32
BF16 = jnp.bfloat16


def dot(a, b, ca, cb):
    return lax.dot_general(a, b, (((ca,), (cb,)), ((), ())), preferred_element_type=F32)


def row_inverse(values):
    return lax.rsqrt(jnp.mean(values * values, axis=1, keepdims=True) + EPSILON)


MESH = pl.DeviceIdType.MESH


def bit_of(index, b):
    return lax.rem(lax.div(index, 1 << b), 2)


def flipped(index, bits):
    for b in bits:
        index = index + (1 << b) * (1 - 2 * bit_of(index, b))
    return index


def split_order(count, turn):
    bits = list(range(count))
    rest = bits[1:][::-1]
    turn = turn % max(1, len(rest))
    return bits[:1] + rest[turn:] + rest[:turn]


def subsets(bits):
    out = [()]
    for b in bits:
        out = out + [s + (b,) for s in out]
    return out


def greet(dp_bits, stages, everyone=False):
    d, z = lax.axis_index("dp"), lax.axis_index("mp")
    barrier = pltpu.get_barrier_semaphore()
    dp = 1 << dp_bits
    if everyone:
        peers = [lax.rem(d + step, dp) for step in range(1, dp)]
    else:
        peers = [flipped(d, (b,)) for b in range(dp_bits)]
    for peer in peers:
        pl.semaphore_signal(barrier, device_id={"dp": peer}, device_id_type=MESH)
    for step in range(1, stages):
        pl.semaphore_signal(
            barrier, device_id={"mp": lax.rem(z + step, stages)}, device_id_type=MESH
        )
    pl.semaphore_wait(barrier, len(peers) + stages - 1)
    return d, z


class Loads:
    def __init__(self, pairs, sems):
        self.pairs, self.sems = pairs, sems

    def copy(self, i):
        return pltpu.make_async_copy(self.pairs[i][0], self.pairs[i][1], self.sems.at[i])

    def start(self, *which):
        for i in which:
            self.copy(i).start()

    def wait(self, *which):
        for i in which:
            self.copy(i).wait()


class Reduction:
    def __init__(self, dp_bits, stages, d, z, grads, outs, refs):
        self.dp_bits, self.stages, self.d, self.z = dp_bits, stages, d, z
        self.grads, self.outs = grads, outs
        self.pool = refs[0]
        self.kept, self.got = refs[0].at[0], refs[1 : 1 + dp_bits]
        self.zsend, self.zgot, self.ks, self.rs, self.rr, self.zs, self.zr = refs[1 + dp_bits :]
        self.half = 1 << (dp_bits - 1)
        self.parts = self.kept.shape[0] // len(outs)
        self.rows, self.features = self.kept.shape[2], self.kept.shape[3]
        self.sent = []

    def start(self, make, *args):
        make(*args).start()
        self.sent.append((make, args))

    def order(self, u):
        return split_order(self.dp_bits, u % self.parts)

    def place(self, u, slot, low):
        rest = self.order(u)[1:]
        at = low
        for i, b in enumerate(rest):
            if slot >> (len(rest) - 1 - i) & 1:
                at = at + (1 << b)
        return at

    def slot_of(self, u, index):
        rest = self.order(u)[1:]
        return sum(bit_of(index, b - 1) << (len(rest) - 1 - i) for i, b in enumerate(rest))

    def source(self, u, slot, low):
        cut = pl.ds(u % self.parts * self.rows, self.rows)
        return self.grads[u // self.parts].at[self.place(u, slot, low), cut]

    def first_copy(self, u, slot):
        return pltpu.make_async_remote_copy(
            src_ref=self.pool.at[1, u, slot]
            if self.grads is None
            else self.source(u, slot, 1 - bit_of(self.d, 0)),
            dst_ref=self.got[0].at[u, slot],
            send_sem=self.rs.at[u, slot], recv_sem=self.rr.at[u, slot],
            device_id={"dp": flipped(self.d, (0,))}, device_id_type=MESH,
        )

    def keep_copy(self, u, slot):
        return pltpu.make_async_copy(
            self.source(u, slot, bit_of(self.d, 0)), self.kept.at[u, slot], self.ks.at[u, slot]
        )

    def round_copy(self, u, k):
        count = self.half >> k
        b = self.order(u)[k]
        other = 1 - bit_of(self.d, b)
        return pltpu.make_async_remote_copy(
            src_ref=self.got[k - 1].at[u, pl.ds(other * count, count)],
            dst_ref=self.got[k].at[u],
            send_sem=self.rs.at[u, self.half + k], recv_sem=self.rr.at[u, self.half + k],
            device_id={"dp": flipped(self.d, (b,))}, device_id_type=MESH,
        )

    def last_copy(self, w, step):
        to = lax.rem(self.z + step, self.stages)
        return pltpu.make_async_remote_copy(
            src_ref=self.zsend.at[w, to], dst_ref=self.zgot.at[w, step],
            send_sem=self.zs.at[w, step], recv_sem=self.zr.at[w, step],
            device_id={"mp": to}, device_id_type=MESH,
        )

    def units(self, w):
        return range(w * self.parts, (w + 1) * self.parts)

    def begin(self, w):
        for u in self.units(w):
            for slot in range(self.half):
                self.start(self.first_copy, u, slot)
                if self.grads is not None:
                    self.keep_copy(u, slot).start()

    def add(self, dst, src, count):
        def step(i, carry):
            dst[i] = dst[i] + src(i)
            return carry

        lax.fori_loop(0, count, step, 0)

    def take(self, w, k):
        for u in self.units(w):
            count = self.half >> k
            if k == 0:
                for slot in range(self.half):
                    if self.grads is not None:
                        self.keep_copy(u, slot).wait()
                    self.first_copy(u, slot).wait_recv()
                self.add(self.got[0].at[u], lambda i: self.kept[u, i], count)
            else:
                self.round_copy(u, k).wait_recv()
                mine = bit_of(self.d, self.order(u)[k]) * count
                self.add(self.got[k].at[u], lambda i: self.got[k - 1][u, mine + i], count)

    def send(self, w, k):
        for u in self.units(w):
            self.start(self.round_copy, u, k)

    def advance(self, w, k):
        self.take(w, k)
        if k + 1 == self.dp_bits:
            self.begin_last(w)
        else:
            self.send(w, k + 1)

    def put(self, w, index, value):
        held = self.parts * self.rows
        for low in range(2):
            which = lax.rem(bit_of(self.d, 0) + low, 2)
            for u in self.units(w):
                cut = low * held + u % self.parts * self.rows
                self.pool[which, u, self.slot_of(u, index)] = value[cut : cut + self.rows]

    def weight_grad(self, w, left, right):
        held = self.parts * self.rows

        def step(t, carry):
            at = pl.ds(pl.multiple_of(t * 2 * held, 2 * held), 2 * held)
            self.put(w, t, dot(left(at), right(), 1, 0).astype(BF16))
            return carry

        lax.fori_loop(0, 1 << (self.dp_bits - 1), step, 0)
        self.begin(w)

    def begin_last(self, w):
        cols = self.features // self.stages
        whole = [self.got[self.dp_bits - 1][u, 0] for u in self.units(w)]
        for s in range(self.stages):
            self.zsend[w, s] = jnp.concatenate(
                [piece[:, s * cols : (s + 1) * cols] for piece in whole], axis=1
            )
        for step in range(1, self.stages):
            self.start(self.last_copy, w, step)

    def finish(self, w):
        value = self.zsend[w, self.z].astype(F32)
        for step in range(1, self.stages):
            self.last_copy(w, step).wait_recv()
            value = value + self.zgot[w, step].astype(F32)
        cols = self.features // self.stages
        for p in range(self.parts):
            at = slice(p * self.rows, (p + 1) * self.rows)
            self.outs[w][at, :] = value[:, p * cols : (p + 1) * cols]

    def close(self):
        for make, args in self.sent:
            make(*args).wait_send()


def reduction_scratch(count, dp, stages, rows, features, local=False):
    dp_bits, half, cols = dp.bit_length() - 1, dp // 2, features // stages
    parts = 2 if rows % 32 == 0 else 1
    dma = pltpu.SemaphoreType.DMA
    units = count * parts
    return (
        [pltpu.VMEM((1 + local, units, half, rows // parts, features), BF16)]
        + [pltpu.VMEM((units, half >> k, rows // parts, features), BF16) for k in range(dp_bits)]
        + [pltpu.VMEM((count, stages, rows // parts, cols * parts), BF16)] * 2
        + [
            dma((units, half)), dma((units, half + dp_bits)), dma((units, half + dp_bits)),
            dma((count, stages)), dma((count, stages)),
        ]
    )


def spans(rows, width, block):
    own = width - rows
    out=[]
    for qb in range(rows//block):
        hi = own + (qb+1)*block
        lo = max(0, (own + qb*block - (DOC_MAX-1))//block*block)
        out.append((lo,hi))
    return out

def head_lanes(h, features):
    first = h*HD
    off = jnp.minimum(lax.div(first, LANES)*LANES, features-2*LANES)
    off = pl.multiple_of(off, LANES)
    lane = lax.broadcasted_iota(jnp.int32,(1,2*LANES),1) + (off-first)
    return pl.ds(off, 2*LANES), (lane>=0)&(lane<HD)

def fill_bias(segments, z, bias, block, own):
    width, rows = bias.shape
    first = z * rows
    for kb in range(width // block):
        start = first + (kb * block - own)
        at = pl.ds(pl.multiple_of(jnp.maximum(start, 0), block), block)
        col = jnp.broadcast_to(segments[:, at], (block, block)).T
        sub = lax.broadcasted_iota(jnp.int32, (block, block), 0) + kb * block
        for qb in range(rows // block):
            row = segments[:, pl.ds(pl.multiple_of(first + qb * block, block), block)]
            last = lax.broadcasted_iota(jnp.int32, (block, block), 1) + (own + qb * block)
            allowed = (col == row) & (sub <= last) & (start >= 0)
            bias[kb * block : (kb + 1) * block, qb * block : (qb + 1) * block] = jnp.where(
                allowed, 0.0, FAR
            )


def transpose_out(src, dst):
    for i in range(src.shape[0]//LANES):
        at = slice(i*LANES,(i+1)*LANES)
        dst[:, at] = src[at,:].T.astype(dst.dtype)

class Gathering:
    def __init__(self, dp_bits, stages, d, z, weights, homes, refs):
        self.dp_bits, self.stages, self.d, self.z = dp_bits, stages, d, z
        self.weights, self.homes = weights, homes
        self.blocks, self.slab, self.zs, self.zr, self.ds, self.dr, self.ls = refs
        self.rows, self.cols = weights[0].shape
        self.parts = self.ds.shape[0] // len(weights)
        self.cut = self.rows // self.parts
        self.sent = []

    def start(self, make, *args):
        make(*args).start()
        self.sent.append((make, args, None))

    def order(self, u):
        return split_order(self.dp_bits, u % self.parts)[::-1]

    def hop_copy(self, w, j, way):
        at = lax.rem(self.z - way * j + self.stages, self.stages)
        to = lax.rem(self.z + way + self.stages, self.stages)
        return pltpu.make_async_remote_copy(
            src_ref=self.blocks.at[w, at], dst_ref=self.blocks.at[w, at],
            send_sem=self.zs.at[w, 2 * j + (way + 1) // 2], recv_sem=self.zr.at[w, at],
            device_id={"mp": to}, device_id_type=MESH,
        )

    def there(self, j, way):
        return self.z >= j if way == 1 else self.z < self.stages - j

    def pack(self, w):
        pieces = [self.weights[w][p * self.cut : (p + 1) * self.cut] for p in range(self.parts)]
        self.blocks[w, self.z] = jnp.concatenate(pieces, axis=1)

    def take(self, w, j):
        for way in (1, -1):

            @pl.when(self.there(j, way))
            def _():
                self.hop_copy(w, j, way).wait_recv()

    def hop(self, w, j):
        if j:
            self.take(w, j)
        for way in (1, -1):
            sends = self.there(j, way) & self.there(1, -way)

            @pl.when(sends)
            def _():
                self.hop_copy(w, j, way).start()

            self.sent.append((self.hop_copy, (w, j, way), sends))

    def place(self, u, which):
        at = which * self.rows + u % self.parts * self.cut
        return self.homes[u // self.parts].at[pl.ds(pl.multiple_of(at, self.cut), self.cut)]

    def piece(self, u):
        at = u % self.parts * self.cut
        return self.slab.at[u // self.parts, pl.ds(at, self.cut)]

    def own_copy(self, u):
        return pltpu.make_async_copy(self.piece(u), self.place(u, self.d), self.ls.at[u])

    def round_copy(self, u, k, slot, held):
        which = flipped(self.d, held)
        return pltpu.make_async_remote_copy(
            src_ref=self.place(u, which) if held else self.piece(u),
            dst_ref=self.place(u, which),
            send_sem=self.ds.at[u, (1 << k) - 1 + slot], recv_sem=self.dr.at[u, which],
            device_id={"dp": flipped(self.d, self.order(u)[k : k + 1])}, device_id_type=MESH,
        )

    def arrival(self, u, k, held):
        which = flipped(self.d, held + tuple(self.order(u)[k : k + 1]))
        return pltpu.make_async_remote_copy(
            src_ref=self.piece(u), dst_ref=self.place(u, which),
            send_sem=self.ds.at[u, 0], recv_sem=self.dr.at[u, which],
            device_id={"dp": flipped(self.d, self.order(u)[k : k + 1])}, device_id_type=MESH,
        )

    def units(self, w):
        return range(w * self.parts, (w + 1) * self.parts)

    def begin_round(self, w, k):
        for u in self.units(w):
            for slot, held in enumerate(subsets(self.order(u)[:k])):
                self.start(self.round_copy, u, k, slot, held)

    def collect(self, w):
        self.take(w, self.stages - 1)
        for p in range(self.parts):
            lanes = slice(p * self.cols, (p + 1) * self.cols)
            self.slab[w, p * self.cut : (p + 1) * self.cut] = jnp.concatenate(
                [self.blocks[w, s, :, lanes] for s in range(self.stages)], axis=1
            )
        for u in self.units(w):
            self.own_copy(u).start()

    def advance(self, w, k):
        for u in self.units(w):
            for held in subsets(self.order(u)[:k]):
                self.arrival(u, k, held).wait_recv()
        if k + 1 < self.dp_bits:
            self.begin_round(w, k + 1)
        else:
            for u in self.units(w):
                self.own_copy(u).wait()

    def close(self):
        for make, args, sends in self.sent:
            if sends is None:
                make(*args).wait_send()
            else:

                @pl.when(sends)
                def _():
                    make(*args).wait_send()


def gathering_scratch(count, dp, stages, rows, cols):
    parts = 2 if rows % 32 == 0 else 1
    dma = pltpu.SemaphoreType.DMA
    units = count * parts
    return [
        pltpu.VMEM((count, stages, rows // parts, cols * parts), BF16),
        pltpu.VMEM((count, rows, cols * stages), BF16),
        dma((count, 2 * stages)), dma((count, stages)), dma((units, dp)), dma((units, dp)), dma((units,)),
    ]


def forward_kernel(block, dp_bits, stages, back, *refs):
    weights, refs = refs[:6], refs[6:]
    tokens, vectors, segments = refs[:3]
    gain, factor = vectors.at[0:1], vectors.at[1:2]
    fulls, refs = refs[3:9], refs[9:]
    bias_full, raw_out, q_out, k_out, v_out, nt_out, o_ref, lse_ref = refs[:8]
    refs = refs[8:]
    home, window, normed, nt, raw, q, k, v, vt, ot, bias, scores, tops, totals, bias_in, bias_all = refs[:16]
    xs, xr, bs, br, os = refs[16:21]
    d, z = greet(dp_bits, stages)
    rows, features = tokens.shape
    width, heads = k.shape[0], features // HD
    own = width - rows
    tile = 2 * LANES
    homes = [home.at[w] for w in range(3)] + list(fulls[3:])
    work = Gathering(dp_bits, stages, d, z, weights, homes, refs[21:])

    def bias_copy(step):
        return pltpu.make_async_remote_copy(
            src_ref=bias_in, dst_ref=bias_all.at[step], send_sem=bs.at[step],
            recv_sem=br.at[step], device_id={"mp": lax.rem(z + step, stages)},
            device_id_type=MESH,
        )

    def token_copy(hop):
        return pltpu.make_async_remote_copy(
            src_ref=tokens if hop == 0 else window.at[hop - 1], dst_ref=window.at[hop],
            send_sem=xs.at[hop], recv_sem=xr.at[hop],
            device_id={"mp": jnp.minimum(z + 1, stages - 1)}, device_id_type=MESH,
        )

    kept = [
        (raw, raw_out), (q, q_out), (k, k_out), (v, v_out), (nt, nt_out),
        (home.at[0], fulls[0]), (home.at[1], fulls[1]), (home.at[2], fulls[2]),
    ]

    def keep(i):
        return pltpu.make_async_copy(kept[i][0], kept[i][1], os.at[i])

    def norm(src, at):
        step_rows = 128

        def step(i, carry):
            part = pl.ds(pl.multiple_of(i * step_rows, step_rows), step_rows)
            x = src[part, :].astype(F32)
            value = (x * row_inverse(x) * gain[...]).astype(BF16)
            to = pl.ds(pl.multiple_of(at + i * step_rows, step_rows), step_rows)
            normed[to, :] = value
            return carry

        lax.fori_loop(0, rows // step_rows, step, 0)
        for c in range(features // tile):
            lanes = slice(c * tile, (c + 1) * tile)
            nt[lanes, at : at + rows] = normed[at : at + rows, lanes].T

    def project(w, at, out, out_t):
        def step(c, carry):
            lanes = pl.ds(pl.multiple_of(c * tile, tile), tile)
            value = dot(normed[at : at + rows, :], home[w, :, lanes], 1, 0).astype(BF16)
            out[at : at + rows, lanes] = value
            if out_t is not None:
                out_t[lanes, at : at + rows] = value.T
            return carry

        lax.fori_loop(0, features // tile, step, 0)

    def project_both(at):
        def step(c, carry):
            lanes = pl.ds(pl.multiple_of(c * tile, tile), tile)
            source = normed[at : at + rows, :]
            k[at : at + rows, lanes] = dot(source, home[1, :, lanes], 1, 0).astype(BF16)
            value = dot(source, home[2, :, lanes], 1, 0).astype(BF16)
            v[at : at + rows, lanes] = value
            vt[lanes, at : at + rows] = value.T
            return carry

        lax.fori_loop(0, features // tile, step, 0)

    first, rest = range(3), range(3, 6)
    for w in range(6):
        work.pack(w)
    for w in first:
        work.hop(w, 0)
    bias_in[...] = vectors[4:5, : features // stages]
    for step in range(1, stages):
        work.start(bias_copy, step)
    bias_all[0] = bias_in[...]
    for hop in range(back):

        @pl.when(z <= hop)
        def _():
            window[hop] = jnp.zeros((rows, features), BF16)

    norm(tokens, own)
    fill_bias(segments, z, bias, block, own)
    for j in range(1, stages - 1):
        for w in first:
            work.hop(w, j)
    for w in rest:
        work.hop(w, 0)
    for w in first:
        work.collect(w)
        work.begin_round(w, 0)
    for j in range(1, stages - 1):
        if j <= 3 and dp_bits > 1:
            work.advance(j - 1, 0)
        for w in rest:
            work.hop(w, j)

    @pl.when(z < stages - 1)
    def _():
        token_copy(0).start()

    if dp_bits > 1:
        for w in range(max(0, min(stages - 2, 3)), 3):
            work.advance(w, 0)
    for w in rest:
        work.collect(w)
    for r in range(1, dp_bits - 1):
        for w in first:
            work.advance(w, r)
    for w in rest:
        work.begin_round(w, 0)
    for w in first:
        work.advance(w, dp_bits - 1)
        keep(5 + w).start()
        if w == 0:

            def query(c, carry):
                lanes = pl.ds(pl.multiple_of(c * tile, tile), tile)
                value = dot(normed[own:, :], home[0, :, lanes], 1, 0)
                raw[:, lanes] = value
                q[:, lanes] = (value * factor[:, lanes]).astype(BF16)
                return carry

            lax.fori_loop(0, features // tile, query, 0)
            keep(0).start()
            keep(1).start()
        else:
            project(w, own, *((k, None) if w == 1 else (v, vt)))

    sp = spans(rows, width, block)

    def attend(low, high, fresh, last, due):
        tiles = []
        for kb in range(low // block, high // block):
            qs = [i for i, (lo, hi) in enumerate(sp) if lo <= kb * block < hi]
            if qs:
                tiles.append((kb, qs))

        def head(h):
            lanes, mine = head_lanes(h, features)
            feats = pl.ds(pl.multiple_of(h * HD, 16), HD)
            query = jnp.where(mine, q[:, lanes], jnp.zeros((), BF16))
            top = [jnp.full((8, block), FAR, F32) for _ in sp]
            for kb, qs in tiles:
                qa, qz = qs[0] * block, (qs[-1] + 1) * block
                at = slice(kb * block, (kb + 1) * block)
                s = dot(k[at, lanes], query[qa:qz], 1, 1) + bias[at, qa:qz]
                scores[at, qa:qz] = s
                for i in qs:
                    cut = s[:, i * block - qa : (i + 1) * block - qa]
                    top[i] = jnp.maximum(top[i], jnp.max(cut.reshape(block // 8, 8, block), axis=0))
            top = jnp.concatenate([jnp.max(t, axis=0, keepdims=True) for t in top], axis=1)
            if not fresh:
                before = tops[pl.ds(h, 1), :]
                top = jnp.maximum(top, before)
                scale = jnp.exp(before - top)
            acc = [jnp.zeros((HD, block), F32) for _ in sp]
            total = [jnp.zeros((8, block), F32) for _ in sp]
            for kb, qs in tiles:
                qa, qz = qs[0] * block, (qs[-1] + 1) * block
                at = slice(kb * block, (kb + 1) * block)
                p = jnp.exp(scores[at, qa:qz] - top[:, qa:qz])
                part = dot(vt[feats, at], p.astype(BF16), 1, 0)
                for i in qs:
                    cut = slice(i * block - qa, (i + 1) * block - qa)
                    total[i] = total[i] + jnp.sum(p[:, cut].reshape(block // 8, 8, block), axis=0)
                    acc[i] = acc[i] + part[:, cut]
            for i in range(len(sp)):
                at = slice(i * block, (i + 1) * block)
                one = jnp.sum(total[i], axis=0, keepdims=True)
                out = acc[i]
                if not fresh:
                    one = one + totals[pl.ds(h, 1), at] * scale[:, at]
                    out = out + ot[feats, at] * scale[:, at]
                if last:
                    ot[feats, at] = out / one
                    lse_ref[pl.ds(h, 1), at] = top[:, at] + jnp.log(one)
                else:
                    ot[feats, at] = out
                    totals[pl.ds(h, 1), at] = one
                    tops[pl.ds(h, 1), at] = top[:, at]

        def pair(i, carry):
            for at in sorted(set(due.values())):

                @pl.when(2 * i == at)
                def _():
                    for w, r in due:
                        if due[w, r] == at:
                            work.advance(w, r)

            head(2 * i)
            head(2 * i + 1)
            return carry

        lax.fori_loop(0, heads // 2, pair, 0)

    inside, ready = {}, []
    if back and dp_bits > 2:
        inside = {(3, 1): heads * 3 // 8, (4, 1): heads * 5 // 8, (5, 1): heads * 7 // 8}
        ready = [(3, 0), (4, 0), (5, 0)]
    for pair in ready[:1]:
        work.advance(*pair)
    for hop in range(back):
        if hop + 1 == back:
            for pair in ready[1:]:
                work.advance(*pair)
            attend(rows, width, True, False, inside)

        @pl.when(z > hop)
        def _():
            token_copy(hop).wait_recv()

        if hop + 1 < back:

            @pl.when((z > hop) & (z < stages - 1))
            def _():
                token_copy(hop + 1).start()

        at = own - (hop + 1) * rows
        norm(window.at[hop], at)
        project_both(at)
    for i in range(2, 5):
        keep(i).start()
    attend(0, rows if back else width, not back, True, {})
    transpose_out(ot, o_ref)
    for r in range(dp_bits):
        for w in rest:
            if (w, r) not in inside and (w, r) not in ready:
                work.advance(w, r)
    for step in range(1, stages):
        bias_copy(step).wait_recv()
    bias_full[...] = jnp.concatenate(
        [bias_all[lax.rem(z - s + stages, stages)] for s in range(stages)], axis=1
    )
    for hop in range(back):

        @pl.when((z >= hop) & (z < stages - 1))
        def _():
            token_copy(hop).wait_send()

    for i in range(len(kept)):
        keep(i).wait()
    work.close()


def attend_forward(weights, tokens, vectors, segments, block, dp, stages, back):
    held, cols = weights[0].shape
    rows, features = tokens.shape
    width, heads = (back + 1) * rows, features // HD
    hbm = pl.BlockSpec(memory_space=pl.ANY)
    vmem = pl.BlockSpec(memory_space=pltpu.VMEM)
    dma = pltpu.SemaphoreType.DMA
    sds = jax.ShapeDtypeStruct
    return pl.pallas_call(
        functools.partial(forward_kernel, block, dp.bit_length() - 1, stages, back),
        in_specs=[vmem] * 9,
        out_specs=[hbm] * 6 + [vmem] + [hbm] * 5 + [vmem] * 2,
        out_shape=[sds((features, features), BF16)] * 6
        + [
            sds((1, features), F32),
            sds((rows, features), F32),
            sds((rows, features), BF16),
            sds((width, features), BF16),
            sds((width, features), BF16),
            sds((features, width), BF16),
            sds((rows, features), BF16),
            sds((heads, rows), F32),
        ],
        scratch_shapes=[
            pltpu.VMEM((3, features, features), BF16),
            pltpu.VMEM((back, rows, features), BF16),
            pltpu.VMEM((width, features), BF16),
            pltpu.VMEM((features, width), BF16),
            pltpu.VMEM((rows, features), F32),
            pltpu.VMEM((rows, features), BF16),
            pltpu.VMEM((width, features), BF16),
            pltpu.VMEM((width, features), BF16),
            pltpu.VMEM((features, width), BF16),
            pltpu.VMEM((features, rows), F32),
            pltpu.VMEM((width, rows), F32),
            pltpu.VMEM((width, rows), F32),
            pltpu.VMEM((heads, rows), F32),
            pltpu.VMEM((heads, rows), F32),
            pltpu.VMEM((1, features // stages), F32),
            pltpu.VMEM((stages, 1, features // stages), F32),
            dma((back,)), dma((back,)), dma((stages,)), dma((stages,)), dma((8,)),
        ]
        + gathering_scratch(6, dp, stages, held, cols),
        compiler_params=pltpu.CompilerParams(
            collective_id=0, has_side_effects=True, vmem_limit_bytes=62 << 20
        ),
        name="attend_forward",
    )(*weights, tokens, vectors, segments)


def middle_kernel(block, dp_bits, stages, *refs):
    sources, refs = refs[:12], refs[12:]
    b_up, vectors, lse_ref, segments = refs[:4]
    factor, gain, b_down = (vectors.at[i : i + 1] for i in (1, 2, 3))
    results, incoming, outs, sums, refs = refs[4:10], refs[10], refs[11:14], refs[14], refs[15:]
    weights, hidden, wide, tmp, tr, keys, values, query_in, grad_in, bias, delta_ref = refs[:11]
    ps, pr, sems, refs = refs[11], refs[12], refs[13], refs[14:]
    d, z = greet(dp_bits, stages)
    work = Reduction(dp_bits, stages, d, z, None, outs, refs)
    rows, features = query_in.shape
    heads, width = features // HD, keys.shape[0]
    back = width // rows - 1
    tile = 2 * LANES
    w_out, w_up, w_down = weights.at[0], weights.at[1], weights.at[2]
    w_key, w_value = weights.at[2], weights.at[1]
    mixed, cot, x, second, active, d_pre, d_attn, spare = (tmp.at[i] for i in range(8))
    dk, dv = tmp.at[: back + 1], tmp.at[back + 1 : 2 * back + 2]
    dq, part = tmp.at[2 * back + 2], tmp.at[2 * back + 3]
    inside = (
        mixed, w_out, x, cot, w_up, w_down, keys, values, query_in, w_key, w_value, hidden,
    )
    half = rows // 2
    outside = (spare, hidden, dq, dk, dv, part.at[half:])
    loads = Loads(list(zip(sources, inside)) + list(zip(outside, results)), sems)
    loads.start(*range(9))
    fill_bias(segments, z, bias, block, width - rows)

    def by_tile(body):
        for c in range(features // tile):
            body(slice(c * tile, (c + 1) * tile), c)

    def by_rows(body, start):
        def step(i, carry):
            return body(pl.ds(pl.multiple_of(i * 64, 64), 64), carry)

        return lax.fori_loop(0, rows // 64, step, start)

    def flip(src):
        for c in range(features // tile):
            lanes = slice(c * tile, (c + 1) * tile)
            tr[lanes, :] = src[:, lanes].T

    nothing = jnp.zeros((1, features), F32)

    def add_attention(lanes, c):
        hidden[:, lanes] = x[:, lanes].astype(F32) + dot(mixed[...], w_out[lanes, :], 1, 1)

    def norm(at, carry):
        h = hidden[at, :]
        second[at, :] = (h * row_inverse(h) * gain[...]).astype(BF16)
        return carry

    def activate(lanes, c):
        pre = dot(second[...], w_up[:, lanes], 1, 0) + b_up[:, lanes]
        sigma = 1.0 / (1.0 + jnp.exp(-pre))
        active[:, lanes] = (pre * sigma).astype(BF16)
        grad = dot(cot[...], w_down[:, lanes], 1, 0)
        grad = (grad * sigma * (1.0 + pre * (1.0 - sigma))).astype(BF16)
        d_pre[:, lanes] = grad
        sums[2:3, lanes] = jnp.sum(grad.astype(F32), axis=0, keepdims=True)

    def finish_layer(lanes, c):
        out = dot(active[...], w_down[lanes, :], 1, 1)
        spare[:, lanes] = (hidden[:, lanes] + out + b_down[:, lanes]).astype(BF16)
        sums[1:2, lanes] = jnp.sum(cot[:, lanes].astype(F32), axis=0, keepdims=True)

    def to_second(lanes, c):
        wide[:, lanes] = dot(d_pre[...], w_up[lanes, :], 1, 1)

    def to_hidden(at, column):
        h, grad = hidden[at, :], wide[at, :]
        inverse = row_inverse(h)
        weighted = grad * gain[...]
        dots = jnp.sum(weighted * h, axis=1, keepdims=True)
        cube = inverse * inverse * inverse
        d_hidden = cot[at, :].astype(F32) + inverse * weighted - h * cube / features * dots
        hidden[at, :] = d_hidden
        d_attn[at, :] = d_hidden.astype(BF16)
        return column + jnp.sum(grad * h * inverse, axis=0, keepdims=True)

    def to_mixed(lanes, c):
        grad = dot(d_attn[...], w_out[:, lanes], 1, 0).astype(BF16)
        grad_in[:, lanes] = grad
        both = grad.astype(F32) * mixed[:, lanes].astype(F32)
        lane = lax.broadcasted_iota(jnp.int32, (heads, tile), 1) + c * tile
        first = lax.broadcasted_iota(jnp.int32, (heads, tile), 0) * HD
        owner = jnp.where((lane >= first) & (lane < first + HD), 1.0, 0.0).astype(BF16)
        high = both.astype(BF16)
        rest = (both - high.astype(F32)).astype(BF16)
        delta_ref[...] += dot(owner, high, 1, 1) + dot(owner, rest, 1, 1)

    sums[3:8, :] = jnp.zeros((5, features), F32)
    delta_ref[...] = jnp.zeros_like(delta_ref)
    loads.wait(0, 1, 2)
    by_tile(add_attention)
    by_rows(norm, 0)
    loads.wait(3, 4, 5)
    by_tile(activate)
    flip(cot)
    work.weight_grad(0, lambda at: tr[at, :], lambda: active[...])
    by_tile(finish_layer)
    loads.start(12, 9)
    by_tile(to_second)
    loads.start(10)
    flip(second)
    work.weight_grad(1, lambda at: tr[at, :], lambda: d_pre[...])
    work.advance(0, 0)
    sums[0:1, :] = by_rows(to_hidden, nothing)
    loads.start(13)
    by_tile(to_mixed)
    flip(d_attn)
    work.weight_grad(2, lambda at: tr[at, :], lambda: mixed[...])
    work.advance(1, 0)
    if dp_bits > 1:
        work.advance(0, 1)
    loads.wait(12)
    for c in range(2 * back + 2):
        tmp[c] = jnp.zeros((rows, features), BF16)
    wide[...] = jnp.zeros_like(wide)
    loads.wait(6, 7, 8)
    sp = spans(rows, width, block)
    steps = heads * (back + 1)
    events = [(2, 0)] + [(w, k) for w in range(3) for k in range(1, dp_bits) if (w, k) != (0, 1)]
    due = {i: int(at * steps) // 2 * 2 for i, at in enumerate(EVENTS[: len(events)])}

    def down():
        return pltpu.make_async_remote_copy(
            src_ref=part.at[:half], dst_ref=incoming, send_sem=ps, recv_sem=pr,
            device_id={"mp": jnp.maximum(z - 1, 0)}, device_id_type=MESH,
        )

    for c in range(back + 1):

        def head(h):
            lanes, mine = head_lanes(h, features)
            zero = jnp.zeros((), BF16)
            query = jnp.where(mine, query_in[:, lanes], zero)
            grad = jnp.where(mine, grad_in[:, lanes], zero)
            lse = lse_ref[pl.ds(h, 1), :]
            delta = delta_ref[pl.ds(h, 1), :]
            for kb in range(c * rows // block, (c + 1) * rows // block):
                qs = [i for i, (lo, hi) in enumerate(sp) if lo <= kb * block < hi]
                if not qs:
                    continue
                qa, qz = qs[0] * block, (qs[-1] + 1) * block
                at = slice(kb * block, (kb + 1) * block)
                to = slice(kb * block - c * rows, (kb + 1) * block - c * rows)
                key = keys[at, lanes]
                s = dot(key, query[qa:qz], 1, 1) + bias[at, qa:qz]
                p = jnp.exp(s - lse[:, qa:qz])
                dp = dot(values[at, lanes], grad[qa:qz], 1, 1)
                ds = (p * (dp - delta[:, qa:qz])).astype(BF16)
                dv[c, to, lanes] += dot(p.astype(BF16), grad[qa:qz], 1, 0).astype(BF16)
                dk[c, to, lanes] += dot(ds, query[qa:qz], 1, 0).astype(BF16)
                wide[qa:qz, lanes] += dot(ds, jnp.where(mine, key, zero), 0, 0)

        def pair(i, carry):
            for at in sorted(set(due.values())):
                if at // heads != c:
                    continue

                @pl.when(2 * i == at % heads)
                def _():
                    for e in due:
                        if due[e] == at:
                            work.advance(*events[e])

            head(2 * i)
            head(2 * i + 1)
            return carry

        lax.fori_loop(0, heads // 2, pair, 0)
        if c == 0:
            loads.wait(9, 10)
            if back:
                back_project(part, ((dk.at[0], w_key), (dv.at[0], w_value)), 0, None)
                loads.start(17)

                @pl.when(z >= back)
                def _():
                    down().start()

            loads.wait(13)
            loads.start(11)

    loads.start(15, 16)
    loads.wait(11)

    def to_query(at, column):
        scaled = wide[at, :].astype(BF16).astype(F32)
        dq[at, :] = (scaled * factor[...]).astype(BF16)
        return column + jnp.sum(scaled * hidden[at, :], axis=0, keepdims=True)

    sums[4:5, :] = by_rows(to_query, nothing)
    loads.start(14)
    for i in range(len(due), len(events)):
        work.advance(*events[i])
    for w in range(3):
        work.finish(w)
    loads.wait(14, 15, 16)
    if back:
        loads.wait(17)

        @pl.when((z + 1 >= back) & (z < stages - 1))
        def _():
            down().wait_recv()

        @pl.when(z >= back)
        def _():
            down().wait_send()

    work.close()


def back_project(out, pairs, at, more):
    rows, features = out.shape
    tile = 2 * LANES

    def step(c, carry):
        lanes = pl.ds(pl.multiple_of(c * tile, tile), tile)
        value = None
        for grad, weight in pairs:
            start = at if grad.shape[0] > rows else 0
            term = dot(grad[start : start + rows, :], weight[lanes, :], 1, 1)
            value = term if value is None else value + term
        if more is not None:
            value = value + more(lanes)
        out[:, lanes] = value.astype(out.dtype)
        return carry

    lax.fori_loop(0, features // tile, step, 0)


def middle(
    mixed, w_out, x, cot, w_up, w_down, k, v, q, w_key, w_value, raw, b_up, vectors,
    lse, segments, block, dp, stages,
):
    rows, features = q.shape
    width, heads = k.shape[0], features // HD
    held, cols = features // dp, features // stages
    chunks = width // rows
    hbm = pl.BlockSpec(memory_space=pl.ANY)
    vmem = pl.BlockSpec(memory_space=pltpu.VMEM)
    dma = pltpu.SemaphoreType.DMA
    sds = jax.ShapeDtypeStruct
    low, high = sds((rows, features), BF16), sds((rows, features), F32)
    many, part = sds((chunks, rows, features), BF16), sds((rows // 2, features), BF16)
    return pl.pallas_call(
        functools.partial(middle_kernel, block, dp.bit_length() - 1, stages),
        in_specs=[hbm] * 12 + [vmem] * 4,
        out_specs=[hbm] * 7 + [vmem] * 4,
        out_shape=[low, high, low, many, many, part, part]
        + [sds((held, cols), F32)] * 3
        + [sds((8, features), F32)],
        scratch_shapes=[
            pltpu.VMEM((3, features, features), BF16),
            pltpu.VMEM((rows, features), F32),
            pltpu.VMEM((rows, features), F32),
            pltpu.VMEM((max(8, 2 * chunks + 2), rows, features), BF16),
            pltpu.VMEM((features, rows), BF16),
            pltpu.VMEM((width, features), BF16),
            pltpu.VMEM((width, features), BF16),
            pltpu.VMEM((rows, features), BF16),
            pltpu.VMEM((rows, features), BF16),
            pltpu.VMEM((width, rows), F32),
            pltpu.VMEM((heads, rows), F32),
            dma, dma, dma((18,)),
        ]
        + reduction_scratch(3, dp, stages, held, features, True),
        compiler_params=pltpu.CompilerParams(
            collective_id=2, has_side_effects=True, vmem_limit_bytes=63 << 20
        ),
        name="middle",
    )(
        mixed, w_out, x, cot, w_up, w_down, k, v, q, w_key, w_value, raw, b_up, vectors,
        lse, segments,
    )


def input_kernel(dp_bits, stages, back, *refs):
    sources, farther, vectors, sums, refs = refs[:10], refs[10], refs[11], refs[12], refs[13:]
    gain = vectors.at[0:1]
    outs, result, total, refs = refs[:3], refs[3], refs[4], refs[5:]
    inside, tokens_grad, refs = refs[:10], refs[10], refs[11:]
    dv, nt, dk, wk, wv, incoming, dq, wq, tokens, d_hidden = inside
    part, landed, d_first, mine, sgot, zgot, ss, sr, ps, pr, sems = refs[:11]
    d, z = greet(dp_bits, stages, True)
    work = Reduction(dp_bits, stages, d, z, None, outs, refs[11:])
    rows, features = tokens.shape
    own, half = back * rows, rows // 2
    inside = inside[:5] + (incoming.at[:half],) + inside[6:]
    loads = Loads(list(zip(sources, inside)) + [(tokens_grad, result)], sems)
    dp = 1 << dp_bits
    held = features >> dp_bits
    grads = {0: (dq, own), 1: (dk, 0), 2: (dv, 0)}

    def down(hop):
        return pltpu.make_async_remote_copy(
            src_ref=part.at[hop - 1] if hop else farther,
            dst_ref=landed.at[hop - 1] if hop else incoming.at[half:],
            send_sem=ps.at[hop], recv_sem=pr.at[hop],
            device_id={"mp": jnp.maximum(z - 1, 0)}, device_id_type=MESH,
        )

    if back:

        @pl.when(z >= back)
        def _():
            down(0).start()

    loads.start(*range(10))

    def arrived(hop):
        source = incoming if hop == 1 else landed.at[hop - 2]
        there = (z + 1 >= back - hop + 1) & (z < stages - 1)

        def take(lanes):
            return jnp.where(there, source[:, lanes].astype(F32), 0.0)

        return there, take

    def weight_grad(w):
        grad, at = grads[w]
        work.weight_grad(w, lambda rows_at: nt[rows_at, at:], lambda: grad[...])

    def sum_copy(axis, step):
        if axis == "dp":
            to, source, target, at = lax.rem(d + step, dp), mine, sgot, step
        else:
            to, source, target, at = lax.rem(z + step, stages), sgot.at[0], zgot, dp + step
        return pltpu.make_async_remote_copy(
            src_ref=source, dst_ref=target.at[step], send_sem=ss.at[at], recv_sem=sr.at[at],
            device_id={axis: to}, device_id_type=MESH,
        )

    def sum_dp():
        for step in range(1, dp):
            sum_copy("dp", step).wait_recv()
        sgot[0] = mine[...]
        value = sgot[lax.rem(d, dp)]
        for e in range(1, dp):
            value = value + sgot[lax.rem(d - e + dp, dp)]
        sgot[0] = value
        for step in range(1, stages):
            work.start(sum_copy, "mp", step)

    def sum_mp():
        for step in range(1, stages):
            sum_copy("mp", step).wait_recv()
        zgot[0] = sgot[0]
        value = zgot[lax.rem(z, stages)]
        for e in range(1, stages):
            value = value + zgot[lax.rem(z - e + stages, stages)]
        total[...] = value

    def pass_down(hop):
        there, take = arrived(hop)
        back_project(d_first, ((dk, wk), (dv, wv)), hop * rows, None)
        if hop == 1:
            work.advance(2, 0)
            weight_grad(1)

        @pl.when(there)
        def _():
            down(hop - 1).wait_recv()

        for c in range(features // LANES):
            lanes = slice(c * LANES, (c + 1) * LANES)
            part[hop - 1, :, lanes] = (d_first[:, lanes] + take(lanes)).astype(BF16)

        @pl.when(z >= back - hop)
        def _():
            down(hop).start()

    loads.wait(0, 1)
    weight_grad(2)
    loads.wait(2, 3, 4, 5)
    if back > 1:
        pass_down(1)
    else:
        work.advance(2, 0)
        weight_grad(1)
    work.advance(1, 0)
    loads.wait(6, 7)
    weight_grad(0)
    for hop in range(2, back):
        pass_down(hop)
    work.advance(0, 0)
    back_project(d_first, ((dk, wk), (dv, wv), (dq, wq)), own, None)
    events = [(w, k) for w in (2, 1, 0) for k in range(1, dp_bits)]
    for event in events[:-2]:
        work.advance(*event)
    loads.wait(8, 9)
    there, take = arrived(back) if back else (None, None)
    if back:

        @pl.when(there)
        def _():
            down(back - 1).wait_recv()

    chunk = 64

    def finish(i, column):
        at = pl.ds(pl.multiple_of(i * chunk, chunk), chunk)
        x = tokens[at, :].astype(F32)
        grad = d_first[at, :]
        if back:
            source = incoming if back == 1 else landed.at[back - 2]
            grad = grad + jnp.where(there, source[at, :].astype(F32), 0.0)
        inverse = row_inverse(x)
        weighted = grad * gain[...]
        dots = jnp.sum(weighted * x, axis=1, keepdims=True)
        cube = inverse * inverse * inverse
        tokens_grad[at, :] = (
            d_hidden[at, :] + inverse * weighted - x * cube / features * dots
        ).astype(BF16)
        return column + jnp.sum(grad * x * inverse, axis=0, keepdims=True)

    column = lax.fori_loop(0, rows // chunk, finish, jnp.zeros((1, features), F32))
    mine[...] = sums[...]
    mine[3:4, :] = column
    for step in range(1, dp):
        work.start(sum_copy, "dp", step)
    loads.start(10)
    follow = [sum_dp, sum_mp]
    for event in events[-2:]:
        work.advance(*event)
        if follow:
            follow.pop(0)()
    for other in follow:
        other()
    for w in (2, 1, 0):
        work.finish(w)
    for hop in range(back):

        @pl.when(z >= back - hop)
        def _():
            down(hop).wait_send()

    loads.wait(10)
    work.close()


def input_gradients(
    nt, dq, dk, dv, wq, wk, wv, incoming, farther, tokens, d_hidden, vectors, sums, dp, stages
):
    rows, features = tokens.shape
    back = dk.shape[0] // rows - 1
    held, cols = features // dp, features // stages
    dp_bits = dp.bit_length() - 1
    hbm = pl.BlockSpec(memory_space=pl.ANY)
    vmem = pl.BlockSpec(memory_space=pltpu.VMEM)
    dma = pltpu.SemaphoreType.DMA
    hops = max(1, back - 1)
    sources = (dv, nt, dk, wk, wv, incoming, dq, wq, tokens, d_hidden)
    out = pl.pallas_call(
        functools.partial(input_kernel, dp_bits, stages, back),
        in_specs=[hbm] * 11 + [vmem] * 2,
        out_specs=[vmem] * 3 + [hbm, vmem],
        out_shape=[jax.ShapeDtypeStruct((held, cols), F32)] * 3
        + [
            jax.ShapeDtypeStruct((rows, features), BF16),
            jax.ShapeDtypeStruct(sums.shape, F32),
        ],
        scratch_shapes=[pltpu.VMEM(tokens.shape if a is incoming else a.shape, a.dtype) for a in sources + (tokens,)]
        + [
            pltpu.VMEM((hops, rows, features), BF16), pltpu.VMEM((hops, rows, features), BF16),
            pltpu.VMEM((rows, features), F32), pltpu.VMEM(sums.shape, F32),
            pltpu.VMEM((dp,) + sums.shape, F32), pltpu.VMEM((stages,) + sums.shape, F32),
            dma((dp + stages,)), dma((dp + stages,)), dma((hops + 1,)), dma((hops + 1,)), dma((11,)),
        ]
        + reduction_scratch(3, dp, stages, held, features, True),
        compiler_params=pltpu.CompilerParams(
            collective_id=1, has_side_effects=True, vmem_limit_bytes=62 << 20
        ),
        name="input_gradients",
    )(*sources, farther, vectors, sums)
    return out[:3], out[3], out[4]


def hand_over_kernel(*refs):
    half = len(refs) // 2
    for source, result in zip(refs[:half], refs[half:]):
        result[...] = source[...]


def hand_over(arrays):
    vmem = pl.BlockSpec(memory_space=pltpu.VMEM)
    return pl.pallas_call(
        hand_over_kernel,
        in_specs=[vmem] * len(arrays),
        out_specs=[vmem] * len(arrays),
        out_shape=[jax.ShapeDtypeStruct(a.shape, a.dtype) for a in arrays],
        name="hand_over",
    )(*arrays)


def body(
    tokens, segments, w_query, w_key, w_value, w_output, w_up, b_up, w_down, b_down,
    gain_attn, gain_mlp, query_scale, cotangent,
):
    stages = lax.axis_size("mp")
    z = lax.axis_index("mp")
    rows, features = tokens.shape
    back = min(stages - 1, -(-(DOC_MAX - 1) // rows))
    own = back * rows
    block = min(256, rows)
    heads = features // HD
    dp = lax.axis_size("dp")
    factor = jax.nn.softplus(query_scale) * (LOG2E / math.sqrt(HD))
    mine = b_up.shape[0]
    vectors = jnp.zeros((8, features), F32)
    row = lax.broadcasted_iota(jnp.int32, (8, features), 0)
    given = (gain_attn, jnp.tile(factor, heads), gain_mlp, b_down, jnp.pad(b_up, (0, features - mine)))
    for i, value in enumerate(given):
        vectors = jnp.where(row == i, value[None], vectors)
    (
        wq, wk, wv, wu, wo, wd, b_full, query_raw, scaled, keys, values, first_t, mixed, lse
    ) = attend_forward(
        (w_query, w_key, w_value, w_up, w_output.T, w_down.T), tokens, vectors, segments,
        block, dp, stages, back,
    )
    layer_out, d_hidden, d_query, d_keys, d_values, farther, incoming, *mlp, sums = middle(
        mixed, wo, tokens, cotangent, wu, wd, keys, values, scaled, wk, wv, query_raw,
        b_full, vectors, lse, segments, block, dp, stages,
    )
    grads, tokens_grad, sums = input_gradients(
        first_t, d_query, d_keys.reshape(own + rows, features),
        d_values.reshape(own + rows, features), wq, wk, wv, incoming, farther, tokens,
        d_hidden, vectors, sums, dp, stages,
    )
    sum_b_up = lax.dynamic_slice_in_dim(sums[2], z * mine, mine, 0)
    scale_total = jnp.sum(sums[4].reshape(heads, HD), axis=0)
    grad_query_scale = scale_total * (LOG2E / math.sqrt(HD)) * jax.nn.sigmoid(query_scale)
    layer_out, tokens_grad, g_query, g_key, g_value, g_up, g_output, g_down = hand_over(
        (layer_out, tokens_grad, *grads, mlp[1], mlp[2], mlp[0])
    )
    return (
        layer_out, tokens_grad, g_query, g_key, g_value, g_output.T, g_up, sum_b_up,
        g_down.T, sums[1], sums[3], sums[0], grad_query_scale,
    )


def solution(mesh):
    tokens, rows_dp, rows_mp = P(("dp", "mp"), None), P("dp", "mp"), P("mp", "dp")
    return jax.shard_map(
        body,
        mesh=mesh,
        in_specs=(
            tokens, P("dp", None), rows_dp, rows_dp, rows_dp, rows_mp, rows_dp, P("mp"), rows_mp,
            P(), P(), P(), P(), tokens,
        ),
        out_specs=(
            tokens, tokens, rows_dp, rows_dp, rows_dp, rows_mp, rows_dp, P("mp"), rows_mp,
            P(), P(), P(), P(),
        ),
        check_vma=False,
    )
```
